32 devices in a mesh: clip: 8 (over z, core), frame: 4 (over y, x).
Axes of the slice: x: 2, y: 2, z: 4, core: 2. Of those that a mesh axis runs over, the one named last changes fastest.
Arguments:
- block_input: bfloat16 [16, 16, 64, 1152], P('clip', 'frame'), may hold values from -6 to 6
- modulation: bfloat16 [16, 6912], P('clip'), may hold values from -4 to 4
- frame_counts: int32 [16], P('clip'), may hold values from 8 to 16, as said below
- qkv_weight: bfloat16 [1152, 3456], replicated, may hold values from -0.1875 to 0.1875
- qv_bias: bfloat16 [2304], replicated, may hold values from -3 to 3
- out_weight: bfloat16 [1152, 1152], replicated, may hold values from -0.375 to 0.375
- out_bias: bfloat16 [1152], replicated, may hold values from -3 to 3
- fc1_weight: bfloat16 [1152, 4608], replicated, may hold values from -0.1875 to 0.1875
- fc1_bias: bfloat16 [4608], replicated, may hold values from -3 to 3
- fc2_weight: bfloat16 [4608, 1152], replicated, may hold values from -0.09375 to 0.09375
- fc2_bias: bfloat16 [1152], replicated, may hold values from -3 to 3
- out_cotangent: bfloat16 [16, 16, 64, 1152], P('clip', 'frame'), may hold values from -6 to 6
Outputs:
- block_output: bfloat16 [16, 16, 64, 1152], P('clip', 'frame')
- input_grad: bfloat16 [16, 16, 64, 1152], P('clip', 'frame')
- modulation_grad: float32 [16, 6912], P('clip', 'frame')
- qkv_weight_grad: float32 [1152, 3456], P('clip', 'frame')
- qv_bias_grad: float32 [2304], P('frame')
- out_weight_grad: float32 [1152, 1152], P('clip', 'frame')
- out_bias_grad: float32 [1152], P('frame')
- fc1_weight_grad: float32 [1152, 4608], P('clip', 'frame')
- fc1_bias_grad: float32 [4608], P('frame')
- fc2_weight_grad: float32 [4608, 1152], P('clip', 'frame')
- fc2_bias_grad: float32 [1152], P('frame')
The draws below stay inside these ranges and needn't reach their ends.
Inputs may be any that keep to these rules, and one draw needn't show every extreme that they name: `frame_counts`: each clip holds 8 to 16 frames in its leading slots; some clip holds 16 and some other clip 16 // 2.
All inputs are finite; a program needn't handle non-finite values.
Results may differ from the reference program's by a relative error of at most 0.013.
The reference program's roundings to bfloat16 on the way count: a program that leaves them out, or rounds other values in their place, can miss the bound.
Values may be sent and summed in bfloat16 or wider, within the bound.
A program may use at most 256 MiB of HBM per device.

```python
import jax
import jax.numpy as jnp
from jax import lax

D = 1152
HEADS = 16
FF = 4608
FRAMES = 16
CLIPS = 16
PATCHES = 64


def draw_frame_counts(key, part):
    counts = jax.random.randint(jax.random.fold_in(key, 11), (CLIPS,), FRAMES // 2, FRAMES + 1)
    longest = jax.random.randint(jax.random.fold_in(key, 12), (), 0, CLIPS)
    offset = jax.random.randint(jax.random.fold_in(key, 13), (), 1, CLIPS)
    shortest = (longest + offset) % CLIPS
    counts = counts.at[longest].set(FRAMES)
    counts = counts.at[shortest].set(FRAMES // 2)
    return counts.astype(jnp.int32)


def level_of(stream_key, extent, cuts, least, high):
    gain, own = 1.0, jax.random.fold_in(stream_key, 6)
    for axis_at, blocks in cuts:
        heights = jnp.exp(jax.random.uniform(jax.random.fold_in(own, axis_at), (blocks,), jnp.float32, least / len(cuts), high / len(cuts)))
        gain = gain * jnp.repeat(heights, extent[axis_at] // blocks).reshape([-1 if axis == axis_at else 1 for axis in range(len(extent))])
    return gain


def gaussian(key, dims, deviation, limit, cuts=(), kind=jnp.bfloat16):
    values = deviation * jax.random.normal(key, dims, jnp.float32)
    if cuts:
        values = values * level_of(key, dims, cuts, -0.22, 0.18)
    return jnp.clip(values, -limit, limit).astype(kind)


def setup_inputs(seed: int = 0) -> dict:
    key_of = jax.random.split(jax.random.key(seed), 13)
    return {
        "block_input": gaussian(key_of[0], (CLIPS, FRAMES, PATCHES, D), 1.0, 6.0, ((0, 8), (1, 4))),
        "modulation": gaussian(key_of[1], (CLIPS, 6 * D), 0.7, 4.0, ((0, 8),)),
        "frame_counts": draw_frame_counts(jax.random.fold_in(key_of[12], 71), 0),
        "qkv_weight": gaussian(key_of[3], (D, 3 * D), D ** -0.5, 0.1875),
        "qv_bias": gaussian(key_of[4], (2 * D,), 0.5, 3.0),
        "out_weight": gaussian(key_of[5], (D, D), (D // 4) ** -0.5, 0.375),
        "out_bias": gaussian(key_of[6], (D,), 0.5, 3.0),
        "fc1_weight": gaussian(key_of[7], (D, FF), D ** -0.5, 0.1875),
        "fc1_bias": gaussian(key_of[8], (FF,), 0.5, 3.0),
        "fc2_weight": gaussian(key_of[9], (FF, D), FF ** -0.5, 0.09375),
        "fc2_bias": gaussian(key_of[10], (D,), 0.5, 3.0),
        "out_cotangent": gaussian(key_of[11], (CLIPS, FRAMES, PATCHES, D), 1.0, 6.0, ((0, 8), (1, 4))),
    }


@jax.custom_vjp
def low(v):
    return lax.optimization_barrier(v.astype(jnp.bfloat16)).astype(jnp.float32)

@jax.custom_vjp
def low_back(v):
    return v

def low_keep(v):
    return (low(v), None)

def low_pass(kept, grad):
    return (grad,)

def back_keep(v):
    return (v, None)

def back_low(kept, grad):
    return (low(grad),)
low.defvjp(low_keep, low_pass)
low_back.defvjp(back_keep, back_low)
EPSILON = 1e-06
NEGATIVE = -1e+30
HIGHEST = lax.Precision.HIGHEST

def normalize(values):
    centred = values - lax.optimization_barrier(jnp.mean(values, axis=-1, keepdims=True))
    variance = lax.optimization_barrier(jnp.mean(centred * centred, axis=-1, keepdims=True))
    return centred * lax.rsqrt(variance + EPSILON)

def modulate(values, shift_term, scale_term):
    return normalize(values) * (1.0 + scale_term) + shift_term

def clip_forward(clip_in, clip_mods, parameters, frame_valid):
    qkv_weight, qv_bias, out_weight, out_bias, fc1_weight, fc1_bias, fc2_weight, fc2_bias = parameters
    frames = clip_in.shape[0]
    patches = clip_in.shape[1]
    model_width = clip_in.shape[2]
    head_width = model_width // HEADS
    normed_one = low(modulate(clip_in, clip_mods[0], clip_mods[1]))
    bias_full = jnp.concatenate([qv_bias[:model_width], jnp.zeros((model_width,), jnp.float32), qv_bias[model_width:]])
    projected = jnp.einsum('fpd,de->fpe', normed_one, qkv_weight, precision=HIGHEST) + bias_full
    projected = low(low_back(projected))
    shaped = projected.reshape(frames, patches, 3, HEADS, head_width)
    queries = shaped[:, :, 0]
    keys_all = shaped[:, :, 1]
    values_all = shaped[:, :, 2]
    scores = jnp.einsum('fphd,gphd->phfg', queries, keys_all, precision=HIGHEST) * head_width ** (-0.5)
    scores = low_back(scores)
    scores = jnp.where(frame_valid[None, None, None, :] > 0.5, scores, NEGATIVE)
    row_peak = lax.optimization_barrier(jnp.max(scores, axis=-1, keepdims=True))
    exponent = jnp.exp(scores - row_peak)
    attention_weights = exponent / lax.optimization_barrier(jnp.sum(exponent, axis=-1, keepdims=True))
    weights_low = low(attention_weights)
    context = jnp.einsum('phfg,gphd->fphd', weights_low, values_all, precision=HIGHEST)
    context = low(low_back(context.reshape(frames, patches, model_width)))
    attended = jnp.einsum('fpd,de->fpe', context, out_weight, precision=HIGHEST) + out_bias
    attended = low_back(attended)
    middle = clip_in + clip_mods[2] * attended
    normed_two = low(modulate(middle, clip_mods[3], clip_mods[4]))
    hidden = jnp.einsum('fpd,de->fpe', normed_two, fc1_weight, precision=HIGHEST) + fc1_bias
    hidden = low_back(hidden)
    activated = low(jax.nn.gelu(hidden, approximate=True))
    branch_two = jnp.einsum('fpe,ed->fpd', activated, fc2_weight, precision=HIGHEST) + fc2_bias
    branch_two = low_back(branch_two)
    return frame_valid[:, None, None] * (middle + clip_mods[5] * branch_two)

def reference(block_input, modulation, frame_counts, qkv_weight, qv_bias, out_weight, out_bias, fc1_weight, fc1_bias, fc2_weight, fc2_bias, out_cotangent):
    parameters = tuple((matrix.astype(jnp.float32) for matrix in (qkv_weight, qv_bias, out_weight, out_bias, fc1_weight, fc1_bias, fc2_weight, fc2_bias)))
    inputs = block_input.astype(jnp.float32)
    cotangent = out_cotangent.astype(jnp.float32)
    modulators = modulation.astype(jnp.float32).reshape(CLIPS, 6, D)
    valid = (jnp.arange(FRAMES).astype(jnp.int32)[None, :] < frame_counts.astype(jnp.int32)[:, None]).astype(jnp.float32)

    def per_clip(totals, pieces):
        clip_in, clip_mods, frame_valid, clip_cot = pieces

        def wrapped(inputs_here, mods_here, params_here):
            return clip_forward(inputs_here, mods_here, params_here, frame_valid)
        output, pullback = jax.vjp(wrapped, clip_in, clip_mods, parameters)
        d_input, d_mods, d_params = pullback(clip_cot)
        totals = jax.tree.map(jnp.add, totals, d_params)
        return (totals, (output.astype(jnp.bfloat16), d_input.astype(jnp.bfloat16), d_mods.reshape(6 * D)))
    initial = jax.tree.map(jnp.zeros_like, parameters)
    totals, stacked = lax.scan(per_clip, initial, (inputs, modulators, valid, cotangent))
    outputs, input_grads, modulation_grads = stacked
    return (outputs, input_grads, modulation_grads, totals[0], totals[1], totals[2], totals[3], totals[4], totals[5], totals[6], totals[7])
```

```python
import jax
import jax.numpy as jnp
from jax import lax
from jax.experimental import pallas as pl
from jax.experimental.pallas import tpu as pltpu
from jax.sharding import PartitionSpec as P

HEADS = 16


EPSILON = 1e-06
NEGATIVE = -1e30


def normalize(values):
    centred = values - jnp.mean(values, axis=-1, keepdims=True)
    variance = jnp.mean(centred * centred, axis=-1, keepdims=True)
    return centred * lax.rsqrt(variance + EPSILON)


def modulate(values, shift_term, scale_term):
    return normalize(values) * (1.0 + scale_term) + shift_term


def gelu_tanh(inputs):
    return jax.nn.gelu(inputs, approximate=True)


def contract_rows(left, right):
    return lax.dot_general(
        left, right, (((0,), (0,)), ((), ())), preferred_element_type=jnp.float32
    )


def contract_cols(left, right):
    return lax.dot_general(
        left, right, (((1,), (1,)), ((), ())), preferred_element_type=jnp.float32
    )


def on_device(
    block_input,
    modulation,
    frame_counts,
    qkv_weight,
    qv_bias,
    out_weight,
    out_bias,
    fc1_weight,
    fc1_bias,
    fc2_weight,
    fc2_bias,
    out_cotangent,
):
    swapped = lax.all_to_all(block_input, "frame", split_axis=2, concat_axis=1, tiled=True)
    clip_count, frames, patches, model_width = swapped.shape
    head_width = model_width // HEADS
    row_count = clip_count * frames * patches
    factor = head_width ** (-0.5)
    frame_valid = (jnp.arange(frames)[None, :] < frame_counts[:, None]).astype(jnp.float32)
    valid_rows = frame_valid[:, :, None, None]
    key_valid = frame_valid[:, None, None, None, :] > 0.5
    modulators = modulation.astype(jnp.float32).reshape(clip_count, 6, model_width)[
        :, :, None, None, :
    ]
    shift_one = modulators[:, 0]
    scale_one = modulators[:, 1]
    gate_one = modulators[:, 2]
    shift_two = modulators[:, 3]
    scale_two = modulators[:, 4]
    gate_two = modulators[:, 5]
    residual = swapped.astype(jnp.float32)
    normed_full, modulate_back_one = jax.vjp(modulate, residual, shift_one, scale_one)
    normed_one = normed_full.astype(jnp.bfloat16).reshape(row_count, model_width)
    bias_full = jnp.concatenate(
        [qv_bias[:model_width], jnp.zeros((model_width,), jnp.bfloat16), qv_bias[model_width:]]
    ).astype(jnp.float32)
    projected = (
        jnp.dot(normed_one, qkv_weight, preferred_element_type=jnp.float32) + bias_full
    ).astype(jnp.bfloat16)
    shaped = projected.reshape(clip_count, frames, patches, 3, HEADS, head_width)
    queries = shaped[:, :, :, 0]
    keys_all = shaped[:, :, :, 1]
    values_all = shaped[:, :, :, 2]
    scores = (
        jnp.einsum("cfphd,cgphd->cphfg", queries, keys_all, preferred_element_type=jnp.float32)
        * factor
    )
    scores = jnp.where(key_valid, scores, NEGATIVE)
    row_peak = jnp.max(scores, axis=-1, keepdims=True)
    exponent = jnp.exp(scores - row_peak)
    attention_weights = exponent / jnp.sum(exponent, axis=-1, keepdims=True)
    weights_low = attention_weights.astype(jnp.bfloat16)
    context = jnp.einsum(
        "cphfg,cgphd->cfphd", weights_low, values_all, preferred_element_type=jnp.float32
    )
    context_low = context.astype(jnp.bfloat16).reshape(row_count, model_width)
    attended = jnp.dot(
        context_low, out_weight, preferred_element_type=jnp.float32
    ) + out_bias.astype(jnp.float32)
    attended = attended.reshape(clip_count, frames, patches, model_width)
    middle = residual + gate_one * attended
    normed_mid, modulate_back_two = jax.vjp(modulate, middle, shift_two, scale_two)
    normed_two = normed_mid.astype(jnp.bfloat16).reshape(row_count, model_width)
    hidden = jnp.dot(normed_two, fc1_weight, preferred_element_type=jnp.float32) + fc1_bias.astype(
        jnp.float32
    )
    activated_full, gelu_back = jax.vjp(gelu_tanh, hidden)
    activated = activated_full.astype(jnp.bfloat16)
    branch_two = jnp.dot(
        activated, fc2_weight, preferred_element_type=jnp.float32
    ) + fc2_bias.astype(jnp.float32)
    branch_two = branch_two.reshape(clip_count, frames, patches, model_width)
    result = valid_rows * (middle + gate_two * branch_two)
    block_output = lax.all_to_all(
        result.astype(jnp.bfloat16), "frame", split_axis=1, concat_axis=2, tiled=True
    )
    cotangent = lax.all_to_all(
        out_cotangent, "frame", split_axis=2, concat_axis=1, tiled=True
    ).astype(jnp.float32)
    d_result = valid_rows * cotangent
    d_gate_two = jnp.sum(d_result * branch_two, axis=(1, 2))
    d_branch = (d_result * gate_two).astype(jnp.bfloat16).reshape(row_count, model_width)
    d_fc2_bias = jnp.sum(d_branch.astype(jnp.float32), axis=0)
    d_fc2_weight = contract_rows(activated, d_branch)
    d_activated = contract_cols(d_branch, fc2_weight)
    d_hidden = gelu_back(d_activated)[0].astype(jnp.bfloat16)
    d_fc1_bias = jnp.sum(d_hidden.astype(jnp.float32), axis=0)
    d_fc1_weight = contract_rows(normed_two, d_hidden)
    d_normed_two = contract_cols(d_hidden, fc1_weight).reshape(
        clip_count, frames, patches, model_width
    )
    d_middle_norm, d_shift_two, d_scale_two = modulate_back_two(d_normed_two)
    d_middle = d_result + d_middle_norm
    d_gate_one = jnp.sum(d_middle * attended, axis=(1, 2))
    d_attended = (d_middle * gate_one).astype(jnp.bfloat16).reshape(row_count, model_width)
    d_out_bias = jnp.sum(d_attended.astype(jnp.float32), axis=0)
    d_out_weight = contract_rows(context_low, d_attended)
    d_context = contract_cols(d_attended, out_weight).astype(jnp.bfloat16)
    d_context = d_context.reshape(clip_count, frames, patches, HEADS, head_width)
    d_weights = jnp.einsum(
        "cfphd,cgphd->cphfg", d_context, values_all, preferred_element_type=jnp.float32
    )
    d_values = jnp.einsum(
        "cphfg,cfphd->cgphd", weights_low, d_context, preferred_element_type=jnp.float32
    )
    d_scores = attention_weights * (
        d_weights - jnp.sum(attention_weights * d_weights, axis=-1, keepdims=True)
    )
    d_scores = d_scores.astype(jnp.bfloat16)
    d_queries = (
        jnp.einsum("cphfg,cgphd->cfphd", d_scores, keys_all, preferred_element_type=jnp.float32)
        * factor
    )
    d_keys = (
        jnp.einsum("cphfg,cfphd->cgphd", d_scores, queries, preferred_element_type=jnp.float32)
        * factor
    )
    d_projected = (
        jnp.stack([d_queries, d_keys, d_values], axis=3)
        .astype(jnp.bfloat16)
        .reshape(row_count, 3 * model_width)
    )
    column_sums = jnp.sum(d_projected.astype(jnp.float32), axis=0)
    d_qv_bias = jnp.concatenate([column_sums[:model_width], column_sums[2 * model_width :]])
    d_qkv_weight = contract_rows(normed_one, d_projected)
    d_normed_one = contract_cols(d_projected, qkv_weight).reshape(
        clip_count, frames, patches, model_width
    )
    d_residual, d_shift_one, d_scale_one = modulate_back_one(d_normed_one)
    d_input = d_middle + d_residual
    input_grad = lax.all_to_all(
        d_input.astype(jnp.bfloat16), "frame", split_axis=1, concat_axis=2, tiled=True
    )
    d_modulation = jnp.stack(
        [
            d_shift_one.reshape(clip_count, model_width),
            d_scale_one.reshape(clip_count, model_width),
            d_gate_one,
            d_shift_two.reshape(clip_count, model_width),
            d_scale_two.reshape(clip_count, model_width),
            d_gate_two,
        ],
        axis=1,
    ).reshape(clip_count, 6 * model_width)
    every_part = (
        lax.psum_scatter(d_qkv_weight, "frame", scatter_dimension=1, tiled=True),
        lax.psum_scatter(d_out_weight, "frame", scatter_dimension=1, tiled=True),
        lax.psum_scatter(d_fc1_weight, "frame", scatter_dimension=1, tiled=True),
        lax.psum_scatter(d_fc2_weight, "frame", scatter_dimension=1, tiled=True),
        lax.psum_scatter(d_modulation, "frame", scatter_dimension=1, tiled=True),
        lax.psum_scatter(d_qv_bias, "frame", scatter_dimension=0, tiled=True),
        lax.psum_scatter(d_out_bias, "frame", scatter_dimension=0, tiled=True),
        lax.psum_scatter(d_fc1_bias, "frame", scatter_dimension=0, tiled=True),
        lax.psum_scatter(d_fc2_bias, "frame", scatter_dimension=0, tiled=True),
    )
    every_mat = (
        lax.psum_scatter(every_part[0], "clip", scatter_dimension=0, tiled=True),
        lax.psum_scatter(every_part[1], "clip", scatter_dimension=0, tiled=True),
        lax.psum_scatter(every_part[2], "clip", scatter_dimension=0, tiled=True),
        lax.psum_scatter(every_part[3], "clip", scatter_dimension=0, tiled=True),
    )
    qkv_grad = every_mat[0]
    out_grad = every_mat[1]
    fc1_grad = every_mat[2]
    fc2_grad = every_mat[3]
    modulation_grad = every_part[4]
    bias_parts = (every_part[5], every_part[6], every_part[7], every_part[8])
    bias_totals = lax.psum((bias_parts[0], bias_parts[1], bias_parts[2], bias_parts[3]), "clip")
    return (
        block_output,
        input_grad,
        modulation_grad,
        qkv_grad,
        bias_totals[0],
        out_grad,
        bias_totals[1],
        fc1_grad,
        bias_totals[2],
        fc2_grad,
        bias_totals[3],
    )


LANES = 128
VMEM_LIMIT = 58 * 1024 * 1024
ROWS_DN = (((0,), (0,)), ((), ()))
COLS_DN = (((1,), (1,)), ((), ()))
F32 = jnp.float32
BF16 = jnp.bfloat16


def mm(left, right):
    return jnp.dot(left, right, preferred_element_type=F32)


def mm_cols(left, right):
    return lax.dot_general(left, right, COLS_DN, preferred_element_type=F32)


def mm_rows(left, right):
    return lax.dot_general(left, right, ROWS_DN, preferred_element_type=F32)


def unit(values):
    centred = values - jnp.mean(values, axis=-1, keepdims=True)
    variance = jnp.mean(centred * centred, axis=-1, keepdims=True)
    inverse = lax.rsqrt(variance + EPSILON)
    return centred * inverse, inverse


def unit_back(unit_values, inverse, grad):
    mean_grad = jnp.mean(grad, axis=-1, keepdims=True)
    mean_dot = jnp.mean(grad * unit_values, axis=-1, keepdims=True)
    return (grad - mean_grad - unit_values * mean_dot) * inverse


def params(**more):
    return pltpu.CompilerParams(vmem_limit_bytes=VMEM_LIMIT, **more)


def cost(flops, moved, transcendentals=0):
    return pl.CostEstimate(flops=int(flops), bytes_accessed=int(moved), transcendentals=int(transcendentals))


def shape(dims, kind):
    return jax.ShapeDtypeStruct(tuple(dims), kind)


def whole(dims, buffers=1):
    zeros = (0,) * len(dims)
    return pl.BlockSpec(tuple(dims), lambda *_: zeros, pipeline_mode=pl.Buffered(buffers))


ANY = pl.BlockSpec(memory_space=pl.ANY)


def head_window(head, width):
    low = head * width
    start = low // LANES * LANES
    size = LANES if low - start + width <= LANES else 2 * LANES
    return low, start, size


def head_mask(head, width):
    low, start, size = head_window(head, width)
    lane = lax.broadcasted_iota(jnp.int32, (1, size), 1) + start
    return jnp.where((lane >= low) & (lane < low + width), 1.0, 0.0).astype(BF16)


class Plan:
    def __init__(self, mesh, x, qkv_weight, fc1_weight):
        self.clip_axis = mesh.shape["clip"]
        self.frame_axis = mesh.shape["frame"]
        self.clips, self.local_frames, self.patches, self.width = x
        self.own_patches = self.patches // self.frame_axis
        self.halves = self.own_patches // 8
        self.frames = self.local_frames * self.frame_axis
        self.ff = fc1_weight[1]
        self.rows = self.clips * self.frames * self.own_patches
        self.clip_rows = self.rows // self.clips
        self.block = self.frames * 8
        self.blocks = self.rows // self.block
        self.piece = self.local_frames * 8
        self.head_width = self.width // HEADS
        self.chunk_dims = (self.clips, self.halves, self.local_frames, 8, self.width)
        self.zs = self.clip_axis // 2

    def row_of(self, clip, half, k):
        return ((clip * self.halves + half) * self.frame_axis + k) * self.piece


def fits(mesh, x, qkv_weight, fc1_weight):
    clip_axis, frame_axis = mesh.shape["clip"], mesh.shape["frame"]
    width, ff = x[3], fc1_weight[1]
    return (
        clip_axis == 8
        and frame_axis == 4
        and x[2] // frame_axis % 8 == 0
        and x[1] * frame_axis * 8 == LANES
        and width == 1152
        and ff == 4 * width
        and qkv_weight[1] == 3 * width
    )


def split_chunks(plan, me, x):
    n, own = plan.frame_axis, plan.own_patches

    def body(me_ref, *refs):
        for k in range(n):
            for half in range(plan.halves):
                refs[n + k][0, half] = refs[k][0, :, half * 8 : half * 8 + 8, :]

    def source(k):
        return pl.BlockSpec(
            (1, plan.local_frames, own, plan.width),
            lambda c, me_ref: (c, 0, jnp.bitwise_xor(me_ref[0], k), 0),
        )

    return pl.pallas_call(
        body,
        grid_spec=pltpu.PrefetchScalarGridSpec(
            num_scalar_prefetch=1,
            grid=(plan.clips,),
            in_specs=[source(k) for k in range(n)],
            out_specs=[pl.BlockSpec((1,) + plan.chunk_dims[1:], lambda c, me_ref: (c, 0, 0, 0, 0))] * n,
        ),
        out_shape=[shape(plan.chunk_dims, BF16)] * n,
        compiler_params=params(),
        cost_estimate=cost(0, 4 * plan.rows * plan.width),
        name="split_chunks",
    )(me, *([x] * n))


def join_chunks(plan, me, chunks):
    n, own = plan.frame_axis, plan.own_patches

    def body(me_ref, *refs):
        out = refs[n]
        for k in range(n):
            place = jnp.bitwise_xor(me_ref[0], k) * own
            for half in range(plan.halves):
                out[0, :, pl.ds(pl.multiple_of(place + half * 8, 8), 8), :] = refs[k][0, half]

    return pl.pallas_call(
        body,
        grid_spec=pltpu.PrefetchScalarGridSpec(
            num_scalar_prefetch=1,
            grid=(plan.clips,),
            in_specs=[pl.BlockSpec((1,) + plan.chunk_dims[1:], lambda c, me_ref: (c, 0, 0, 0, 0))] * n,
            out_specs=pl.BlockSpec((1, plan.local_frames, plan.patches, plan.width), lambda c, me_ref: (c, 0, 0, 0)),
        ),
        out_shape=shape((plan.clips, plan.local_frames, plan.patches, plan.width), BF16),
        compiler_params=params(),
        cost_estimate=cost(0, 4 * plan.rows * plan.width),
        name="join_chunks",
    )(me, *chunks)


def exchange(plan, chunks):
    n = plan.frame_axis
    return [chunks[0]] + [
        lax.ppermute(chunks[k], "frame", [(i, i ^ k) for i in range(n)]) for k in range(1, n)
    ]


def forward(plan, chunks, mods, score_mask, qkv_weight, bias_full, out_weight, out_bias, fc1_weight, fc1_bias):
    n, rows, width, ff = plan.frame_axis, plan.rows, plan.width, plan.ff
    fblocks = ff // width
    first_attn, after_attn = 3, 3 + plan.blocks
    steps = after_attn + 1 + fblocks
    block = plan.block

    def body(*refs):
        xs = refs[:n]
        (mod, mask, wqkv, bqkv, wout, bout, w1, b1, probs, gp, act) = refs[n : n + 11]
        outs = refs[n + 11 : n + 18]
        x_s, n1_s, proj_s, ctx_s, att_s, mid_s, n2_s, acc_s, sems = refs[n + 18 :]
        stores = (x_s, n1_s, proj_s, ctx_s, att_s, mid_s, n2_s)
        step = pl.program_id(0)

        def push(i):
            pltpu.make_async_copy(stores[i], outs[i], sems.at[i]).start()

        @pl.when(step == 0)
        def _():
            for c in range(plan.clips):
                shift, scale = mod[c, 0:1, :], 1.0 + mod[c, 1:2, :]
                for half in range(plan.halves):
                    for k in range(n):
                        row = plan.row_of(c, half, k)
                        piece = xs[k][c, half].astype(F32).reshape(plan.piece, width)
                        x_s[row : row + plan.piece, :] = piece
                        normed, _ = unit(piece)
                        n1_s[row : row + plan.piece, :] = (normed * scale + shift).astype(BF16)
            push(0)
            push(1)

        @pl.when(step < first_attn)
        def _():
            proj_s[step] = (mm(n1_s[...], wqkv[...]) + bqkv[...]).astype(BF16)

        @pl.when(step == first_attn)
        def _():
            push(2)

        @pl.when((step >= first_attn) & (step < after_attn))
        def _():
            at = step - first_attn
            here = pl.ds(pl.multiple_of(at * block, block), block)
            allowed = mask[at // plan.halves]
            acc_s[...] = jnp.zeros_like(acc_s)
            for h in range(HEADS):
                _, start, size = head_window(h, plan.head_width)
                keep = head_mask(h, plan.head_width)
                cols = slice(start, start + size)
                q = proj_s[0, here, cols] * keep
                v = proj_s[2, here, cols] * keep
                score = mm_cols(q, proj_s[1, here, cols]) * (plan.head_width ** (-0.5)) + allowed
                grown = jnp.exp(score - jnp.max(score, axis=-1, keepdims=True))
                weight = grown * (1.0 / jnp.sum(grown, axis=-1, keepdims=True))
                probs[0, h] = weight
                acc_s[:, cols] += mm(weight.astype(BF16), v)
            ctx_s[here, :] = acc_s[...].astype(BF16)

        @pl.when(step == after_attn)
        def _():
            push(3)
            att_s[...] = mm(ctx_s[...], wout[...]) + bout[...]
            push(4)
            for c in range(plan.clips):
                here = slice(c * plan.clip_rows, (c + 1) * plan.clip_rows)
                middle = x_s[here, :] + mod[c, 2:3, :] * att_s[here, :]
                mid_s[here, :] = middle
                normed, _ = unit(middle)
                n2_s[here, :] = (normed * (1.0 + mod[c, 4:5, :]) + mod[c, 3:4, :]).astype(BF16)
            push(5)
            push(6)

        @pl.when(step > after_attn)
        def _():
            hidden = mm(n2_s[...], w1[...]) + b1[...]
            square = hidden * hidden
            inner = 0.7978845608028654 * hidden * (1.0 + 0.044715 * square)
            bent = jnp.tanh(inner)
            act[...] = (0.5 * hidden * (1.0 + bent)).astype(BF16)
            slope = 0.7978845608028654 * (1.0 + 3.0 * 0.044715 * square)
            gp[...] = 0.5 * (1.0 + bent) + 0.5 * hidden * (1.0 - bent * bent) * slope

        @pl.when(step == steps - 1)
        def _():
            for i in range(len(stores)):
                pltpu.make_async_copy(stores[i], outs[i], sems.at[i]).wait()

    ff_at = lambda i: (0, jnp.clip(i - after_attn - 1, 0, fblocks - 1))
    saved = [
        shape((rows, width), F32),
        shape((rows, width), BF16),
        shape((3, rows, width), BF16),
        shape((rows, width), BF16),
        shape((rows, width), F32),
        shape((rows, width), F32),
        shape((rows, width), BF16),
    ]
    result = pl.pallas_call(
        body,
        grid=(steps,),
        in_specs=[whole(plan.chunk_dims)] * n
        + [
            whole((plan.clips, 6, width)),
            whole((plan.clips, block, block)),
            pl.BlockSpec((width, width), lambda i: (0, jnp.minimum(i, 2))),
            pl.BlockSpec((1, width), lambda i: (0, jnp.minimum(i, 2))),
            whole((width, width)),
            whole((1, width)),
            pl.BlockSpec((width, width), ff_at),
            pl.BlockSpec((1, width), ff_at),
        ],
        out_specs=[
            pl.BlockSpec(
                (1, HEADS, block, block),
                lambda i: (jnp.clip(i - first_attn, 0, plan.blocks - 1), 0, 0, 0),
            ),
            pl.BlockSpec((rows, width), ff_at),
            pl.BlockSpec((rows, width), ff_at),
        ]
        + [ANY] * len(saved),
        out_shape=[
            shape((plan.blocks, HEADS, block, block), F32),
            shape((rows, ff), F32),
            shape((rows, ff), BF16),
        ]
        + saved,
        scratch_shapes=[pltpu.VMEM(s.shape, s.dtype) for s in saved]
        + [pltpu.VMEM((block, width), F32), pltpu.SemaphoreType.DMA((len(saved),))],
        compiler_params=params(),
        cost_estimate=cost(18e9, 60e6, 4e6),
        name="forward",
    )(*chunks, mods, score_mask, qkv_weight, bias_full, out_weight, out_bias, fc1_weight, fc1_bias)
    names = ("probs", "gp", "act", "x", "n1", "proj", "ctx", "att", "mid", "n2")
    return dict(zip(names, result))


def put_slabs(ref, z, f, at, values, tiles):
    rows = values.shape[0]
    for j in range(tiles):
        ref[z, f, at + j * rows : at + (j + 1) * rows, :] = values[:, j * LANES : (j + 1) * LANES].astype(BF16)


def fold_tile(tile, folds, used):
    rows = tile.shape[0] // folds
    total = tile[:rows]
    for g in range(1, folds):
        total = total + pltpu.roll(tile[g * rows : (g + 1) * rows], g * used, 1)
    return total


def fc2_grad(plan, core, cot_chunks, mods, row_valid, act):
    n, rows, width = plan.frame_axis, plan.rows, plan.width
    span = plan.ff // plan.clip_axis
    wide = width // n
    padded = -(-wide // LANES) * LANES
    tail = wide % LANES
    folds = LANES // tail
    slab_rows = wide // LANES * span + span // folds

    def body(core_ref, *refs):
        cots = refs[:n]
        mod, valid, a, send, keep, dbr, dres, bias, padded_s, res_s, bias_s = refs[n:]
        step = pl.program_id(0)

        @pl.when(step == 0)
        def _():
            padded_s[...] = jnp.zeros_like(padded_s)
            total = jnp.zeros((1, width), F32)
            for c in range(plan.clips):
                for half in range(plan.halves):
                    for k in range(n):
                        row = plan.row_of(c, half, k)
                        here = slice(row, row + plan.piece)
                        piece = cots[k][c, half].astype(F32).reshape(plan.piece, width)
                        piece = piece * valid[here, 0:1]
                        dres[here, :] = piece.astype(BF16)
                        low = (piece * mod[c, 5:6, :]).astype(BF16)
                        dbr[here, :] = low
                        total = total + jnp.sum(low.astype(F32), axis=0, keepdims=True)
            bias[...] = total
            for f in range(n):
                padded_s[:, f * padded : f * padded + wide] = dbr[:, f * wide : (f + 1) * wide]

        res_s[...] = mm_rows(a[...], padded_s[...])
        for ref, part in ((send, 1 - core_ref[0]), (keep, core_ref[0])):
            at = pl.ds(pl.multiple_of(part * span, 8), span)
            for f in range(n):
                main = padded - LANES
                for j in range(main // LANES):
                    lanes = slice(f * padded + j * LANES, f * padded + (j + 1) * LANES)
                    ref[0, f, j * span : (j + 1) * span, :] = res_s[at, lanes].astype(BF16)
                lanes = slice(f * padded + main, (f + 1) * padded)
                ref[0, f, main // LANES * span :, :] = fold_tile(res_s[at, lanes], folds, tail).astype(BF16)

    slab = (1, n, slab_rows, LANES)
    return pl.pallas_call(
        body,
        grid_spec=pltpu.PrefetchScalarGridSpec(
            num_scalar_prefetch=1,
            grid=(plan.zs,),
            in_specs=[whole(plan.chunk_dims)] * n
            + [
                whole((plan.clips, 6, width)),
                whole((rows, LANES)),
                pl.BlockSpec((rows, 2 * span), lambda i, core_ref: (0, i)),
            ],
            out_specs=[pl.BlockSpec(slab, lambda i, core_ref: (i, 0, 0, 0))] * 2
            + [whole((rows, width)), whole((rows, width)), whole((1, width))],
            scratch_shapes=[
                pltpu.VMEM((rows, n * padded), BF16),
                pltpu.VMEM((2 * span, n * padded), F32),
                pltpu.VMEM((1, width), F32),
            ],
        ),
        out_shape=[shape((plan.zs, n, slab_rows, LANES), BF16)] * 2
        + [shape((rows, width), BF16), shape((rows, width), BF16), shape((1, width), F32)],
        compiler_params=params(),
        cost_estimate=cost(7e9, 20e6),
        name="fc2_grad",
    )(core, *cot_chunks, mods, row_valid, act)


def hidden_grad(plan, d_branch, fc2_weight, gp):
    rows, width, ff = plan.rows, plan.width, plan.ff

    def body(dbr, w2, slope, dh, bias):
        low = (mm_cols(dbr[...], w2[...]) * slope[...]).astype(BF16)
        dh[...] = low
        bias[...] = jnp.sum(low.astype(F32), axis=0, keepdims=True)

    return pl.pallas_call(
        body,
        grid=(ff // width,),
        in_specs=[
            whole((rows, width)),
            pl.BlockSpec((width, width), lambda i: (i, 0)),
            pl.BlockSpec((rows, width), lambda i: (0, i)),
        ],
        out_specs=[pl.BlockSpec((rows, width), lambda i: (0, i)), pl.BlockSpec((1, width), lambda i: (0, i))],
        out_shape=[shape((rows, ff), BF16), shape((1, ff), F32)],
        compiler_params=params(),
        cost_estimate=cost(5.4e9, 26e6),
        name="hidden_grad",
    )(d_branch, fc2_weight, gp)


def fc1_grad(plan, core, n2, d_hidden):
    n, rows, width, ff = plan.frame_axis, plan.rows, plan.width, plan.ff
    span = width // plan.clip_axis
    wide = ff // n
    slab_rows = wide // LANES * span

    def body(core_ref, left, dh, send, keep, turned_s, res_s):
        @pl.when(pl.program_id(0) == 0)
        def _():
            turned_s[...] = left[...].T

        res_s[...] = mm(turned_s[...], dh[...])
        for ref, part in ((send, 1 - core_ref[0]), (keep, core_ref[0])):
            for z in range(plan.zs):
                at = pl.ds(pl.multiple_of((2 * z + part) * span, 8), span)
                for j in range(wide // LANES):
                    ref[z, 0, j * span : (j + 1) * span, :] = res_s[at, j * LANES : (j + 1) * LANES].astype(BF16)

    slab = (plan.zs, 1, slab_rows, LANES)
    return pl.pallas_call(
        body,
        grid_spec=pltpu.PrefetchScalarGridSpec(
            num_scalar_prefetch=1,
            grid=(n,),
            in_specs=[whole((rows, width)), pl.BlockSpec((rows, wide), lambda i, core_ref: (0, i))],
            out_specs=[pl.BlockSpec(slab, lambda i, core_ref: (0, i, 0, 0))] * 2,
            scratch_shapes=[pltpu.VMEM((width, rows), BF16), pltpu.VMEM((width, wide), F32)],
        ),
        out_shape=[shape((plan.zs, n, slab_rows, LANES), BF16)] * 2,
        compiler_params=params(),
        cost_estimate=cost(5.4e9, 17e6),
        name="fc1_grad",
    )(core, n2, d_hidden)


def middle_grad(plan, d_hidden, fc1_weight, mods, mid, att, d_result, out_weight):
    rows, width, ff = plan.rows, plan.width, plan.ff
    steps = ff // width

    def body(dh, w1, mod, mid_r, att_r, dres, wout, dmid, datt, dctx, dmod, bias, acc):
        step = pl.program_id(0)

        @pl.when(step == 0)
        def _():
            acc[...] = mm_cols(dh[...], w1[...])

        @pl.when(step > 0)
        def _():
            acc[...] += mm_cols(dh[...], w1[...])

        @pl.when(step == steps - 1)
        def _():
            total = jnp.zeros((1, width), F32)
            for c in range(plan.clips):
                here = slice(c * plan.clip_rows, (c + 1) * plan.clip_rows)
                normed, inverse = unit(mid_r[here, :])
                grad = acc[here, :]
                dmod[c, 1:2, :] = jnp.sum(grad, axis=0, keepdims=True)
                dmod[c, 2:3, :] = jnp.sum(grad * normed, axis=0, keepdims=True)
                d_middle = dres[here, :].astype(F32) + unit_back(normed, inverse, grad * (1.0 + mod[c, 4:5, :]))
                dmid[here, :] = d_middle
                dmod[c, 0:1, :] = jnp.sum(d_middle * att_r[here, :], axis=0, keepdims=True)
                low = (d_middle * mod[c, 2:3, :]).astype(BF16)
                datt[here, :] = low
                total = total + jnp.sum(low.astype(F32), axis=0, keepdims=True)
            bias[...] = total
            dctx[...] = mm_cols(datt[...], wout[...]).astype(BF16)

    return pl.pallas_call(
        body,
        grid=(steps,),
        in_specs=[
            pl.BlockSpec((rows, width), lambda i: (0, i)),
            pl.BlockSpec((width, width), lambda i: (0, i)),
            whole((plan.clips, 6, width)),
            whole((rows, width)),
            whole((rows, width)),
            whole((rows, width)),
            whole((width, width)),
        ],
        out_specs=[
            whole((rows, width)),
            whole((rows, width)),
            whole((rows, width)),
            whole((plan.clips, 3, width)),
            whole((1, width)),
        ],
        out_shape=[
            shape((rows, width), F32),
            shape((rows, width), BF16),
            shape((rows, width), BF16),
            shape((plan.clips, 3, width), F32),
            shape((1, width), F32),
        ],
        scratch_shapes=[pltpu.VMEM((rows, width), F32)],
        compiler_params=params(),
        cost_estimate=cost(7e9, 30e6),
        name="middle_grad",
    )(d_hidden, fc1_weight, mods, mid, att, d_result, out_weight)


def attention_grad(plan, proj, probs, d_context):
    rows, width, block = plan.rows, plan.width, plan.block
    factor = plan.head_width ** (-0.5)

    def body(p, w, dctx, dproj, sums, acc):
        acc[...] = jnp.zeros_like(acc)
        for h in range(HEADS):
            _, start, size = head_window(h, plan.head_width)
            keep = head_mask(h, plan.head_width)
            cols = slice(start, start + size)
            weight = w[0, h]
            low = weight.astype(BF16)
            d_c = dctx[:, cols] * keep
            d_weight = mm_cols(d_c, p[2, :, cols])
            mixed = weight * d_weight
            d_score = (mixed - weight * jnp.sum(mixed, axis=-1, keepdims=True)).astype(BF16)
            acc[2, :, cols] += mm_rows(low, d_c)
            acc[0, :, cols] += mm(d_score, p[1, :, cols] * keep)
            acc[1, :, cols] += mm_rows(d_score, p[0, :, cols] * keep)
        for part in range(3):
            values = acc[part] if part == 2 else acc[part] * factor
            low = values.astype(BF16)
            dproj[part] = low
            sums[0, part : part + 1, :] = jnp.sum(low.astype(F32), axis=0, keepdims=True)

    return pl.pallas_call(
        body,
        grid=(plan.blocks,),
        in_specs=[
            pl.BlockSpec((3, block, width), lambda i: (0, i, 0)),
            pl.BlockSpec((1, HEADS, block, block), lambda i: (i, 0, 0, 0)),
            pl.BlockSpec((block, width), lambda i: (i, 0)),
        ],
        out_specs=[
            pl.BlockSpec((3, block, width), lambda i: (0, i, 0)),
            pl.BlockSpec((1, 3, width), lambda i: (i, 0, 0)),
        ],
        out_shape=[shape((3, rows, width), BF16), shape((plan.blocks, 3, width), F32)],
        scratch_shapes=[pltpu.VMEM((3, block, width), F32)],
        compiler_params=params(),
        cost_estimate=cost(4e9, 14e6),
        name="attention_grad",
    )(proj, probs, d_context)


def attention_weight_grads(plan, core, n1, ctx, d_proj, d_att):
    n, rows, width = plan.frame_axis, plan.rows, plan.width
    span = width // plan.clip_axis
    wide = 3 * width // n
    padded = -(-wide // LANES) * LANES
    out_wide = width // n
    out_padded = -(-out_wide // LANES) * LANES
    out_tail = out_wide % LANES
    folds = 3
    first_rows = padded // LANES * span
    slab_rows = first_rows + out_wide // LANES * span + span // folds

    def body(core_ref, left_q, left_o, dp, da, send, keep, turn_q, turn_o, right_q, right_o, res_q, res_o):
        f_now = pl.program_id(0)

        @pl.when(f_now == 0)
        def _():
            turn_q[...] = left_q[...].T
            turn_o[...] = left_o[...].T
            right_q[...] = jnp.zeros_like(right_q)
            right_o[...] = jnp.zeros_like(right_o)
            for f in range(n):
                right_o[f, :, :out_wide] = da[:, f * out_wide : (f + 1) * out_wide]
                low, high = f * wide, (f + 1) * wide
                for part in range(3):
                    a, b = max(low, part * width), min(high, (part + 1) * width)
                    if a < b:
                        right_q[f, :, a - low : b - low] = dp[part, :, a - part * width : b - part * width]

        res_q[...] = mm(turn_q[...], right_q[f_now])
        res_o[...] = mm(turn_o[...], right_o[f_now])
        for ref, part in ((send, 1 - core_ref[0]), (keep, core_ref[0])):
            for z in range(plan.zs):
                at = pl.ds(pl.multiple_of((2 * z + part) * span, 8), span)
                for j in range(padded // LANES):
                    ref[z, 0, j * span : (j + 1) * span, :] = res_q[at, j * LANES : (j + 1) * LANES].astype(BF16)
                for j in range(out_wide // LANES):
                    row = first_rows + j * span
                    ref[z, 0, row : row + span, :] = res_o[at, j * LANES : (j + 1) * LANES].astype(BF16)
                row = first_rows + out_wide // LANES * span
                tile = fold_tile(res_o[at, out_padded - LANES : out_padded], folds, out_tail)
                ref[z, 0, row : row + span // folds, :] = tile.astype(BF16)

    slab = (plan.zs, 1, slab_rows, LANES)
    return pl.pallas_call(
        body,
        grid_spec=pltpu.PrefetchScalarGridSpec(
            num_scalar_prefetch=1,
            grid=(n,),
            in_specs=[
                whole((rows, width)),
                whole((rows, width)),
                whole((3, rows, width)),
                whole((rows, width)),
            ],
            out_specs=[pl.BlockSpec(slab, lambda i, core_ref: (0, i, 0, 0))] * 2,
            scratch_shapes=[
                pltpu.VMEM((width, rows), BF16),
                pltpu.VMEM((width, rows), BF16),
                pltpu.VMEM((n, rows, padded), BF16),
                pltpu.VMEM((n, rows, out_padded), BF16),
                pltpu.VMEM((width, padded), F32),
                pltpu.VMEM((width, out_padded), F32),
            ],
        ),
        out_shape=[shape((plan.zs, n, slab_rows, LANES), BF16)] * 2,
        compiler_params=params(),
        cost_estimate=cost(6e9, 18e6),
        name="attention_weight_grads",
    )(core, n1, ctx, d_proj, d_att)


def input_grad_rows(plan, d_proj, qkv_weight, mods, x, d_middle):
    n, rows, width = plan.frame_axis, plan.rows, plan.width

    def body(dp, w, mod, x_r, dmid, *refs):
        outs, dmod, acc = refs[:n], refs[n], refs[n + 1]
        step = pl.program_id(0)

        @pl.when(step == 0)
        def _():
            acc[...] = mm_cols(dp[0], w[...])

        @pl.when(step > 0)
        def _():
            acc[...] += mm_cols(dp[0], w[...])

        @pl.when(step == 2)
        def _():
            for c in range(plan.clips):
                here = slice(c * plan.clip_rows, (c + 1) * plan.clip_rows)
                normed, inverse = unit(x_r[here, :])
                grad = acc[here, :]
                dmod[c, 0:1, :] = jnp.sum(grad, axis=0, keepdims=True)
                dmod[c, 1:2, :] = jnp.sum(grad * normed, axis=0, keepdims=True)
                total = dmid[here, :] + unit_back(normed, inverse, grad * (1.0 + mod[c, 1:2, :]))
                for half in range(plan.halves):
                    for k in range(n):
                        row = plan.row_of(0, half, k)
                        piece = total[row : row + plan.piece, :].reshape(plan.local_frames, 8, width)
                        outs[k][c, half] = piece.astype(BF16)

    return pl.pallas_call(
        body,
        grid=(3,),
        in_specs=[
            pl.BlockSpec((1, rows, width), lambda i: (i, 0, 0)),
            pl.BlockSpec((width, width), lambda i: (0, i)),
            whole((plan.clips, 6, width)),
            whole((rows, width)),
            whole((rows, width)),
        ],
        out_specs=[whole(plan.chunk_dims)] * n + [whole((plan.clips, 2, width))],
        out_shape=[shape(plan.chunk_dims, BF16)] * n + [shape((plan.clips, 2, width), F32)],
        scratch_shapes=[pltpu.VMEM((rows, width), F32)],
        compiler_params=params(),
        cost_estimate=cost(4e9, 20e6),
        name="input_grad_rows",
    )(d_proj, qkv_weight, mods, x, d_middle)


def output_rows(plan, act, fc2_weight, fc2_bias, mods, mid, d_result, row_valid):
    n, rows, width, ff = plan.frame_axis, plan.rows, plan.width, plan.ff
    steps = ff // width

    def body(a, w, bias, mod, mid_r, dres, valid, *refs):
        outs, dmod, acc = refs[:n], refs[n], refs[n + 1]
        step = pl.program_id(0)

        @pl.when(step == 0)
        def _():
            acc[...] = mm(a[...], w[...])

        @pl.when(step > 0)
        def _():
            acc[...] += mm(a[...], w[...])

        @pl.when(step == steps - 1)
        def _():
            for c in range(plan.clips):
                here = slice(c * plan.clip_rows, (c + 1) * plan.clip_rows)
                branch = acc[here, :] + bias[...]
                dmod[c, 0:1, :] = jnp.sum(dres[here, :].astype(F32) * branch, axis=0, keepdims=True)
                total = valid[here, 0:1] * (mid_r[here, :] + mod[c, 5:6, :] * branch)
                for half in range(plan.halves):
                    for k in range(n):
                        row = plan.row_of(0, half, k)
                        piece = total[row : row + plan.piece, :].reshape(plan.local_frames, 8, width)
                        outs[k][c, half] = piece.astype(BF16)

    return pl.pallas_call(
        body,
        grid=(steps,),
        in_specs=[
            pl.BlockSpec((rows, width), lambda i: (0, i)),
            pl.BlockSpec((width, width), lambda i: (i, 0)),
            whole((1, width)),
            whole((plan.clips, 6, width)),
            whole((rows, width)),
            whole((rows, width)),
            whole((rows, LANES)),
        ],
        out_specs=[whole(plan.chunk_dims)] * n + [whole((plan.clips, 1, width))],
        out_shape=[shape(plan.chunk_dims, BF16)] * n + [shape((plan.clips, 1, width), F32)],
        scratch_shapes=[pltpu.VMEM((rows, width), F32)],
        compiler_params=params(),
        cost_estimate=cost(5.4e9, 26e6),
        name="output_rows",
    )(act, fc2_weight, fc2_bias, mods, mid, d_result, row_valid)


BIT_OF = {"core": ("clip", 1), "z0": ("clip", 2), "z1": ("clip", 4), "x": ("frame", 1), "y": ("frame", 2)}
BIT_AT = ("core", "x", "y", "z0", "z1")
ORDERS = (("x", "z0", "z1", "y"), ("y", "z0", "z1", "x"))


def swap(plan, value, bit):
    axis, step = BIT_OF[bit]
    size = plan.clip_axis if axis == "clip" else plan.frame_axis
    return lax.ppermute(value, axis, [(i, i ^ step) for i in range(size)])


def add_split(bits, parts):
    count = 2 ** (len(parts[0][5]) - 1)

    def body(bits_ref, *refs):
        m = len(parts)
        for i in range(m):
            a_send, a_keep, b_send, b_keep = refs[4 * i : 4 * i + 4]
            send, keep = refs[4 * m + 2 * i : 4 * m + 2 * i + 2]
            send[...] = (a_send[...].astype(F32) + b_send[...].astype(F32)).astype(BF16)
            keep[...] = (a_keep[...].astype(F32) + b_keep[...].astype(F32)).astype(BF16)

    in_specs, operands, out_specs, out_shape = [], [], [], []
    moved = 0
    for kept, kept_at, received, received_at, rows, left, bit in parts:
        place = len(left) - 1 - left.index(bit)
        which = BIT_AT.index(bit)

        def at(row_block, mine, place=place, which=which):
            def index(i, bits_ref):
                value = bits_ref[which] if mine else 1 - bits_ref[which]
                low = i % (2**place)
                return ((i // (2**place)) * (2 ** (place + 1)) + value * (2**place) + low, row_block, 0)

            return index

        for array, row_block in ((kept, kept_at), (received, received_at)):
            for mine in (False, True):
                in_specs.append(pl.BlockSpec((1, rows, LANES), at(row_block, mine)))
                operands.append(array)
        out_specs += [pl.BlockSpec((1, rows, LANES), lambda i, bits_ref: (i, 0, 0))] * 2
        out_shape += [shape((count, rows, LANES), BF16)] * 2
        moved += 6 * count * rows * LANES * 2
    result = pl.pallas_call(
        body,
        grid_spec=pltpu.PrefetchScalarGridSpec(
            num_scalar_prefetch=1, grid=(count,), in_specs=in_specs, out_specs=out_specs
        ),
        out_shape=out_shape,
        compiler_params=params(),
        cost_estimate=cost(moved // 4, moved),
        name="add_split",
    )(bits, *operands)
    return [(result[2 * i], result[2 * i + 1]) for i in range(len(parts))]


class Scatter:
    def __init__(self, plan, bits, send, keep, orders):
        zs, n, rows, lanes = send.shape
        self.plan, self.bits, self.orders = plan, bits, orders
        self.rows = rows // len(orders)
        received = swap(plan, send.reshape(zs * n, rows, lanes), "core")
        keep = keep.reshape(zs * n, rows, lanes)
        self.state = [(keep, t, received, t) for t in range(len(orders))]
        self.left = [("z1", "z0", "y", "x")] * len(orders)
        self.stage = 0

    def advance(self):
        parts = [
            state + (self.rows, left, order[self.stage])
            for state, left, order in zip(self.state, self.left, self.orders)
        ]
        halves = add_split(self.bits, parts)
        new_state, new_left = [], []
        for (send, keep), left, order in zip(halves, self.left, self.orders):
            bit = order[self.stage]
            new_state.append((keep, 0, swap(self.plan, send, bit), 0))
            new_left.append(tuple(b for b in left if b != bit))
        self.state, self.left = new_state, new_left
        self.stage += 1

    def last(self):
        return [s[0] for s in self.state], [s[2] for s in self.state]


def finish(plan, scatter, layouts):
    kept, received = scatter.last()
    m, rows = len(kept), scatter.rows

    def body(*refs):
        outs, total = refs[2 * m : -1], refs[-1]
        for t in range(m):
            total[t * rows : (t + 1) * rows, :] = refs[t][0].astype(F32) + refs[m + t][0].astype(F32)
        for out, (first, span, tiles, used, folds) in zip(outs, layouts):
            for j in range(tiles):
                out[:, j * LANES : (j + 1) * LANES] = total[first + j * span : first + (j + 1) * span, :]
            if used:
                tile = total[first + tiles * span : first + tiles * span + span // folds, :]
                for g in range(folds):
                    moved = tile if g == 0 else pltpu.roll(tile, LANES - g * used, 1)
                    here = slice(g * (span // folds), (g + 1) * (span // folds))
                    out[here, tiles * LANES : tiles * LANES + used] = moved[:, :used]

    block = whole((1, rows, LANES))
    out_shape = [shape((span, tiles * LANES + used), F32) for _, span, tiles, used, _ in layouts]
    return pl.pallas_call(
        body,
        grid=(1,),
        in_specs=[block] * (2 * m),
        out_specs=[whole(s.shape) for s in out_shape],
        out_shape=out_shape,
        scratch_shapes=[pltpu.VMEM((m * rows, LANES), F32)],
        compiler_params=params(),
        cost_estimate=cost(m * rows * LANES, 8 * m * rows * LANES),
        name="finish",
    )(*kept, *received)


def fast_layer(
    mesh,
    block_input,
    modulation,
    frame_counts,
    qkv_weight,
    qv_bias,
    out_weight,
    out_bias,
    fc1_weight,
    fc1_bias,
    fc2_weight,
    fc2_bias,
    out_cotangent,
):
    plan = Plan(mesh, block_input.shape, qkv_weight.shape, fc1_weight.shape)
    n, width, rows = plan.frame_axis, plan.width, plan.rows
    frame_at = lax.axis_index("frame").astype(jnp.int32)
    clip_at = lax.axis_index("clip").astype(jnp.int32)
    me = frame_at.reshape(1)
    core = (clip_at % 2).reshape(1)
    bits = jnp.stack([clip_at % 2, frame_at % 2, frame_at // 2, clip_at // 2 % 2, clip_at // 4])

    slot = jnp.arange(plan.frames, dtype=jnp.int32)
    frame_of = jnp.bitwise_xor(slot // plan.local_frames, frame_at) * plan.local_frames + slot % plan.local_frames
    valid = frame_of[None, :] < frame_counts[:, None]
    place = jnp.arange(plan.block, dtype=jnp.int32)
    same = place[:, None] % 8 == place[None, :] % 8
    allowed = same[None] & jnp.repeat(valid, 8, axis=1)[:, None, :]
    score_mask = jnp.where(allowed, 0.0, NEGATIVE).astype(F32)
    row_valid = jnp.broadcast_to(
        valid.astype(F32)[:, None, :, None, None], (plan.clips, plan.halves, plan.frames, 8, LANES)
    ).reshape(rows, LANES)
    mods = modulation.astype(F32).reshape(plan.clips, 6, width)
    bias_full = jnp.concatenate(
        [qv_bias[:width], jnp.zeros((width,), BF16), qv_bias[width:]]
    ).astype(F32)[None, :]

    def line(vector):
        return vector.astype(F32)[None, :]

    inputs = exchange(plan, split_chunks(plan, me, block_input))
    cotangents = exchange(plan, split_chunks(plan, me, out_cotangent))
    saved = forward(
        plan, inputs, mods, score_mask, qkv_weight, bias_full, out_weight, line(out_bias), fc1_weight, line(fc1_bias)
    )
    send2, keep2, d_branch, d_result, d_fc2_bias = fc2_grad(plan, core, cotangents, mods, row_valid, saved["act"])
    two = Scatter(plan, bits, send2, keep2, ORDERS)
    d_hidden, d_fc1_bias = hidden_grad(plan, d_branch, fc2_weight, saved["gp"])
    two.advance()
    send1, keep1 = fc1_grad(plan, core, saved["n2"], d_hidden)
    one = Scatter(plan, bits, send1, keep1, ORDERS)
    d_middle, d_att, d_context, d_mods_two, d_out_bias = middle_grad(
        plan, d_hidden, fc1_weight, mods, saved["mid"], saved["att"], d_result, out_weight
    )
    one.advance()
    two.advance()
    d_proj, d_proj_sums = attention_grad(plan, saved["proj"], saved["probs"], d_context)
    send0, keep0 = attention_weight_grads(plan, core, saved["n1"], saved["ctx"], d_proj, d_att)
    zero = Scatter(plan, bits, send0, keep0, ORDERS)
    *in_rows, d_mods_one = input_grad_rows(plan, d_proj, qkv_weight, mods, saved["x"], d_middle)
    *out_rows, d_gate_two = output_rows(
        plan, saved["act"], fc2_weight, line(fc2_bias), mods, saved["mid"], d_result, row_valid
    )
    block_output = join_chunks(plan, me, exchange(plan, out_rows))
    input_grad = join_chunks(plan, me, exchange(plan, in_rows))
    one.advance()
    zero.advance()
    two.advance()
    one.advance()
    zero.advance()
    two.advance()
    one.advance()
    zero.advance()
    zero.advance()

    span2, span1 = plan.ff // plan.clip_axis, width // plan.clip_axis
    (fc2_out,) = finish(plan, two, [(0, span2, 2, 32, 4)])
    (fc1_out,) = finish(plan, one, [(0, span1, 9, 0, 1)])
    qkv_out, out_out = finish(plan, zero, [(0, span1, 6, 96, 1), (7 * span1, span1, 2, 32, 3)])

    d_modulation = jnp.concatenate([d_mods_one, d_mods_two, d_gate_two], axis=1).reshape(plan.clips, 6 * width)
    sums = jnp.sum(d_proj_sums, axis=0)
    small = [
        d_modulation,
        jnp.concatenate([sums[0], sums[2]])[None, :],
        d_out_bias,
        d_fc1_bias,
        d_fc2_bias,
    ]
    cut = [v.reshape(v.shape[0], n, v.shape[1] // n) for v in small]
    flat = jnp.concatenate([v.transpose(1, 0, 2).reshape(n, -1) for v in cut], axis=1)
    at = [0]
    for v in cut:
        at.append(at[-1] + v.shape[0] * v.shape[2])
    pieces = [lax.dynamic_index_in_dim(flat, jnp.bitwise_xor(frame_at, k), 0, keepdims=True) for k in range(n)]
    mine = pieces[0]
    for k in range(1, n):
        mine = mine + lax.ppermute(pieces[k], "frame", [(i, i ^ k) for i in range(n)])
    modulation_grad = mine[0, : at[1]].reshape(plan.clips, 6 * width // n)
    biases = mine[:, at[1] :]
    for bit in ("core", "z0", "z1"):
        biases = biases + swap(plan, biases, bit)
    biases = biases[0]
    ends = [p - at[1] for p in at[1:]]
    return (
        block_output,
        input_grad,
        modulation_grad,
        qkv_out,
        biases[ends[0] : ends[1]],
        out_out,
        biases[ends[1] : ends[2]],
        fc1_out,
        biases[ends[2] : ends[3]],
        fc2_out,
        biases[ends[3] : ends[4]],
    )


def solution(mesh):
    placed = (
        P("clip", "frame", None, None),
        P("clip", None),
        P("clip"),
        P(),
        P(),
        P(),
        P(),
        P(),
        P(),
        P(),
        P(),
        P("clip", "frame", None, None),
    )
    def layer(*arrays):
        if fits(mesh, arrays[0].shape, arrays[3].shape, arrays[7].shape):
            return fast_layer(mesh, *arrays)
        return on_device(*arrays)

    return jax.shard_map(
        layer,
        mesh=mesh,
        in_specs=placed,
        out_specs=(
            P("clip", "frame", None, None),
            P("clip", "frame", None, None),
            P("clip", "frame"),
            P("clip", "frame"),
            P("frame"),
            P("clip", "frame"),
            P("frame"),
            P("clip", "frame"),
            P("frame"),
            P("clip", "frame"),
            P("frame"),
        ),
        check_vma=False,
    )
```

```python
import jax
import jax.numpy as jnp
from jax import lax
from jax.experimental import pallas as pl
from jax.experimental.pallas import tpu as pltpu
from jax.sharding import PartitionSpec as P

HEADS = 16


EPSILON = 1e-06
NEGATIVE = -1e30


def normalize(values):
    centred = values - jnp.mean(values, axis=-1, keepdims=True)
    variance = jnp.mean(centred * centred, axis=-1, keepdims=True)
    return centred * lax.rsqrt(variance + EPSILON)


def modulate(values, shift_term, scale_term):
    return normalize(values) * (1.0 + scale_term) + shift_term


def gelu_tanh(inputs):
    return jax.nn.gelu(inputs, approximate=True)


def contract_rows(left, right):
    return lax.dot_general(
        left, right, (((0,), (0,)), ((), ())), preferred_element_type=jnp.float32
    )


def contract_cols(left, right):
    return lax.dot_general(
        left, right, (((1,), (1,)), ((), ())), preferred_element_type=jnp.float32
    )


def on_device(
    block_input,
    modulation,
    frame_counts,
    qkv_weight,
    qv_bias,
    out_weight,
    out_bias,
    fc1_weight,
    fc1_bias,
    fc2_weight,
    fc2_bias,
    out_cotangent,
):
    swapped = lax.all_to_all(block_input, "frame", split_axis=2, concat_axis=1, tiled=True)
    clip_count, frames, patches, model_width = swapped.shape
    head_width = model_width // HEADS
    row_count = clip_count * frames * patches
    factor = head_width ** (-0.5)
    frame_valid = (jnp.arange(frames)[None, :] < frame_counts[:, None]).astype(jnp.float32)
    valid_rows = frame_valid[:, :, None, None]
    key_valid = frame_valid[:, None, None, None, :] > 0.5
    modulators = modulation.astype(jnp.float32).reshape(clip_count, 6, model_width)[
        :, :, None, None, :
    ]
    shift_one = modulators[:, 0]
    scale_one = modulators[:, 1]
    gate_one = modulators[:, 2]
    shift_two = modulators[:, 3]
    scale_two = modulators[:, 4]
    gate_two = modulators[:, 5]
    residual = swapped.astype(jnp.float32)
    normed_full, modulate_back_one = jax.vjp(modulate, residual, shift_one, scale_one)
    normed_one = normed_full.astype(jnp.bfloat16).reshape(row_count, model_width)
    bias_full = jnp.concatenate(
        [qv_bias[:model_width], jnp.zeros((model_width,), jnp.bfloat16), qv_bias[model_width:]]
    ).astype(jnp.float32)
    projected = (
        jnp.dot(normed_one, qkv_weight, preferred_element_type=jnp.float32) + bias_full
    ).astype(jnp.bfloat16)
    shaped = projected.reshape(clip_count, frames, patches, 3, HEADS, head_width)
    queries = shaped[:, :, :, 0]
    keys_all = shaped[:, :, :, 1]
    values_all = shaped[:, :, :, 2]
    scores = (
        jnp.einsum("cfphd,cgphd->cphfg", queries, keys_all, preferred_element_type=jnp.float32)
        * factor
    )
    scores = jnp.where(key_valid, scores, NEGATIVE)
    row_peak = jnp.max(scores, axis=-1, keepdims=True)
    exponent = jnp.exp(scores - row_peak)
    attention_weights = exponent / jnp.sum(exponent, axis=-1, keepdims=True)
    weights_low = attention_weights.astype(jnp.bfloat16)
    context = jnp.einsum(
        "cphfg,cgphd->cfphd", weights_low, values_all, preferred_element_type=jnp.float32
    )
    context_low = context.astype(jnp.bfloat16).reshape(row_count, model_width)
    attended = jnp.dot(
        context_low, out_weight, preferred_element_type=jnp.float32
    ) + out_bias.astype(jnp.float32)
    attended = attended.reshape(clip_count, frames, patches, model_width)
    middle = residual + gate_one * attended
    normed_mid, modulate_back_two = jax.vjp(modulate, middle, shift_two, scale_two)
    normed_two = normed_mid.astype(jnp.bfloat16).reshape(row_count, model_width)
    hidden = jnp.dot(normed_two, fc1_weight, preferred_element_type=jnp.float32) + fc1_bias.astype(
        jnp.float32
    )
    activated_full, gelu_back = jax.vjp(gelu_tanh, hidden)
    activated = activated_full.astype(jnp.bfloat16)
    branch_two = jnp.dot(
        activated, fc2_weight, preferred_element_type=jnp.float32
    ) + fc2_bias.astype(jnp.float32)
    branch_two = branch_two.reshape(clip_count, frames, patches, model_width)
    result = valid_rows * (middle + gate_two * branch_two)
    block_output = lax.all_to_all(
        result.astype(jnp.bfloat16), "frame", split_axis=1, concat_axis=2, tiled=True
    )
    cotangent = lax.all_to_all(
        out_cotangent, "frame", split_axis=2, concat_axis=1, tiled=True
    ).astype(jnp.float32)
    d_result = valid_rows * cotangent
    d_gate_two = jnp.sum(d_result * branch_two, axis=(1, 2))
    d_branch = (d_result * gate_two).astype(jnp.bfloat16).reshape(row_count, model_width)
    d_fc2_bias = jnp.sum(d_branch.astype(jnp.float32), axis=0)
    d_fc2_weight = contract_rows(activated, d_branch)
    d_activated = contract_cols(d_branch, fc2_weight)
    d_hidden = gelu_back(d_activated)[0].astype(jnp.bfloat16)
    d_fc1_bias = jnp.sum(d_hidden.astype(jnp.float32), axis=0)
    d_fc1_weight = contract_rows(normed_two, d_hidden)
    d_normed_two = contract_cols(d_hidden, fc1_weight).reshape(
        clip_count, frames, patches, model_width
    )
    d_middle_norm, d_shift_two, d_scale_two = modulate_back_two(d_normed_two)
    d_middle = d_result + d_middle_norm
    d_gate_one = jnp.sum(d_middle * attended, axis=(1, 2))
    d_attended = (d_middle * gate_one).astype(jnp.bfloat16).reshape(row_count, model_width)
    d_out_bias = jnp.sum(d_attended.astype(jnp.float32), axis=0)
    d_out_weight = contract_rows(context_low, d_attended)
    d_context = contract_cols(d_attended, out_weight).astype(jnp.bfloat16)
    d_context = d_context.reshape(clip_count, frames, patches, HEADS, head_width)
    d_weights = jnp.einsum(
        "cfphd,cgphd->cphfg", d_context, values_all, preferred_element_type=jnp.float32
    )
    d_values = jnp.einsum(
        "cphfg,cfphd->cgphd", weights_low, d_context, preferred_element_type=jnp.float32
    )
    d_scores = attention_weights * (
        d_weights - jnp.sum(attention_weights * d_weights, axis=-1, keepdims=True)
    )
    d_scores = d_scores.astype(jnp.bfloat16)
    d_queries = (
        jnp.einsum("cphfg,cgphd->cfphd", d_scores, keys_all, preferred_element_type=jnp.float32)
        * factor
    )
    d_keys = (
        jnp.einsum("cphfg,cfphd->cgphd", d_scores, queries, preferred_element_type=jnp.float32)
        * factor
    )
    d_projected = (
        jnp.stack([d_queries, d_keys, d_values], axis=3)
        .astype(jnp.bfloat16)
        .reshape(row_count, 3 * model_width)
    )
    column_sums = jnp.sum(d_projected.astype(jnp.float32), axis=0)
    d_qv_bias = jnp.concatenate([column_sums[:model_width], column_sums[2 * model_width :]])
    d_qkv_weight = contract_rows(normed_one, d_projected)
    d_normed_one = contract_cols(d_projected, qkv_weight).reshape(
        clip_count, frames, patches, model_width
    )
    d_residual, d_shift_one, d_scale_one = modulate_back_one(d_normed_one)
    d_input = d_middle + d_residual
    input_grad = lax.all_to_all(
        d_input.astype(jnp.bfloat16), "frame", split_axis=1, concat_axis=2, tiled=True
    )
    d_modulation = jnp.stack(
        [
            d_shift_one.reshape(clip_count, model_width),
            d_scale_one.reshape(clip_count, model_width),
            d_gate_one,
            d_shift_two.reshape(clip_count, model_width),
            d_scale_two.reshape(clip_count, model_width),
            d_gate_two,
        ],
        axis=1,
    ).reshape(clip_count, 6 * model_width)
    every_part = (
        lax.psum_scatter(d_qkv_weight, "frame", scatter_dimension=1, tiled=True),
        lax.psum_scatter(d_out_weight, "frame", scatter_dimension=1, tiled=True),
        lax.psum_scatter(d_fc1_weight, "frame", scatter_dimension=1, tiled=True),
        lax.psum_scatter(d_fc2_weight, "frame", scatter_dimension=1, tiled=True),
        lax.psum_scatter(d_modulation, "frame", scatter_dimension=1, tiled=True),
        lax.psum_scatter(d_qv_bias, "frame", scatter_dimension=0, tiled=True),
        lax.psum_scatter(d_out_bias, "frame", scatter_dimension=0, tiled=True),
        lax.psum_scatter(d_fc1_bias, "frame", scatter_dimension=0, tiled=True),
        lax.psum_scatter(d_fc2_bias, "frame", scatter_dimension=0, tiled=True),
    )
    every_mat = (
        lax.psum_scatter(every_part[0], "clip", scatter_dimension=0, tiled=True),
        lax.psum_scatter(every_part[1], "clip", scatter_dimension=0, tiled=True),
        lax.psum_scatter(every_part[2], "clip", scatter_dimension=0, tiled=True),
        lax.psum_scatter(every_part[3], "clip", scatter_dimension=0, tiled=True),
    )
    qkv_grad = every_mat[0]
    out_grad = every_mat[1]
    fc1_grad = every_mat[2]
    fc2_grad = every_mat[3]
    modulation_grad = every_part[4]
    bias_parts = (every_part[5], every_part[6], every_part[7], every_part[8])
    bias_totals = lax.psum((bias_parts[0], bias_parts[1], bias_parts[2], bias_parts[3]), "clip")
    return (
        block_output,
        input_grad,
        modulation_grad,
        qkv_grad,
        bias_totals[0],
        out_grad,
        bias_totals[1],
        fc1_grad,
        bias_totals[2],
        fc2_grad,
        bias_totals[3],
    )


LANES = 128
VMEM_LIMIT = 58 * 1024 * 1024
ROWS_DN = (((0,), (0,)), ((), ()))
COLS_DN = (((1,), (1,)), ((), ()))
F32 = jnp.float32
BF16 = jnp.bfloat16


def mm(left, right):
    return jnp.dot(left, right, preferred_element_type=F32)


def mm_cols(left, right):
    return lax.dot_general(left, right, COLS_DN, preferred_element_type=F32)


def mm_rows(left, right):
    return lax.dot_general(left, right, ROWS_DN, preferred_element_type=F32)


def unit(values):
    centred = values - jnp.mean(values, axis=-1, keepdims=True)
    variance = jnp.mean(centred * centred, axis=-1, keepdims=True)
    inverse = lax.rsqrt(variance + EPSILON)
    return centred * inverse, inverse


def unit_back(unit_values, inverse, grad):
    mean_grad = jnp.mean(grad, axis=-1, keepdims=True)
    mean_dot = jnp.mean(grad * unit_values, axis=-1, keepdims=True)
    return (grad - mean_grad - unit_values * mean_dot) * inverse


def params(**more):
    return pltpu.CompilerParams(vmem_limit_bytes=VMEM_LIMIT, **more)


def cost(flops, moved, transcendentals=0):
    return pl.CostEstimate(flops=int(flops), bytes_accessed=int(moved), transcendentals=int(transcendentals))


def shape(dims, kind):
    return jax.ShapeDtypeStruct(tuple(dims), kind)


def whole(dims, buffers=1):
    zeros = (0,) * len(dims)
    return pl.BlockSpec(tuple(dims), lambda *_: zeros, pipeline_mode=pl.Buffered(buffers))


ANY = pl.BlockSpec(memory_space=pl.ANY)


def head_window(head, width):
    low = head * width
    start = low // LANES * LANES
    size = LANES if low - start + width <= LANES else 2 * LANES
    return low, start, size


def head_mask(head, width):
    low, start, size = head_window(head, width)
    lane = lax.broadcasted_iota(jnp.int32, (1, size), 1) + start
    return jnp.where((lane >= low) & (lane < low + width), 1.0, 0.0).astype(BF16)


class Plan:
    def __init__(self, mesh, x, qkv_weight, fc1_weight):
        self.clip_axis = mesh.shape["clip"]
        self.frame_axis = mesh.shape["frame"]
        self.clips, self.local_frames, self.patches, self.width = x
        self.own_patches = self.patches // self.frame_axis
        self.halves = self.own_patches // 8
        self.frames = self.local_frames * self.frame_axis
        self.ff = fc1_weight[1]
        self.rows = self.clips * self.frames * self.own_patches
        self.clip_rows = self.rows // self.clips
        self.block = self.frames * 8
        self.blocks = self.rows // self.block
        self.piece = self.local_frames * 8
        self.head_width = self.width // HEADS
        self.chunk_dims = (self.clips, self.halves, self.local_frames, 8, self.width)
        self.zs = self.clip_axis // 2

    def row_of(self, clip, half, k):
        return ((clip * self.halves + half) * self.frame_axis + k) * self.piece


def fits(mesh, x, qkv_weight, fc1_weight):
    clip_axis, frame_axis = mesh.shape["clip"], mesh.shape["frame"]
    width, ff = x[3], fc1_weight[1]
    return (
        clip_axis == 8
        and frame_axis == 4
        and x[2] // frame_axis % 8 == 0
        and x[1] * frame_axis * 8 == LANES
        and width == 1152
        and ff == 4 * width
        and qkv_weight[1] == 3 * width
    )


def split_chunks(plan, me, x):
    n, own = plan.frame_axis, plan.own_patches

    def body(me_ref, *refs):
        for k in range(n):
            for half in range(plan.halves):
                refs[n + k][0, half] = refs[k][0, :, half * 8 : half * 8 + 8, :]

    def source(k):
        return pl.BlockSpec(
            (1, plan.local_frames, own, plan.width),
            lambda c, me_ref: (c, 0, jnp.bitwise_xor(me_ref[0], k), 0),
        )

    return pl.pallas_call(
        body,
        grid_spec=pltpu.PrefetchScalarGridSpec(
            num_scalar_prefetch=1,
            grid=(plan.clips,),
            in_specs=[source(k) for k in range(n)],
            out_specs=[pl.BlockSpec((1,) + plan.chunk_dims[1:], lambda c, me_ref: (c, 0, 0, 0, 0))] * n,
        ),
        out_shape=[shape(plan.chunk_dims, BF16)] * n,
        compiler_params=params(),
        cost_estimate=cost(0, 4 * plan.rows * plan.width),
        name="split_chunks",
    )(me, *([x] * n))


def exchange(plan, chunks):
    n = plan.frame_axis
    return [chunks[0]] + [
        lax.ppermute(chunks[k], "frame", [(i, i ^ k) for i in range(n)]) for k in range(1, n)
    ]


def forward(plan, chunks, mods, score_mask, qkv_weight, bias_full, out_weight, out_bias):
    n, rows, width = plan.frame_axis, plan.rows, plan.width
    first_attn, after_attn = 3, 3 + plan.blocks
    steps = after_attn + 1
    block = plan.block

    def body(*refs):
        xs = refs[:n]
        (mod, mask, wqkv, bqkv, wout, bout, probs) = refs[n : n + 7]
        outs = refs[n + 7 : n + 14]
        x_s, n1_s, proj_s, ctx_s, att_s, mid_s, n2_s, acc_s, sems = refs[n + 14 :]
        stores = (x_s, n1_s, proj_s, ctx_s, att_s, mid_s, n2_s)
        step = pl.program_id(0)

        def push(i):
            pltpu.make_async_copy(stores[i], outs[i], sems.at[i]).start()

        @pl.when(step == 0)
        def _():
            for c in range(plan.clips):
                shift, scale = mod[c, 0:1, :], 1.0 + mod[c, 1:2, :]
                for half in range(plan.halves):
                    for k in range(n):
                        row = plan.row_of(c, half, k)
                        piece = xs[k][c, half].astype(F32).reshape(plan.piece, width)
                        x_s[row : row + plan.piece, :] = piece
                        normed, _ = unit(piece)
                        n1_s[row : row + plan.piece, :] = (normed * scale + shift).astype(BF16)
            push(0)
            push(1)

        @pl.when(step < first_attn)
        def _():
            proj_s[step] = (mm(n1_s[...], wqkv[...]) + bqkv[...]).astype(BF16)

        @pl.when(step == first_attn)
        def _():
            push(2)

        @pl.when((step >= first_attn) & (step < after_attn))
        def _():
            at = step - first_attn
            here = pl.ds(pl.multiple_of(at * block, block), block)
            allowed = mask[at // plan.halves]
            acc_s[...] = jnp.zeros_like(acc_s)
            for h in range(HEADS):
                _, start, size = head_window(h, plan.head_width)
                keep = head_mask(h, plan.head_width)
                cols = slice(start, start + size)
                q = proj_s[0, here, cols] * keep
                v = proj_s[2, here, cols] * keep
                score = mm_cols(q, proj_s[1, here, cols]) * (plan.head_width ** (-0.5)) + allowed
                grown = jnp.exp(score - jnp.max(score, axis=-1, keepdims=True))
                weight = grown * (1.0 / jnp.sum(grown, axis=-1, keepdims=True))
                probs[0, h] = weight
                acc_s[:, cols] += mm(weight.astype(BF16), v)
            ctx_s[here, :] = acc_s[...].astype(BF16)

        @pl.when(step == after_attn)
        def _():
            push(3)
            att_s[...] = mm(ctx_s[...], wout[...]) + bout[...]
            push(4)
            for c in range(plan.clips):
                here = slice(c * plan.clip_rows, (c + 1) * plan.clip_rows)
                middle = x_s[here, :] + mod[c, 2:3, :] * att_s[here, :]
                mid_s[here, :] = middle
                normed, _ = unit(middle)
                n2_s[here, :] = (normed * (1.0 + mod[c, 4:5, :]) + mod[c, 3:4, :]).astype(BF16)
            push(5)
            push(6)

        @pl.when(step == steps - 1)
        def _():
            for i in range(len(stores)):
                pltpu.make_async_copy(stores[i], outs[i], sems.at[i]).wait()

    saved = [
        shape((rows, width), F32),
        shape((rows, width), BF16),
        shape((3, rows, width), BF16),
        shape((rows, width), BF16),
        shape((rows, width), F32),
        shape((rows, width), F32),
        shape((rows, width), BF16),
    ]
    result = pl.pallas_call(
        body,
        grid=(steps,),
        in_specs=[whole(plan.chunk_dims)] * n
        + [
            whole((plan.clips, 6, width)),
            whole((plan.clips, block, block)),
            pl.BlockSpec((width, width), lambda i: (0, jnp.minimum(i, 2))),
            pl.BlockSpec((1, width), lambda i: (0, jnp.minimum(i, 2))),
            whole((width, width)),
            whole((1, width)),
        ],
        out_specs=[
            pl.BlockSpec(
                (1, HEADS, block, block),
                lambda i: (jnp.clip(i - first_attn, 0, plan.blocks - 1), 0, 0, 0),
            ),
        ]
        + [ANY] * len(saved),
        out_shape=[
            shape((plan.blocks, HEADS, block, block), F32),
        ]
        + saved,
        scratch_shapes=[pltpu.VMEM(s.shape, s.dtype) for s in saved]
        + [pltpu.VMEM((block, width), F32), pltpu.SemaphoreType.DMA((len(saved),))],
        compiler_params=params(),
        cost_estimate=cost(8e9, 30e6, 1e6),
        name="forward",
    )(*chunks, mods, score_mask, qkv_weight, bias_full, out_weight, out_bias)
    names = ("probs", "x", "n1", "proj", "ctx", "att", "mid", "n2")
    return dict(zip(names, result))


def fold_tile(tile, folds, used):
    rows = tile.shape[0] // folds
    total = tile[:rows]
    for g in range(1, folds):
        total = total + pltpu.roll(tile[g * rows : (g + 1) * rows], g * used, 1)
    return total


MESH = pl.DeviceIdType.MESH


def unit_rows(ref, here):
    return unit(ref[here, :])


class Sems:
    def __init__(self):
        self.count, self.base = 0, {}

    def add(self, name, count=1):
        self.base[name] = self.count
        self.count += count


REMOTE = Sems()
for _name, _count in (
    ("c2", 4), ("c1", 4), ("c0", 8),
    ("2ax", 4), ("2by", 4), ("2ay", 4), ("2bx", 4), ("2z", 1), ("2zz", 1),
    ("1z", 4), ("1zz", 4), ("1ax", 1), ("1by", 1), ("1ay", 1), ("1bx", 1),
    ("0ax", 2), ("0by", 2), ("0ay", 2), ("0bx", 2), ("0z", 2), ("0zz", 1),
    ("out", 4), ("in", 4), ("sm", 4), ("smc", 3),
):
    REMOTE.add(_name, _count)
LOCAL = Sems()
for _name, _count in (
    ("w", 4), ("cot", 4), ("n2", 1), ("a", 4), ("b", 4), ("c", 4), ("mid", 1), ("att", 1), ("x", 1), ("proj", 1), ("probs", 2),
    ("n1", 1), ("ctx", 1), ("own", 2),
):
    LOCAL.add(_name, _count)


def backward(plan, cots, saved, mods, row_valid, fc1_weight, fc1_bias, fc2_weight, fc2_bias, out_weight, qkv_weight):
    n, rows, width, ff = plan.frame_axis, plan.rows, plan.width, plan.ff
    own, fl, clips = plan.own_patches, plan.local_frames, plan.clips
    span2, span1 = ff // plan.clip_axis, width // plan.clip_axis
    s1, s0 = 9 * span1, 7 * span1 + 2 * span1 + span1 // 3
    a1, a0 = 640, s0 // 2
    pad2, padq, wq = 384, 896, 3 * width // n
    blocks, block = plan.blocks, plan.block
    factor = plan.head_width ** (-0.5)
    half_rows = 64
    parts_per_clip = plan.clip_rows // half_rows

    def body(*refs):
        refs = list(refs)

        def take(count):
            got = refs[:count]
            del refs[:count]
            return got

        cot_h = take(n)
        (n2_h, n1_h, ctx_h, proj_h, probs_h, att_h, mid_h, x_h, fc1_h, fc2_h, wout_h, wqkv_h) = take(12)
        mod, valid, b1, b2 = take(4)
        (out_h, in_h) = take(2)
        sum2, sum1, sum0, small = take(4)
        (rc2, rc1, rc0, r2ax, r2by, r2ay, r2bx, r2z, r2zz) = take(9)
        (r1z, r1zz, r1ax, r1by, r1ay, r1bx) = take(6)
        (r0ax, r0by, r0ay, r0bx, r0z, r0zz, rsm, rsmc) = take(8)
        (keep2, keep1, r2, stage, tmp_a, tmp_b, tmp_c, dres, acc, f1, f2, ring, rows_out, sm, smc) = take(15)
        send_sem, recv_sem, local_sem = take(3)

        frame, clip = lax.axis_index("frame"), lax.axis_index("clip")
        mx, my = frame % 2, frame // 2
        core, z0, z1 = clip % 2, clip // 2 % 2, clip // 4
        partner = {
            "core": ("clip", clip + 1 - 2 * core),
            "z0": ("clip", clip + 2 - 4 * z0),
            "z1": ("clip", clip + 4 - 8 * z1),
            "x": ("frame", frame + 1 - 2 * mx),
            "y": ("frame", frame + 2 - 4 * my),
            "xy": ("frame", n - 1 - frame),
        }

        def remote(name, index, src, dst, bit):
            axis, where = partner[bit]
            at = REMOTE.base[name] + index
            return pltpu.make_async_remote_copy(
                src_ref=src,
                dst_ref=dst,
                send_sem=send_sem.at[at],
                recv_sem=recv_sem.at[at],
                device_id={axis: where},
                device_id_type=MESH,
            )

        def local(name, index, src, dst):
            return pltpu.make_async_copy(src, dst, local_sem.at[LOCAL.base[name] + index])

        lo1, hi1 = pl.ds(0, a1), pl.ds(a1, s1 - a1)
        lo0, hi0 = pl.ds(0, a0), pl.ds(a0, s0 - a0)
        all1 = pl.ds(0, s1)

        def c2(z):
            return remote("c2", z, stage.at[0, :, :, all1], rc2.at[z], "core")

        def c1(f):
            return remote("c1", f, stage.at[1, :, :, all1], rc1.at[f], "core")

        def c0(j, f):
            return remote("c0", 4 * j + f, stage.at[:, f // 2, f % 2], rc0.at[j, :, f // 2, f % 2], "core")

        def t2ax(z):
            return remote("2ax", z, keep2.at[z // 2, z % 2, :, 1 - mx, lo1], r2ax.at[z], "x")

        def t2by(z):
            return remote("2by", z, keep2.at[z // 2, z % 2, 1 - my, :, hi1], r2by.at[z], "y")

        def t2ay(z):
            return remote("2ay", z, keep2.at[z // 2, z % 2, 1 - my, mx, lo1], r2ay.at[z], "y")

        def t2bx(z):
            return remote("2bx", z, keep2.at[z // 2, z % 2, my, 1 - mx, hi1], r2bx.at[z], "x")

        def t2z():
            return remote("2z", 0, r2.at[:, 1 - z0], r2z, "z0")

        def t2zz():
            return remote("2zz", 0, r2.at[1 - z1, z0], r2zz, "z1")

        def t1z(f):
            return remote("1z", f, keep1.at[f // 2, f % 2, :, 1 - z0], r1z.at[f], "z0")

        def t1zz(f):
            return remote("1zz", f, keep1.at[f // 2, f % 2, 1 - z1, z0], r1zz.at[f], "z1")

        def t1ax():
            return remote("1ax", 0, keep1.at[:, 1 - mx, z1, z0, lo1], r1ax, "x")

        def t1by():
            return remote("1by", 0, keep1.at[1 - my, :, z1, z0, hi1], r1by, "y")

        def t1ay():
            return remote("1ay", 0, keep1.at[1 - my, mx, z1, z0, lo1], r1ay, "y")

        def t1bx():
            return remote("1bx", 0, keep1.at[my, 1 - mx, z1, z0, hi1], r1bx, "x")

        def t0ax(j):
            return remote("0ax", j, keep2.at[j, :, :, 1 - mx, lo0], r0ax.at[j], "x")

        def t0by(j):
            return remote("0by", j, keep2.at[j, :, 1 - my, :, hi0], r0by.at[j], "y")

        def t0ay(j):
            return remote("0ay", j, keep2.at[j, :, 1 - my, mx, lo0], r0ay.at[j], "y")

        def t0bx(j):
            return remote("0bx", j, keep2.at[j, :, my, 1 - mx, hi0], r0bx.at[j], "x")

        def t0z(j):
            return remote("0z", j, keep2.at[j, 1 - z0, my, mx], r0z.at[j], "z0")

        def t0zz():
            return remote("0zz", 0, keep2.at[1 - z1, z0, my, mx], r0zz, "z1")

        def row_send(name, k, dst, arriving=False):
            bit = (None, "x", "y", "xy")[k]
            place = partner[bit][1] if arriving else frame
            return remote(name, k, rows_out.at[k], dst.at[:, :, pl.ds(place * own, own)], bit)

        def row_own(index, dst):
            return local("own", index, rows_out.at[0], dst.at[:, :, pl.ds(frame * own, own)])

        def sm_send(k):
            return remote("sm", k, sm, rsm.at[k - 1], (None, "x", "y", "xy")[k])

        def smc_send(i):
            return remote("smc", i, smc.at[i], rsmc.at[i], ("core", "z0", "z1")[i])

        def add_to(ref, at, other, other_at):
            ref[at] = ref[at] + other[other_at]

        def load_c1(f):
            c1(f).wait_recv()
            local("a", 0, rc1.at[f], tmp_a.at[:, :, all1]).start()

        def run_c1(f):
            local("a", 0, rc1.at[f], tmp_a.at[:, :, all1]).wait()
            for i in range(2):
                for j in range(2):
                    add_to(keep1, (f // 2, f % 2, i, j), tmp_a, (i, j, all1))
            t1z(f).start()

        def load_c2(z):
            c2(z).wait_recv()
            local("b", 0, rc2.at[z], tmp_b.at[:, :, all1]).start()

        def run_c2(z):
            local("b", 0, rc2.at[z], tmp_b.at[:, :, all1]).wait()
            for i in range(2):
                for j in range(2):
                    add_to(keep2, (z // 2, z % 2, i, j, all1), tmp_b, (i, j, all1))
            t2ax(z).start()
            t2by(z).start()

        def z0_copies(f):
            return [local("a", 1, r1z.at[f], tmp_a.at[0, :, all1])]

        def load_z0(f):
            t1z(f).wait_recv()
            for copy in z0_copies(f):
                copy.start()

        def run_z0(f):
            for copy in z0_copies(f):
                copy.wait()
            for i in range(2):
                add_to(keep1, (f // 2, f % 2, i, z0), tmp_a, (0, i, all1))
            t1zz(f).start()

        def z1_copies(f, tmp, name, slot):
            return [local(name, 2 + slot, r1zz.at[f], tmp.at[1, slot, all1])]

        def load_z1(f, tmp, name, slot):
            t1zz(f).wait_recv()
            for copy in z1_copies(f, tmp, name, slot):
                copy.start()

        def run_z1(f, tmp, name, slot):
            for copy in z1_copies(f, tmp, name, slot):
                copy.wait()
            add_to(keep1, (f // 2, f % 2, z1, z0), tmp, (1, slot, all1))

        def xy1_copies(z):
            return [
                local("b", 0, r2ax.at[z], tmp_b.at[0, :, lo1]),
                local("b", 1, r2by.at[z], tmp_b.at[0, :, hi1]),
            ]

        def load_xy1(z):
            t2ax(z).wait_recv()
            t2by(z).wait_recv()
            for copy in xy1_copies(z):
                copy.start()

        def run_xy1(z):
            for copy in xy1_copies(z):
                copy.wait()
            for i in range(2):
                add_to(keep2, (z // 2, z % 2, i, mx, lo1), tmp_b, (0, i, lo1))
                add_to(keep2, (z // 2, z % 2, my, i, hi1), tmp_b, (0, i, hi1))
            t2ay(z).start()
            t2bx(z).start()

        def xy2_copies(z):
            return [
                local("c", 0, r2ay.at[z], tmp_c.at[0, lo1]),
                local("c", 1, r2bx.at[z], tmp_c.at[0, hi1]),
            ]

        def load_xy2(z):
            t2ay(z).wait_recv()
            t2bx(z).wait_recv()
            for copy in xy2_copies(z):
                copy.start()

        def run_xy2(z):
            for copy in xy2_copies(z):
                copy.wait()
            r2[z // 2, z % 2] = keep2[z // 2, z % 2, my, mx, all1] + tmp_c[0, all1]

        def weight(slot, src):
            return local("w", slot, src, ring.at[slot])

        def fc1_block(f):
            return weight(2 * (f % 2), fc1_h.at[:, pl.ds(pl.multiple_of(f * width, LANES), width)])

        def fc2_block(f):
            return weight(2 * (f % 2) + 1, fc2_h.at[pl.ds(pl.multiple_of(f * width, 16), width)])

        def qkv_block(i, slot):
            return weight(slot, wqkv_h.at[:, i * width : (i + 1) * width])

        def own_copies(src, dst, name):
            return local(name, 0, src, dst)

        barrier = pltpu.get_barrier_semaphore()
        for axis, where in partner.values():
            pl.semaphore_signal(barrier, inc=1, device_id={axis: where}, device_id_type=MESH)

        fc1_block(0).start()
        fc2_block(0).start()
        sm[...] = jnp.zeros_like(sm)

        def mlp(n2, n2_turned, dbr, padded, act, act_turned, dh, res):
            own_copies(n2_h, n2, "n2").start()

            def prepare(cot):
                for k in range(n):
                    local("cot", k, cot_h[k], cot.at[k]).start()
                padded[...] = jnp.zeros_like(padded)
                f1[...] = jnp.zeros_like(f1)
                acc[...] = jnp.zeros_like(acc)
                for k in range(n):
                    local("cot", k, cot_h[k], cot.at[k]).wait()
                total = jnp.zeros((1, width), F32)
                for c in range(clips):
                    for half in range(plan.halves):
                        for k in range(n):
                            row = plan.row_of(c, half, k)
                            here = slice(row, row + plan.piece)
                            piece = cot[k, c, half].astype(F32).reshape(plan.piece, width) * valid[here, 0:1]
                            dres[here, :] = piece.astype(BF16)
                            low = (piece * mod[c, 5:6, :]).astype(BF16)
                            dbr[here, :] = low
                            total = total + jnp.sum(low.astype(F32), axis=0, keepdims=True)
                sm[0, 7:8, :] = total
                for f in range(n):
                    padded[:, f * pad2 : f * pad2 + width // n] = dbr[:, f * (width // n) : (f + 1) * (width // n)]

            pl.run_scoped(prepare, pltpu.VMEM((n,) + plan.chunk_dims, BF16))
            own_copies(n2_h, n2, "n2").wait()
            n2_turned[...] = n2[...].T
            pl.semaphore_wait(barrier, len(partner))

            @pl.loop(0, n)
            def _(f):
                slot = 2 * (f % 2)

                @pl.when(f < n - 1)
                def _():
                    fc1_block(f + 1).start()
                    fc2_block(f + 1).start()

                @pl.when(f == n - 1)
                def _():
                    weight(0, wout_h).start()
                    qkv_block(0, 1).start()

                fc1_block(f).wait()
                f2[...] = mm(n2[...], ring[slot])
                bias = b1[f]

                @pl.loop(0, rows // half_rows)
                def _(i):
                    here = pl.ds(pl.multiple_of(i * half_rows, half_rows), half_rows)
                    hidden = f2[here, :] + bias
                    square = hidden * hidden
                    bent = jnp.tanh(0.7978845608028654 * hidden * (1.0 + 0.044715 * square))
                    act[here, :] = (0.5 * hidden * (1.0 + bent)).astype(BF16)
                    slope = 0.7978845608028654 * (1.0 + 3.0 * 0.044715 * square)
                    f2[here, :] = 0.5 * (1.0 + bent) + 0.5 * hidden * (1.0 - bent * bent) * slope

                @pl.when(f >= 2)
                def _():
                    load_z0(f - 2)

                fc2_block(f).wait()
                dh[...] = (mm_cols(dbr[...], ring[slot + 1]) * f2[...]).astype(BF16)
                sm[0, pl.ds(3 + f, 1), :] = jnp.sum(dh[...].astype(F32), axis=0, keepdims=True)

                @pl.when(f >= 2)
                def _():
                    run_z0(f - 2)

                @pl.when(f >= 1)
                def _():
                    load_xy1(f - 1)
                    c1(f - 1).wait_send()

                for first, tiles in ((0, 5), (5, 4)):
                    lanes = slice(first * LANES, (first + tiles) * LANES)
                    res[:, : tiles * LANES] = mm(n2_turned[...], dh[:, lanes])
                    for mine in (False, True):
                        part = core if mine else 1 - core
                        for i in range(2):
                            for j in range(2):
                                at = pl.ds(pl.multiple_of((4 * i + 2 * j + part) * span1, 8), span1)
                                for t in range(tiles):
                                    slab = slice((first + t) * span1, (first + t + 1) * span1)
                                    values = res[at, t * LANES : (t + 1) * LANES].astype(BF16)
                                    if mine:
                                        keep1[f // 2, f % 2, i, j, slab, :] = values
                                    else:
                                        stage[1, i, j, slab, :] = values
                c1(f).start()

                @pl.when(f >= 1)
                def _():
                    run_xy1(f - 1)
                    c2(f - 1).wait_send()

                act_turned[...] = act[...].T
                for i in range(2):
                    res[...] = mm(act_turned[...], padded[:, i * 2 * pad2 : (i + 1) * 2 * pad2])
                    for mine in (False, True):
                        part = core if mine else 1 - core
                        at = pl.ds(pl.multiple_of(part * span2, 8), span2)
                        for j in range(2):
                            pieces = [
                                res[at, j * pad2 + t * LANES : j * pad2 + (t + 1) * LANES] for t in range(3)
                            ]
                            pieces[2] = fold_tile(pieces[2], 4, 32)
                            row = 0
                            for piece in pieces:
                                slab = slice(row, row + piece.shape[0])
                                if mine:
                                    keep2[f // 2, f % 2, i, j, slab, :] = piece.astype(BF16)
                                else:
                                    stage[0, i, j, slab, :] = piece.astype(BF16)
                                row += piece.shape[0]
                c2(f).start()
                load_c1(f)

                @pl.when(f >= 1)
                def _():
                    load_xy2(f - 1)

                acc[...] += mm_cols(dh[...], ring[slot])
                run_c1(f)

                @pl.when(f >= 1)
                def _():
                    run_xy2(f - 1)

                load_c2(f)
                f1[...] += mm(act[...], ring[slot + 1])
                run_c2(f)

        pl.run_scoped(
            mlp,
            pltpu.VMEM((rows, width), BF16),
            pltpu.VMEM((width, rows), BF16),
            pltpu.VMEM((rows, width), BF16),
            pltpu.VMEM((rows, n * pad2), BF16),
            pltpu.VMEM((rows, width), BF16),
            pltpu.VMEM((width, rows), BF16),
            pltpu.VMEM((rows, width), BF16),
            pltpu.VMEM((width, 2 * pad2), F32),
        )

        def rest(datt, proj):
            own_copies(mid_h, f2, "mid").start()
            own_copies(proj_h, proj, "proj").start()
            qkv_block(1, 3).start()
            load_z0(2)

            def attend(dctx, probs, acc3):
                def middle(att):
                    own_copies(att_h, att, "att").start()
                    own_copies(mid_h, f2, "mid").wait()
                    own_copies(att_h, att, "att").wait()

                    @pl.loop(0, rows // half_rows)
                    def _(i):
                        here = pl.ds(pl.multiple_of(i * half_rows, half_rows), half_rows)
                        c = i // parts_per_clip
                        normed, inverse = unit_rows(f2, here)
                        grad = acc[here, :]
                        sm[1 + c, 3:4, :] += jnp.sum(grad, axis=0, keepdims=True)
                        sm[1 + c, 4:5, :] += jnp.sum(grad * normed, axis=0, keepdims=True)
                        d_middle = dres[here, :].astype(F32) + unit_back(normed, inverse, grad * (1.0 + mod[c, 4:5, :]))
                        acc[here, :] = d_middle
                        sm[1 + c, 2:3, :] += jnp.sum(d_middle * att[here, :], axis=0, keepdims=True)
                        low = (d_middle * mod[c, 2:3, :]).astype(BF16)
                        datt[here, :] = low
                        sm[0, 2:3, :] += jnp.sum(low.astype(F32), axis=0, keepdims=True)

                pl.run_scoped(middle, pltpu.VMEM((rows, width), F32))
                run_z0(2)
                load_xy1(3)
                local("probs", 0, probs_h.at[0], probs.at[0]).start()
                weight(0, wout_h).wait()
                dctx[...] = mm_cols(datt[...], ring[0]).astype(BF16)
                run_xy1(3)
                load_z0(3)
                qkv_block(2, 0).start()

                @pl.loop(0, clips)
                def _(c):
                    for half in range(plan.halves):
                        for k in range(n):
                            here = pl.ds(pl.multiple_of(c * plan.clip_rows + plan.row_of(0, half, k), 8), plan.piece)
                            branch = f1[here, :] + b2[...]
                            sm[1 + c, 5:6, :] += jnp.sum(dres[here, :].astype(F32) * branch, axis=0, keepdims=True)
                            total = valid[here, 0:1] * (f2[here, :] + mod[c, 5:6, :] * branch)
                            rows_out[k, c, :, half * 8 : half * 8 + 8, :] = total.reshape(fl, 8, width).astype(BF16)

                for k in (3, 1, 2):
                    row_send("out", k, out_h).start()
                row_own(0, out_h).start()
                own_copies(x_h, f2, "x").start()
                run_z0(3)
                load_xy2(3)
                own_copies(proj_h, proj, "proj").wait()

                @pl.loop(0, blocks)
                def _(b):
                    slot = b % 2
                    here = pl.ds(pl.multiple_of(b * block, block), block)

                    @pl.when(b < blocks - 1)
                    def _():
                        local("probs", 1 - slot, probs_h.at[b + 1], probs.at[1 - slot]).start()

                    local("probs", slot, probs_h.at[b], probs.at[slot]).wait()
                    acc3[...] = jnp.zeros_like(acc3)
                    for h in range(HEADS):
                        _, start, size = head_window(h, plan.head_width)
                        keep = head_mask(h, plan.head_width)
                        cols = slice(start, start + size)
                        weights = probs[slot, h]
                        d_c = dctx[here, cols] * keep
                        d_weight = mm_cols(d_c, proj[2, here, cols])
                        mixed = weights * d_weight
                        d_score = (mixed - weights * jnp.sum(mixed, axis=-1, keepdims=True)).astype(BF16)
                        acc3[2, :, cols] += mm_rows(weights.astype(BF16), d_c)
                        acc3[0, :, cols] += mm(d_score, proj[1, here, cols] * keep)
                        acc3[1, :, cols] += mm_rows(d_score, proj[0, here, cols] * keep)
                    for part in range(3):
                        values = acc3[part] if part == 2 else acc3[part] * factor
                        low = values.astype(BF16)
                        proj[part, here, :] = low
                        if part != 1:
                            at = part // 2
                            sm[0, at : at + 1, :] += jnp.sum(low.astype(F32), axis=0, keepdims=True)

                    @pl.when(b == 0)
                    def _():
                        run_xy2(3)
                        t2z().start()
                        load_z1(0, tmp_a, "a", 0)
                        load_z1(1, tmp_a, "a", 1)

                    @pl.when(b == 1)
                    def _():
                        run_z1(0, tmp_a, "a", 0)
                        run_z1(1, tmp_a, "a", 1)
                        load_z1(2, tmp_b, "b", 0)

                    @pl.when(b == 2)
                    def _():
                        run_z1(2, tmp_b, "b", 0)
                        load_z1(3, tmp_b, "b", 1)

                    @pl.when(b == 3)
                    def _():
                        run_z1(3, tmp_b, "b", 1)
                        t1ax().start()
                        t1by().start()

            pl.run_scoped(
                attend,
                pltpu.VMEM((rows, width), BF16),
                pltpu.VMEM((2, HEADS, block, block), F32),
                pltpu.VMEM((3, block, width), F32),
            )

            def z_copy():
                return local("c", 2, r2z, tmp_c.at[:, all1])

            def xy_copies():
                return [
                    local("a", 0, r1ax, tmp_a.at[0, :, lo1]),
                    local("a", 1, r1by, tmp_a.at[0, :, hi1]),
                ]

            def c0_copies(j):
                return [local("a", 0, rc0.at[j, 0], tmp_a), local("b", 0, rc0.at[j, 1], tmp_b)]

            def load_c0(j):
                for f in range(n):
                    c0(j, f).wait_recv()
                for copy in c0_copies(j):
                    copy.start()

            def run_c0(j):
                for copy in c0_copies(j):
                    copy.wait()
                for i in range(2):
                    for k in range(2):
                        add_to(keep2, (j, 0, i, k), tmp_a, (i, k))
                        add_to(keep2, (j, 1, i, k), tmp_b, (i, k))
                t0ax(j).start()
                t0by(j).start()

            def weight_grads(right_q, right_o, left, res):
                own_copies(n1_h, left.at[0], "n1").start()
                own_copies(ctx_h, left.at[1], "ctx").start()
                t2z().wait_recv()
                z_copy().start()
                right_q[...] = jnp.zeros_like(right_q)
                right_o[...] = jnp.zeros_like(right_o)
                wide = width // n
                for f in range(n):
                    right_o[f, :, :wide] = datt[:, f * wide : (f + 1) * wide]
                    low, high = f * wq, (f + 1) * wq
                    for part in range(3):
                        a, b = max(low, part * width), min(high, (part + 1) * width)
                        if a < b:
                            right_q[f, :, a - low : b - low] = proj[part, :, a - part * width : b - part * width]
                own_copies(n1_h, left.at[0], "n1").wait()
                ring[2, :, :rows] = left[0].T
                own_copies(ctx_h, left.at[1], "ctx").wait()
                ring[2, :, rows : 2 * rows] = left[1].T
                for z in range(4):
                    t2ax(z).wait_send()
                    t2by(z).wait_send()
                    t2ay(z).wait_send()
                    t2bx(z).wait_send()
                c1(3).wait_send()
                c2(3).wait_send()

                @pl.loop(0, 2 * n)
                def _(step):
                    j, f = step // n, step % n
                    lines = pl.ds(pl.multiple_of(j * 4 * span1, 16), 4 * span1)

                    @pl.when(j == 1)
                    def _():
                        c0(0, f).wait_send()

                    res[:, :padq] = mm(ring[2, lines, :rows], right_q[f])
                    res[:, padq:] = mm(ring[2, lines, rows : 2 * rows], right_o[f])
                    for mine in (False, True):
                        part = core if mine else 1 - core
                        for i in range(2):
                            at = pl.ds(pl.multiple_of((2 * i + part) * span1, 8), span1)
                            pieces = [res[at, t * LANES : (t + 1) * LANES] for t in range(10)]
                            pieces[9] = fold_tile(pieces[9], 3, 32)
                            row = 0
                            for piece in pieces:
                                slab = slice(row, row + piece.shape[0])
                                if mine:
                                    keep2[j, i, f // 2, f % 2, slab, :] = piece.astype(BF16)
                                else:
                                    stage[i, f // 2, f % 2, slab, :] = piece.astype(BF16)
                                row += piece.shape[0]
                    c0(j, f).start()

                    @pl.when(step == 2)
                    def _():
                        z_copy().wait()
                        for i in range(2):
                            add_to(r2, (i, z0), tmp_c, (i, all1))
                        t2zz().start()
                        t1ax().wait_recv()
                        t1by().wait_recv()
                        for copy in xy_copies():
                            copy.start()

                    @pl.when(step == 4)
                    def _():
                        for copy in xy_copies():
                            copy.wait()
                        for i in range(2):
                            add_to(keep1, (i, mx, z1, z0, lo1), tmp_a, (0, i, lo1))
                            add_to(keep1, (my, i, z1, z0, hi1), tmp_a, (0, i, hi1))
                        t1ay().start()
                        t1bx().start()

                    @pl.when(step == 5)
                    def _():
                        load_c0(0)

                    @pl.when(step == 6)
                    def _():
                        run_c0(0)

            pl.run_scoped(
                weight_grads,
                pltpu.VMEM((n, rows, padq), BF16),
                pltpu.VMEM((n, rows, pad2), BF16),
                pltpu.VMEM((2, rows, width), BF16),
                pltpu.VMEM((4 * span1, padq + pad2), F32),
            )

            qkv_block(0, 1).wait()
            f1[...] = mm_cols(proj[0], ring[1])
            load_c0(1)
            qkv_block(1, 3).wait()
            f1[...] += mm_cols(proj[1], ring[3])
            run_c0(1)
            qkv_block(2, 0).wait()
            f1[...] += mm_cols(proj[2], ring[0])
            own_copies(x_h, f2, "x").wait()
            for k in (1, 2, 3):
                row_send("out", k, out_h).wait_send()
            row_own(0, out_h).wait()

            @pl.loop(0, clips)
            def _(c):
                for half in range(plan.halves):
                    for k in range(n):
                        here = pl.ds(pl.multiple_of(c * plan.clip_rows + plan.row_of(0, half, k), 8), plan.piece)
                        normed, inverse = unit_rows(f2, here)
                        grad = f1[here, :]
                        sm[1 + c, 0:1, :] += jnp.sum(grad, axis=0, keepdims=True)
                        sm[1 + c, 1:2, :] += jnp.sum(grad * normed, axis=0, keepdims=True)
                        total = acc[here, :] + unit_back(normed, inverse, grad * (1.0 + mod[c, 1:2, :]))
                        rows_out[k, c, :, half * 8 : half * 8 + 8, :] = total.reshape(fl, 8, width).astype(BF16)

            for k in (1, 2, 3):
                sm_send(k).start()
            for k in (3, 1, 2):
                row_send("in", k, in_h).start()
            row_own(1, in_h).start()

            def q1_copies(j, tmp, name):
                return [
                    local(name, 2, r0ax.at[j], tmp.at[:, :, lo0]),
                    local(name, 3, r0by.at[j], tmp.at[:, :, hi0]),
                ]

            def load_q1(j, tmp, name):
                t0ax(j).wait_recv()
                t0by(j).wait_recv()
                for copy in q1_copies(j, tmp, name):
                    copy.start()

            def run_q1(j, tmp, name):
                for copy in q1_copies(j, tmp, name):
                    copy.wait()
                for i in range(2):
                    for k in range(2):
                        add_to(keep2, (j, i, k, mx, lo0), tmp, (i, k, lo0))
                        add_to(keep2, (j, i, my, k, hi0), tmp, (i, k, hi0))
                t0ay(j).start()
                t0bx(j).start()

            def q2(j):
                t0ay(j).wait_recv()
                t0bx(j).wait_recv()
                copies = [
                    local("a", 0, r0ay.at[j], tmp_a.at[0, :, lo0]),
                    local("a", 1, r0bx.at[j], tmp_a.at[0, :, hi0]),
                ]
                for copy in copies:
                    copy.start()
                for copy in copies:
                    copy.wait()
                for i in range(2):
                    add_to(keep2, (j, i, my, mx), tmp_a, (0, i))
                t0z(j).start()

            copies = [
                local("c", 0, r1ay, tmp_c.at[0, lo1]),
                local("c", 1, r1bx, tmp_c.at[0, hi1]),
                local("c", 2, r2zz, tmp_c.at[1, all1]),
            ]
            t1ay().wait_recv()
            t1bx().wait_recv()
            t2zz().wait_recv()
            for copy in copies:
                copy.start()
            load_q1(0, tmp_a, "a")
            for copy in copies:
                copy.wait()
            sum1[...] = keep1[my, mx, z1, z0].astype(F32) + tmp_c[0, all1].astype(F32)
            sum2[...] = r2[z1, z0].astype(F32) + tmp_c[1, all1].astype(F32)
            run_q1(0, tmp_a, "a")

            def small_sums(tmp, tmpc):
                for k in (1, 2, 3):
                    sm_send(k).wait_recv()
                    local("c", k, rsm.at[k - 1], tmp.at[k - 1]).start()
                for k in (1, 2, 3):
                    local("c", k, rsm.at[k - 1], tmp.at[k - 1]).wait()
                small[...] = sm[...] + tmp[0] + tmp[1] + tmp[2]
                smc[0] = small[0]
                smc_send(0).start()
                load_q1(1, tmp_b, "b")
                run_q1(1, tmp_b, "b")
                for i in range(3):
                    smc_send(i).wait_recv()
                    copy = local("c", 0, rsmc.at[i], tmpc)
                    copy.start()
                    copy.wait()
                    if i < 2:
                        smc[i + 1] = smc[i] + tmpc[...]
                        smc_send(i + 1).start()
                        q2(i)
                    else:
                        small[0] = smc[i] + tmpc[...]

            pl.run_scoped(
                small_sums, pltpu.VMEM((n - 1, 1 + clips, 8, width), F32), pltpu.VMEM((8, width), F32)
            )

            for j in range(2):
                t0z(j).wait_recv()
                local("c", j, r0z.at[j], tmp_c.at[j]).start()
            for j in range(2):
                local("c", j, r0z.at[j], tmp_c.at[j]).wait()
                add_to(keep2, (j, z0, my, mx), tmp_c, (j,))
            t0zz().start()
            t0zz().wait_recv()
            copy = local("c", 0, r0zz, tmp_c.at[0])
            copy.start()
            copy.wait()
            sum0[...] = keep2[z1, z0, my, mx].astype(F32) + tmp_c[0].astype(F32)

            row_own(1, in_h).wait()
            for k in (1, 2, 3):
                row_send("out", k, out_h, True).wait_recv()
                row_send("in", k, in_h, True).wait_recv()
                row_send("in", k, in_h).wait_send()
                sm_send(k).wait_send()
            for i in range(3):
                smc_send(i).wait_send()
            for f in range(n):
                t1z(f).wait_send()
                t1zz(f).wait_send()
                c0(1, f).wait_send()
            for j in range(2):
                for transfer in (t0ax, t0by, t0ay, t0bx, t0z):
                    transfer(j).wait_send()
            for transfer in (t2z, t2zz, t1ax, t1by, t1ay, t1bx, t0zz):
                transfer().wait_send()

        pl.run_scoped(rest, pltpu.VMEM((rows, width), BF16), pltpu.VMEM((3, rows, width), BF16))

    lanes = LANES
    image = shape((clips, fl, plan.patches, width), BF16)
    arriving = [
        (4, 2, 2, s1), (4, 2, 2, s1), (2, 2, 2, 2, s0),
        (4, 2, a1), (4, 2, s1 - a1), (4, a1), (4, s1 - a1), (2, s1), (s1,),
        (4, 2, s1), (4, s1), (2, a1), (2, s1 - a1), (a1,), (s1 - a1,),
        (2, 2, 2, a0), (2, 2, 2, s0 - a0), (2, 2, a0), (2, 2, s0 - a0), (2, s0), (s0,),
    ]
    vmem = pl.BlockSpec(memory_space=pltpu.VMEM)
    smalls = (1 + clips, 8, width)
    out_shape = (
        [image, image, shape((s1, lanes), F32), shape((s1, lanes), F32), shape((s0, lanes), F32), shape(smalls, F32)]
        + [shape(dims + (lanes,), BF16) for dims in arriving]
        + [shape((n - 1,) + smalls, F32), shape((3, 8, width), F32)]
    )
    out_specs = [ANY, ANY] + [vmem] * 4 + [ANY] * (len(arriving) + 2)
    scratch = [
        pltpu.VMEM((2, 2, 2, 2, s0, lanes), BF16),
        pltpu.VMEM((2, 2, 2, 2, s1, lanes), BF16),
        pltpu.VMEM((2, 2, s1, lanes), BF16),
        pltpu.VMEM((2, 2, 2, s0, lanes), BF16),
        pltpu.VMEM((2, 2, s0, lanes), BF16),
        pltpu.VMEM((2, 2, s0, lanes), BF16),
        pltpu.VMEM((2, s0, lanes), BF16),
        pltpu.VMEM((rows, width), BF16),
        pltpu.VMEM((rows, width), F32),
        pltpu.VMEM((rows, width), F32),
        pltpu.VMEM((rows, width), F32),
        pltpu.VMEM((4, width, width), BF16),
        pltpu.VMEM((n, clips, fl, own, width), BF16),
        pltpu.VMEM(smalls, F32),
        pltpu.VMEM((3, 8, width), F32),
        pltpu.SemaphoreType.DMA((REMOTE.count,)),
        pltpu.SemaphoreType.DMA((REMOTE.count,)),
        pltpu.SemaphoreType.DMA((LOCAL.count,)),
    ]
    result = pl.pallas_call(
        body,
        in_specs=[ANY] * (n + 12) + [vmem] * 4,
        out_specs=out_specs,
        out_shape=out_shape,
        scratch_shapes=scratch,
        compiler_params=pltpu.CompilerParams(
            vmem_limit_bytes=VMEM_LIMIT, collective_id=0, has_side_effects=True
        ),
        cost_estimate=cost(45e9, 200e6),
        name="backward",
    )(
        *cots,
        *[saved[k] for k in ("n2", "n1", "ctx", "proj", "probs", "att", "mid", "x")],
        fc1_weight,
        fc2_weight,
        out_weight,
        qkv_weight,
        mods,
        row_valid,
        fc1_bias,
        fc2_bias,
    )
    return result[:6]


def unpack(sums, layouts):
    def body(*refs):
        ins, outs = refs[: len(sums)], refs[len(sums) : len(sums) + len(layouts)]
        turn = refs[-1]
        for out, (which, first, span, tiles, used, folds, turned) in zip(outs, layouts):
            ref = ins[which]
            to = turn if turned else out
            for j in range(tiles):
                to[:, j * LANES : (j + 1) * LANES] = ref[first + j * span : first + (j + 1) * span, :]
            if used:
                tile = ref[first + tiles * span : first + tiles * span + span // folds, :]
                for g in range(folds):
                    moved = tile if g == 0 else pltpu.roll(tile, LANES - g * used, 1)
                    here = slice(g * (span // folds), (g + 1) * (span // folds))
                    to[here, tiles * LANES : tiles * LANES + used] = moved[:, :used]
            if turned:
                out[...] = turn[...].T

    dims = [(span, tiles * LANES + used) for _, _, span, tiles, used, _, _ in layouts]
    out_shape = [shape(d[::-1] if layout[-1] else d, F32) for d, layout in zip(dims, layouts)]
    return pl.pallas_call(
        body,
        grid=(1,),
        in_specs=[whole(s.shape) for s in sums],
        out_specs=[whole(s.shape) for s in out_shape],
        out_shape=out_shape,
        scratch_shapes=[pltpu.VMEM(dims[0], F32)],
        compiler_params=params(),
        cost_estimate=cost(0, 8e6),
        name="unpack",
    )(*sums)


def fast_layer(
    mesh,
    block_input,
    modulation,
    frame_counts,
    qkv_weight,
    qv_bias,
    out_weight,
    out_bias,
    fc1_weight,
    fc1_bias,
    fc2_weight,
    fc2_bias,
    out_cotangent,
):
    plan = Plan(mesh, block_input.shape, qkv_weight.shape, fc1_weight.shape)
    n, width, rows = plan.frame_axis, plan.width, plan.rows
    frame_at = lax.axis_index("frame").astype(jnp.int32)
    me = frame_at.reshape(1)

    slot = jnp.arange(plan.frames, dtype=jnp.int32)
    frame_of = jnp.bitwise_xor(slot // plan.local_frames, frame_at) * plan.local_frames + slot % plan.local_frames
    valid = frame_of[None, :] < frame_counts[:, None]
    place = jnp.arange(plan.block, dtype=jnp.int32)
    same = place[:, None] % 8 == place[None, :] % 8
    allowed = same[None] & jnp.repeat(valid, 8, axis=1)[:, None, :]
    score_mask = jnp.where(allowed, 0.0, NEGATIVE).astype(F32)
    row_valid = jnp.broadcast_to(
        valid.astype(F32)[:, None, :, None, None], (plan.clips, plan.halves, plan.frames, 8, LANES)
    ).reshape(rows, LANES)
    mods = modulation.astype(F32).reshape(plan.clips, 6, width)
    bias_full = jnp.concatenate(
        [qv_bias[:width], jnp.zeros((width,), BF16), qv_bias[width:]]
    ).astype(F32)[None, :]

    def line(vector):
        return vector.astype(F32)[None, :]

    inputs = exchange(plan, split_chunks(plan, me, block_input))
    cotangents = exchange(plan, split_chunks(plan, me, out_cotangent))
    saved = forward(plan, inputs, mods, score_mask, qkv_weight, bias_full, out_weight, line(out_bias))
    block_output, input_grad, sum2, sum1, sum0, small = backward(
        plan,
        cotangents,
        saved,
        mods,
        row_valid,
        fc1_weight,
        fc1_bias.astype(F32).reshape(plan.ff // width, 1, width),
        fc2_weight,
        line(fc2_bias),
        out_weight,
        qkv_weight,
    )
    span2, span1 = plan.ff // plan.clip_axis, width // plan.clip_axis
    fc2_turned, fc1_out, qkv_out, out_out = unpack(
        (sum2, sum1, sum0),
        (
            (0, 0, span2, 2, 32, 4, True),
            (1, 0, span1, 9, 0, 1, False),
            (2, 0, span1, 6, 96, 1, False),
            (2, 7 * span1, span1, 2, 32, 3, False),
        ),
    )

    def share(vector):
        size = vector.shape[-1] // n
        return lax.dynamic_slice_in_dim(vector, frame_at * size, size, vector.ndim - 1)

    biases = small[0]
    return (
        block_output,
        input_grad,
        share(small[1:, :6].reshape(plan.clips, 6 * width)),
        qkv_out,
        share(biases[0:2].reshape(-1)),
        out_out,
        share(biases[2]),
        fc1_out,
        share(biases[3:7].reshape(-1)),
        fc2_turned.T,
        share(biases[7]),
    )


def solution(mesh):
    placed = (
        P("clip", "frame", None, None),
        P("clip", None),
        P("clip"),
        P(),
        P(),
        P(),
        P(),
        P(),
        P(),
        P(),
        P(),
        P("clip", "frame", None, None),
    )
    def layer(*arrays):
        if fits(mesh, arrays[0].shape, arrays[3].shape, arrays[7].shape):
            return fast_layer(mesh, *arrays)
        return on_device(*arrays)

    return jax.shard_map(
        layer,
        mesh=mesh,
        in_specs=placed,
        out_specs=(
            P("clip", "frame", None, None),
            P("clip", "frame", None, None),
            P("clip", "frame"),
            P("clip", "frame"),
            P("frame"),
            P("clip", "frame"),
            P("frame"),
            P("clip", "frame"),
            P("frame"),
            P("clip", "frame"),
            P("frame"),
        ),
        check_vma=False,
    )
```

```python
import functools

import jax
import jax.numpy as jnp
from jax import lax
from jax.experimental import pallas as pl
from jax.experimental.pallas import tpu as pltpu
from jax.sharding import PartitionSpec as P

HEADS = 16


EPSILON = 1e-06
NEGATIVE = -1e30


def normalize(values):
    centred = values - jnp.mean(values, axis=-1, keepdims=True)
    variance = jnp.mean(centred * centred, axis=-1, keepdims=True)
    return centred * lax.rsqrt(variance + EPSILON)


def modulate(values, shift_term, scale_term):
    return normalize(values) * (1.0 + scale_term) + shift_term


def gelu_tanh(inputs):
    return jax.nn.gelu(inputs, approximate=True)


def contract_rows(left, right):
    return lax.dot_general(
        left, right, (((0,), (0,)), ((), ())), preferred_element_type=jnp.float32
    )


def contract_cols(left, right):
    return lax.dot_general(
        left, right, (((1,), (1,)), ((), ())), preferred_element_type=jnp.float32
    )


def on_device(
    block_input,
    modulation,
    frame_counts,
    qkv_weight,
    qv_bias,
    out_weight,
    out_bias,
    fc1_weight,
    fc1_bias,
    fc2_weight,
    fc2_bias,
    out_cotangent,
):
    swapped = lax.all_to_all(block_input, "frame", split_axis=2, concat_axis=1, tiled=True)
    clip_count, frames, patches, model_width = swapped.shape
    head_width = model_width // HEADS
    row_count = clip_count * frames * patches
    factor = head_width ** (-0.5)
    frame_valid = (jnp.arange(frames)[None, :] < frame_counts[:, None]).astype(jnp.float32)
    valid_rows = frame_valid[:, :, None, None]
    key_valid = frame_valid[:, None, None, None, :] > 0.5
    modulators = modulation.astype(jnp.float32).reshape(clip_count, 6, model_width)[
        :, :, None, None, :
    ]
    shift_one = modulators[:, 0]
    scale_one = modulators[:, 1]
    gate_one = modulators[:, 2]
    shift_two = modulators[:, 3]
    scale_two = modulators[:, 4]
    gate_two = modulators[:, 5]
    residual = swapped.astype(jnp.float32)
    normed_full, modulate_back_one = jax.vjp(modulate, residual, shift_one, scale_one)
    normed_one = normed_full.astype(jnp.bfloat16).reshape(row_count, model_width)
    bias_full = jnp.concatenate(
        [qv_bias[:model_width], jnp.zeros((model_width,), jnp.bfloat16), qv_bias[model_width:]]
    ).astype(jnp.float32)
    projected = (
        jnp.dot(normed_one, qkv_weight, preferred_element_type=jnp.float32) + bias_full
    ).astype(jnp.bfloat16)
    shaped = projected.reshape(clip_count, frames, patches, 3, HEADS, head_width)
    queries = shaped[:, :, :, 0]
    keys_all = shaped[:, :, :, 1]
    values_all = shaped[:, :, :, 2]
    scores = (
        jnp.einsum("cfphd,cgphd->cphfg", queries, keys_all, preferred_element_type=jnp.float32)
        * factor
    )
    scores = jnp.where(key_valid, scores, NEGATIVE)
    row_peak = jnp.max(scores, axis=-1, keepdims=True)
    exponent = jnp.exp(scores - row_peak)
    attention_weights = exponent / jnp.sum(exponent, axis=-1, keepdims=True)
    weights_low = attention_weights.astype(jnp.bfloat16)
    context = jnp.einsum(
        "cphfg,cgphd->cfphd", weights_low, values_all, preferred_element_type=jnp.float32
    )
    context_low = context.astype(jnp.bfloat16).reshape(row_count, model_width)
    attended = jnp.dot(
        context_low, out_weight, preferred_element_type=jnp.float32
    ) + out_bias.astype(jnp.float32)
    attended = attended.reshape(clip_count, frames, patches, model_width)
    middle = residual + gate_one * attended
    normed_mid, modulate_back_two = jax.vjp(modulate, middle, shift_two, scale_two)
    normed_two = normed_mid.astype(jnp.bfloat16).reshape(row_count, model_width)
    hidden = jnp.dot(normed_two, fc1_weight, preferred_element_type=jnp.float32) + fc1_bias.astype(
        jnp.float32
    )
    activated_full, gelu_back = jax.vjp(gelu_tanh, hidden)
    activated = activated_full.astype(jnp.bfloat16)
    branch_two = jnp.dot(
        activated, fc2_weight, preferred_element_type=jnp.float32
    ) + fc2_bias.astype(jnp.float32)
    branch_two = branch_two.reshape(clip_count, frames, patches, model_width)
    result = valid_rows * (middle + gate_two * branch_two)
    block_output = lax.all_to_all(
        result.astype(jnp.bfloat16), "frame", split_axis=1, concat_axis=2, tiled=True
    )
    cotangent = lax.all_to_all(
        out_cotangent, "frame", split_axis=2, concat_axis=1, tiled=True
    ).astype(jnp.float32)
    d_result = valid_rows * cotangent
    d_gate_two = jnp.sum(d_result * branch_two, axis=(1, 2))
    d_branch = (d_result * gate_two).astype(jnp.bfloat16).reshape(row_count, model_width)
    d_fc2_bias = jnp.sum(d_branch.astype(jnp.float32), axis=0)
    d_fc2_weight = contract_rows(activated, d_branch)
    d_activated = contract_cols(d_branch, fc2_weight)
    d_hidden = gelu_back(d_activated)[0].astype(jnp.bfloat16)
    d_fc1_bias = jnp.sum(d_hidden.astype(jnp.float32), axis=0)
    d_fc1_weight = contract_rows(normed_two, d_hidden)
    d_normed_two = contract_cols(d_hidden, fc1_weight).reshape(
        clip_count, frames, patches, model_width
    )
    d_middle_norm, d_shift_two, d_scale_two = modulate_back_two(d_normed_two)
    d_middle = d_result + d_middle_norm
    d_gate_one = jnp.sum(d_middle * attended, axis=(1, 2))
    d_attended = (d_middle * gate_one).astype(jnp.bfloat16).reshape(row_count, model_width)
    d_out_bias = jnp.sum(d_attended.astype(jnp.float32), axis=0)
    d_out_weight = contract_rows(context_low, d_attended)
    d_context = contract_cols(d_attended, out_weight).astype(jnp.bfloat16)
    d_context = d_context.reshape(clip_count, frames, patches, HEADS, head_width)
    d_weights = jnp.einsum(
        "cfphd,cgphd->cphfg", d_context, values_all, preferred_element_type=jnp.float32
    )
    d_values = jnp.einsum(
        "cphfg,cfphd->cgphd", weights_low, d_context, preferred_element_type=jnp.float32
    )
    d_scores = attention_weights * (
        d_weights - jnp.sum(attention_weights * d_weights, axis=-1, keepdims=True)
    )
    d_scores = d_scores.astype(jnp.bfloat16)
    d_queries = (
        jnp.einsum("cphfg,cgphd->cfphd", d_scores, keys_all, preferred_element_type=jnp.float32)
        * factor
    )
    d_keys = (
        jnp.einsum("cphfg,cfphd->cgphd", d_scores, queries, preferred_element_type=jnp.float32)
        * factor
    )
    d_projected = (
        jnp.stack([d_queries, d_keys, d_values], axis=3)
        .astype(jnp.bfloat16)
        .reshape(row_count, 3 * model_width)
    )
    column_sums = jnp.sum(d_projected.astype(jnp.float32), axis=0)
    d_qv_bias = jnp.concatenate([column_sums[:model_width], column_sums[2 * model_width :]])
    d_qkv_weight = contract_rows(normed_one, d_projected)
    d_normed_one = contract_cols(d_projected, qkv_weight).reshape(
        clip_count, frames, patches, model_width
    )
    d_residual, d_shift_one, d_scale_one = modulate_back_one(d_normed_one)
    d_input = d_middle + d_residual
    input_grad = lax.all_to_all(
        d_input.astype(jnp.bfloat16), "frame", split_axis=1, concat_axis=2, tiled=True
    )
    d_modulation = jnp.stack(
        [
            d_shift_one.reshape(clip_count, model_width),
            d_scale_one.reshape(clip_count, model_width),
            d_gate_one,
            d_shift_two.reshape(clip_count, model_width),
            d_scale_two.reshape(clip_count, model_width),
            d_gate_two,
        ],
        axis=1,
    ).reshape(clip_count, 6 * model_width)
    every_part = (
        lax.psum_scatter(d_qkv_weight, "frame", scatter_dimension=1, tiled=True),
        lax.psum_scatter(d_out_weight, "frame", scatter_dimension=1, tiled=True),
        lax.psum_scatter(d_fc1_weight, "frame", scatter_dimension=1, tiled=True),
        lax.psum_scatter(d_fc2_weight, "frame", scatter_dimension=1, tiled=True),
        lax.psum_scatter(d_modulation, "frame", scatter_dimension=1, tiled=True),
        lax.psum_scatter(d_qv_bias, "frame", scatter_dimension=0, tiled=True),
        lax.psum_scatter(d_out_bias, "frame", scatter_dimension=0, tiled=True),
        lax.psum_scatter(d_fc1_bias, "frame", scatter_dimension=0, tiled=True),
        lax.psum_scatter(d_fc2_bias, "frame", scatter_dimension=0, tiled=True),
    )
    every_mat = (
        lax.psum_scatter(every_part[0], "clip", scatter_dimension=0, tiled=True),
        lax.psum_scatter(every_part[1], "clip", scatter_dimension=0, tiled=True),
        lax.psum_scatter(every_part[2], "clip", scatter_dimension=0, tiled=True),
        lax.psum_scatter(every_part[3], "clip", scatter_dimension=0, tiled=True),
    )
    qkv_grad = every_mat[0]
    out_grad = every_mat[1]
    fc1_grad = every_mat[2]
    fc2_grad = every_mat[3]
    modulation_grad = every_part[4]
    bias_parts = (every_part[5], every_part[6], every_part[7], every_part[8])
    bias_totals = lax.psum((bias_parts[0], bias_parts[1], bias_parts[2], bias_parts[3]), "clip")
    return (
        block_output,
        input_grad,
        modulation_grad,
        qkv_grad,
        bias_totals[0],
        out_grad,
        bias_totals[1],
        fc1_grad,
        bias_totals[2],
        fc2_grad,
        bias_totals[3],
    )


LANES = 128
VMEM_LIMIT = 58 * 1024 * 1024
ROWS_DN = (((0,), (0,)), ((), ()))
COLS_DN = (((1,), (1,)), ((), ()))
F32 = jnp.float32
BF16 = jnp.bfloat16


def mm(left, right):
    return jnp.dot(left, right, preferred_element_type=F32)


def mm_cols(left, right):
    return lax.dot_general(left, right, COLS_DN, preferred_element_type=F32)


def mm_rows(left, right):
    return lax.dot_general(left, right, ROWS_DN, preferred_element_type=F32)


def unit(values):
    centred = values - jnp.mean(values, axis=-1, keepdims=True)
    variance = jnp.mean(centred * centred, axis=-1, keepdims=True)
    inverse = lax.rsqrt(variance + EPSILON)
    return centred * inverse, inverse


def unit_back(unit_values, inverse, grad):
    mean_grad = jnp.mean(grad, axis=-1, keepdims=True)
    mean_dot = jnp.mean(grad * unit_values, axis=-1, keepdims=True)
    return (grad - mean_grad - unit_values * mean_dot) * inverse


def params(**more):
    return pltpu.CompilerParams(vmem_limit_bytes=VMEM_LIMIT, **more)


def cost(flops, moved, transcendentals=0):
    return pl.CostEstimate(flops=int(flops), bytes_accessed=int(moved), transcendentals=int(transcendentals))


def shape(dims, kind):
    return jax.ShapeDtypeStruct(tuple(dims), kind)


def whole(dims, buffers=1):
    zeros = (0,) * len(dims)
    return pl.BlockSpec(tuple(dims), lambda *_: zeros, pipeline_mode=pl.Buffered(buffers))


ANY = pl.BlockSpec(memory_space=pl.ANY)


def head_window(head, width):
    low = head * width
    start = low // LANES * LANES
    size = LANES if low - start + width <= LANES else 2 * LANES
    return low, start, size


def head_mask(head, width):
    low, start, size = head_window(head, width)
    lane = lax.broadcasted_iota(jnp.int32, (1, size), 1) + start
    return jnp.where((lane >= low) & (lane < low + width), 1.0, 0.0).astype(BF16)


class Plan:
    def __init__(self, mesh, x, qkv_weight, fc1_weight):
        self.clip_axis = mesh.shape["clip"]
        self.frame_axis = mesh.shape["frame"]
        self.clips, self.local_frames, self.patches, self.width = x
        self.own_patches = self.patches // self.frame_axis
        self.halves = self.own_patches // 8
        self.frames = self.local_frames * self.frame_axis
        self.ff = fc1_weight[1]
        self.rows = self.clips * self.frames * self.own_patches
        self.clip_rows = self.rows // self.clips
        self.block = self.frames * 8
        self.blocks = self.rows // self.block
        self.piece = self.local_frames * 8
        self.head_width = self.width // HEADS
        self.chunk_dims = (self.clips, self.halves, self.local_frames, 8, self.width)
        self.zs = self.clip_axis // 2

    def row_of(self, clip, half, k):
        return ((clip * self.halves + half) * self.frame_axis + k) * self.piece


def fits(mesh, x, qkv_weight, fc1_weight):
    clip_axis, frame_axis = mesh.shape["clip"], mesh.shape["frame"]
    width, ff = x[3], fc1_weight[1]
    return (
        clip_axis == 8
        and frame_axis == 4
        and x[2] // frame_axis % 8 == 0
        and x[1] * frame_axis * 8 == LANES
        and width == 1152
        and ff == 4 * width
        and qkv_weight[1] == 3 * width
    )


def fold_tile(tile, folds, used):
    rows = tile.shape[0] // folds
    total = tile[:rows]
    for g in range(1, folds):
        total = total + pltpu.roll(tile[g * rows : (g + 1) * rows], g * used, 1)
    return total


MESH = pl.DeviceIdType.MESH


def unit_rows(ref, here):
    return unit(ref[here, :])


class Later:
    def __init__(self, make):
        self.make = make

    def start(self):
        self.make().start()

    def wait(self):
        self.make().wait()

    def wait_recv(self):
        self.make().wait_recv()

    def wait_send(self):
        self.make().wait_send()


REMOTE_SIZES = (4, 4, 8, 1, 4, 4, 4, 4, 1, 1, 4, 2, 2, 1, 1, 1, 1, 1, 1, 1, 1, 1, 2, 2, 2, 2, 2, 2, 2, 2, 1, 4, 4, 1, 1, 3, 4, 4)
(
    R_C2, R_C1, R_C0, R_CO, R_2AX, R_2BY, R_2AY, R_2BX, R_2Z, R_2ZZ, R_1Z, R_1AX, R_1BY, R_1AY, R_1BX, R_1ZZ, R_OAX, R_OBY, R_OAY, R_OBX, R_OZ, R_OZZ, R_0AX, R_0BY, R_0CZ, R_0AY, R_0BX, R_0CX, R_0ABZ, R_0CY, R_0ZZ, R_OUT, R_IN, R_SMX, R_SMY, R_SMC, R_XIN, R_CIN,
) = REMOTE_AT = tuple(sum(REMOTE_SIZES[:i]) for i in range(len(REMOTE_SIZES)))
LOCAL_SIZES = (4, 6, 6, 6, 6, 1, 1, 1, 1, 2, 1, 1, 4)
(
    L_W, L_A, L_B, L_C, L_D, L_S, L_MID, L_ATT, L_PROJ, L_PROBS, L_N1, L_CTX, L_OWN,
) = LOCAL_AT = tuple(sum(LOCAL_SIZES[:i]) for i in range(len(LOCAL_SIZES)))
CORE, Z0, Z1, X, Y, XY = range(6)


LOAD, RUN, SEND = range(3)
TMP_A, TMP_B, TMP_C, TMP_D, TMP_S = range(5)
(J_C1, J_C2, J_Z0, J_XY1, J_XY2, J_1A, J_1B, J_1XY2, J_2Z, J_CO, J_O1, J_O2, J_OZ, J_C0, J_Q1, J_Q2, J_Q3, J_FIN2, J_FIN1, J_FINO, J_FIN0, J_SM1, J_SM2, J_SM3, J_SM4, J_SM5) = range(26)
(S_1AX, S_1BY, S_1AY, S_1BX, S_2Z, S_0ZZ, S_SMX, S_OUT, S_IN) = range(9)
P_A = tuple((0, k) for k in range(4))
P_B = tuple((1, k) for k in range(4))
P_C = tuple((2, k) for k in range(4))
P_D = tuple((3, k) for k in range(4))
P_E = tuple((4, k) for k in range(4))
P_G = tuple((5, k) for k in range(4))
P_AB = tuple((6, k) for k in range(4))
P_WQ = tuple((7, k) for k in range(8))
P_M1, P_O, P_WO, P_DC, P_PK, P_IN0, P_IN1, P_IN2, P_INE = ((8, k) for k in range(9))
SCHEDULE = {
    P_G[0]: (
        (LOAD, J_C2, 0),
    ),
    P_A[1]: (
        (LOAD, J_C1, 0),
    ),
    P_C[1]: (
        (RUN, J_C2, 0),
        (RUN, J_C1, 0),
    ),
    P_E[1]: (
        (LOAD, J_C2, 1),
    ),
    P_G[1]: (
        (RUN, J_C2, 1),
    ),
    P_A[2]: (
        (LOAD, J_XY1, 0),
    ),
    P_B[2]: (
        (LOAD, J_C1, 1),
        (RUN, J_XY1, 0),
    ),
    P_C[2]: (
        (RUN, J_C1, 1),
    ),
    P_D[2]: (
        (LOAD, J_C2, 2),
    ),
    P_E[2]: (
        (RUN, J_C2, 2),
    ),
    P_A[3]: (
        (LOAD, J_C1, 2),
        (LOAD, J_XY1, 1),
    ),
    P_B[3]: (
        (RUN, J_XY1, 1),
    ),
    P_C[3]: (
        (LOAD, J_XY1, 2),
    ),
    P_D[3]: (
        (RUN, J_C1, 2),
    ),
    P_E[3]: (
        (LOAD, J_C2, 3),
        (RUN, J_XY1, 2),
        (LOAD, J_Z0, 0),
    ),
    P_G[3]: (
        (LOAD, J_XY2, 0),
        (RUN, J_C2, 3),
    ),
    P_O: (
        (SEND, S_OUT, 3),
        (SEND, S_OUT, 1),
        (SEND, S_OUT, 2),
        (RUN, J_Z0, 0),
        (RUN, J_XY2, 0),
        (LOAD, J_C1, 3),
        (LOAD, J_Z0, 1),
    ),
    P_WO: (
        (RUN, J_Z0, 1),
        (RUN, J_C1, 3),
        (LOAD, J_XY2, 2),
        (LOAD, J_Z0, 2),
    ),
    P_DC: (
        (RUN, J_Z0, 2),
        (LOAD, J_XY1, 3),
    ),
    P_AB[0]: (
        (LOAD, J_CO, 0),
        (RUN, J_XY1, 3),
        (RUN, J_XY2, 2),
        (RUN, J_CO, 0),
    ),
    P_AB[1]: (
        (LOAD, J_XY2, 1),
    ),
    P_AB[2]: (
        (SEND, S_1BY, 0),
        (SEND, S_1AX, 0),
        (LOAD, J_Z0, 3),
    ),
    P_AB[3]: (
        (RUN, J_XY2, 1),
        (LOAD, J_XY2, 3),
        (RUN, J_XY2, 3),
        (SEND, S_2Z, 0),
    ),
    P_PK: (
        (RUN, J_Z0, 3),
        (SEND, S_1AX, 1),
    ),
    P_WQ[0]: (
        (LOAD, J_O1, 0),
        (SEND, S_1BY, 1),
    ),
    P_WQ[1]: (
        (LOAD, J_1B, 0),
    ),
    P_WQ[4]: (
        (RUN, J_1B, 0),
        (RUN, J_O1, 0),
    ),
    P_WQ[5]: (
        (LOAD, J_C0, 0),
        (RUN, J_C0, 0),
        (LOAD, J_1A, 1),
    ),
    P_WQ[7]: (
        (RUN, J_1A, 1),
        (LOAD, J_1A, 0),
        (LOAD, J_C0, 1),
        (LOAD, J_1B, 1),
        (RUN, J_1A, 0),
        (RUN, J_C0, 1),
        (RUN, J_1B, 1),
    ),
    P_IN0: (
        (LOAD, J_2Z, 0),
        (RUN, J_2Z, 0),
        (LOAD, J_Q1, 0),
        (SEND, S_1BX, 0),
    ),
    P_IN1: (
        (SEND, S_1AY, 0),
    ),
    P_IN2: (
        (LOAD, J_O2, 0),
        (RUN, J_O2, 0),
        (LOAD, J_Q1, 1),
        (RUN, J_Q1, 0),
    ),
    P_INE: (
        (LOAD, J_1XY2, 0),
        (RUN, J_1XY2, 0),
        (RUN, J_Q1, 1),
        (LOAD, J_Q2, 0),
        (RUN, J_Q2, 0),
        (LOAD, J_Q2, 1),
        (SEND, S_SMX, 0),
        (RUN, J_Q2, 1),
        (LOAD, J_SM1, 0),
        (RUN, J_SM1, 0),
        (LOAD, J_OZ, 0),
        (RUN, J_OZ, 0),
        (LOAD, J_Q3, 0),
        (LOAD, J_Q3, 1),
        (RUN, J_Q3, 0),
        (RUN, J_Q3, 1),
        (SEND, S_0ZZ, 0),
        (SEND, S_IN, 3),
        (SEND, S_IN, 1),
        (SEND, S_IN, 2),
        (LOAD, J_FIN2, 0),
        (RUN, J_FIN2, 0),
        (LOAD, J_SM2, 0),
        (RUN, J_SM2, 0),
        (LOAD, J_FINO, 0),
        (RUN, J_FINO, 0),
        (LOAD, J_SM3, 0),
        (RUN, J_SM3, 0),
        (LOAD, J_SM4, 0),
        (RUN, J_SM4, 0),
        (LOAD, J_FIN1, 0),
        (RUN, J_FIN1, 0),
        (LOAD, J_FIN0, 0),
        (LOAD, J_SM5, 0),
        (RUN, J_FIN0, 0),
        (RUN, J_SM5, 0),
    ),
}
TMPS = {
    (J_1A, 0): TMP_C,
    (J_1A, 1): TMP_D,
    (J_1B, 0): TMP_C,
    (J_1B, 1): TMP_D,
    (J_1XY2, 0): TMP_C,
    (J_2Z, 0): TMP_C,
    (J_C1, 0): TMP_A,
    (J_C1, 1): TMP_A,
    (J_C1, 2): TMP_A,
    (J_C1, 3): TMP_A,
    (J_C2, 0): TMP_B,
    (J_C2, 1): TMP_B,
    (J_C2, 2): TMP_B,
    (J_C2, 3): TMP_B,
    (J_FIN0, 0): TMP_C,
    (J_FIN1, 0): TMP_D,
    (J_FIN2, 0): TMP_C,
    (J_FINO, 0): TMP_D,
    (J_O1, 0): TMP_D,
    (J_O2, 0): TMP_C,
    (J_OZ, 0): TMP_C,
    (J_Q1, 0): TMP_A,
    (J_Q1, 1): TMP_B,
    (J_Q2, 0): TMP_D,
    (J_Q2, 1): TMP_C,
    (J_Q3, 0): TMP_C,
    (J_Q3, 1): TMP_D,
    (J_XY1, 0): TMP_C,
    (J_XY1, 1): TMP_D,
    (J_XY1, 2): TMP_C,
    (J_XY1, 3): TMP_D,
    (J_XY2, 0): TMP_C,
    (J_XY2, 1): TMP_D,
    (J_XY2, 2): TMP_C,
    (J_XY2, 3): TMP_D,
    (J_Z0, 0): TMP_D,
    (J_Z0, 1): TMP_D,
    (J_Z0, 2): TMP_D,
    (J_Z0, 3): TMP_C,
}


def whole_layer(plan, x, cotangent, modulation, counts, biases, qkv_weight, out_weight, fc1_weight, fc2_weight):
    n, rows, width, ff = plan.frame_axis, plan.rows, plan.width, plan.ff
    own, fl, clips = plan.own_patches, plan.local_frames, plan.clips
    span2, span1 = ff // plan.clip_axis, width // plan.clip_axis
    s1, s0, so = 9 * span1, 7 * span1, 2 * span1 + span1 // 3
    a1, a0 = 640, s0 // 3
    pad2, padq, wq = 384, 896, 3 * width // n
    blocks, block = plan.blocks, plan.block
    factor = plan.head_width ** (-0.5)
    half_rows = 64
    parts_per_clip = plan.clip_rows // half_rows

    def body(*refs):
        refs = list(refs)

        def take(count):
            got = refs[:count]
            del refs[:count]
            return got

        (x_h, cot_h, wqkv_h, wout_h, fc1_h, fc2_h, raw_mod, counts_ref, qv_bias, out_bias, fc1_bias, fc2_bias) = take(12)
        (out_h, in_h) = take(2)
        sum2, sum1, sum0, sumo, small = take(5)
        (rc2, rc1, rc0, rco, r2ax, r2by, r2ay, r2bx, r2z, r2zz) = take(10)
        (r1z, r1ax, r1by, r1ay, r1bx, r1zz) = take(6)
        (roax, roby, roay, robx, roz, rozz) = take(6)
        (r0ax, r0by, r0cz, r0ay, r0bx, r0cx, r0abz, r0cy, r0zz, rsm, rsmc) = take(11)
        (n1_h, ctx_h, proj_h, probs_h, att_h, mid_h) = take(6)
        (keep2, keep1, keepo, r2, stage, tmp_a, tmp_b, tmp_c, tmp_d, dres, acc, f1, f2, ring, rows_out, sm, sm_b, sm_t, smc) = take(19)
        (xin, cin, mod, bias, allowed, valid) = take(6)
        send_sem, recv_sem, local_sem = take(3)

        frame, clip = lax.axis_index("frame"), lax.axis_index("clip")
        mx, my = frame % 2, frame // 2
        core, z0, z1 = clip % 2, clip // 2 % 2, clip // 4
        partner = (
            ("clip", clip + 1 - 2 * core),
            ("clip", clip + 2 - 4 * z0),
            ("clip", clip + 4 - 8 * z1),
            ("frame", frame + 1 - 2 * mx),
            ("frame", frame + 2 - 4 * my),
            ("frame", n - 1 - frame),
        )

        def remote(name, index, src, dst, bit):
            axis, where = partner[bit]
            at = name + index
            return Later(
                lambda: pltpu.make_async_remote_copy(
                    src_ref=src,
                    dst_ref=dst,
                    send_sem=send_sem.at[at],
                    recv_sem=recv_sem.at[at],
                    device_id={axis: where},
                    device_id_type=MESH,
                )
            )

        def local(name, index, src, dst):
            return Later(lambda: pltpu.make_async_copy(src, dst, local_sem.at[name + index]))

        lo1, hi1 = pl.ds(0, a1), pl.ds(a1, s1 - a1)
        pa, pb, pc, pab, all0 = pl.ds(0, a0), pl.ds(a0, a0), pl.ds(2 * a0, a0), pl.ds(0, 2 * a0), pl.ds(0, s0)
        oa, ob, oab = pl.ds(0, so), pl.ds(so, so), pl.ds(0, 2 * so)
        all1 = pl.ds(0, s1)

        def c2(z):
            return remote(R_C2, z, stage.at[0, :, :, all1], rc2.at[z], CORE)

        def c1(f):
            return remote(R_C1, f, stage.at[1, :, :, all1], rc1.at[f], CORE)

        def c0(j, f):
            return remote(R_C0, 4 * j + f, stage.at[:, f // 2, f % 2, all0], rc0.at[j, :, f // 2, f % 2], CORE)

        def co():
            return remote(R_CO, 0, stage.at[:, :, :, oab], rco, CORE)

        def t2ax(z):
            return remote(R_2AX, z, keep2.at[z // 2, z % 2, :, 1 - mx, lo1], r2ax.at[z], X)

        def t2by(z):
            return remote(R_2BY, z, keep2.at[z // 2, z % 2, 1 - my, :, hi1], r2by.at[z], Y)

        def t2ay(z):
            return remote(R_2AY, z, keep2.at[z // 2, z % 2, 1 - my, mx, lo1], r2ay.at[z], Y)

        def t2bx(z):
            return remote(R_2BX, z, keep2.at[z // 2, z % 2, my, 1 - mx, hi1], r2bx.at[z], X)

        def t2z():
            return remote(R_2Z, 0, r2.at[:, 1 - z0], r2z, Z0)

        def t2zz():
            return remote(R_2ZZ, 0, r2.at[1 - z1, z0], r2zz, Z1)

        def t1z(f):
            return remote(R_1Z, f, keep1.at[f // 2, f % 2, :, 1 - z0], r1z.at[f], Z0)

        def t1ax(y):
            return remote(R_1AX, y, keep1.at[y, 1 - mx, :, z0, lo1], r1ax.at[y], X)

        def t1by(x):
            return remote(R_1BY, x, keep1.at[1 - my, x, :, z0, hi1], r1by.at[x], Y)

        def t1ay():
            return remote(R_1AY, 0, keep1.at[1 - my, mx, :, z0, lo1], r1ay, Y)

        def t1bx():
            return remote(R_1BX, 0, keep1.at[my, 1 - mx, :, z0, hi1], r1bx, X)

        def t1zz():
            return remote(R_1ZZ, 0, keep1.at[my, mx, 1 - z1, z0], r1zz, Z1)

        def toax():
            return remote(R_OAX, 0, keepo.at[:, :, 1 - mx, oa], roax, X)

        def toby():
            return remote(R_OBY, 0, keepo.at[:, 1 - my, :, ob], roby, Y)

        def toay():
            return remote(R_OAY, 0, keepo.at[:, 1 - my, mx, oa], roay, Y)

        def tobx():
            return remote(R_OBX, 0, keepo.at[:, my, 1 - mx, ob], robx, X)

        def toz():
            return remote(R_OZ, 0, keepo.at[1 - z0, my, mx], roz, Z0)

        def tozz():
            there = pl.ds(pl.multiple_of((1 - z1) * so, 16), so)
            return remote(R_OZZ, 0, keepo.at[z0, my, mx, there], rozz, Z1)

        def t0ax(j):
            return remote(R_0AX, j, keep2.at[j, :, :, 1 - mx, pa], r0ax.at[j], X)

        def t0by(j):
            return remote(R_0BY, j, keep2.at[j, :, 1 - my, :, pb], r0by.at[j], Y)

        def t0cz(j):
            return remote(R_0CZ, j, keep2.at[j, 1 - z0, :, :, pc], r0cz.at[j], Z0)

        def t0ay(j):
            return remote(R_0AY, j, keep2.at[j, :, 1 - my, mx, pa], r0ay.at[j], Y)

        def t0bx(j):
            return remote(R_0BX, j, keep2.at[j, :, my, 1 - mx, pb], r0bx.at[j], X)

        def t0cx(j):
            return remote(R_0CX, j, keep2.at[j, z0, :, 1 - mx, pc], r0cx.at[j], X)

        def t0abz(j):
            return remote(R_0ABZ, j, keep2.at[j, 1 - z0, my, mx, pab], r0abz.at[j], Z0)

        def t0cy(j):
            return remote(R_0CY, j, keep2.at[j, z0, 1 - my, mx, pc], r0cy.at[j], Y)

        def t0zz():
            return remote(R_0ZZ, 0, keep2.at[1 - z1, z0, my, mx, all0], r0zz, Z1)

        def row_send(name, k, dst, arriving=False):
            bit = (None, X, Y, XY)[k]
            place = partner[bit][1] if arriving else frame
            return remote(name, k, rows_out.at[k], dst.at[:, :, pl.ds(place * own, own)], bit)

        def row_own(index, dst):
            return local(L_OWN, index, rows_out.at[0], dst.at[:, :, pl.ds(frame * own, own)])

        def smx_send():
            return remote(R_SMX, 0, sm, rsm.at[0], X)

        def smy_send():
            return remote(R_SMY, 0, sm_b, rsm.at[1], Y)

        def smc_send(i):
            return remote(R_SMC, i, smc.at[i], rsmc.at[i], (CORE, Z0, Z1)[i])

        def add_to(ref, at, other, other_at):
            ref[at] = ref[at] + other[other_at]

        def add_chunks(ref, at, other, other_at, count):
            for i in range(2):
                for k in range(2 if count == 2 else 1):
                    fill = iter((i, k))
                    here = tuple(next(fill) if p is None else p for p in at)
                    fill = iter((i, k))
                    there = tuple(next(fill) if p is None else p for p in other_at)
                    add_to(ref, here, other, there)

        def pump(arrivals, copies, work, sends):
            def load():
                for transfer in arrivals:
                    transfer.wait_recv()
                for copy in copies:
                    copy.start()

            def run():
                for copy in copies:
                    copy.wait()
                work()
                for transfer in sends:
                    transfer.start()

            return load, run

        def job(kind, index, tmps):
            tmp = (tmp_a, tmp_b, tmp_c, tmp_d, None)[tmps]
            sem = (L_A, L_B, L_C, L_D, L_S)[tmps]
            pair = (index // 2, index % 2)
            if kind == J_C1:

                def work():
                    add_chunks(keep1, pair + (None, None), tmp, (None, None, all1), 2)

                return pump([c1(index)], [local(sem, 0, rc1.at[index], tmp.at[:, :, all1])], work, [t1z(index)])
            if kind == J_C2:

                def work():
                    add_chunks(keep2, pair + (None, None, all1), tmp, (None, None, all1), 2)

                sends = [t2ax(index), t2by(index)]
                return pump([c2(index)], [local(sem, 0, rc2.at[index], tmp.at[:, :, all1])], work, sends)
            if kind == J_Z0:

                def work():
                    add_chunks(keep1, pair + (None, z0), tmp, (None, all1), 1)

                return pump([t1z(index)], [local(sem, 0, r1z.at[index], tmp.at[:, all1])], work, [])
            if kind == J_XY1:

                def work():
                    add_chunks(keep2, pair + (None, mx, lo1), tmp, (None, lo1), 1)
                    add_chunks(keep2, pair + (my, None, hi1), tmp, (None, hi1), 1)

                copies = [
                    local(sem, 0, r2ax.at[index], tmp.at[:, lo1]),
                    local(sem, 1, r2by.at[index], tmp.at[:, hi1]),
                ]
                return pump([t2ax(index), t2by(index)], copies, work, [t2ay(index), t2bx(index)])
            if kind == J_XY2:

                def work():
                    r2[pair] = keep2[pair + (my, mx, all1)] + tmp[0, all1]

                copies = [
                    local(sem, 0, r2ay.at[index], tmp.at[0, lo1]),
                    local(sem, 1, r2bx.at[index], tmp.at[0, hi1]),
                ]
                return pump([t2ay(index), t2bx(index)], copies, work, [])
            if kind == J_1A:

                def work():
                    add_chunks(keep1, (index, mx, None, z0, lo1), tmp, (None, lo1), 1)

                return pump([t1ax(index)], [local(sem, 0, r1ax.at[index], tmp.at[:, lo1])], work, [])
            if kind == J_1B:

                def work():
                    add_chunks(keep1, (my, index, None, z0, hi1), tmp, (None, hi1), 1)

                return pump([t1by(index)], [local(sem, 0, r1by.at[index], tmp.at[:, hi1])], work, [])
            if kind == J_1XY2:

                def work():
                    add_chunks(keep1, (my, mx, None, z0, all1), tmp, (None, all1), 1)

                copies = [local(sem, 0, r1ay, tmp.at[:, lo1]), local(sem, 1, r1bx, tmp.at[:, hi1])]
                return pump([t1ay(), t1bx()], copies, work, [t1zz()])
            if kind == J_2Z:

                def work():
                    add_chunks(r2, (None, z0), tmp, (None, all1), 1)

                return pump([t2z()], [local(sem, 0, r2z, tmp.at[:, all1])], work, [t2zz()])
            if kind == J_CO:

                def work():
                    add_chunks(keepo, (0, None, None), tmp_a, (None, None, oab), 2)
                    add_chunks(keepo, (1, None, None), tmp_b, (None, None, oab), 2)

                copies = [
                    local(L_A, 0, rco.at[0], tmp_a.at[:, :, oab]),
                    local(L_B, 0, rco.at[1], tmp_b.at[:, :, oab]),
                ]
                return pump([co()], copies, work, [toax(), toby()])
            if kind == J_O1:

                def work():
                    for i in range(2):
                        add_chunks(keepo, (i, None, mx, oa), tmp, (None, pl.ds(i * so, so)), 1)
                        add_chunks(keepo, (i, my, None, ob), tmp, (None, pl.ds((2 + i) * so, so)), 1)

                copies = [local(sem, i, roax.at[i], tmp.at[:, pl.ds(i * so, so)]) for i in range(2)]
                copies += [local(sem, 2 + i, roby.at[i], tmp.at[:, pl.ds((2 + i) * so, so)]) for i in range(2)]
                return pump([toax(), toby()], copies, work, [toay(), tobx()])
            if kind == J_O2:

                def work():
                    add_chunks(keepo, (None, my, mx, oab), tmp, (None, oab), 1)

                copies = [local(sem, 0, roay, tmp.at[:, oa]), local(sem, 1, robx, tmp.at[:, ob])]
                return pump([toay(), tobx()], copies, work, [toz()])
            if kind == J_OZ:

                def work():
                    add_to(keepo, (z0, my, mx), tmp, (0, oab))

                return pump([toz()], [local(sem, 0, roz, tmp.at[0, oab])], work, [tozz()])
            if kind == J_C0:

                def work():
                    add_chunks(keep2, (index, 0, None, None, all0), tmp_a, (None, None, all0), 2)
                    add_chunks(keep2, (index, 1, None, None, all0), tmp_b, (None, None, all0), 2)

                copies = [
                    local(L_A, 0, rc0.at[index, 0], tmp_a.at[:, :, all0]),
                    local(L_B, 0, rc0.at[index, 1], tmp_b.at[:, :, all0]),
                ]
                sends = [t0ax(index), t0by(index), t0cz(index)]
                return pump([c0(index, f) for f in range(n)], copies, work, sends)
            if kind == J_Q1:

                def work():
                    add_chunks(keep2, (index, None, None, mx, pa), tmp, (None, None, pa), 2)
                    add_chunks(keep2, (index, None, my, None, pb), tmp, (None, None, pb), 2)
                    add_chunks(keep2, (index, z0, None, None, pc), tmp, (None, None, pc), 2)

                copies = [
                    local(sem, i, r.at[index], tmp.at[:, :, p])
                    for i, (r, p) in enumerate(((r0ax, pa), (r0by, pb), (r0cz, pc)))
                ]
                arrivals = [t0ax(index), t0by(index), t0cz(index)]
                return pump(arrivals, copies, work, [t0ay(index), t0bx(index), t0cx(index)])
            if kind == J_Q2:

                def work():
                    add_chunks(keep2, (index, None, my, mx, pab), tmp, (None, pab), 1)
                    add_chunks(keep2, (index, z0, None, mx, pc), tmp, (None, pc), 1)

                copies = [
                    local(sem, i, r.at[index], tmp.at[:, p])
                    for i, (r, p) in enumerate(((r0ay, pa), (r0bx, pb), (r0cx, pc)))
                ]
                return pump([t0ay(index), t0bx(index), t0cx(index)], copies, work, [t0abz(index), t0cy(index)])
            if kind == J_Q3:

                def work():
                    add_to(keep2, (index, z0, my, mx, all0), tmp, (0, all0))

                copies = [local(sem, 0, r0abz.at[index], tmp.at[0, pab]), local(sem, 1, r0cy.at[index], tmp.at[0, pc])]
                return pump([t0abz(index), t0cy(index)], copies, work, [])
            if kind == J_FIN2:

                def work():
                    sum2[...] = r2[z1, z0].astype(F32) + tmp[0, all1].astype(F32)

                return pump([t2zz()], [local(sem, 0, r2zz, tmp.at[0, all1])], work, [])
            if kind == J_FIN1:

                def work():
                    sum1[...] = keep1[my, mx, z1, z0].astype(F32) + tmp[0, all1].astype(F32)

                return pump([t1zz()], [local(sem, 0, r1zz, tmp.at[0, all1])], work, [])
            if kind == J_FINO:

                def work():
                    here = pl.ds(pl.multiple_of(z1 * so, 16), so)
                    sumo[...] = keepo[z0, my, mx, here].astype(F32) + tmp[0, oa].astype(F32)

                return pump([tozz()], [local(sem, 0, rozz, tmp.at[0, oa])], work, [])
            if kind == J_FIN0:

                def work():
                    sum0[...] = keep2[z1, z0, my, mx, all0].astype(F32) + tmp[0, all0].astype(F32)

                return pump([t0zz()], [local(sem, 0, r0zz, tmp.at[0, all0])], work, [])
            if kind == J_SM1:

                def work():
                    sm_b[...] = sm[...] + sm_t[...]

                return pump([smx_send()], [local(L_S, 0, rsm.at[0], sm_t)], work, [smy_send()])
            if kind == J_SM2:

                def work():
                    small[...] = sm_b[...] + sm_t[...]
                    smc[0] = small[0]

                return pump([smy_send()], [local(L_S, 0, rsm.at[1], sm_t)], work, [smc_send(0)])
            step = kind - J_SM3

            def work():
                if step < 2:
                    smc[step + 1] = smc[step] + sm_t[0]
                else:
                    small[0] = smc[step] + sm_t[0]

            sends = [smc_send(step + 1)] if step < 2 else []
            return pump([smc_send(step)], [local(L_S, 0, rsmc.at[step], sm_t.at[0])], work, sends)

        plain_sends = {
            S_1AX: t1ax,
            S_1BY: t1by,
            S_1AY: lambda _: t1ay(),
            S_1BX: lambda _: t1bx(),
            S_2Z: lambda _: t2z(),
            S_0ZZ: lambda _: t0zz(),
            S_SMX: lambda _: smx_send(),
            S_OUT: lambda k: row_send(R_OUT, k, out_h),
            S_IN: lambda k: row_send(R_IN, k, in_h),
        }

        def do(point):
            for what, kind, index in SCHEDULE.get(point, ()):
                if what == SEND:
                    plain_sends[kind](index).start()
                else:
                    job(kind, index, TMPS.get((kind, index), TMP_S))[what]()

        def do_in(points, index):
            for k, point in enumerate(points):
                if point in SCHEDULE:
                    pl.when(index == k)(lambda point=point: do(point))

        def weight(slot, src):
            return local(L_W, slot, src, ring.at[slot])

        def fc1_block(f):
            return weight(2 * (f % 2), fc1_h.at[:, pl.ds(pl.multiple_of(f * width, LANES), width)])

        def fc2_block(f):
            return weight(2 * (f % 2) + 1, fc2_h.at[pl.ds(pl.multiple_of(f * width, 16), width)])

        def qkv_block(i, slot):
            return weight(slot, wqkv_h.at[:, i * width : (i + 1) * width])

        def own_copies(src, dst, name):
            return local(name, 0, src, dst)

        def piece_of(ref, k, c, half):
            return ref[k, c, :, half * 8 : half * 8 + 8, :].astype(F32).reshape(plan.piece, width)

        def rows_at(c, half, k):
            return pl.ds(pl.multiple_of(c * plan.clip_rows + plan.row_of(0, half, k), 8), plan.piece)

        def arrive(name, k, src, dst):
            bit = (None, X, Y, XY)[k]
            return remote(name, k, src.at[:, :, pl.ds(partner[bit][1] * own, own)], dst.at[k], bit)

        barrier = pltpu.get_barrier_semaphore()
        for axis, where in partner:
            pl.semaphore_signal(barrier, inc=1, device_id={axis: where}, device_id_type=MESH)
        mine = pl.ds(frame * own, own)
        own_x = local(L_OWN, 2, x_h.at[:, :, mine], xin.at[0])
        own_x.start()
        for i in range(3):
            qkv_block(i, i).start()
        weight(3, wout_h).start()
        pl.semaphore_wait(barrier, len(partner))
        for k in (3, 1, 2):
            arrive(R_XIN, k, x_h, xin).start()
        sm[...] = jnp.zeros_like(sm)
        for i in range(6):
            values = raw_mod[:, i * width : (i + 1) * width].astype(F32)
            for c in range(clips):
                mod[c, i : i + 1, :] = values[c : c + 1, :]
        parts = [(qv_bias, 0), None, (qv_bias, 1), (out_bias, 0)] + [(fc1_bias, f) for f in range(n)] + [(fc2_bias, 0)]
        for i, part in enumerate(parts):
            if part is None:
                bias[i] = jnp.zeros((1, width), F32)
            else:
                bias[i] = part[0][pl.ds(part[1] * width, width)].astype(F32).reshape(1, width)

        def frame_of(axis):
            slot = lax.broadcasted_iota(jnp.int32, (block, block), axis) // 8
            k, local_frame = slot // fl, slot % fl
            low, high = k % 2, k // 2
            source = low + mx - 2 * low * mx + 2 * (high + my - 2 * high * my)
            return source * fl + local_frame

        lane_patch = lax.broadcasted_iota(jnp.int32, (block, block), 1) % 8
        row_patch = lax.broadcasted_iota(jnp.int32, (block, block), 0) % 8
        row_frame, lane_frame = frame_of(0), frame_of(1)
        for c in range(clips):
            count = counts_ref[c]
            valid[c] = jnp.where(row_frame < count, 1.0, 0.0)
            allowed[c] = jnp.where((lane_patch == row_patch) & (lane_frame < count), 0.0, NEGATIVE)

        def first_half(n1, proj, ctx, heads_out, probs, n2):
            own_x.wait()

            @pl.loop(0, clips)
            def _(c):
                shift, scale = mod[c, 0:1, :], 1.0 + mod[c, 1:2, :]
                for half in range(plan.halves):
                    for k in range(n):
                        normed, _ = unit(piece_of(xin, k, c, half))
                        n1[rows_at(c, half, k), :] = (normed * scale + shift).astype(BF16)

            own_copies(n1, n1_h, L_N1).start()

            @pl.loop(0, 3)
            def _(i):
                local(L_W, i, fc2_h.at[pl.ds(0, width)], ring.at[i]).wait()
                proj[i] = (mm(n1[...], ring[i]) + bias[i]).astype(BF16)

            fc1_block(0).start()
            fc2_block(0).start()
            own_copies(proj, proj_h, L_PROJ).start()

            @pl.loop(0, blocks)
            def _(b):
                slot = b % 2
                here = pl.ds(pl.multiple_of(b * block, block), block)

                @pl.when(b >= 2)
                def _():
                    local(L_PROBS, slot, probs.at[slot], probs_h.at[b - 2]).wait()

                heads_out[...] = jnp.zeros_like(heads_out)
                for h in range(HEADS):
                    _, start, size = head_window(h, plan.head_width)
                    keep = head_mask(h, plan.head_width)
                    cols = slice(start, start + size)
                    q = proj[0, here, cols] * keep
                    v = proj[2, here, cols] * keep
                    score = mm_cols(q, proj[1, here, cols]) * factor + allowed[b // plan.halves]
                    grown = jnp.exp(score - jnp.max(score, axis=-1, keepdims=True))
                    weights = grown * (1.0 / jnp.sum(grown, axis=-1, keepdims=True))
                    probs[slot, h] = weights
                    heads_out[:, cols] += mm(weights.astype(BF16), v)
                ctx[here, :] = heads_out[...].astype(BF16)
                local(L_PROBS, slot, probs.at[slot], probs_h.at[b]).start()

            own_copies(ctx, ctx_h, L_CTX).start()
            weight(3, wout_h).wait()
            f1[...] = mm(ctx[...], ring[3]) + bias[3]
            own_copies(f1, att_h, L_ATT).start()

            @pl.loop(0, clips)
            def _(c):
                for half in range(plan.halves):
                    for k in range(n):
                        here = rows_at(c, half, k)
                        middle = piece_of(xin, k, c, half) + mod[c, 2:3, :] * f1[here, :]
                        f2[here, :] = middle
                        normed, _ = unit(middle)
                        n2[here, :] = (normed * (1.0 + mod[c, 4:5, :]) + mod[c, 3:4, :]).astype(BF16)

            own_copies(f2, mid_h, L_MID).start()
            own_copies(n1, n1_h, L_N1).wait()
            own_copies(proj, proj_h, L_PROJ).wait()
            own_copies(ctx, ctx_h, L_CTX).wait()
            for b in (blocks - 2, blocks - 1):
                local(L_PROBS, b % 2, probs.at[b % 2], probs_h.at[b]).wait()

        def mlp(n2, cin, own_cot, n2_turned, dbr, padded, act, act_turned, dh, res):
            padded[...] = jnp.zeros_like(padded)
            n2_turned[...] = n2[...].T
            acc[...] = jnp.zeros_like(acc)
            own_cot.wait()
            for k in (1, 2, 3):
                arrive(R_CIN, k, cot_h, cin).wait_recv()

            @pl.loop(0, clips)
            def _(c):
                for half in range(plan.halves):
                    for k in range(n):
                        here = rows_at(c, half, k)
                        piece = piece_of(cin, k, c, half) * valid[c, k * plan.piece : (k + 1) * plan.piece, 0:1]
                        dres[here, :] = piece.astype(BF16)
                        low = (piece * mod[c, 5:6, :]).astype(BF16)
                        dbr[here, :] = low
                        sm[0, 7:8, :] += jnp.sum(low.astype(F32), axis=0, keepdims=True)

            for f in range(n):
                padded[:, f * pad2 : f * pad2 + width // n] = dbr[:, f * (width // n) : (f + 1) * (width // n)]
            own_copies(f1, att_h, L_ATT).wait()
            f1[...] = jnp.zeros_like(f1)
            own_copies(f2, mid_h, L_MID).wait()

            @pl.loop(0, n)
            def _(f):
                slot = 2 * (f % 2)

                @pl.when(f < n - 1)
                def _():
                    fc1_block(f + 1).start()
                    fc2_block(f + 1).start()

                @pl.when(f == n - 1)
                def _():
                    weight(0, wout_h).start()
                    qkv_block(0, 1).start()

                fc1_block(f).wait()
                f2[...] = mm(n2[...], ring[slot])
                first_bias = bias[4 + f]

                @pl.loop(0, rows // half_rows)
                def _(i):
                    here = pl.ds(pl.multiple_of(i * half_rows, half_rows), half_rows)
                    hidden = f2[here, :] + first_bias
                    square = hidden * hidden
                    bent = jnp.tanh(0.7978845608028654 * hidden * (1.0 + 0.044715 * square))
                    act[here, :] = (0.5 * hidden * (1.0 + bent)).astype(BF16)
                    slope = 0.7978845608028654 * (1.0 + 3.0 * 0.044715 * square)
                    f2[here, :] = 0.5 * (1.0 + bent) + 0.5 * hidden * (1.0 - bent * bent) * slope

                do_in(P_A, f)

                @pl.when(f >= 1)
                def _():
                    c1(f - 1).wait_send()
                    c2(f - 1).wait_send()

                act_turned[...] = act[...].T
                for i in range(2):
                    res[...] = mm(act_turned[...], padded[:, i * 2 * pad2 : (i + 1) * 2 * pad2])
                    for mine in (False, True):
                        part = core if mine else 1 - core
                        at = pl.ds(pl.multiple_of(part * span2, 8), span2)
                        for j in range(2):
                            pieces = [
                                res[at, j * pad2 + t * LANES : j * pad2 + (t + 1) * LANES] for t in range(3)
                            ]
                            pieces[2] = fold_tile(pieces[2], 4, 32)
                            row = 0
                            for piece in pieces:
                                slab = slice(row, row + piece.shape[0])
                                if mine:
                                    keep2[f // 2, f % 2, i, j, slab, :] = piece.astype(BF16)
                                else:
                                    stage[0, i, j, slab, :] = piece.astype(BF16)
                                row += piece.shape[0]
                c2(f).start()
                do_in(P_B, f)

                fc2_block(f).wait()
                dh[...] = (mm_cols(dbr[...], ring[slot + 1]) * f2[...]).astype(BF16)
                sm[0, pl.ds(3 + f, 1), :] = jnp.sum(dh[...].astype(F32), axis=0, keepdims=True)

                do_in(P_C, f)

                for first, tiles in ((0, 5), (5, 4)):
                    lanes = slice(first * LANES, (first + tiles) * LANES)
                    res[:, : tiles * LANES] = mm(n2_turned[...], dh[:, lanes])
                    for mine in (False, True):
                        part = core if mine else 1 - core
                        for i in range(2):
                            for j in range(2):
                                at = pl.ds(pl.multiple_of((4 * i + 2 * j + part) * span1, 8), span1)
                                for t in range(tiles):
                                    slab = slice((first + t) * span1, (first + t + 1) * span1)
                                    values = res[at, t * LANES : (t + 1) * LANES].astype(BF16)
                                    if mine:
                                        keep1[f // 2, f % 2, i, j, slab, :] = values
                                    else:
                                        stage[1, i, j, slab, :] = values
                c1(f).start()

                do_in(P_D, f)
                acc[...] += mm_cols(dh[...], ring[slot])
                do_in(P_E, f)
                f1[...] += mm(act[...], ring[slot + 1])
                do_in(P_G, f)

        def two_halves(n2):
            own_cot = local(L_OWN, 3, cot_h.at[:, :, mine], cin.at[0])
            own_cot.start()
            for k in (1, 2, 3):
                arrive(R_XIN, k, x_h, xin).wait_recv()
            for k in (3, 1, 2):
                arrive(R_CIN, k, cot_h, cin).start()
            pl.run_scoped(
                functools.partial(first_half, n2=n2),
                pltpu.VMEM((rows, width), BF16),
                pltpu.VMEM((3, rows, width), BF16),
                pltpu.VMEM((rows, width), BF16),
                pltpu.VMEM((block, width), F32),
                pltpu.VMEM((2, HEADS, block, block), F32),
            )
            pl.run_scoped(
                functools.partial(mlp, n2, cin, own_cot),
                pltpu.VMEM((width, rows), BF16),
                pltpu.VMEM((rows, width), BF16),
                pltpu.VMEM((rows, n * pad2), BF16),
                pltpu.VMEM((rows, width), BF16),
                pltpu.VMEM((width, rows), BF16),
                pltpu.VMEM((rows, width), BF16),
                pltpu.VMEM((width, 2 * pad2), F32),
            )

        pl.run_scoped(two_halves, pltpu.VMEM((rows, width), BF16))

        def rest(datt, proj):
            own_copies(mid_h, f2, L_MID).start()
            own_copies(proj_h, proj, L_PROJ).start()
            qkv_block(1, 3).start()
            own_copies(ctx_h, ring.at[2, :rows], L_CTX).start()

            def attend(dctx, probs, acc3):
                def middle(att):
                    own_copies(att_h, att, L_ATT).start()
                    own_copies(mid_h, f2, L_MID).wait()
                    own_copies(att_h, att, L_ATT).wait()

                    @pl.loop(0, rows // half_rows)
                    def _(i):
                        here = pl.ds(pl.multiple_of(i * half_rows, half_rows), half_rows)
                        c = i // parts_per_clip
                        normed, inverse = unit_rows(f2, here)
                        grad = acc[here, :]
                        sm[1 + c, 3:4, :] += jnp.sum(grad, axis=0, keepdims=True)
                        sm[1 + c, 4:5, :] += jnp.sum(grad * normed, axis=0, keepdims=True)
                        d_middle = dres[here, :].astype(F32) + unit_back(normed, inverse, grad * (1.0 + mod[c, 4:5, :]))
                        acc[here, :] = d_middle
                        sm[1 + c, 2:3, :] += jnp.sum(d_middle * att[here, :], axis=0, keepdims=True)
                        low = (d_middle * mod[c, 2:3, :]).astype(BF16)
                        datt[here, :] = low
                        sm[0, 2:3, :] += jnp.sum(low.astype(F32), axis=0, keepdims=True)

                pl.run_scoped(middle, pltpu.VMEM((rows, width), F32))
                do(P_M1)
                local(L_PROBS, 0, probs_h.at[0], probs.at[0]).start()

                @pl.loop(0, clips)
                def _(c):
                    for half in range(plan.halves):
                        for k in range(n):
                            here = rows_at(c, half, k)
                            branch = f1[here, :] + bias[8]
                            sm[1 + c, 5:6, :] += jnp.sum(dres[here, :].astype(F32) * branch, axis=0, keepdims=True)
                            total = valid[c, k * plan.piece : (k + 1) * plan.piece, 0:1] * (f2[here, :] + mod[c, 5:6, :] * branch)
                            rows_out[k, c, :, half * 8 : half * 8 + 8, :] = total.reshape(fl, 8, width).astype(BF16)

                row_own(0, out_h).start()
                do(P_O)
                c1(3).wait_send()
                c2(3).wait_send()

                def out_grad(right_o, res):
                    wide = width // n
                    right_o[...] = jnp.zeros_like(right_o)
                    for f in range(n):
                        right_o[f, :, :wide] = datt[:, f * wide : (f + 1) * wide]
                    own_copies(ctx_h, ring.at[2, :rows], L_CTX).wait()
                    turned = ring[2, :rows, :].T
                    ring[2, :, rows : 2 * rows] = turned

                    @pl.loop(0, n)
                    def _(f):
                        res[...] = mm(ring[2, :, rows : 2 * rows], right_o[f])
                        for mine in (False, True):
                            part = core if mine else 1 - core
                            for i in range(2):
                                for j in range(2):
                                    at = pl.ds(pl.multiple_of((4 * i + 2 * j + part) * span1, 8), span1)
                                    pieces = [res[at, t * LANES : (t + 1) * LANES] for t in range(3)]
                                    pieces[2] = fold_tile(pieces[2], 3, 32)
                                    row = i * so
                                    for piece in pieces:
                                        slab = slice(row, row + piece.shape[0])
                                        if mine:
                                            keepo[j, f // 2, f % 2, slab, :] = piece.astype(BF16)
                                        else:
                                            stage[j, f // 2, f % 2, slab, :] = piece.astype(BF16)
                                        row += piece.shape[0]

                pl.run_scoped(
                    out_grad, pltpu.VMEM((n, rows, pad2), BF16), pltpu.VMEM((width, pad2), F32)
                )
                co().start()
                do(P_WO)
                weight(0, wout_h).wait()
                dctx[...] = mm_cols(datt[...], ring[0]).astype(BF16)
                qkv_block(2, 0).start()
                do(P_DC)
                own_copies(proj_h, proj, L_PROJ).wait()

                @pl.loop(0, blocks)
                def _(b):
                    slot = b % 2
                    here = pl.ds(pl.multiple_of(b * block, block), block)

                    @pl.when(b < blocks - 1)
                    def _():
                        local(L_PROBS, 1 - slot, probs_h.at[b + 1], probs.at[1 - slot]).start()

                    local(L_PROBS, slot, probs_h.at[b], probs.at[slot]).wait()
                    acc3[...] = jnp.zeros_like(acc3)
                    for h in range(HEADS):
                        _, start, size = head_window(h, plan.head_width)
                        keep = head_mask(h, plan.head_width)
                        cols = slice(start, start + size)
                        weights = probs[slot, h]
                        d_c = dctx[here, cols] * keep
                        d_weight = mm_cols(d_c, proj[2, here, cols])
                        mixed = weights * d_weight
                        d_score = (mixed - weights * jnp.sum(mixed, axis=-1, keepdims=True)).astype(BF16)
                        acc3[2, :, cols] += mm_rows(weights.astype(BF16), d_c)
                        acc3[0, :, cols] += mm(d_score, proj[1, here, cols] * keep)
                        acc3[1, :, cols] += mm_rows(d_score, proj[0, here, cols] * keep)
                    for part in range(3):
                        values = acc3[part] if part == 2 else acc3[part] * factor
                        low = values.astype(BF16)
                        proj[part, here, :] = low
                        if part != 1:
                            at = part // 2
                            sm[0, at : at + 1, :] += jnp.sum(low.astype(F32), axis=0, keepdims=True)

                    do_in(P_AB, b)

            pl.run_scoped(
                attend,
                pltpu.VMEM((rows, width), BF16),
                pltpu.VMEM((2, HEADS, block, block), F32),
                pltpu.VMEM((3, block, width), F32),
            )

            def weight_grads(right_q, left, res):
                own_copies(n1_h, left, L_N1).start()
                right_q[...] = jnp.zeros_like(right_q)
                for f in range(n):
                    low, high = f * wq, (f + 1) * wq
                    for part in range(3):
                        a, b = max(low, part * width), min(high, (part + 1) * width)
                        if a < b:
                            right_q[f, :, a - low : b - low] = proj[part, :, a - part * width : b - part * width]
                own_copies(n1_h, left, L_N1).wait()
                ring[2, :, :rows] = left[...].T
                do(P_PK)
                for z in range(4):
                    t2ax(z).wait_send()
                    t2by(z).wait_send()
                    t2ay(z).wait_send()
                    t2bx(z).wait_send()
                co().wait_send()

                @pl.loop(0, 2 * n)
                def _(step):
                    j, f = step // n, step % n
                    lines = pl.ds(pl.multiple_of(j * 4 * span1, 16), 4 * span1)

                    @pl.when(j == 1)
                    def _():
                        c0(0, f).wait_send()

                    res[...] = mm(ring[2, lines, :rows], right_q[f])
                    for mine in (False, True):
                        part = core if mine else 1 - core
                        for i in range(2):
                            at = pl.ds(pl.multiple_of((2 * i + part) * span1, 8), span1)
                            for t in range(padq // LANES):
                                slab = slice(t * span1, (t + 1) * span1)
                                piece = res[at, t * LANES : (t + 1) * LANES].astype(BF16)
                                if mine:
                                    keep2[j, i, f // 2, f % 2, slab, :] = piece
                                else:
                                    stage[i, f // 2, f % 2, slab, :] = piece
                    c0(j, f).start()
                    do_in(P_WQ, step)

            pl.run_scoped(
                weight_grads,
                pltpu.VMEM((n, rows, padq), BF16),
                pltpu.VMEM((rows, width), BF16),
                pltpu.VMEM((4 * span1, padq), F32),
            )

            qkv_block(0, 1).wait()
            f1[...] = mm_cols(proj[0], ring[1])
            do(P_IN0)
            qkv_block(1, 3).wait()
            f1[...] += mm_cols(proj[1], ring[3])
            do(P_IN1)
            qkv_block(2, 0).wait()
            f1[...] += mm_cols(proj[2], ring[0])
            do(P_IN2)
            for k in (1, 2, 3):
                row_send(R_OUT, k, out_h).wait_send()
            row_own(0, out_h).wait()

            @pl.loop(0, clips)
            def _(c):
                for half in range(plan.halves):
                    for k in range(n):
                        here = rows_at(c, half, k)
                        normed, inverse = unit(piece_of(xin, k, c, half))
                        grad = f1[here, :]
                        sm[1 + c, 0:1, :] += jnp.sum(grad, axis=0, keepdims=True)
                        sm[1 + c, 1:2, :] += jnp.sum(grad * normed, axis=0, keepdims=True)
                        total = acc[here, :] + unit_back(normed, inverse, grad * (1.0 + mod[c, 1:2, :]))
                        rows_out[k, c, :, half * 8 : half * 8 + 8, :] = total.reshape(fl, 8, width).astype(BF16)

            row_own(1, in_h).start()
            do(P_INE)

            for k in (1, 2, 3):
                arrive(R_XIN, k, x_h, xin).wait_send()
                arrive(R_CIN, k, cot_h, cin).wait_send()
            row_own(1, in_h).wait()
            for k in (1, 2, 3):
                row_send(R_OUT, k, out_h, True).wait_recv()
                row_send(R_IN, k, in_h, True).wait_recv()
                row_send(R_IN, k, in_h).wait_send()
            smx_send().wait_send()
            smy_send().wait_send()
            for i in range(3):
                smc_send(i).wait_send()
            for f in range(n):
                t1z(f).wait_send()
                c0(1, f).wait_send()
            for j in range(2):
                for transfer in (t1ax, t1by, t0ax, t0by, t0cz, t0ay, t0bx, t0cx, t0abz, t0cy):
                    transfer(j).wait_send()
            for transfer in (t2z, t2zz, t1ay, t1bx, t1zz, toax, toby, toay, tobx, toz, tozz, t0zz):
                transfer().wait_send()

        pl.run_scoped(rest, pltpu.VMEM((rows, width), BF16), pltpu.VMEM((3, rows, width), BF16))

    lanes = LANES
    image = shape((clips, fl, plan.patches, width), BF16)
    arriving = [
        (4, 2, 2, s1), (4, 2, 2, s1), (2, 2, 2, 2, s0), (2, 2, 2, 2 * so),
        (4, 2, a1), (4, 2, s1 - a1), (4, a1), (4, s1 - a1), (2, s1), (s1,),
        (4, 2, s1), (2, 2, a1), (2, 2, s1 - a1), (2, a1), (2, s1 - a1), (s1,),
        (2, 2, so), (2, 2, so), (2, so), (2, so), (2 * so,), (so,),
        (2, 2, 2, a0), (2, 2, 2, a0), (2, 2, 2, a0), (2, 2, a0), (2, 2, a0), (2, 2, a0), (2, 2 * a0), (2, a0), (s0,),
    ]
    vmem = pl.BlockSpec(memory_space=pltpu.VMEM)
    smalls = (1 + clips, 8, width)
    out_shape = (
        [image, image, shape((s1, lanes), F32), shape((s1, lanes), F32), shape((s0, lanes), F32), shape((so, lanes), F32), shape(smalls, F32)]
        + [shape(dims + (lanes,), BF16) for dims in arriving]
        + [shape((2,) + smalls, F32), shape((3, 8, width), F32)]
        + [shape((rows, width), BF16)] * 2
        + [shape((3, rows, width), BF16), shape((blocks, HEADS, block, block), F32)]
        + [shape((rows, width), F32)] * 2
    )
    out_specs = [ANY, ANY] + [vmem] * 5 + [ANY] * (len(arriving) + 8)
    scratch = [
        pltpu.VMEM((2, 2, 2, 2, s1, lanes), BF16),
        pltpu.VMEM((2, 2, 2, 2, s1, lanes), BF16),
        pltpu.VMEM((2, 2, 2, 2 * so, lanes), BF16),
        pltpu.VMEM((2, 2, s1, lanes), BF16),
        pltpu.VMEM((2, 2, 2, s1, lanes), BF16),
        pltpu.VMEM((2, 2, s1, lanes), BF16),
        pltpu.VMEM((2, 2, s1, lanes), BF16),
        pltpu.VMEM((2, 4 * so, lanes), BF16),
        pltpu.VMEM((2, 4 * so, lanes), BF16),
        pltpu.VMEM((rows, width), BF16),
        pltpu.VMEM((rows, width), F32),
        pltpu.VMEM((rows, width), F32),
        pltpu.VMEM((rows, width), F32),
        pltpu.VMEM((4, width, width), BF16),
        pltpu.VMEM((n, clips, fl, own, width), BF16),
        pltpu.VMEM(smalls, F32),
        pltpu.VMEM(smalls, F32),
        pltpu.VMEM(smalls, F32),
        pltpu.VMEM((3, 8, width), F32),
        pltpu.VMEM((n, clips, fl, own, width), BF16),
        pltpu.VMEM((n, clips, fl, own, width), BF16),
        pltpu.VMEM((clips, 8, width), F32),
        pltpu.VMEM((9, 1, width), F32),
        pltpu.VMEM((clips, block, block), F32),
        pltpu.VMEM((clips, block, block), F32),
        pltpu.SemaphoreType.DMA((sum(REMOTE_SIZES),)),
        pltpu.SemaphoreType.DMA((sum(REMOTE_SIZES),)),
        pltpu.SemaphoreType.DMA((sum(LOCAL_SIZES),)),
    ]
    result = pl.pallas_call(
        body,
        in_specs=[ANY] * 6 + [vmem, pl.BlockSpec(memory_space=pltpu.SMEM)] + [vmem] * 4,
        out_specs=out_specs,
        out_shape=out_shape,
        scratch_shapes=scratch,
        compiler_params=pltpu.CompilerParams(
            vmem_limit_bytes=VMEM_LIMIT, collective_id=0, has_side_effects=True
        ),
        cost_estimate=cost(45e9, 200e6),
        name="layer",
    )(x, cotangent, qkv_weight, out_weight, fc1_weight, fc2_weight, modulation, counts, *biases)
    return result[:7]


def close(plan, images, small, sums, layouts):
    n, width, clips = plan.frame_axis, plan.width, plan.clips
    m = len(images)

    def body(*refs):
        image_in, vectors, ins = refs[:m], refs[m], refs[m + 1 : m + 1 + len(sums)]
        rest = refs[m + 1 + len(sums) :]
        image_out, outs = rest[:m], rest[m : m + len(layouts)]
        d_mod, d_qv, d_out, d_fc1, d_fc2, turn, held, sems = rest[m + len(layouts) :]
        arrive = [pltpu.make_async_copy(image_in[i], held.at[i], sems.at[i]) for i in range(m)]
        leave = [pltpu.make_async_copy(held.at[i], image_out[i], sems.at[m + i]) for i in range(m)]
        for copy in arrive:
            copy.start()
        frame = lax.axis_index("frame")

        def cut(first, k, size):
            low, high, pieces = k * size, (k + 1) * size, []
            while low < high:
                row, at = low // width, low % width
                end = min(width, at + high - low)
                pieces.append(vectors[first[0], first[1] + row : first[1] + row + 1, at:end])
                low += end - at
            return pieces[0] if len(pieces) == 1 else jnp.concatenate(pieces, axis=1)

        for k in range(n):

            @pl.when(frame == k)
            def _(k=k):
                for c in range(clips):
                    d_mod[c : c + 1, :] = cut((1 + c, 0), k, 6 * width // n)
                d_qv[...] = cut((0, 0), k, 2 * width // n).reshape(2 * width // n)
                d_out[...] = cut((0, 2), k, width // n).reshape(width // n)
                d_fc1[...] = cut((0, 3), k, width).reshape(width)
                d_fc2[...] = cut((0, 7), k, width // n).reshape(width // n)

        for i in range(m):
            arrive[i].wait()
            leave[i].start()
        for out, (which, first, span, tiles, used, folds, turned) in zip(outs, layouts):
            ref = ins[which]
            to = turn if turned else out
            for j in range(tiles):
                to[:, j * LANES : (j + 1) * LANES] = ref[first + j * span : first + (j + 1) * span, :]
            if used:
                tile = ref[first + tiles * span : first + tiles * span + span // folds, :]
                for g in range(folds):
                    moved = tile if g == 0 else pltpu.roll(tile, LANES - g * used, 1)
                    here = slice(g * (span // folds), (g + 1) * (span // folds))
                    to[here, tiles * LANES : tiles * LANES + used] = moved[:, :used]
            if turned:
                out[...] = turn[...].T
        for copy in leave:
            copy.wait()

    dims = [(span, tiles * LANES + used) for _, _, span, tiles, used, _, _ in layouts]
    grads = [shape(d[::-1] if layout[-1] else d, F32) for d, layout in zip(dims, layouts)]
    sizes = (2 * width // n, width // n, width, width // n)
    vectors = [shape((clips, 6 * width // n), F32)] + [shape((size,), F32) for size in sizes]
    made = grads + vectors
    return pl.pallas_call(
        body,
        grid=(1,),
        in_specs=[ANY] * m + [whole(small.shape)] + [whole(s.shape) for s in sums],
        out_specs=[ANY] * m + [whole(s.shape) for s in made],
        out_shape=[shape(image.shape, image.dtype) for image in images] + made,
        scratch_shapes=[
            pltpu.VMEM(dims[0], F32),
            pltpu.VMEM((m,) + images[0].shape, images[0].dtype),
            pltpu.SemaphoreType.DMA((2 * m,)),
        ],
        compiler_params=params(),
        cost_estimate=cost(0, 14e6),
        name="close",
    )(*images, small, *sums)


def fast_layer(
    mesh,
    block_input,
    modulation,
    frame_counts,
    qkv_weight,
    qv_bias,
    out_weight,
    out_bias,
    fc1_weight,
    fc1_bias,
    fc2_weight,
    fc2_bias,
    out_cotangent,
):
    plan = Plan(mesh, block_input.shape, qkv_weight.shape, fc1_weight.shape)
    n, width = plan.frame_axis, plan.width
    biases = (qv_bias, out_bias, fc1_bias, fc2_bias)
    block_output, input_grad, sum2, sum1, sum0, sumo, small = whole_layer(
        plan, block_input, out_cotangent, modulation, frame_counts, biases, qkv_weight, out_weight, fc1_weight, fc2_weight
    )
    span2, span1 = plan.ff // plan.clip_axis, width // plan.clip_axis
    (block_output, input_grad, fc2_turned, fc1_out, qkv_out, out_out, d_modulation, d_qv, d_out, d_fc1, d_fc2) = close(
        plan,
        (block_output, input_grad),
        small,
        (sum2, sum1, sum0, sumo),
        (
            (0, 0, span2, 2, 32, 4, True),
            (1, 0, span1, 9, 0, 1, False),
            (2, 0, span1, 6, 96, 1, False),
            (3, 0, span1, 2, 32, 3, False),
        ),
    )
    return (
        block_output,
        input_grad,
        d_modulation,
        qkv_out,
        d_qv,
        out_out,
        d_out,
        fc1_out,
        d_fc1,
        fc2_turned.T,
        d_fc2,
    )


def solution(mesh):
    placed = (
        P("clip", "frame", None, None),
        P("clip", None),
        P("clip"),
        P(),
        P(),
        P(),
        P(),
        P(),
        P(),
        P(),
        P(),
        P("clip", "frame", None, None),
    )
    def layer(*arrays):
        if fits(mesh, arrays[0].shape, arrays[3].shape, arrays[7].shape):
            return fast_layer(mesh, *arrays)
        return on_device(*arrays)

    return jax.shard_map(
        layer,
        mesh=mesh,
        in_specs=placed,
        out_specs=(
            P("clip", "frame", None, None),
            P("clip", "frame", None, None),
            P("clip", "frame"),
            P("clip", "frame"),
            P("frame"),
            P("clip", "frame"),
            P("frame"),
            P("clip", "frame"),
            P("frame"),
            P("clip", "frame"),
            P("frame"),
        ),
        check_vma=False,
    )
```

```python
import functools

import jax
import jax.numpy as jnp
from jax import lax
from jax.experimental import pallas as pl
from jax.experimental.pallas import tpu as pltpu
from jax.sharding import PartitionSpec as P

HEADS = 16


EPSILON = 1e-06
NEGATIVE = -1e30


def normalize(values):
    centred = values - jnp.mean(values, axis=-1, keepdims=True)
    variance = jnp.mean(centred * centred, axis=-1, keepdims=True)
    return centred * lax.rsqrt(variance + EPSILON)


def modulate(values, shift_term, scale_term):
    return normalize(values) * (1.0 + scale_term) + shift_term


def gelu_tanh(inputs):
    return jax.nn.gelu(inputs, approximate=True)


def contract_rows(left, right):
    return lax.dot_general(
        left, right, (((0,), (0,)), ((), ())), preferred_element_type=jnp.float32
    )


def contract_cols(left, right):
    return lax.dot_general(
        left, right, (((1,), (1,)), ((), ())), preferred_element_type=jnp.float32
    )


def on_device(
    block_input,
    modulation,
    frame_counts,
    qkv_weight,
    qv_bias,
    out_weight,
    out_bias,
    fc1_weight,
    fc1_bias,
    fc2_weight,
    fc2_bias,
    out_cotangent,
):
    swapped = lax.all_to_all(block_input, "frame", split_axis=2, concat_axis=1, tiled=True)
    clip_count, frames, patches, model_width = swapped.shape
    head_width = model_width // HEADS
    row_count = clip_count * frames * patches
    factor = head_width ** (-0.5)
    frame_valid = (jnp.arange(frames)[None, :] < frame_counts[:, None]).astype(jnp.float32)
    valid_rows = frame_valid[:, :, None, None]
    key_valid = frame_valid[:, None, None, None, :] > 0.5
    modulators = modulation.astype(jnp.float32).reshape(clip_count, 6, model_width)[
        :, :, None, None, :
    ]
    shift_one = modulators[:, 0]
    scale_one = modulators[:, 1]
    gate_one = modulators[:, 2]
    shift_two = modulators[:, 3]
    scale_two = modulators[:, 4]
    gate_two = modulators[:, 5]
    residual = swapped.astype(jnp.float32)
    normed_full, modulate_back_one = jax.vjp(modulate, residual, shift_one, scale_one)
    normed_one = normed_full.astype(jnp.bfloat16).reshape(row_count, model_width)
    bias_full = jnp.concatenate(
        [qv_bias[:model_width], jnp.zeros((model_width,), jnp.bfloat16), qv_bias[model_width:]]
    ).astype(jnp.float32)
    projected = (
        jnp.dot(normed_one, qkv_weight, preferred_element_type=jnp.float32) + bias_full
    ).astype(jnp.bfloat16)
    shaped = projected.reshape(clip_count, frames, patches, 3, HEADS, head_width)
    queries = shaped[:, :, :, 0]
    keys_all = shaped[:, :, :, 1]
    values_all = shaped[:, :, :, 2]
    scores = (
        jnp.einsum("cfphd,cgphd->cphfg", queries, keys_all, preferred_element_type=jnp.float32)
        * factor
    )
    scores = jnp.where(key_valid, scores, NEGATIVE)
    row_peak = jnp.max(scores, axis=-1, keepdims=True)
    exponent = jnp.exp(scores - row_peak)
    attention_weights = exponent / jnp.sum(exponent, axis=-1, keepdims=True)
    weights_low = attention_weights.astype(jnp.bfloat16)
    context = jnp.einsum(
        "cphfg,cgphd->cfphd", weights_low, values_all, preferred_element_type=jnp.float32
    )
    context_low = context.astype(jnp.bfloat16).reshape(row_count, model_width)
    attended = jnp.dot(
        context_low, out_weight, preferred_element_type=jnp.float32
    ) + out_bias.astype(jnp.float32)
    attended = attended.reshape(clip_count, frames, patches, model_width)
    middle = residual + gate_one * attended
    normed_mid, modulate_back_two = jax.vjp(modulate, middle, shift_two, scale_two)
    normed_two = normed_mid.astype(jnp.bfloat16).reshape(row_count, model_width)
    hidden = jnp.dot(normed_two, fc1_weight, preferred_element_type=jnp.float32) + fc1_bias.astype(
        jnp.float32
    )
    activated_full, gelu_back = jax.vjp(gelu_tanh, hidden)
    activated = activated_full.astype(jnp.bfloat16)
    branch_two = jnp.dot(
        activated, fc2_weight, preferred_element_type=jnp.float32
    ) + fc2_bias.astype(jnp.float32)
    branch_two = branch_two.reshape(clip_count, frames, patches, model_width)
    result = valid_rows * (middle + gate_two * branch_two)
    block_output = lax.all_to_all(
        result.astype(jnp.bfloat16), "frame", split_axis=1, concat_axis=2, tiled=True
    )
    cotangent = lax.all_to_all(
        out_cotangent, "frame", split_axis=2, concat_axis=1, tiled=True
    ).astype(jnp.float32)
    d_result = valid_rows * cotangent
    d_gate_two = jnp.sum(d_result * branch_two, axis=(1, 2))
    d_branch = (d_result * gate_two).astype(jnp.bfloat16).reshape(row_count, model_width)
    d_fc2_bias = jnp.sum(d_branch.astype(jnp.float32), axis=0)
    d_fc2_weight = contract_rows(activated, d_branch)
    d_activated = contract_cols(d_branch, fc2_weight)
    d_hidden = gelu_back(d_activated)[0].astype(jnp.bfloat16)
    d_fc1_bias = jnp.sum(d_hidden.astype(jnp.float32), axis=0)
    d_fc1_weight = contract_rows(normed_two, d_hidden)
    d_normed_two = contract_cols(d_hidden, fc1_weight).reshape(
        clip_count, frames, patches, model_width
    )
    d_middle_norm, d_shift_two, d_scale_two = modulate_back_two(d_normed_two)
    d_middle = d_result + d_middle_norm
    d_gate_one = jnp.sum(d_middle * attended, axis=(1, 2))
    d_attended = (d_middle * gate_one).astype(jnp.bfloat16).reshape(row_count, model_width)
    d_out_bias = jnp.sum(d_attended.astype(jnp.float32), axis=0)
    d_out_weight = contract_rows(context_low, d_attended)
    d_context = contract_cols(d_attended, out_weight).astype(jnp.bfloat16)
    d_context = d_context.reshape(clip_count, frames, patches, HEADS, head_width)
    d_weights = jnp.einsum(
        "cfphd,cgphd->cphfg", d_context, values_all, preferred_element_type=jnp.float32
    )
    d_values = jnp.einsum(
        "cphfg,cfphd->cgphd", weights_low, d_context, preferred_element_type=jnp.float32
    )
    d_scores = attention_weights * (
        d_weights - jnp.sum(attention_weights * d_weights, axis=-1, keepdims=True)
    )
    d_scores = d_scores.astype(jnp.bfloat16)
    d_queries = (
        jnp.einsum("cphfg,cgphd->cfphd", d_scores, keys_all, preferred_element_type=jnp.float32)
        * factor
    )
    d_keys = (
        jnp.einsum("cphfg,cfphd->cgphd", d_scores, queries, preferred_element_type=jnp.float32)
        * factor
    )
    d_projected = (
        jnp.stack([d_queries, d_keys, d_values], axis=3)
        .astype(jnp.bfloat16)
        .reshape(row_count, 3 * model_width)
    )
    column_sums = jnp.sum(d_projected.astype(jnp.float32), axis=0)
    d_qv_bias = jnp.concatenate([column_sums[:model_width], column_sums[2 * model_width :]])
    d_qkv_weight = contract_rows(normed_one, d_projected)
    d_normed_one = contract_cols(d_projected, qkv_weight).reshape(
        clip_count, frames, patches, model_width
    )
    d_residual, d_shift_one, d_scale_one = modulate_back_one(d_normed_one)
    d_input = d_middle + d_residual
    input_grad = lax.all_to_all(
        d_input.astype(jnp.bfloat16), "frame", split_axis=1, concat_axis=2, tiled=True
    )
    d_modulation = jnp.stack(
        [
            d_shift_one.reshape(clip_count, model_width),
            d_scale_one.reshape(clip_count, model_width),
            d_gate_one,
            d_shift_two.reshape(clip_count, model_width),
            d_scale_two.reshape(clip_count, model_width),
            d_gate_two,
        ],
        axis=1,
    ).reshape(clip_count, 6 * model_width)
    every_part = (
        lax.psum_scatter(d_qkv_weight, "frame", scatter_dimension=1, tiled=True),
        lax.psum_scatter(d_out_weight, "frame", scatter_dimension=1, tiled=True),
        lax.psum_scatter(d_fc1_weight, "frame", scatter_dimension=1, tiled=True),
        lax.psum_scatter(d_fc2_weight, "frame", scatter_dimension=1, tiled=True),
        lax.psum_scatter(d_modulation, "frame", scatter_dimension=1, tiled=True),
        lax.psum_scatter(d_qv_bias, "frame", scatter_dimension=0, tiled=True),
        lax.psum_scatter(d_out_bias, "frame", scatter_dimension=0, tiled=True),
        lax.psum_scatter(d_fc1_bias, "frame", scatter_dimension=0, tiled=True),
        lax.psum_scatter(d_fc2_bias, "frame", scatter_dimension=0, tiled=True),
    )
    every_mat = (
        lax.psum_scatter(every_part[0], "clip", scatter_dimension=0, tiled=True),
        lax.psum_scatter(every_part[1], "clip", scatter_dimension=0, tiled=True),
        lax.psum_scatter(every_part[2], "clip", scatter_dimension=0, tiled=True),
        lax.psum_scatter(every_part[3], "clip", scatter_dimension=0, tiled=True),
    )
    qkv_grad = every_mat[0]
    out_grad = every_mat[1]
    fc1_grad = every_mat[2]
    fc2_grad = every_mat[3]
    modulation_grad = every_part[4]
    bias_parts = (every_part[5], every_part[6], every_part[7], every_part[8])
    bias_totals = lax.psum((bias_parts[0], bias_parts[1], bias_parts[2], bias_parts[3]), "clip")
    return (
        block_output,
        input_grad,
        modulation_grad,
        qkv_grad,
        bias_totals[0],
        out_grad,
        bias_totals[1],
        fc1_grad,
        bias_totals[2],
        fc2_grad,
        bias_totals[3],
    )


LANES = 128
VMEM_LIMIT = 58 * 1024 * 1024
ROWS_DN = (((0,), (0,)), ((), ()))
COLS_DN = (((1,), (1,)), ((), ()))
F32 = jnp.float32
BF16 = jnp.bfloat16


def mm(left, right):
    return jnp.dot(left, right, preferred_element_type=F32)


def mm_cols(left, right):
    return lax.dot_general(left, right, COLS_DN, preferred_element_type=F32)


def mm_rows(left, right):
    return lax.dot_general(left, right, ROWS_DN, preferred_element_type=F32)


def unit(values):
    centred = values - jnp.mean(values, axis=-1, keepdims=True)
    variance = jnp.mean(centred * centred, axis=-1, keepdims=True)
    inverse = lax.rsqrt(variance + EPSILON)
    return centred * inverse, inverse


def unit_back(unit_values, inverse, grad):
    mean_grad = jnp.mean(grad, axis=-1, keepdims=True)
    mean_dot = jnp.mean(grad * unit_values, axis=-1, keepdims=True)
    return (grad - mean_grad - unit_values * mean_dot) * inverse


def params(**more):
    return pltpu.CompilerParams(vmem_limit_bytes=VMEM_LIMIT, **more)


def cost(flops, moved, transcendentals=0):
    return pl.CostEstimate(flops=int(flops), bytes_accessed=int(moved), transcendentals=int(transcendentals))


def shape(dims, kind):
    return jax.ShapeDtypeStruct(tuple(dims), kind)


def whole(dims, buffers=1):
    zeros = (0,) * len(dims)
    return pl.BlockSpec(tuple(dims), lambda *_: zeros, pipeline_mode=pl.Buffered(buffers))


ANY = pl.BlockSpec(memory_space=pl.ANY)


def head_window(head, width):
    low = head * width
    start = low // LANES * LANES
    size = LANES if low - start + width <= LANES else 2 * LANES
    return low, start, size


def head_mask(head, width):
    low, start, size = head_window(head, width)
    lane = lax.broadcasted_iota(jnp.int32, (1, size), 1) + start
    return jnp.where((lane >= low) & (lane < low + width), 1.0, 0.0).astype(BF16)


class Plan:
    def __init__(self, mesh, x, qkv_weight, fc1_weight):
        self.clip_axis = mesh.shape["clip"]
        self.frame_axis = mesh.shape["frame"]
        self.clips, self.local_frames, self.patches, self.width = x
        self.own_patches = self.patches // self.frame_axis
        self.halves = self.own_patches // 8
        self.frames = self.local_frames * self.frame_axis
        self.ff = fc1_weight[1]
        self.rows = self.clips * self.frames * self.own_patches
        self.clip_rows = self.rows // self.clips
        self.block = self.frames * 8
        self.blocks = self.rows // self.block
        self.piece = self.local_frames * 8
        self.head_width = self.width // HEADS
        self.chunk_dims = (self.clips, self.halves, self.local_frames, 8, self.width)
        self.zs = self.clip_axis // 2

    def row_of(self, clip, half, k):
        return ((clip * self.halves + half) * self.frame_axis + k) * self.piece


def fits(mesh, x, qkv_weight, fc1_weight):
    clip_axis, frame_axis = mesh.shape["clip"], mesh.shape["frame"]
    width, ff = x[3], fc1_weight[1]
    return (
        clip_axis == 8
        and frame_axis == 4
        and x[2] // frame_axis % 8 == 0
        and x[1] * frame_axis * 8 == LANES
        and width == 1152
        and ff == 4 * width
        and qkv_weight[1] == 3 * width
    )


def fold_tile(tile, folds, used):
    rows = tile.shape[0] // folds
    total = tile[:rows]
    for g in range(1, folds):
        total = total + pltpu.roll(tile[g * rows : (g + 1) * rows], g * used, 1)
    return total


MESH = pl.DeviceIdType.MESH


def unit_rows(ref, here):
    return unit(ref[here, :])


class Later:
    def __init__(self, make):
        self.make = make

    def start(self):
        self.make().start()

    def wait(self):
        self.make().wait()

    def wait_recv(self):
        self.make().wait_recv()

    def wait_send(self):
        self.make().wait_send()


REMOTE_SIZES = (4, 4, 8, 1, 4, 4, 4, 4, 1, 1, 4, 2, 2, 1, 1, 1, 1, 1, 1, 1, 1, 1, 2, 2, 2, 2, 2, 2, 2, 2, 1, 4, 4, 2, 2, 3, 4, 4)
(
    R_C2, R_C1, R_C0, R_CO, R_2AX, R_2BY, R_2AY, R_2BX, R_2Z, R_2ZZ, R_1Z, R_1AX, R_1BY, R_1AY, R_1BX, R_1ZZ, R_OAX, R_OBY, R_OAY, R_OBX, R_OZ, R_OZZ, R_0AX, R_0BY, R_0CZ, R_0AY, R_0BX, R_0CX, R_0ABZ, R_0CY, R_0ZZ, R_OUT, R_IN, R_SMX, R_SMY, R_SMC, R_XIN, R_CIN,
) = REMOTE_AT = tuple(sum(REMOTE_SIZES[:i]) for i in range(len(REMOTE_SIZES)))
LOCAL_SIZES = (4, 6, 6, 6, 6, 2, 1, 1, 1, 2, 1, 1, 4, 1, 4)
(
    L_W, L_A, L_B, L_C, L_D, L_S, L_MID, L_ATT, L_PROJ, L_PROBS, L_N1, L_CTX, L_OWN, L_ACT, L_ACTS,
) = LOCAL_AT = tuple(sum(LOCAL_SIZES[:i]) for i in range(len(LOCAL_SIZES)))
CORE, Z0, Z1, X, Y, XY = range(6)


LOAD, RUN, SEND = range(3)
TMP_A, TMP_B, TMP_C, TMP_D, TMP_S = range(5)
(J_C1, J_C2, J_Z0, J_XY1, J_XY2, J_1A, J_1B, J_1XY2, J_2Z, J_CO, J_O1, J_O2, J_OZ, J_C0, J_Q1, J_Q2, J_Q3, J_FIN2, J_FIN1, J_FINO, J_FIN0, J_SM1, J_SM2, J_SM3, J_SM4, J_SM5, J_MD1, J_MD2) = range(28)
(S_1AX, S_1BY, S_1AY, S_1BX, S_2Z, S_0ZZ, S_SMX, S_MDX, S_OUT, S_IN) = range(10)
P_A = tuple((0, k) for k in range(4))
P_B = tuple((1, k) for k in range(4))
P_C = tuple((2, k) for k in range(4))
P_D = tuple((3, k) for k in range(4))
P_E = tuple((4, k) for k in range(4))
P_G = tuple((5, k) for k in range(4))
P_AB = tuple((6, k) for k in range(4))
P_WQ = tuple((7, k) for k in range(8))
P_M1, P_O, P_WO, P_DC, P_PK, P_IN0, P_IN1, P_IN2, P_INE = ((8, k) for k in range(9))
SCHEDULE = {
    P_D[0]: (
        (LOAD, J_C2, 0),
    ),
    P_E[0]: (
        (RUN, J_C2, 0),
    ),
    P_A[1]: (
        (LOAD, J_C1, 0),
    ),
    P_C[1]: (
        (RUN, J_C1, 0),
    ),
    P_D[1]: (
        (LOAD, J_C2, 1),
    ),
    P_A[2]: (
        (LOAD, J_C1, 1),
        (RUN, J_C2, 1),
    ),
    P_B[2]: (
        (LOAD, J_XY1, 0),
    ),
    P_C[2]: (
        (RUN, J_C1, 1),
    ),
    P_E[2]: (
        (LOAD, J_C2, 2),
    ),
    P_A[3]: (
        (RUN, J_XY1, 0),
        (LOAD, J_C1, 2),
    ),
    P_B[3]: (
        (RUN, J_C1, 2),
        (RUN, J_C2, 2),
        (LOAD, J_Z0, 0),
    ),
    P_C[3]: (
        (LOAD, J_XY2, 0),
    ),
    P_D[3]: (
        (LOAD, J_C2, 3),
        (RUN, J_Z0, 0),
        (LOAD, J_XY1, 1),
    ),
    P_E[3]: (
        (RUN, J_C2, 3),
        (RUN, J_XY1, 1),
    ),
    P_M1: (
        (LOAD, J_Z0, 1),
    ),
    P_WO: (
        (RUN, J_Z0, 1),
        (LOAD, J_XY1, 2),
        (LOAD, J_C1, 3),
    ),
    P_DC: (
        (RUN, J_C1, 3),
        (RUN, J_XY1, 2),
        (RUN, J_XY2, 0),
        (LOAD, J_XY1, 3),
        (LOAD, J_CO, 0),
    ),
    P_AB[0]: (
        (RUN, J_XY1, 3),
        (LOAD, J_Z0, 2),
        (LOAD, J_XY2, 1),
    ),
    P_AB[1]: (
        (RUN, J_Z0, 2),
        (SEND, S_1BY, 0),
        (SEND, S_1AX, 0),
        (RUN, J_XY2, 1),
        (LOAD, J_XY2, 2),
    ),
    P_AB[2]: (
        (RUN, J_XY2, 2),
        (LOAD, J_XY2, 3),
    ),
    P_AB[3]: (
        (RUN, J_XY2, 3),
        (RUN, J_CO, 0),
    ),
    P_PK: (
        (LOAD, J_Z0, 3),
    ),
    P_WQ[0]: (
        (RUN, J_Z0, 3),
    ),
    P_WQ[1]: (
        (LOAD, J_1A, 0),
        (SEND, S_2Z, 0),
        (SEND, S_1BY, 1),
    ),
    P_WQ[2]: (
        (SEND, S_1AX, 1),
    ),
    P_WQ[3]: (
        (LOAD, J_O1, 0),
    ),
    P_WQ[4]: (
        (LOAD, J_C0, 0),
        (RUN, J_1A, 0),
        (RUN, J_O1, 0),
        (LOAD, J_1B, 0),
    ),
    P_WQ[6]: (
        (RUN, J_C0, 0),
    ),
    P_WQ[7]: (
        (RUN, J_1B, 0),
        (LOAD, J_C0, 1),
        (LOAD, J_1B, 1),
        (LOAD, J_1A, 1),
    ),
    P_IN0: (
        (RUN, J_1A, 1),
        (RUN, J_C0, 1),
        (RUN, J_1B, 1),
    ),
    P_IN1: (
        (LOAD, J_O2, 0),
        (LOAD, J_2Z, 0),
    ),
    P_IN2: (
        (SEND, S_1BX, 0),
        (RUN, J_2Z, 0),
    ),
    P_INE: (
        (SEND, S_1AY, 0),
        (LOAD, J_Q1, 0),
        (SEND, S_SMX, 0),
    ),
    P_G[0]: (
        (RUN, J_O2, 0),
        (RUN, J_Q1, 0),
        (LOAD, J_SM1, 0),
    ),
    P_G[1]: (
        (LOAD, J_Q1, 1),
        (RUN, J_SM1, 0),
        (LOAD, J_SM2, 0),
    ),
    P_G[2]: (
        (LOAD, J_OZ, 0),
        (RUN, J_Q1, 1),
        (RUN, J_OZ, 0),
        (RUN, J_SM2, 0),
        (LOAD, J_Q2, 0),
    ),
    P_G[3]: (
        (RUN, J_Q2, 0),
        (LOAD, J_SM3, 0),
        (LOAD, J_1XY2, 0),
        (RUN, J_1XY2, 0),
        (SEND, S_IN, 3),
        (SEND, S_IN, 1),
        (SEND, S_IN, 2),
    ),
    P_O: (
        (LOAD, J_Q2, 1),
        (RUN, J_Q2, 1),
        (LOAD, J_FIN2, 0),
        (RUN, J_FIN2, 0),
        (SEND, S_MDX, 0),
        (LOAD, J_Q3, 0),
        (RUN, J_Q3, 0),
        (LOAD, J_Q3, 1),
        (LOAD, J_FIN1, 0),
        (SEND, S_OUT, 3),
        (SEND, S_OUT, 1),
        (SEND, S_OUT, 2),
        (RUN, J_SM3, 0),
        (RUN, J_Q3, 1),
        (SEND, S_0ZZ, 0),
        (LOAD, J_MD1, 0),
        (RUN, J_MD1, 0),
        (RUN, J_FIN1, 0),
        (LOAD, J_MD2, 0),
        (RUN, J_MD2, 0),
        (LOAD, J_SM4, 0),
        (RUN, J_SM4, 0),
        (LOAD, J_FINO, 0),
        (RUN, J_FINO, 0),
        (LOAD, J_FIN0, 0),
        (LOAD, J_SM5, 0),
        (RUN, J_FIN0, 0),
        (RUN, J_SM5, 0),
    ),
}
TMPS = {
    (J_1A, 0): TMP_C,
    (J_1A, 1): TMP_D,
    (J_1B, 0): TMP_D,
    (J_1B, 1): TMP_C,
    (J_1XY2, 0): TMP_C,
    (J_2Z, 0): TMP_C,
    (J_C1, 0): TMP_A,
    (J_C1, 1): TMP_A,
    (J_C1, 2): TMP_A,
    (J_C1, 3): TMP_A,
    (J_C2, 0): TMP_B,
    (J_C2, 1): TMP_B,
    (J_C2, 2): TMP_B,
    (J_C2, 3): TMP_B,
    (J_FIN0, 0): TMP_C,
    (J_FIN1, 0): TMP_C,
    (J_FIN2, 0): TMP_C,
    (J_FINO, 0): TMP_D,
    (J_O1, 0): TMP_D,
    (J_O2, 0): TMP_D,
    (J_OZ, 0): TMP_C,
    (J_Q1, 0): TMP_A,
    (J_Q1, 1): TMP_B,
    (J_Q2, 0): TMP_C,
    (J_Q2, 1): TMP_C,
    (J_Q3, 0): TMP_D,
    (J_Q3, 1): TMP_D,
    (J_XY1, 0): TMP_C,
    (J_XY1, 1): TMP_C,
    (J_XY1, 2): TMP_C,
    (J_XY1, 3): TMP_C,
    (J_XY2, 0): TMP_D,
    (J_XY2, 1): TMP_C,
    (J_XY2, 2): TMP_D,
    (J_XY2, 3): TMP_D,
    (J_Z0, 0): TMP_C,
    (J_Z0, 1): TMP_C,
    (J_Z0, 2): TMP_D,
    (J_Z0, 3): TMP_D,
}


def join_heads(width, head_parts, put):
    waiting = {}
    for h in range(HEADS):
        _, start, size = head_window(h, width)
        values = head_parts(h)
        for t in range(size // LANES):
            tiles = [value[:, t * LANES : (t + 1) * LANES] for value in values]
            j = start // LANES + t
            waiting[j] = [a + b for a, b in zip(waiting[j], tiles)] if j in waiting else tiles
        ahead = head_window(h + 1, width)[1] // LANES if h + 1 < HEADS else HEADS * width
        for j in sorted(waiting):
            if j < ahead:
                put(j, waiting.pop(j))


def whole_layer(plan, x, cotangent, modulation, counts, biases, qkv_weight, out_weight, fc1_weight, fc2_weight):
    n, rows, width, ff = plan.frame_axis, plan.rows, plan.width, plan.ff
    own, fl, clips = plan.own_patches, plan.local_frames, plan.clips
    span2, span1 = ff // plan.clip_axis, width // plan.clip_axis
    s1, s0, so = 9 * span1, 7 * span1, 2 * span1 + span1 // 3
    a1, a0 = 640, s0 // 3
    pad2, padq, wq = 384, 896, 3 * width // n
    blocks, block = plan.blocks, plan.block
    factor = plan.head_width ** (-0.5)
    half_rows = 64
    parts_per_clip = plan.clip_rows // half_rows

    def body(*refs):
        refs = list(refs)

        def take(count):
            got = refs[:count]
            del refs[:count]
            return got

        (x_h, cot_h, wqkv_h, wout_h, fc1_h, fc2_h, raw_mod, counts_ref, qv_bias, out_bias, fc1_bias, fc2_bias) = take(12)
        (out_h, in_h) = take(2)
        sum2, sum1, sum0, sumo, small = take(5)
        (rc2, rc1, rc0, rco, r2ax, r2by, r2ay, r2bx, r2z, r2zz) = take(10)
        (r1z, r1ax, r1by, r1ay, r1bx, r1zz) = take(6)
        (roax, roby, roay, robx, roz, rozz) = take(6)
        (r0ax, r0by, r0cz, r0ay, r0bx, r0cx, r0abz, r0cy, r0zz, rsm, rsmc) = take(11)
        (n1_h, ctx_h, proj_h, probs_h, att_h, mid_h, act_h) = take(7)
        (keep2, keep1, keepo, r2, stage, tmp_a, tmp_b, tmp_c, tmp_d, dres, acc, f1, f2, ring, rows_out, sm, sm_b, sm_t, smc) = take(19)
        (xin, cin, mod, bias, allowed, valid) = take(6)
        send_sem, recv_sem, local_sem = take(3)

        frame, clip = lax.axis_index("frame"), lax.axis_index("clip")
        mx, my = frame % 2, frame // 2
        core, z0, z1 = clip % 2, clip // 2 % 2, clip // 4
        partner = (
            ("clip", clip + 1 - 2 * core),
            ("clip", clip + 2 - 4 * z0),
            ("clip", clip + 4 - 8 * z1),
            ("frame", frame + 1 - 2 * mx),
            ("frame", frame + 2 - 4 * my),
            ("frame", n - 1 - frame),
        )

        def remote(name, index, src, dst, bit):
            axis, where = partner[bit]
            at = name + index
            return Later(
                lambda: pltpu.make_async_remote_copy(
                    src_ref=src,
                    dst_ref=dst,
                    send_sem=send_sem.at[at],
                    recv_sem=recv_sem.at[at],
                    device_id={axis: where},
                    device_id_type=MESH,
                )
            )

        def local(name, index, src, dst):
            return Later(lambda: pltpu.make_async_copy(src, dst, local_sem.at[name + index]))

        lo1, hi1 = pl.ds(0, a1), pl.ds(a1, s1 - a1)
        pa, pb, pc, pab, all0 = pl.ds(0, a0), pl.ds(a0, a0), pl.ds(2 * a0, a0), pl.ds(0, 2 * a0), pl.ds(0, s0)
        oa, ob, oab = pl.ds(0, so), pl.ds(so, so), pl.ds(0, 2 * so)
        all1 = pl.ds(0, s1)

        def c2(z):
            return remote(R_C2, z, stage.at[0, :, :, all1], rc2.at[z], CORE)

        def c1(f):
            return remote(R_C1, f, stage.at[1, :, :, all1], rc1.at[f], CORE)

        def c0(j, f):
            return remote(R_C0, 4 * j + f, stage.at[:, f // 2, f % 2, all0], rc0.at[j, :, f // 2, f % 2], CORE)

        def co():
            return remote(R_CO, 0, stage.at[:, :, :, oab], rco, CORE)

        def t2ax(z):
            return remote(R_2AX, z, keep2.at[z // 2, z % 2, :, 1 - mx, lo1], r2ax.at[z], X)

        def t2by(z):
            return remote(R_2BY, z, keep2.at[z // 2, z % 2, 1 - my, :, hi1], r2by.at[z], Y)

        def t2ay(z):
            return remote(R_2AY, z, keep2.at[z // 2, z % 2, 1 - my, mx, lo1], r2ay.at[z], Y)

        def t2bx(z):
            return remote(R_2BX, z, keep2.at[z // 2, z % 2, my, 1 - mx, hi1], r2bx.at[z], X)

        def t2z():
            return remote(R_2Z, 0, r2.at[:, 1 - z0], r2z, Z0)

        def t2zz():
            return remote(R_2ZZ, 0, r2.at[1 - z1, z0], r2zz, Z1)

        def t1z(f):
            return remote(R_1Z, f, keep1.at[f // 2, f % 2, :, 1 - z0], r1z.at[f], Z0)

        def t1ax(y):
            return remote(R_1AX, y, keep1.at[y, 1 - mx, :, z0, lo1], r1ax.at[y], X)

        def t1by(x):
            return remote(R_1BY, x, keep1.at[1 - my, x, :, z0, hi1], r1by.at[x], Y)

        def t1ay():
            return remote(R_1AY, 0, keep1.at[1 - my, mx, :, z0, lo1], r1ay, Y)

        def t1bx():
            return remote(R_1BX, 0, keep1.at[my, 1 - mx, :, z0, hi1], r1bx, X)

        def t1zz():
            return remote(R_1ZZ, 0, keep1.at[my, mx, 1 - z1, z0], r1zz, Z1)

        def toax():
            return remote(R_OAX, 0, keepo.at[:, :, 1 - mx, oa], roax, X)

        def toby():
            return remote(R_OBY, 0, keepo.at[:, 1 - my, :, ob], roby, Y)

        def toay():
            return remote(R_OAY, 0, keepo.at[:, 1 - my, mx, oa], roay, Y)

        def tobx():
            return remote(R_OBX, 0, keepo.at[:, my, 1 - mx, ob], robx, X)

        def toz():
            return remote(R_OZ, 0, keepo.at[1 - z0, my, mx], roz, Z0)

        def tozz():
            there = pl.ds(pl.multiple_of((1 - z1) * so, 16), so)
            return remote(R_OZZ, 0, keepo.at[z0, my, mx, there], rozz, Z1)

        def t0ax(j):
            return remote(R_0AX, j, keep2.at[j, :, :, 1 - mx, pa], r0ax.at[j], X)

        def t0by(j):
            return remote(R_0BY, j, keep2.at[j, :, 1 - my, :, pb], r0by.at[j], Y)

        def t0cz(j):
            return remote(R_0CZ, j, keep2.at[j, 1 - z0, :, :, pc], r0cz.at[j], Z0)

        def t0ay(j):
            return remote(R_0AY, j, keep2.at[j, :, 1 - my, mx, pa], r0ay.at[j], Y)

        def t0bx(j):
            return remote(R_0BX, j, keep2.at[j, :, my, 1 - mx, pb], r0bx.at[j], X)

        def t0cx(j):
            return remote(R_0CX, j, keep2.at[j, z0, :, 1 - mx, pc], r0cx.at[j], X)

        def t0abz(j):
            return remote(R_0ABZ, j, keep2.at[j, 1 - z0, my, mx, pab], r0abz.at[j], Z0)

        def t0cy(j):
            return remote(R_0CY, j, keep2.at[j, z0, 1 - my, mx, pc], r0cy.at[j], Y)

        def t0zz():
            return remote(R_0ZZ, 0, keep2.at[1 - z1, z0, my, mx, all0], r0zz, Z1)

        def row_send(name, k, dst, arriving=False):
            bit = (None, X, Y, XY)[k]
            place = partner[bit][1] if arriving else frame
            src = rows_out if name == R_IN else cin
            return remote(name, k, src.at[k], dst.at[:, :, pl.ds(place * own, own)], bit)

        def row_own(index, src, dst):
            return local(L_OWN, index, src.at[0], dst.at[:, :, pl.ds(frame * own, own)])

        def smx_send():
            return remote(R_SMX, 0, sm.at[0], rsm.at[0, 0], X)

        def smy_send():
            return remote(R_SMY, 0, sm_b.at[0], rsm.at[1, 0], Y)

        def mdx_send():
            return remote(R_SMX, 1, sm.at[pl.ds(1, clips)], rsm.at[0, pl.ds(1, clips)], X)

        def mdy_send():
            return remote(R_SMY, 1, sm_b.at[pl.ds(1, clips)], rsm.at[1, pl.ds(1, clips)], Y)

        def smc_send(i):
            return remote(R_SMC, i, smc.at[i], rsmc.at[i], (CORE, Z0, Z1)[i])

        def add_to(ref, at, other, other_at):
            ref[at] = ref[at] + other[other_at]

        def add_chunks(ref, at, other, other_at, count):
            for i in range(2):
                for k in range(2 if count == 2 else 1):
                    fill = iter((i, k))
                    here = tuple(next(fill) if p is None else p for p in at)
                    fill = iter((i, k))
                    there = tuple(next(fill) if p is None else p for p in other_at)
                    add_to(ref, here, other, there)

        def pump(arrivals, copies, work, sends):
            def load():
                for transfer in arrivals:
                    transfer.wait_recv()
                for copy in copies:
                    copy.start()

            def run():
                for copy in copies:
                    copy.wait()
                work()
                for transfer in sends:
                    transfer.start()

            return load, run

        def job(kind, index, tmps):
            tmp = (tmp_a, tmp_b, tmp_c, tmp_d, None)[tmps]
            sem = (L_A, L_B, L_C, L_D, L_S)[tmps]
            pair = (index // 2, index % 2)
            if kind == J_C1:

                def work():
                    add_chunks(keep1, pair + (None, None), tmp, (None, None, all1), 2)

                return pump([c1(index)], [local(sem, 0, rc1.at[index], tmp.at[:, :, all1])], work, [t1z(index)])
            if kind == J_C2:

                def work():
                    add_chunks(keep2, pair + (None, None, all1), tmp, (None, None, all1), 2)

                sends = [t2ax(index), t2by(index)]
                return pump([c2(index)], [local(sem, 0, rc2.at[index], tmp.at[:, :, all1])], work, sends)
            if kind == J_Z0:

                def work():
                    add_chunks(keep1, pair + (None, z0), tmp, (None, all1), 1)

                return pump([t1z(index)], [local(sem, 0, r1z.at[index], tmp.at[:, all1])], work, [])
            if kind == J_XY1:

                def work():
                    add_chunks(keep2, pair + (None, mx, lo1), tmp, (None, lo1), 1)
                    add_chunks(keep2, pair + (my, None, hi1), tmp, (None, hi1), 1)

                copies = [
                    local(sem, 0, r2ax.at[index], tmp.at[:, lo1]),
                    local(sem, 1, r2by.at[index], tmp.at[:, hi1]),
                ]
                return pump([t2ax(index), t2by(index)], copies, work, [t2ay(index), t2bx(index)])
            if kind == J_XY2:

                def work():
                    r2[pair] = keep2[pair + (my, mx, all1)] + tmp[0, all1]

                copies = [
                    local(sem, 0, r2ay.at[index], tmp.at[0, lo1]),
                    local(sem, 1, r2bx.at[index], tmp.at[0, hi1]),
                ]
                return pump([t2ay(index), t2bx(index)], copies, work, [])
            if kind == J_1A:

                def work():
                    add_chunks(keep1, (index, mx, None, z0, lo1), tmp, (None, lo1), 1)

                return pump([t1ax(index)], [local(sem, 0, r1ax.at[index], tmp.at[:, lo1])], work, [])
            if kind == J_1B:

                def work():
                    add_chunks(keep1, (my, index, None, z0, hi1), tmp, (None, hi1), 1)

                return pump([t1by(index)], [local(sem, 0, r1by.at[index], tmp.at[:, hi1])], work, [])
            if kind == J_1XY2:

                def work():
                    add_chunks(keep1, (my, mx, None, z0, all1), tmp, (None, all1), 1)

                copies = [local(sem, 0, r1ay, tmp.at[:, lo1]), local(sem, 1, r1bx, tmp.at[:, hi1])]
                return pump([t1ay(), t1bx()], copies, work, [t1zz()])
            if kind == J_2Z:

                def work():
                    add_chunks(r2, (None, z0), tmp, (None, all1), 1)

                return pump([t2z()], [local(sem, 0, r2z, tmp.at[:, all1])], work, [t2zz()])
            if kind == J_CO:

                def work():
                    add_chunks(keepo, (0, None, None), tmp_a, (None, None, oab), 2)
                    add_chunks(keepo, (1, None, None), tmp_b, (None, None, oab), 2)

                copies = [
                    local(L_A, 0, rco.at[0], tmp_a.at[:, :, oab]),
                    local(L_B, 0, rco.at[1], tmp_b.at[:, :, oab]),
                ]
                return pump([co()], copies, work, [toax(), toby()])
            if kind == J_O1:

                def work():
                    for i in range(2):
                        add_chunks(keepo, (i, None, mx, oa), tmp, (None, pl.ds(i * so, so)), 1)
                        add_chunks(keepo, (i, my, None, ob), tmp, (None, pl.ds((2 + i) * so, so)), 1)

                copies = [local(sem, i, roax.at[i], tmp.at[:, pl.ds(i * so, so)]) for i in range(2)]
                copies += [local(sem, 2 + i, roby.at[i], tmp.at[:, pl.ds((2 + i) * so, so)]) for i in range(2)]
                return pump([toax(), toby()], copies, work, [toay(), tobx()])
            if kind == J_O2:

                def work():
                    add_chunks(keepo, (None, my, mx, oab), tmp, (None, oab), 1)

                copies = [local(sem, 0, roay, tmp.at[:, oa]), local(sem, 1, robx, tmp.at[:, ob])]
                return pump([toay(), tobx()], copies, work, [toz()])
            if kind == J_OZ:

                def work():
                    add_to(keepo, (z0, my, mx), tmp, (0, oab))

                return pump([toz()], [local(sem, 0, roz, tmp.at[0, oab])], work, [tozz()])
            if kind == J_C0:

                def work():
                    add_chunks(keep2, (index, 0, None, None, all0), tmp_a, (None, None, all0), 2)
                    add_chunks(keep2, (index, 1, None, None, all0), tmp_b, (None, None, all0), 2)

                copies = [
                    local(L_A, 0, rc0.at[index, 0], tmp_a.at[:, :, all0]),
                    local(L_B, 0, rc0.at[index, 1], tmp_b.at[:, :, all0]),
                ]
                sends = [t0ax(index), t0by(index), t0cz(index)]
                return pump([c0(index, f) for f in range(n)], copies, work, sends)
            if kind == J_Q1:

                def work():
                    add_chunks(keep2, (index, None, None, mx, pa), tmp, (None, None, pa), 2)
                    add_chunks(keep2, (index, None, my, None, pb), tmp, (None, None, pb), 2)
                    add_chunks(keep2, (index, z0, None, None, pc), tmp, (None, None, pc), 2)

                copies = [
                    local(sem, i, r.at[index], tmp.at[:, :, p])
                    for i, (r, p) in enumerate(((r0ax, pa), (r0by, pb), (r0cz, pc)))
                ]
                arrivals = [t0ax(index), t0by(index), t0cz(index)]
                return pump(arrivals, copies, work, [t0ay(index), t0bx(index), t0cx(index)])
            if kind == J_Q2:

                def work():
                    add_chunks(keep2, (index, None, my, mx, pab), tmp, (None, pab), 1)
                    add_chunks(keep2, (index, z0, None, mx, pc), tmp, (None, pc), 1)

                copies = [
                    local(sem, i, r.at[index], tmp.at[:, p])
                    for i, (r, p) in enumerate(((r0ay, pa), (r0bx, pb), (r0cx, pc)))
                ]
                return pump([t0ay(index), t0bx(index), t0cx(index)], copies, work, [t0abz(index), t0cy(index)])
            if kind == J_Q3:

                def work():
                    add_to(keep2, (index, z0, my, mx, all0), tmp, (0, all0))

                copies = [local(sem, 0, r0abz.at[index], tmp.at[0, pab]), local(sem, 1, r0cy.at[index], tmp.at[0, pc])]
                return pump([t0abz(index), t0cy(index)], copies, work, [])
            if kind == J_FIN2:

                def work():
                    sum2[...] = r2[z1, z0].astype(F32) + tmp[0, all1].astype(F32)

                return pump([t2zz()], [local(sem, 0, r2zz, tmp.at[0, all1])], work, [])
            if kind == J_FIN1:

                def work():
                    sum1[...] = keep1[my, mx, z1, z0].astype(F32) + tmp[0, all1].astype(F32)

                return pump([t1zz()], [local(sem, 0, r1zz, tmp.at[0, all1])], work, [])
            if kind == J_FINO:

                def work():
                    here = pl.ds(pl.multiple_of(z1 * so, 16), so)
                    sumo[...] = keepo[z0, my, mx, here].astype(F32) + tmp[0, oa].astype(F32)

                return pump([tozz()], [local(sem, 0, rozz, tmp.at[0, oa])], work, [])
            if kind == J_FIN0:

                def work():
                    sum0[...] = keep2[z1, z0, my, mx, all0].astype(F32) + tmp[0, all0].astype(F32)

                return pump([t0zz()], [local(sem, 0, r0zz, tmp.at[0, all0])], work, [])
            if kind == J_SM1:

                def work():
                    sm_b[0] = sm[0] + sm_t[0]

                return pump([smx_send()], [local(L_S, 0, rsm.at[0, 0], sm_t.at[0])], work, [smy_send()])
            if kind == J_SM2:

                def work():
                    smc[0] = sm_b[0] + sm_t[0]

                return pump([smy_send()], [local(L_S, 0, rsm.at[1, 0], sm_t.at[0])], work, [smc_send(0)])
            if kind in (J_MD1, J_MD2):
                step, some = kind - J_MD1, pl.ds(1, clips)
                arrival, sends = (mdx_send, [mdy_send()]) if step == 0 else (mdy_send, [])
                source, result = (sm, sm_b) if step == 0 else (sm_b, small)

                def work():
                    result[some] = source[some] + sm_t[some]

                return pump([arrival()], [local(L_S, 1, rsm.at[step, some], sm_t.at[some])], work, sends)
            step = kind - J_SM3

            def work():
                if step < 2:
                    smc[step + 1] = smc[step] + sm_t[0]
                else:
                    small[0] = smc[step] + sm_t[0]

            sends = [smc_send(step + 1)] if step < 2 else []
            return pump([smc_send(step)], [local(L_S, 0, rsmc.at[step], sm_t.at[0])], work, sends)

        plain_sends = {
            S_1AX: t1ax,
            S_1BY: t1by,
            S_1AY: lambda _: t1ay(),
            S_1BX: lambda _: t1bx(),
            S_2Z: lambda _: t2z(),
            S_0ZZ: lambda _: t0zz(),
            S_SMX: lambda _: smx_send(),
            S_MDX: lambda _: mdx_send(),
            S_OUT: lambda k: row_send(R_OUT, k, out_h),
            S_IN: lambda k: row_send(R_IN, k, in_h),
        }

        def do(point):
            for what, kind, index in SCHEDULE.get(point, ()):
                if what == SEND:
                    plain_sends[kind](index).start()
                else:
                    job(kind, index, TMPS.get((kind, index), TMP_S))[what]()

        def do_in(points, index):
            for k, point in enumerate(points):
                if point in SCHEDULE:
                    pl.when(index == k)(lambda point=point: do(point))

        def weight(slot, src):
            return local(L_W, slot, src, ring.at[slot])

        def fc1_block(f):
            return weight(2 * (f % 2), fc1_h.at[:, pl.ds(pl.multiple_of(f * width, LANES), width)])

        def fc2_block(f):
            return weight(2 * (f % 2) + 1, fc2_h.at[pl.ds(pl.multiple_of(f * width, 16), width)])

        def fc2_block_at(f):
            return local(L_W, f, fc2_h.at[pl.ds(pl.multiple_of(f * width, 16), width)], ring.at[f])

        def qkv_block(i, slot):
            return weight(slot, wqkv_h.at[:, i * width : (i + 1) * width])

        def own_copies(src, dst, name):
            return local(name, 0, src, dst)

        def piece_of(ref, k, c, half):
            return ref[k, c, :, half * 8 : half * 8 + 8, :].astype(F32).reshape(plan.piece, width)

        def rows_at(c, half, k):
            return pl.ds(pl.multiple_of(c * plan.clip_rows + plan.row_of(0, half, k), 8), plan.piece)

        def arrive(name, k, src, dst):
            bit = (None, X, Y, XY)[k]
            return remote(name, k, src.at[:, :, pl.ds(partner[bit][1] * own, own)], dst.at[k], bit)

        barrier = pltpu.get_barrier_semaphore()
        for axis, where in partner:
            pl.semaphore_signal(barrier, inc=1, device_id={axis: where}, device_id_type=MESH)
        mine = pl.ds(frame * own, own)
        own_x = local(L_OWN, 2, x_h.at[:, :, mine], xin.at[0])
        own_x.start()
        for i in range(3):
            qkv_block(i, i).start()
        weight(3, wout_h).start()
        pl.semaphore_wait(barrier, len(partner))
        for k in (3, 1, 2):
            arrive(R_XIN, k, x_h, xin).start()
        sm[...] = jnp.zeros_like(sm)
        for i in range(6):
            values = raw_mod[:, i * width : (i + 1) * width].astype(F32)
            for c in range(clips):
                mod[c, i : i + 1, :] = values[c : c + 1, :]
        parts = [(qv_bias, 0), None, (qv_bias, 1), (out_bias, 0)] + [(fc1_bias, f) for f in range(n)] + [(fc2_bias, 0)]
        for i, part in enumerate(parts):
            if part is None:
                bias[i] = jnp.zeros((1, width), F32)
            else:
                bias[i] = part[0][pl.ds(part[1] * width, width)].astype(F32).reshape(1, width)

        def frame_of(axis):
            slot = lax.broadcasted_iota(jnp.int32, (block, block), axis) // 8
            k, local_frame = slot // fl, slot % fl
            low, high = k % 2, k // 2
            source = low + mx - 2 * low * mx + 2 * (high + my - 2 * high * my)
            return source * fl + local_frame

        lane_patch = lax.broadcasted_iota(jnp.int32, (block, block), 1) % 8
        row_patch = lax.broadcasted_iota(jnp.int32, (block, block), 0) % 8
        row_frame, lane_frame = frame_of(0), frame_of(1)
        for c in range(clips):
            count = counts_ref[c]
            valid[c] = jnp.where(row_frame < count, 1.0, 0.0)
            allowed[c] = jnp.where((lane_patch == row_patch) & (lane_frame < count), 0.0, NEGATIVE)

        def first_half(n1, proj, ctx, scores, lows, probs, n2):
            own_x.wait()

            @pl.loop(0, clips)
            def _(c):
                shift, scale = mod[c, 0:1, :], 1.0 + mod[c, 1:2, :]
                for half in range(plan.halves):
                    for k in range(n):
                        normed, _ = unit(piece_of(xin, k, c, half))
                        n1[rows_at(c, half, k), :] = (normed * scale + shift).astype(BF16)

            own_copies(n1, n1_h, L_N1).start()

            @pl.loop(0, 3)
            def _(i):
                local(L_W, i, fc2_h.at[pl.ds(0, width)], ring.at[i]).wait()
                proj[i] = (mm(n1[...], ring[i]) + bias[i]).astype(BF16)

            fc1_block(0).start()
            fc2_block(0).start()
            own_copies(proj, proj_h, L_PROJ).start()

            @pl.loop(0, blocks)
            def _(b):
                slot = b % 2
                here = pl.ds(pl.multiple_of(b * block, block), block)

                @pl.when(b >= 2)
                def _():
                    local(L_PROBS, slot, probs.at[slot], probs_h.at[b - 2]).wait()

                for h in range(HEADS):
                    _, start, size = head_window(h, plan.head_width)
                    cols = slice(start, start + size)
                    q = proj[0, here, cols] * head_mask(h, plan.head_width)
                    scores[h] = mm_cols(q, proj[1, here, cols]) * factor + allowed[b // plan.halves]
                for h in range(HEADS):
                    score = scores[h]
                    grown = jnp.exp(score - jnp.max(score, axis=-1, keepdims=True))
                    weights = grown * (1.0 / jnp.sum(grown, axis=-1, keepdims=True))
                    probs[slot, h] = weights
                    lows[h] = weights.astype(BF16)

                def head_context(h):
                    _, start, size = head_window(h, plan.head_width)
                    return [mm(lows[h], proj[2, here, start : start + size] * head_mask(h, plan.head_width))]

                def put_context(j, tiles):
                    ctx[here, j * LANES : (j + 1) * LANES] = tiles[0].astype(BF16)

                join_heads(plan.head_width, head_context, put_context)
                local(L_PROBS, slot, probs.at[slot], probs_h.at[b]).start()

            own_copies(ctx, ctx_h, L_CTX).start()
            weight(3, wout_h).wait()
            f1[...] = mm(ctx[...], ring[3]) + bias[3]
            own_copies(f1, att_h, L_ATT).start()

            @pl.loop(0, clips)
            def _(c):
                for half in range(plan.halves):
                    for k in range(n):
                        here = rows_at(c, half, k)
                        middle = piece_of(xin, k, c, half) + mod[c, 2:3, :] * f1[here, :]
                        f2[here, :] = middle
                        normed, _ = unit(middle)
                        n2[here, :] = (normed * (1.0 + mod[c, 4:5, :]) + mod[c, 3:4, :]).astype(BF16)

            own_copies(f2, mid_h, L_MID).start()
            own_copies(n1, n1_h, L_N1).wait()
            own_copies(proj, proj_h, L_PROJ).wait()
            own_copies(ctx, ctx_h, L_CTX).wait()
            for b in (blocks - 2, blocks - 1):
                local(L_PROBS, b % 2, probs.at[b % 2], probs_h.at[b]).wait()

        def mlp(n2, cin, own_cot, n2_turned, dbr, padded, act, act_turned, dh, res):
            padded[...] = jnp.zeros_like(padded)
            n2_turned[...] = n2[...].T
            acc[...] = jnp.zeros_like(acc)
            own_cot.wait()
            for k in (1, 2, 3):
                arrive(R_CIN, k, cot_h, cin).wait_recv()

            @pl.loop(0, clips)
            def _(c):
                for half in range(plan.halves):
                    for k in range(n):
                        here = rows_at(c, half, k)
                        piece = piece_of(cin, k, c, half) * valid[c, k * plan.piece : (k + 1) * plan.piece, 0:1]
                        dres[here, :] = piece.astype(BF16)
                        low = (piece * mod[c, 5:6, :]).astype(BF16)
                        dbr[here, :] = low
                        sm[0, 7:8, :] += jnp.sum(low.astype(F32), axis=0, keepdims=True)

            for f in range(n):
                padded[:, f * pad2 : f * pad2 + width // n] = dbr[:, f * (width // n) : (f + 1) * (width // n)]
            own_copies(f1, att_h, L_ATT).wait()
            own_copies(f2, mid_h, L_MID).wait()

            @pl.loop(0, n)
            def _(f):
                slot = 2 * (f % 2)

                @pl.when(f < n - 1)
                def _():
                    fc1_block(f + 1).start()
                    fc2_block(f + 1).start()

                @pl.when(f == n - 1)
                def _():
                    weight(0, wout_h).start()
                    qkv_block(0, 1).start()

                fc1_block(f).wait()
                f2[...] = mm(n2[...], ring[slot])
                first_bias = bias[4 + f]

                @pl.when(f >= 1)
                def _():
                    local(L_ACT, 0, act, act_h.at[f - 1]).wait()

                @pl.loop(0, rows // half_rows)
                def _(i):
                    here = pl.ds(pl.multiple_of(i * half_rows, half_rows), half_rows)
                    hidden = f2[here, :] + first_bias
                    square = hidden * hidden
                    bent = jnp.tanh(0.7978845608028654 * hidden * (1.0 + 0.044715 * square))
                    act[here, :] = (0.5 * hidden * (1.0 + bent)).astype(BF16)
                    slope = 0.7978845608028654 * (1.0 + 3.0 * 0.044715 * square)
                    f2[here, :] = 0.5 * (1.0 + bent) + 0.5 * hidden * (1.0 - bent * bent) * slope

                local(L_ACT, 0, act, act_h.at[f]).start()

                do_in(P_A, f)

                @pl.when(f >= 1)
                def _():
                    c1(f - 1).wait_send()
                    c2(f - 1).wait_send()

                act_turned[...] = act[...].T
                for i in range(2):
                    res[...] = mm(act_turned[...], padded[:, i * 2 * pad2 : (i + 1) * 2 * pad2])
                    for mine in (False, True):
                        part = core if mine else 1 - core
                        at = pl.ds(pl.multiple_of(part * span2, 8), span2)
                        for j in range(2):
                            pieces = [
                                res[at, j * pad2 + t * LANES : j * pad2 + (t + 1) * LANES] for t in range(3)
                            ]
                            pieces[2] = fold_tile(pieces[2], 4, 32)
                            row = 0
                            for piece in pieces:
                                slab = slice(row, row + piece.shape[0])
                                if mine:
                                    keep2[f // 2, f % 2, i, j, slab, :] = piece.astype(BF16)
                                else:
                                    stage[0, i, j, slab, :] = piece.astype(BF16)
                                row += piece.shape[0]
                c2(f).start()
                do_in(P_B, f)

                fc2_block(f).wait()
                dh[...] = (mm_cols(dbr[...], ring[slot + 1]) * f2[...]).astype(BF16)
                sm[0, pl.ds(3 + f, 1), :] = jnp.sum(dh[...].astype(F32), axis=0, keepdims=True)

                do_in(P_C, f)

                for first, tiles in ((0, 5), (5, 4)):
                    lanes = slice(first * LANES, (first + tiles) * LANES)
                    res[:, : tiles * LANES] = mm(n2_turned[...], dh[:, lanes])
                    for mine in (False, True):
                        part = core if mine else 1 - core
                        for i in range(2):
                            for j in range(2):
                                at = pl.ds(pl.multiple_of((4 * i + 2 * j + part) * span1, 8), span1)
                                for t in range(tiles):
                                    slab = slice((first + t) * span1, (first + t + 1) * span1)
                                    values = res[at, t * LANES : (t + 1) * LANES].astype(BF16)
                                    if mine:
                                        keep1[f // 2, f % 2, i, j, slab, :] = values
                                    else:
                                        stage[1, i, j, slab, :] = values
                c1(f).start()

                do_in(P_D, f)
                acc[...] += mm_cols(dh[...], ring[slot])
                do_in(P_E, f)

            local(L_ACT, 0, act, act_h.at[n - 1]).wait()

        def two_halves(n2):
            own_cot = local(L_OWN, 3, cot_h.at[:, :, mine], cin.at[0])
            own_cot.start()
            for k in (1, 2, 3):
                arrive(R_XIN, k, x_h, xin).wait_recv()
            for k in (3, 1, 2):
                arrive(R_CIN, k, cot_h, cin).start()
            pl.run_scoped(
                functools.partial(first_half, n2=n2),
                pltpu.VMEM((rows, width), BF16),
                pltpu.VMEM((3, rows, width), BF16),
                pltpu.VMEM((rows, width), BF16),
                pltpu.VMEM((HEADS, block, block), F32),
                pltpu.VMEM((HEADS, block, block), BF16),
                pltpu.VMEM((2, HEADS, block, block), F32),
            )
            pl.run_scoped(
                functools.partial(mlp, n2, cin, own_cot),
                pltpu.VMEM((width, rows), BF16),
                pltpu.VMEM((rows, width), BF16),
                pltpu.VMEM((rows, n * pad2), BF16),
                pltpu.VMEM((rows, width), BF16),
                pltpu.VMEM((width, rows), BF16),
                pltpu.VMEM((rows, width), BF16),
                pltpu.VMEM((width, 2 * pad2), F32),
            )

        pl.run_scoped(two_halves, pltpu.VMEM((rows, width), BF16))

        def rest(datt, proj):
            own_copies(mid_h, f2, L_MID).start()
            own_copies(proj_h, proj, L_PROJ).start()
            qkv_block(1, 3).start()
            own_copies(ctx_h, ring.at[2, :rows], L_CTX).start()

            def attend(dctx, probs, scores, lows):
                def middle(att):
                    own_copies(att_h, att, L_ATT).start()
                    own_copies(mid_h, f2, L_MID).wait()
                    own_copies(att_h, att, L_ATT).wait()

                    @pl.loop(0, rows // half_rows)
                    def _(i):
                        here = pl.ds(pl.multiple_of(i * half_rows, half_rows), half_rows)
                        c = i // parts_per_clip
                        normed, inverse = unit_rows(f2, here)
                        grad = acc[here, :]
                        sm[1 + c, 3:4, :] += jnp.sum(grad, axis=0, keepdims=True)
                        sm[1 + c, 4:5, :] += jnp.sum(grad * normed, axis=0, keepdims=True)
                        d_middle = dres[here, :].astype(F32) + unit_back(normed, inverse, grad * (1.0 + mod[c, 4:5, :]))
                        acc[here, :] = d_middle
                        sm[1 + c, 2:3, :] += jnp.sum(d_middle * att[here, :], axis=0, keepdims=True)
                        low = (d_middle * mod[c, 2:3, :]).astype(BF16)
                        datt[here, :] = low
                        sm[0, 2:3, :] += jnp.sum(low.astype(F32), axis=0, keepdims=True)

                pl.run_scoped(middle, pltpu.VMEM((rows, width), F32))
                do(P_M1)
                local(L_PROBS, 0, probs_h.at[0], probs.at[0]).start()

                c1(3).wait_send()
                c2(3).wait_send()

                def out_grad(right_o, res):
                    wide = width // n
                    right_o[...] = jnp.zeros_like(right_o)
                    for f in range(n):
                        right_o[f, :, :wide] = datt[:, f * wide : (f + 1) * wide]
                    own_copies(ctx_h, ring.at[2, :rows], L_CTX).wait()
                    turned = ring[2, :rows, :].T
                    ring[2, :, rows : 2 * rows] = turned

                    @pl.loop(0, n)
                    def _(f):
                        res[...] = mm(ring[2, :, rows : 2 * rows], right_o[f])
                        for mine in (False, True):
                            part = core if mine else 1 - core
                            for i in range(2):
                                for j in range(2):
                                    at = pl.ds(pl.multiple_of((4 * i + 2 * j + part) * span1, 8), span1)
                                    pieces = [res[at, t * LANES : (t + 1) * LANES] for t in range(3)]
                                    pieces[2] = fold_tile(pieces[2], 3, 32)
                                    row = i * so
                                    for piece in pieces:
                                        slab = slice(row, row + piece.shape[0])
                                        if mine:
                                            keepo[j, f // 2, f % 2, slab, :] = piece.astype(BF16)
                                        else:
                                            stage[j, f // 2, f % 2, slab, :] = piece.astype(BF16)
                                        row += piece.shape[0]

                pl.run_scoped(
                    out_grad, pltpu.VMEM((n, rows, pad2), BF16), pltpu.VMEM((width, pad2), F32)
                )
                co().start()
                do(P_WO)
                weight(0, wout_h).wait()
                dctx[...] = mm_cols(datt[...], ring[0]).astype(BF16)
                qkv_block(2, 0).start()
                do(P_DC)
                own_copies(proj_h, proj, L_PROJ).wait()

                @pl.loop(0, blocks)
                def _(b):
                    slot = b % 2
                    here = pl.ds(pl.multiple_of(b * block, block), block)

                    @pl.when(b < blocks - 1)
                    def _():
                        local(L_PROBS, 1 - slot, probs_h.at[b + 1], probs.at[1 - slot]).start()

                    local(L_PROBS, slot, probs_h.at[b], probs.at[slot]).wait()
                    for h in range(HEADS):
                        _, start, size = head_window(h, plan.head_width)
                        cols = slice(start, start + size)
                        scores[h] = mm_cols(dctx[here, cols] * head_mask(h, plan.head_width), proj[2, here, cols])
                    for h in range(HEADS):
                        weights = probs[slot, h]
                        mixed = weights * scores[h]
                        d_score = mixed - weights * jnp.sum(mixed, axis=-1, keepdims=True)
                        lows[0, h] = d_score.astype(BF16)
                        lows[1, h] = weights.astype(BF16)

                    def head_grads(h):
                        _, start, size = head_window(h, plan.head_width)
                        keep = head_mask(h, plan.head_width)
                        cols = slice(start, start + size)
                        return [
                            mm(lows[0, h], proj[1, here, cols] * keep),
                            mm_rows(lows[0, h], proj[0, here, cols] * keep),
                            mm_rows(lows[1, h], dctx[here, cols] * keep),
                        ]

                    def put_grads(j, tiles):
                        lanes = slice(j * LANES, (j + 1) * LANES)
                        for part in range(3):
                            values = tiles[part] if part == 2 else tiles[part] * factor
                            low = values.astype(BF16)
                            proj[part, here, lanes] = low
                            if part != 1:
                                at = part // 2
                                sm[0, at : at + 1, lanes] += jnp.sum(low.astype(F32), axis=0, keepdims=True)

                    join_heads(plan.head_width, head_grads, put_grads)

                    do_in(P_AB, b)

            pl.run_scoped(
                attend,
                pltpu.VMEM((rows, width), BF16),
                pltpu.VMEM((2, HEADS, block, block), F32),
                pltpu.VMEM((HEADS, block, block), F32),
                pltpu.VMEM((2, HEADS, block, block), BF16),
            )

            def weight_grads(right_q, left, res):
                own_copies(n1_h, left, L_N1).start()
                right_q[...] = jnp.zeros_like(right_q)
                for f in range(n):
                    low, high = f * wq, (f + 1) * wq
                    for part in range(3):
                        a, b = max(low, part * width), min(high, (part + 1) * width)
                        if a < b:
                            right_q[f, :, a - low : b - low] = proj[part, :, a - part * width : b - part * width]
                own_copies(n1_h, left, L_N1).wait()
                ring[2, :, :rows] = left[...].T
                do(P_PK)
                for z in range(4):
                    t2ax(z).wait_send()
                    t2by(z).wait_send()
                    t2ay(z).wait_send()
                    t2bx(z).wait_send()
                co().wait_send()

                @pl.loop(0, 2 * n)
                def _(step):
                    j, f = step // n, step % n
                    lines = pl.ds(pl.multiple_of(j * 4 * span1, 16), 4 * span1)

                    @pl.when(j == 1)
                    def _():
                        c0(0, f).wait_send()

                    res[...] = mm(ring[2, lines, :rows], right_q[f])
                    for mine in (False, True):
                        part = core if mine else 1 - core
                        for i in range(2):
                            at = pl.ds(pl.multiple_of((2 * i + part) * span1, 8), span1)
                            for t in range(padq // LANES):
                                slab = slice(t * span1, (t + 1) * span1)
                                piece = res[at, t * LANES : (t + 1) * LANES].astype(BF16)
                                if mine:
                                    keep2[j, i, f // 2, f % 2, slab, :] = piece
                                else:
                                    stage[i, f // 2, f % 2, slab, :] = piece
                    c0(j, f).start()
                    do_in(P_WQ, step)

            pl.run_scoped(
                weight_grads,
                pltpu.VMEM((n, rows, padq), BF16),
                pltpu.VMEM((rows, width), BF16),
                pltpu.VMEM((4 * span1, padq), F32),
            )

            qkv_block(0, 1).wait()
            f1[...] = mm_cols(proj[0], ring[1])
            do(P_IN0)
            qkv_block(1, 3).wait()
            f1[...] += mm_cols(proj[1], ring[3])
            do(P_IN1)
            qkv_block(2, 0).wait()
            f1[...] += mm_cols(proj[2], ring[0])
            do(P_IN2)
            for f in range(n):
                weight(f, fc2_h.at[pl.ds(f * width, width)]).start()

            @pl.loop(0, clips)
            def _(c):
                for half in range(plan.halves):
                    for k in range(n):
                        here = rows_at(c, half, k)
                        normed, inverse = unit(piece_of(xin, k, c, half))
                        grad = f1[here, :]
                        sm[1 + c, 0:1, :] += jnp.sum(grad, axis=0, keepdims=True)
                        sm[1 + c, 1:2, :] += jnp.sum(grad * normed, axis=0, keepdims=True)
                        total = acc[here, :] + unit_back(normed, inverse, grad * (1.0 + mod[c, 1:2, :]))
                        rows_out[k, c, :, half * 8 : half * 8 + 8, :] = total.reshape(fl, 8, width).astype(BF16)

            row_own(1, rows_out, in_h).start()
            do(P_INE)

            def branch(acts):
                for f in range(n):
                    local(L_ACTS, f, act_h.at[f], acts.at[f]).start()
                f1[...] = jnp.zeros_like(f1)

                @pl.loop(0, n)
                def _(f):
                    local(L_ACTS, f, act_h.at[f], acts.at[f]).wait()
                    fc2_block_at(f).wait()
                    f1[...] += mm(acts[f], ring[f])
                    do_in(P_G, f)

            pl.run_scoped(branch, pltpu.VMEM((n, rows, width), BF16))

            @pl.loop(0, clips)
            def _(c):
                for half in range(plan.halves):
                    for k in range(n):
                        here = rows_at(c, half, k)
                        value = f1[here, :] + bias[8]
                        sm[1 + c, 5:6, :] += jnp.sum(dres[here, :].astype(F32) * value, axis=0, keepdims=True)
                        total = valid[c, k * plan.piece : (k + 1) * plan.piece, 0:1] * (
                            f2[here, :] + mod[c, 5:6, :] * value
                        )
                        cin[k, c, :, half * 8 : half * 8 + 8, :] = total.reshape(fl, 8, width).astype(BF16)

            row_own(0, cin, out_h).start()
            do(P_O)

            for k in (1, 2, 3):
                arrive(R_XIN, k, x_h, xin).wait_send()
                arrive(R_CIN, k, cot_h, cin).wait_send()
            row_own(1, rows_out, in_h).wait()
            row_own(0, cin, out_h).wait()
            for k in (1, 2, 3):
                row_send(R_OUT, k, out_h, True).wait_recv()
                row_send(R_IN, k, in_h, True).wait_recv()
                row_send(R_IN, k, in_h).wait_send()
                row_send(R_OUT, k, out_h).wait_send()
            for transfer in (smx_send, smy_send, mdx_send, mdy_send):
                transfer().wait_send()
            for i in range(3):
                smc_send(i).wait_send()
            for f in range(n):
                t1z(f).wait_send()
                c0(1, f).wait_send()
            for j in range(2):
                for transfer in (t1ax, t1by, t0ax, t0by, t0cz, t0ay, t0bx, t0cx, t0abz, t0cy):
                    transfer(j).wait_send()
            for transfer in (t2z, t2zz, t1ay, t1bx, t1zz, toax, toby, toay, tobx, toz, tozz, t0zz):
                transfer().wait_send()

        pl.run_scoped(rest, pltpu.VMEM((rows, width), BF16), pltpu.VMEM((3, rows, width), BF16))

    lanes = LANES
    image = shape((clips, fl, plan.patches, width), BF16)
    arriving = [
        (4, 2, 2, s1), (4, 2, 2, s1), (2, 2, 2, 2, s0), (2, 2, 2, 2 * so),
        (4, 2, a1), (4, 2, s1 - a1), (4, a1), (4, s1 - a1), (2, s1), (s1,),
        (4, 2, s1), (2, 2, a1), (2, 2, s1 - a1), (2, a1), (2, s1 - a1), (s1,),
        (2, 2, so), (2, 2, so), (2, so), (2, so), (2 * so,), (so,),
        (2, 2, 2, a0), (2, 2, 2, a0), (2, 2, 2, a0), (2, 2, a0), (2, 2, a0), (2, 2, a0), (2, 2 * a0), (2, a0), (s0,),
    ]
    vmem = pl.BlockSpec(memory_space=pltpu.VMEM)
    smalls = (1 + clips, 8, width)
    out_shape = (
        [image, image, shape((s1, lanes), F32), shape((s1, lanes), F32), shape((s0, lanes), F32), shape((so, lanes), F32), shape(smalls, F32)]
        + [shape(dims + (lanes,), BF16) for dims in arriving]
        + [shape((2,) + smalls, F32), shape((3, 8, width), F32)]
        + [shape((rows, width), BF16)] * 2
        + [shape((3, rows, width), BF16), shape((blocks, HEADS, block, block), F32)]
        + [shape((rows, width), F32)] * 2
        + [shape((n, rows, width), BF16)]
    )
    out_specs = [ANY, ANY] + [vmem] * 5 + [ANY] * (len(arriving) + 9)
    scratch = [
        pltpu.VMEM((2, 2, 2, 2, s1, lanes), BF16),
        pltpu.VMEM((2, 2, 2, 2, s1, lanes), BF16),
        pltpu.VMEM((2, 2, 2, 2 * so, lanes), BF16),
        pltpu.VMEM((2, 2, s1, lanes), BF16),
        pltpu.VMEM((2, 2, 2, s1, lanes), BF16),
        pltpu.VMEM((2, 2, s1, lanes), BF16),
        pltpu.VMEM((2, 2, s1, lanes), BF16),
        pltpu.VMEM((2, 4 * so, lanes), BF16),
        pltpu.VMEM((2, 4 * so, lanes), BF16),
        pltpu.VMEM((rows, width), BF16),
        pltpu.VMEM((rows, width), F32),
        pltpu.VMEM((rows, width), F32),
        pltpu.VMEM((rows, width), F32),
        pltpu.VMEM((4, width, width), BF16),
        pltpu.VMEM((n, clips, fl, own, width), BF16),
        pltpu.VMEM(smalls, F32),
        pltpu.VMEM(smalls, F32),
        pltpu.VMEM(smalls, F32),
        pltpu.VMEM((3, 8, width), F32),
        pltpu.VMEM((n, clips, fl, own, width), BF16),
        pltpu.VMEM((n, clips, fl, own, width), BF16),
        pltpu.VMEM((clips, 8, width), F32),
        pltpu.VMEM((9, 1, width), F32),
        pltpu.VMEM((clips, block, block), F32),
        pltpu.VMEM((clips, block, block), F32),
        pltpu.SemaphoreType.DMA((sum(REMOTE_SIZES),)),
        pltpu.SemaphoreType.DMA((sum(REMOTE_SIZES),)),
        pltpu.SemaphoreType.DMA((sum(LOCAL_SIZES),)),
    ]
    result = pl.pallas_call(
        body,
        in_specs=[ANY] * 6 + [vmem, pl.BlockSpec(memory_space=pltpu.SMEM)] + [vmem] * 4,
        out_specs=out_specs,
        out_shape=out_shape,
        scratch_shapes=scratch,
        compiler_params=pltpu.CompilerParams(
            vmem_limit_bytes=VMEM_LIMIT, collective_id=0, has_side_effects=True
        ),
        cost_estimate=cost(45e9, 200e6),
        name="layer",
    )(x, cotangent, qkv_weight, out_weight, fc1_weight, fc2_weight, modulation, counts, *biases)
    return result[:7]


def close(plan, images, small, sums, layouts):
    n, width, clips = plan.frame_axis, plan.width, plan.clips
    m = len(images)

    def body(*refs):
        image_in, vectors, ins = refs[:m], refs[m], refs[m + 1 : m + 1 + len(sums)]
        rest = refs[m + 1 + len(sums) :]
        image_out, outs = rest[:m], rest[m : m + len(layouts)]
        d_mod, d_qv, d_out, d_fc1, d_fc2, turn, held, sems = rest[m + len(layouts) :]
        arrive = [pltpu.make_async_copy(image_in[i], held.at[i], sems.at[i]) for i in range(m)]
        leave = [pltpu.make_async_copy(held.at[i], image_out[i], sems.at[m + i]) for i in range(m)]
        for copy in arrive:
            copy.start()
        frame = lax.axis_index("frame")

        def cut(first, k, size):
            low, high, pieces = k * size, (k + 1) * size, []
            while low < high:
                row, at = low // width, low % width
                end = min(width, at + high - low)
                pieces.append(vectors[first[0], first[1] + row : first[1] + row + 1, at:end])
                low += end - at
            return pieces[0] if len(pieces) == 1 else jnp.concatenate(pieces, axis=1)

        for k in range(n):

            @pl.when(frame == k)
            def _(k=k):
                for c in range(clips):
                    d_mod[c : c + 1, :] = cut((1 + c, 0), k, 6 * width // n)
                d_qv[...] = cut((0, 0), k, 2 * width // n).reshape(2 * width // n)
                d_out[...] = cut((0, 2), k, width // n).reshape(width // n)
                d_fc1[...] = cut((0, 3), k, width).reshape(width)
                d_fc2[...] = cut((0, 7), k, width // n).reshape(width // n)

        for i in range(m):
            arrive[i].wait()
            leave[i].start()
        for out, (which, first, span, tiles, used, folds, turned) in zip(outs, layouts):
            ref = ins[which]
            to = turn if turned else out
            for j in range(tiles):
                to[:, j * LANES : (j + 1) * LANES] = ref[first + j * span : first + (j + 1) * span, :]
            if used:
                tile = ref[first + tiles * span : first + tiles * span + span // folds, :]
                for g in range(folds):
                    moved = tile if g == 0 else pltpu.roll(tile, LANES - g * used, 1)
                    here = slice(g * (span // folds), (g + 1) * (span // folds))
                    to[here, tiles * LANES : tiles * LANES + used] = moved[:, :used]
            if turned:
                out[...] = turn[...].T
        for copy in leave:
            copy.wait()

    dims = [(span, tiles * LANES + used) for _, _, span, tiles, used, _, _ in layouts]
    grads = [shape(d[::-1] if layout[-1] else d, F32) for d, layout in zip(dims, layouts)]
    sizes = (2 * width // n, width // n, width, width // n)
    vectors = [shape((clips, 6 * width // n), F32)] + [shape((size,), F32) for size in sizes]
    made = grads + vectors
    return pl.pallas_call(
        body,
        grid=(1,),
        in_specs=[ANY] * m + [whole(small.shape)] + [whole(s.shape) for s in sums],
        out_specs=[ANY] * m + [whole(s.shape) for s in made],
        out_shape=[shape(image.shape, image.dtype) for image in images] + made,
        scratch_shapes=[
            pltpu.VMEM(dims[0], F32),
            pltpu.VMEM((m,) + images[0].shape, images[0].dtype),
            pltpu.SemaphoreType.DMA((2 * m,)),
        ],
        compiler_params=params(),
        cost_estimate=cost(0, 14e6),
        name="close",
    )(*images, small, *sums)


def fast_layer(
    mesh,
    block_input,
    modulation,
    frame_counts,
    qkv_weight,
    qv_bias,
    out_weight,
    out_bias,
    fc1_weight,
    fc1_bias,
    fc2_weight,
    fc2_bias,
    out_cotangent,
):
    plan = Plan(mesh, block_input.shape, qkv_weight.shape, fc1_weight.shape)
    n, width = plan.frame_axis, plan.width
    biases = (qv_bias, out_bias, fc1_bias, fc2_bias)
    block_output, input_grad, sum2, sum1, sum0, sumo, small = whole_layer(
        plan, block_input, out_cotangent, modulation, frame_counts, biases, qkv_weight, out_weight, fc1_weight, fc2_weight
    )
    span2, span1 = plan.ff // plan.clip_axis, width // plan.clip_axis
    (block_output, input_grad, fc2_turned, fc1_out, qkv_out, out_out, d_modulation, d_qv, d_out, d_fc1, d_fc2) = close(
        plan,
        (block_output, input_grad),
        small,
        (sum2, sum1, sum0, sumo),
        (
            (0, 0, span2, 2, 32, 4, True),
            (1, 0, span1, 9, 0, 1, False),
            (2, 0, span1, 6, 96, 1, False),
            (3, 0, span1, 2, 32, 3, False),
        ),
    )
    return (
        block_output,
        input_grad,
        d_modulation,
        qkv_out,
        d_qv,
        out_out,
        d_out,
        fc1_out,
        d_fc1,
        fc2_turned.T,
        d_fc2,
    )


def solution(mesh):
    placed = (
        P("clip", "frame", None, None),
        P("clip", None),
        P("clip"),
        P(),
        P(),
        P(),
        P(),
        P(),
        P(),
        P(),
        P(),
        P("clip", "frame", None, None),
    )
    def layer(*arrays):
        if fits(mesh, arrays[0].shape, arrays[3].shape, arrays[7].shape):
            return fast_layer(mesh, *arrays)
        return on_device(*arrays)

    return jax.shard_map(
        layer,
        mesh=mesh,
        in_specs=placed,
        out_specs=(
            P("clip", "frame", None, None),
            P("clip", "frame", None, None),
            P("clip", "frame"),
            P("clip", "frame"),
            P("frame"),
            P("clip", "frame"),
            P("frame"),
            P("clip", "frame"),
            P("frame"),
            P("clip", "frame"),
            P("frame"),
        ),
        check_vma=False,
    )
```

```python
import functools

import jax
import jax.numpy as jnp
from jax import lax
from jax.experimental import pallas as pl
from jax.experimental.pallas import tpu as pltpu
from jax.sharding import PartitionSpec as P

HEADS = 16


EPSILON = 1e-06
NEGATIVE = -1e30


def normalize(values):
    centred = values - jnp.mean(values, axis=-1, keepdims=True)
    variance = jnp.mean(centred * centred, axis=-1, keepdims=True)
    return centred * lax.rsqrt(variance + EPSILON)


def modulate(values, shift_term, scale_term):
    return normalize(values) * (1.0 + scale_term) + shift_term


def gelu_tanh(inputs):
    return jax.nn.gelu(inputs, approximate=True)


def contract_rows(left, right):
    return lax.dot_general(
        left, right, (((0,), (0,)), ((), ())), preferred_element_type=jnp.float32
    )


def contract_cols(left, right):
    return lax.dot_general(
        left, right, (((1,), (1,)), ((), ())), preferred_element_type=jnp.float32
    )


def on_device(
    block_input,
    modulation,
    frame_counts,
    qkv_weight,
    qv_bias,
    out_weight,
    out_bias,
    fc1_weight,
    fc1_bias,
    fc2_weight,
    fc2_bias,
    out_cotangent,
):
    swapped = lax.all_to_all(block_input, "frame", split_axis=2, concat_axis=1, tiled=True)
    clip_count, frames, patches, model_width = swapped.shape
    head_width = model_width // HEADS
    row_count = clip_count * frames * patches
    factor = head_width ** (-0.5)
    frame_valid = (jnp.arange(frames)[None, :] < frame_counts[:, None]).astype(jnp.float32)
    valid_rows = frame_valid[:, :, None, None]
    key_valid = frame_valid[:, None, None, None, :] > 0.5
    modulators = modulation.astype(jnp.float32).reshape(clip_count, 6, model_width)[
        :, :, None, None, :
    ]
    shift_one = modulators[:, 0]
    scale_one = modulators[:, 1]
    gate_one = modulators[:, 2]
    shift_two = modulators[:, 3]
    scale_two = modulators[:, 4]
    gate_two = modulators[:, 5]
    residual = swapped.astype(jnp.float32)
    normed_full, modulate_back_one = jax.vjp(modulate, residual, shift_one, scale_one)
    normed_one = normed_full.astype(jnp.bfloat16).reshape(row_count, model_width)
    bias_full = jnp.concatenate(
        [qv_bias[:model_width], jnp.zeros((model_width,), jnp.bfloat16), qv_bias[model_width:]]
    ).astype(jnp.float32)
    projected = (
        jnp.dot(normed_one, qkv_weight, preferred_element_type=jnp.float32) + bias_full
    ).astype(jnp.bfloat16)
    shaped = projected.reshape(clip_count, frames, patches, 3, HEADS, head_width)
    queries = shaped[:, :, :, 0]
    keys_all = shaped[:, :, :, 1]
    values_all = shaped[:, :, :, 2]
    scores = (
        jnp.einsum("cfphd,cgphd->cphfg", queries, keys_all, preferred_element_type=jnp.float32)
        * factor
    )
    scores = jnp.where(key_valid, scores, NEGATIVE)
    row_peak = jnp.max(scores, axis=-1, keepdims=True)
    exponent = jnp.exp(scores - row_peak)
    attention_weights = exponent / jnp.sum(exponent, axis=-1, keepdims=True)
    weights_low = attention_weights.astype(jnp.bfloat16)
    context = jnp.einsum(
        "cphfg,cgphd->cfphd", weights_low, values_all, preferred_element_type=jnp.float32
    )
    context_low = context.astype(jnp.bfloat16).reshape(row_count, model_width)
    attended = jnp.dot(
        context_low, out_weight, preferred_element_type=jnp.float32
    ) + out_bias.astype(jnp.float32)
    attended = attended.reshape(clip_count, frames, patches, model_width)
    middle = residual + gate_one * attended
    normed_mid, modulate_back_two = jax.vjp(modulate, middle, shift_two, scale_two)
    normed_two = normed_mid.astype(jnp.bfloat16).reshape(row_count, model_width)
    hidden = jnp.dot(normed_two, fc1_weight, preferred_element_type=jnp.float32) + fc1_bias.astype(
        jnp.float32
    )
    activated_full, gelu_back = jax.vjp(gelu_tanh, hidden)
    activated = activated_full.astype(jnp.bfloat16)
    branch_two = jnp.dot(
        activated, fc2_weight, preferred_element_type=jnp.float32
    ) + fc2_bias.astype(jnp.float32)
    branch_two = branch_two.reshape(clip_count, frames, patches, model_width)
    result = valid_rows * (middle + gate_two * branch_two)
    block_output = lax.all_to_all(
        result.astype(jnp.bfloat16), "frame", split_axis=1, concat_axis=2, tiled=True
    )
    cotangent = lax.all_to_all(
        out_cotangent, "frame", split_axis=2, concat_axis=1, tiled=True
    ).astype(jnp.float32)
    d_result = valid_rows * cotangent
    d_gate_two = jnp.sum(d_result * branch_two, axis=(1, 2))
    d_branch = (d_result * gate_two).astype(jnp.bfloat16).reshape(row_count, model_width)
    d_fc2_bias = jnp.sum(d_branch.astype(jnp.float32), axis=0)
    d_fc2_weight = contract_rows(activated, d_branch)
    d_activated = contract_cols(d_branch, fc2_weight)
    d_hidden = gelu_back(d_activated)[0].astype(jnp.bfloat16)
    d_fc1_bias = jnp.sum(d_hidden.astype(jnp.float32), axis=0)
    d_fc1_weight = contract_rows(normed_two, d_hidden)
    d_normed_two = contract_cols(d_hidden, fc1_weight).reshape(
        clip_count, frames, patches, model_width
    )
    d_middle_norm, d_shift_two, d_scale_two = modulate_back_two(d_normed_two)
    d_middle = d_result + d_middle_norm
    d_gate_one = jnp.sum(d_middle * attended, axis=(1, 2))
    d_attended = (d_middle * gate_one).astype(jnp.bfloat16).reshape(row_count, model_width)
    d_out_bias = jnp.sum(d_attended.astype(jnp.float32), axis=0)
    d_out_weight = contract_rows(context_low, d_attended)
    d_context = contract_cols(d_attended, out_weight).astype(jnp.bfloat16)
    d_context = d_context.reshape(clip_count, frames, patches, HEADS, head_width)
    d_weights = jnp.einsum(
        "cfphd,cgphd->cphfg", d_context, values_all, preferred_element_type=jnp.float32
    )
    d_values = jnp.einsum(
        "cphfg,cfphd->cgphd", weights_low, d_context, preferred_element_type=jnp.float32
    )
    d_scores = attention_weights * (
        d_weights - jnp.sum(attention_weights * d_weights, axis=-1, keepdims=True)
    )
    d_scores = d_scores.astype(jnp.bfloat16)
    d_queries = (
        jnp.einsum("cphfg,cgphd->cfphd", d_scores, keys_all, preferred_element_type=jnp.float32)
        * factor
    )
    d_keys = (
        jnp.einsum("cphfg,cfphd->cgphd", d_scores, queries, preferred_element_type=jnp.float32)
        * factor
    )
    d_projected = (
        jnp.stack([d_queries, d_keys, d_values], axis=3)
        .astype(jnp.bfloat16)
        .reshape(row_count, 3 * model_width)
    )
    column_sums = jnp.sum(d_projected.astype(jnp.float32), axis=0)
    d_qv_bias = jnp.concatenate([column_sums[:model_width], column_sums[2 * model_width :]])
    d_qkv_weight = contract_rows(normed_one, d_projected)
    d_normed_one = contract_cols(d_projected, qkv_weight).reshape(
        clip_count, frames, patches, model_width
    )
    d_residual, d_shift_one, d_scale_one = modulate_back_one(d_normed_one)
    d_input = d_middle + d_residual
    input_grad = lax.all_to_all(
        d_input.astype(jnp.bfloat16), "frame", split_axis=1, concat_axis=2, tiled=True
    )
    d_modulation = jnp.stack(
        [
            d_shift_one.reshape(clip_count, model_width),
            d_scale_one.reshape(clip_count, model_width),
            d_gate_one,
            d_shift_two.reshape(clip_count, model_width),
            d_scale_two.reshape(clip_count, model_width),
            d_gate_two,
        ],
        axis=1,
    ).reshape(clip_count, 6 * model_width)
    every_part = (
        lax.psum_scatter(d_qkv_weight, "frame", scatter_dimension=1, tiled=True),
        lax.psum_scatter(d_out_weight, "frame", scatter_dimension=1, tiled=True),
        lax.psum_scatter(d_fc1_weight, "frame", scatter_dimension=1, tiled=True),
        lax.psum_scatter(d_fc2_weight, "frame", scatter_dimension=1, tiled=True),
        lax.psum_scatter(d_modulation, "frame", scatter_dimension=1, tiled=True),
        lax.psum_scatter(d_qv_bias, "frame", scatter_dimension=0, tiled=True),
        lax.psum_scatter(d_out_bias, "frame", scatter_dimension=0, tiled=True),
        lax.psum_scatter(d_fc1_bias, "frame", scatter_dimension=0, tiled=True),
        lax.psum_scatter(d_fc2_bias, "frame", scatter_dimension=0, tiled=True),
    )
    every_mat = (
        lax.psum_scatter(every_part[0], "clip", scatter_dimension=0, tiled=True),
        lax.psum_scatter(every_part[1], "clip", scatter_dimension=0, tiled=True),
        lax.psum_scatter(every_part[2], "clip", scatter_dimension=0, tiled=True),
        lax.psum_scatter(every_part[3], "clip", scatter_dimension=0, tiled=True),
    )
    qkv_grad = every_mat[0]
    out_grad = every_mat[1]
    fc1_grad = every_mat[2]
    fc2_grad = every_mat[3]
    modulation_grad = every_part[4]
    bias_parts = (every_part[5], every_part[6], every_part[7], every_part[8])
    bias_totals = lax.psum((bias_parts[0], bias_parts[1], bias_parts[2], bias_parts[3]), "clip")
    return (
        block_output,
        input_grad,
        modulation_grad,
        qkv_grad,
        bias_totals[0],
        out_grad,
        bias_totals[1],
        fc1_grad,
        bias_totals[2],
        fc2_grad,
        bias_totals[3],
    )


LANES = 128
VMEM_LIMIT = 61 * 1024 * 1024
ROWS_DN = (((0,), (0,)), ((), ()))
COLS_DN = (((1,), (1,)), ((), ()))
F32 = jnp.float32
BF16 = jnp.bfloat16


def mm(left, right):
    return jnp.dot(left, right, preferred_element_type=F32)


def mm_cols(left, right):
    return lax.dot_general(left, right, COLS_DN, preferred_element_type=F32)


def mm_rows(left, right):
    return lax.dot_general(left, right, ROWS_DN, preferred_element_type=F32)


def unit(values):
    centred = values - jnp.mean(values, axis=-1, keepdims=True)
    variance = jnp.mean(centred * centred, axis=-1, keepdims=True)
    inverse = lax.rsqrt(variance + EPSILON)
    return centred * inverse, inverse


def unit_back(unit_values, inverse, grad):
    mean_grad = jnp.mean(grad, axis=-1, keepdims=True)
    mean_dot = jnp.mean(grad * unit_values, axis=-1, keepdims=True)
    return (grad - mean_grad - unit_values * mean_dot) * inverse


def params(**more):
    return pltpu.CompilerParams(vmem_limit_bytes=VMEM_LIMIT, **more)


def cost(flops, moved, transcendentals=0):
    return pl.CostEstimate(flops=int(flops), bytes_accessed=int(moved), transcendentals=int(transcendentals))


def shape(dims, kind):
    return jax.ShapeDtypeStruct(tuple(dims), kind)


def whole(dims, buffers=1):
    zeros = (0,) * len(dims)
    return pl.BlockSpec(tuple(dims), lambda *_: zeros, pipeline_mode=pl.Buffered(buffers))


ANY = pl.BlockSpec(memory_space=pl.ANY)


def head_window(head, width):
    low = head * width
    start = low // LANES * LANES
    size = LANES if low - start + width <= LANES else 2 * LANES
    return low, start, size


def head_mask(head, width):
    low, start, size = head_window(head, width)
    lane = lax.broadcasted_iota(jnp.int32, (1, size), 1) + start
    return jnp.where((lane >= low) & (lane < low + width), 1.0, 0.0).astype(BF16)


class Plan:
    def __init__(self, mesh, x, qkv_weight, fc1_weight):
        self.clip_axis = mesh.shape["clip"]
        self.frame_axis = mesh.shape["frame"]
        self.clips, self.local_frames, self.patches, self.width = x
        self.own_patches = self.patches // self.frame_axis
        self.halves = self.own_patches // 8
        self.frames = self.local_frames * self.frame_axis
        self.ff = fc1_weight[1]
        self.rows = self.clips * self.frames * self.own_patches
        self.clip_rows = self.rows // self.clips
        self.block = self.frames * 8
        self.blocks = self.rows // self.block
        self.piece = self.local_frames * 8
        self.head_width = self.width // HEADS
        self.chunk_dims = (self.clips, self.halves, self.local_frames, 8, self.width)
        self.zs = self.clip_axis // 2

    def row_of(self, clip, half, k):
        return ((clip * self.halves + half) * self.frame_axis + k) * self.piece


def fits(mesh, x, qkv_weight, fc1_weight):
    clip_axis, frame_axis = mesh.shape["clip"], mesh.shape["frame"]
    width, ff = x[3], fc1_weight[1]
    return (
        clip_axis == 8
        and frame_axis == 4
        and x[2] // frame_axis % 8 == 0
        and x[1] * frame_axis * 8 == LANES
        and width == 1152
        and ff == 4 * width
        and qkv_weight[1] == 3 * width
    )


def fold_tile(tile, folds, used):
    rows = tile.shape[0] // folds
    total = tile[:rows]
    for g in range(1, folds):
        total = total + pltpu.roll(tile[g * rows : (g + 1) * rows], g * used, 1)
    return total


MESH = pl.DeviceIdType.MESH


def unit_rows(ref, here):
    return unit(ref[here, :])


class Later:
    def __init__(self, make):
        self.make = make

    def start(self):
        self.make().start()

    def wait(self):
        self.make().wait()

    def wait_recv(self):
        self.make().wait_recv()

    def wait_send(self):
        self.make().wait_send()


REMOTE_SIZES = (4, 4, 8, 1, 4, 4, 4, 4, 1, 1, 4, 2, 2, 1, 1, 1, 1, 1, 1, 1, 1, 1, 2, 2, 2, 2, 2, 2, 2, 2, 1, 4, 4, 2, 2, 3, 4, 4)
(
    R_C2, R_C1, R_C0, R_CO, R_2AX, R_2BY, R_2AY, R_2BX, R_2Z, R_2ZZ, R_1Z, R_1AX, R_1BY, R_1AY, R_1BX, R_1ZZ, R_OAX, R_OBY, R_OAY, R_OBX, R_OZ, R_OZZ, R_0AX, R_0BY, R_0CZ, R_0AY, R_0BX, R_0CX, R_0ABZ, R_0CY, R_0ZZ, R_OUT, R_IN, R_SMX, R_SMY, R_SMC, R_XIN, R_CIN,
) = REMOTE_AT = tuple(sum(REMOTE_SIZES[:i]) for i in range(len(REMOTE_SIZES)))
LOCAL_SIZES = (4, 6, 6, 6, 6, 2, 1, 1, 1, 2, 1, 1, 4, 1, 4)
(
    L_W, L_A, L_B, L_C, L_D, L_S, L_MID, L_ATT, L_PROJ, L_PROBS, L_N1, L_CTX, L_OWN, L_ACT, L_ACTS,
) = LOCAL_AT = tuple(sum(LOCAL_SIZES[:i]) for i in range(len(LOCAL_SIZES)))
CORE, Z0, Z1, X, Y, XY = range(6)


LOAD, RUN, SEND = range(3)
TMP_A, TMP_B, TMP_C, TMP_D, TMP_S = range(5)
(J_C1, J_C2, J_Z0, J_XY1, J_XY2, J_1A, J_1B, J_1XY2, J_2Z, J_CO, J_O1, J_O2, J_OZ, J_C0, J_Q1, J_Q2, J_Q3, J_FIN2, J_FIN1, J_FINO, J_FIN0, J_SM1, J_SM2, J_SM3, J_SM4, J_SM5, J_MD1, J_MD2) = range(28)
(S_1AX, S_1BY, S_1AY, S_1BX, S_2Z, S_0ZZ, S_SMX, S_MDX, S_OUT, S_IN) = range(10)
P_A = tuple((0, k) for k in range(4))
P_B = tuple((1, k) for k in range(4))
P_C = tuple((2, k) for k in range(4))
P_D = tuple((3, k) for k in range(4))
P_E = tuple((4, k) for k in range(4))
P_G = tuple((5, k) for k in range(4))
P_AB = tuple((6, k) for k in range(4))
P_WQ = tuple((7, k) for k in range(8))
P_IN = tuple((9, k) for k in range(3))
P_M1, P_O, P_WO, P_DC, P_PK, P_INE = ((8, k) for k in range(6))
SCHEDULE = {
    P_E[0]: (
        (LOAD, J_C2, 0),
    ),
    P_A[1]: (
        (RUN, J_C2, 0),
        (LOAD, J_C1, 0),
    ),
    P_B[1]: (
        (RUN, J_C1, 0),
    ),
    P_D[1]: (
        (LOAD, J_C2, 1),
    ),
    P_E[1]: (
        (RUN, J_C2, 1),
    ),
    P_A[2]: (
        (LOAD, J_C1, 1),
        (LOAD, J_XY1, 0),
    ),
    P_B[2]: (
        (RUN, J_C1, 1),
    ),
    P_D[2]: (
        (RUN, J_XY1, 0),
    ),
    P_E[2]: (
        (LOAD, J_XY1, 1),
    ),
    P_A[3]: (
        (LOAD, J_C2, 2),
        (RUN, J_XY1, 1),
        (LOAD, J_C1, 2),
    ),
    P_B[3]: (
        (LOAD, J_Z0, 0),
        (RUN, J_C2, 2),
        (LOAD, J_XY2, 0),
    ),
    P_C[3]: (
        (RUN, J_C1, 2),
    ),
    P_D[3]: (
        (RUN, J_Z0, 0),
        (LOAD, J_C2, 3),
    ),
    P_E[3]: (
        (RUN, J_C2, 3),
        (RUN, J_XY2, 0),
    ),
    P_M1: (
        (LOAD, J_C1, 3),
        (LOAD, J_XY1, 2),
    ),
    P_WO: (
        (RUN, J_C1, 3),
        (LOAD, J_XY2, 1),
        (RUN, J_XY1, 2),
    ),
    P_DC: (
        (RUN, J_XY2, 1),
        (LOAD, J_XY1, 3),
    ),
    P_AB[0]: (
        (RUN, J_XY1, 3),
    ),
    P_AB[1]: (
        (LOAD, J_CO, 0),
    ),
    P_AB[2]: (
        (RUN, J_CO, 0),
        (LOAD, J_XY2, 2),
        (RUN, J_XY2, 2),
        (LOAD, J_XY2, 3),
    ),
    P_AB[3]: (
        (RUN, J_XY2, 3),
        (LOAD, J_Z0, 1),
    ),
    P_PK: (
        (RUN, J_Z0, 1),
        (SEND, S_1AX, 0),
    ),
    P_WQ[0]: (
        (LOAD, J_Z0, 2),
    ),
    P_WQ[1]: (
        (RUN, J_Z0, 2),
    ),
    P_WQ[2]: (
        (SEND, S_1BY, 0),
        (SEND, S_2Z, 0),
    ),
    P_WQ[4]: (
        (LOAD, J_Z0, 3),
    ),
    P_WQ[5]: (
        (RUN, J_Z0, 3),
        (SEND, S_1AX, 1),
        (SEND, S_1BY, 1),
    ),
    P_WQ[6]: (
        (LOAD, J_C0, 0),
    ),
    P_WQ[7]: (
        (LOAD, J_O1, 0),
        (RUN, J_O1, 0),
    ),
    P_IN[0]: (
        (LOAD, J_1A, 0),
        (RUN, J_1A, 0),
        (RUN, J_C0, 0),
    ),
    P_IN[1]: (
        (LOAD, J_1B, 0),
    ),
    P_IN[2]: (
        (RUN, J_1B, 0),
        (LOAD, J_C0, 1),
    ),
    P_INE: (
        (RUN, J_C0, 1),
        (SEND, S_SMX, 0),
    ),
    P_G[0]: (
        (LOAD, J_2Z, 0),
        (RUN, J_2Z, 0),
        (LOAD, J_1B, 1),
        (RUN, J_1B, 1),
    ),
    P_G[1]: (
        (SEND, S_1BX, 0),
        (LOAD, J_1A, 1),
    ),
    P_G[2]: (
        (RUN, J_1A, 1),
        (LOAD, J_O2, 0),
        (LOAD, J_SM1, 0),
        (LOAD, J_Q1, 0),
        (RUN, J_Q1, 0),
        (RUN, J_O2, 0),
        (RUN, J_SM1, 0),
        (SEND, S_1AY, 0),
        (LOAD, J_Q1, 1),
        (LOAD, J_SM2, 0),
        (RUN, J_SM2, 0),
        (LOAD, J_SM3, 0),
        (RUN, J_SM3, 0),
        (RUN, J_Q1, 1),
        (LOAD, J_OZ, 0),
    ),
    P_G[3]: (
        (LOAD, J_SM4, 0),
        (RUN, J_OZ, 0),
        (LOAD, J_Q2, 0),
        (RUN, J_SM4, 0),
        (RUN, J_Q2, 0),
        (LOAD, J_1XY2, 0),
    ),
    P_O: (
        (SEND, S_OUT, 3),
        (SEND, S_OUT, 1),
        (SEND, S_OUT, 2),
        (RUN, J_1XY2, 0),
        (LOAD, J_SM5, 0),
        (LOAD, J_Q2, 1),
        (RUN, J_Q2, 1),
        (LOAD, J_FINO, 0),
        (SEND, S_MDX, 0),
        (RUN, J_FINO, 0),
        (LOAD, J_FIN2, 0),
        (LOAD, J_Q3, 0),
        (RUN, J_Q3, 0),
        (LOAD, J_MD1, 0),
        (RUN, J_MD1, 0),
        (RUN, J_SM5, 0),
        (LOAD, J_Q3, 1),
        (RUN, J_FIN2, 0),
        (SEND, S_IN, 3),
        (SEND, S_IN, 1),
        (SEND, S_IN, 2),
        (RUN, J_Q3, 1),
        (SEND, S_0ZZ, 0),
        (LOAD, J_FIN1, 0),
        (RUN, J_FIN1, 0),
        (LOAD, J_MD2, 0),
        (LOAD, J_FIN0, 0),
        (RUN, J_MD2, 0),
        (RUN, J_FIN0, 0),
    ),
}
TMPS = {
    (J_1A, 0): TMP_C,
    (J_1A, 1): TMP_C,
    (J_1B, 0): TMP_C,
    (J_1B, 1): TMP_D,
    (J_1XY2, 0): TMP_D,
    (J_2Z, 0): TMP_C,
    (J_C1, 0): TMP_A,
    (J_C1, 1): TMP_A,
    (J_C1, 2): TMP_A,
    (J_C1, 3): TMP_A,
    (J_C2, 0): TMP_B,
    (J_C2, 1): TMP_B,
    (J_C2, 2): TMP_B,
    (J_C2, 3): TMP_B,
    (J_FIN0, 0): TMP_D,
    (J_FIN1, 0): TMP_D,
    (J_FIN2, 0): TMP_C,
    (J_FINO, 0): TMP_C,
    (J_O1, 0): TMP_C,
    (J_O2, 0): TMP_C,
    (J_OZ, 0): TMP_C,
    (J_Q1, 0): TMP_A,
    (J_Q1, 1): TMP_B,
    (J_Q2, 0): TMP_C,
    (J_Q2, 1): TMP_D,
    (J_Q3, 0): TMP_D,
    (J_Q3, 1): TMP_D,
    (J_XY1, 0): TMP_D,
    (J_XY1, 1): TMP_C,
    (J_XY1, 2): TMP_D,
    (J_XY1, 3): TMP_D,
    (J_XY2, 0): TMP_D,
    (J_XY2, 1): TMP_C,
    (J_XY2, 2): TMP_C,
    (J_XY2, 3): TMP_D,
    (J_Z0, 0): TMP_C,
    (J_Z0, 1): TMP_D,
    (J_Z0, 2): TMP_C,
    (J_Z0, 3): TMP_D,
}


def join_heads(width, head_parts, put):
    waiting = {}
    for h in range(HEADS):
        _, start, size = head_window(h, width)
        values = head_parts(h)
        for t in range(size // LANES):
            tiles = [value[:, t * LANES : (t + 1) * LANES] for value in values]
            j = start // LANES + t
            waiting[j] = [a + b for a, b in zip(waiting[j], tiles)] if j in waiting else tiles
        ahead = head_window(h + 1, width)[1] // LANES if h + 1 < HEADS else HEADS * width
        for j in sorted(waiting):
            if j < ahead:
                put(j, waiting.pop(j))


def whole_layer(plan, x, cotangent, modulation, counts, biases, qkv_weight, out_weight, fc1_weight, fc2_weight):
    n, rows, width, ff = plan.frame_axis, plan.rows, plan.width, plan.ff
    own, fl, clips = plan.own_patches, plan.local_frames, plan.clips
    span2, span1 = ff // plan.clip_axis, width // plan.clip_axis
    s1, s0, so = 9 * span1, 7 * span1, 2 * span1 + span1 // 3
    a1, a0 = 640, s0 // 3
    pad2, padq, wq = 384, 896, 3 * width // n
    blocks, block = plan.blocks, plan.block
    factor = plan.head_width ** (-0.5)
    half_rows = 64
    parts_per_clip = plan.clip_rows // half_rows

    def body(*refs):
        refs = list(refs)

        def take(count):
            got = refs[:count]
            del refs[:count]
            return got

        (x_h, cot_h, wqkv_h, wout_h, fc1_h, fc2_h, raw_mod, counts_ref, qv_bias, out_bias, fc1_bias, fc2_bias) = take(12)
        (out_h, in_h) = take(2)
        sum2, sum1, sum0, sumo, small = take(5)
        (rc2, rc1, rc0, rco, r2ax, r2by, r2ay, r2bx, r2z, r2zz) = take(10)
        (r1z, r1ax, r1by, r1ay, r1bx, r1zz) = take(6)
        (roax, roby, roay, robx, roz, rozz) = take(6)
        (r0ax, r0by, r0cz, r0ay, r0bx, r0cx, r0abz, r0cy, r0zz, rsm, rsmc) = take(11)
        (n1_h, ctx_h, proj_h, probs_h, att_h, mid_h, act_h) = take(7)
        (keep2, keep1, keepo, r2, stage, tmp_a, tmp_b, tmp_c, tmp_d, dres, acc, f1, f2, ring, rows_out, sm, sm_b, sm_t, smc) = take(19)
        (xin, cin, mod, bias, allowed, valid) = take(6)
        send_sem, recv_sem, local_sem = take(3)

        frame, clip = lax.axis_index("frame"), lax.axis_index("clip")
        mx, my = frame % 2, frame // 2
        core, z0, z1 = clip % 2, clip // 2 % 2, clip // 4
        partner = (
            ("clip", clip + 1 - 2 * core),
            ("clip", clip + 2 - 4 * z0),
            ("clip", clip + 4 - 8 * z1),
            ("frame", frame + 1 - 2 * mx),
            ("frame", frame + 2 - 4 * my),
            ("frame", n - 1 - frame),
        )

        def remote(name, index, src, dst, bit):
            axis, where = partner[bit]
            at = name + index
            return Later(
                lambda: pltpu.make_async_remote_copy(
                    src_ref=src,
                    dst_ref=dst,
                    send_sem=send_sem.at[at],
                    recv_sem=recv_sem.at[at],
                    device_id={axis: where},
                    device_id_type=MESH,
                )
            )

        def local(name, index, src, dst):
            return Later(lambda: pltpu.make_async_copy(src, dst, local_sem.at[name + index]))

        lo1, hi1 = pl.ds(0, a1), pl.ds(a1, s1 - a1)
        pa, pb, pc, pab, all0 = pl.ds(0, a0), pl.ds(a0, a0), pl.ds(2 * a0, a0), pl.ds(0, 2 * a0), pl.ds(0, s0)
        oa, ob, oab = pl.ds(0, so), pl.ds(so, so), pl.ds(0, 2 * so)
        all1 = pl.ds(0, s1)

        def c2(z):
            return remote(R_C2, z, stage.at[0, :, :, all1], rc2.at[z], CORE)

        def c1(f):
            return remote(R_C1, f, stage.at[1, :, :, all1], rc1.at[f], CORE)

        def c0(j, f):
            return remote(R_C0, 4 * j + f, stage.at[:, f // 2, f % 2, all0], rc0.at[j, :, f // 2, f % 2], CORE)

        def co():
            return remote(R_CO, 0, stage.at[:, :, :, oab], rco, CORE)

        def t2ax(z):
            return remote(R_2AX, z, keep2.at[z // 2, z % 2, :, 1 - mx, lo1], r2ax.at[z], X)

        def t2by(z):
            return remote(R_2BY, z, keep2.at[z // 2, z % 2, 1 - my, :, hi1], r2by.at[z], Y)

        def t2ay(z):
            return remote(R_2AY, z, keep2.at[z // 2, z % 2, 1 - my, mx, lo1], r2ay.at[z], Y)

        def t2bx(z):
            return remote(R_2BX, z, keep2.at[z // 2, z % 2, my, 1 - mx, hi1], r2bx.at[z], X)

        def t2z():
            return remote(R_2Z, 0, r2.at[:, 1 - z0], r2z, Z0)

        def t2zz():
            return remote(R_2ZZ, 0, r2.at[1 - z1, z0], r2zz, Z1)

        def t1z(f):
            return remote(R_1Z, f, keep1.at[f // 2, f % 2, :, 1 - z0], r1z.at[f], Z0)

        def t1ax(y):
            return remote(R_1AX, y, keep1.at[y, 1 - mx, :, z0, lo1], r1ax.at[y], X)

        def t1by(x):
            return remote(R_1BY, x, keep1.at[1 - my, x, :, z0, hi1], r1by.at[x], Y)

        def t1ay():
            return remote(R_1AY, 0, keep1.at[1 - my, mx, :, z0, lo1], r1ay, Y)

        def t1bx():
            return remote(R_1BX, 0, keep1.at[my, 1 - mx, :, z0, hi1], r1bx, X)

        def t1zz():
            return remote(R_1ZZ, 0, keep1.at[my, mx, 1 - z1, z0], r1zz, Z1)

        def toax():
            return remote(R_OAX, 0, keepo.at[:, :, 1 - mx, oa], roax, X)

        def toby():
            return remote(R_OBY, 0, keepo.at[:, 1 - my, :, ob], roby, Y)

        def toay():
            return remote(R_OAY, 0, keepo.at[:, 1 - my, mx, oa], roay, Y)

        def tobx():
            return remote(R_OBX, 0, keepo.at[:, my, 1 - mx, ob], robx, X)

        def toz():
            return remote(R_OZ, 0, keepo.at[1 - z0, my, mx], roz, Z0)

        def tozz():
            there = pl.ds(pl.multiple_of((1 - z1) * so, 16), so)
            return remote(R_OZZ, 0, keepo.at[z0, my, mx, there], rozz, Z1)

        def t0ax(j):
            return remote(R_0AX, j, keep2.at[j, :, :, 1 - mx, pa], r0ax.at[j], X)

        def t0by(j):
            return remote(R_0BY, j, keep2.at[j, :, 1 - my, :, pb], r0by.at[j], Y)

        def t0cz(j):
            return remote(R_0CZ, j, keep2.at[j, 1 - z0, :, :, pc], r0cz.at[j], Z0)

        def t0ay(j):
            return remote(R_0AY, j, keep2.at[j, :, 1 - my, mx, pa], r0ay.at[j], Y)

        def t0bx(j):
            return remote(R_0BX, j, keep2.at[j, :, my, 1 - mx, pb], r0bx.at[j], X)

        def t0cx(j):
            return remote(R_0CX, j, keep2.at[j, z0, :, 1 - mx, pc], r0cx.at[j], X)

        def t0abz(j):
            return remote(R_0ABZ, j, keep2.at[j, 1 - z0, my, mx, pab], r0abz.at[j], Z0)

        def t0cy(j):
            return remote(R_0CY, j, keep2.at[j, z0, 1 - my, mx, pc], r0cy.at[j], Y)

        def t0zz():
            return remote(R_0ZZ, 0, keep2.at[1 - z1, z0, my, mx, all0], r0zz, Z1)

        def row_send(name, k, dst, arriving=False):
            bit = (None, X, Y, XY)[k]
            place = partner[bit][1] if arriving else frame
            src = rows_out if name == R_IN else cin
            return remote(name, k, src.at[k], dst.at[:, :, pl.ds(place * own, own)], bit)

        def row_own(index, src, dst):
            return local(L_OWN, index, src.at[0], dst.at[:, :, pl.ds(frame * own, own)])

        def smx_send():
            return remote(R_SMX, 0, sm.at[0], rsm.at[0, 0], X)

        def smy_send():
            return remote(R_SMY, 0, sm_b.at[0], rsm.at[1, 0], Y)

        def mdx_send():
            return remote(R_SMX, 1, sm.at[pl.ds(1, clips)], rsm.at[0, pl.ds(1, clips)], X)

        def mdy_send():
            return remote(R_SMY, 1, sm_b.at[pl.ds(1, clips)], rsm.at[1, pl.ds(1, clips)], Y)

        def smc_send(i):
            return remote(R_SMC, i, smc.at[i], rsmc.at[i], (CORE, Z0, Z1)[i])

        def add_to(ref, at, other, other_at):
            ref[at] = ref[at] + other[other_at]

        def add_chunks(ref, at, other, other_at, count):
            for i in range(2):
                for k in range(2 if count == 2 else 1):
                    fill = iter((i, k))
                    here = tuple(next(fill) if p is None else p for p in at)
                    fill = iter((i, k))
                    there = tuple(next(fill) if p is None else p for p in other_at)
                    add_to(ref, here, other, there)

        def pump(arrivals, copies, work, sends):
            def load():
                for transfer in arrivals:
                    transfer.wait_recv()
                for copy in copies:
                    copy.start()

            def run():
                for copy in copies:
                    copy.wait()
                work()
                for transfer in sends:
                    transfer.start()

            return load, run

        def job(kind, index, tmps):
            tmp = (tmp_a, tmp_b, tmp_c, tmp_d, None)[tmps]
            sem = (L_A, L_B, L_C, L_D, L_S)[tmps]
            pair = (index // 2, index % 2)
            if kind == J_C1:

                def work():
                    add_chunks(keep1, pair + (None, None), tmp, (None, None, all1), 2)

                return pump([c1(index)], [local(sem, 0, rc1.at[index], tmp.at[:, :, all1])], work, [t1z(index)])
            if kind == J_C2:

                def work():
                    add_chunks(keep2, pair + (None, None, all1), tmp, (None, None, all1), 2)

                sends = [t2ax(index), t2by(index)]
                return pump([c2(index)], [local(sem, 0, rc2.at[index], tmp.at[:, :, all1])], work, sends)
            if kind == J_Z0:

                def work():
                    add_chunks(keep1, pair + (None, z0), tmp, (None, all1), 1)

                return pump([t1z(index)], [local(sem, 0, r1z.at[index], tmp.at[:, all1])], work, [])
            if kind == J_XY1:

                def work():
                    add_chunks(keep2, pair + (None, mx, lo1), tmp, (None, lo1), 1)
                    add_chunks(keep2, pair + (my, None, hi1), tmp, (None, hi1), 1)

                copies = [
                    local(sem, 0, r2ax.at[index], tmp.at[:, lo1]),
                    local(sem, 1, r2by.at[index], tmp.at[:, hi1]),
                ]
                return pump([t2ax(index), t2by(index)], copies, work, [t2ay(index), t2bx(index)])
            if kind == J_XY2:

                def work():
                    r2[pair] = keep2[pair + (my, mx, all1)] + tmp[0, all1]

                copies = [
                    local(sem, 0, r2ay.at[index], tmp.at[0, lo1]),
                    local(sem, 1, r2bx.at[index], tmp.at[0, hi1]),
                ]
                return pump([t2ay(index), t2bx(index)], copies, work, [])
            if kind == J_1A:

                def work():
                    add_chunks(keep1, (index, mx, None, z0, lo1), tmp, (None, lo1), 1)

                return pump([t1ax(index)], [local(sem, 0, r1ax.at[index], tmp.at[:, lo1])], work, [])
            if kind == J_1B:

                def work():
                    add_chunks(keep1, (my, index, None, z0, hi1), tmp, (None, hi1), 1)

                return pump([t1by(index)], [local(sem, 0, r1by.at[index], tmp.at[:, hi1])], work, [])
            if kind == J_1XY2:

                def work():
                    add_chunks(keep1, (my, mx, None, z0, all1), tmp, (None, all1), 1)

                copies = [local(sem, 0, r1ay, tmp.at[:, lo1]), local(sem, 1, r1bx, tmp.at[:, hi1])]
                return pump([t1ay(), t1bx()], copies, work, [t1zz()])
            if kind == J_2Z:

                def work():
                    add_chunks(r2, (None, z0), tmp, (None, all1), 1)

                return pump([t2z()], [local(sem, 0, r2z, tmp.at[:, all1])], work, [t2zz()])
            if kind == J_CO:

                def work():
                    add_chunks(keepo, (0, None, None), tmp_a, (None, None, oab), 2)
                    add_chunks(keepo, (1, None, None), tmp_b, (None, None, oab), 2)

                copies = [
                    local(L_A, 0, rco.at[0], tmp_a.at[:, :, oab]),
                    local(L_B, 0, rco.at[1], tmp_b.at[:, :, oab]),
                ]
                return pump([co()], copies, work, [toax(), toby()])
            if kind == J_O1:

                def work():
                    for i in range(2):
                        add_chunks(keepo, (i, None, mx, oa), tmp, (None, pl.ds(i * so, so)), 1)
                        add_chunks(keepo, (i, my, None, ob), tmp, (None, pl.ds((2 + i) * so, so)), 1)

                copies = [local(sem, i, roax.at[i], tmp.at[:, pl.ds(i * so, so)]) for i in range(2)]
                copies += [local(sem, 2 + i, roby.at[i], tmp.at[:, pl.ds((2 + i) * so, so)]) for i in range(2)]
                return pump([toax(), toby()], copies, work, [toay(), tobx()])
            if kind == J_O2:

                def work():
                    add_chunks(keepo, (None, my, mx, oab), tmp, (None, oab), 1)

                copies = [local(sem, 0, roay, tmp.at[:, oa]), local(sem, 1, robx, tmp.at[:, ob])]
                return pump([toay(), tobx()], copies, work, [toz()])
            if kind == J_OZ:

                def work():
                    add_to(keepo, (z0, my, mx), tmp, (0, oab))

                return pump([toz()], [local(sem, 0, roz, tmp.at[0, oab])], work, [tozz()])
            if kind == J_C0:

                def work():
                    add_chunks(keep2, (index, 0, None, None, all0), tmp_a, (None, None, all0), 2)
                    add_chunks(keep2, (index, 1, None, None, all0), tmp_b, (None, None, all0), 2)

                copies = [
                    local(L_A, 0, rc0.at[index, 0], tmp_a.at[:, :, all0]),
                    local(L_B, 0, rc0.at[index, 1], tmp_b.at[:, :, all0]),
                ]
                sends = [t0ax(index), t0by(index), t0cz(index)]
                return pump([c0(index, f) for f in range(n)], copies, work, sends)
            if kind == J_Q1:

                def work():
                    add_chunks(keep2, (index, None, None, mx, pa), tmp, (None, None, pa), 2)
                    add_chunks(keep2, (index, None, my, None, pb), tmp, (None, None, pb), 2)
                    add_chunks(keep2, (index, z0, None, None, pc), tmp, (None, None, pc), 2)

                copies = [
                    local(sem, i, r.at[index], tmp.at[:, :, p])
                    for i, (r, p) in enumerate(((r0ax, pa), (r0by, pb), (r0cz, pc)))
                ]
                arrivals = [t0ax(index), t0by(index), t0cz(index)]
                return pump(arrivals, copies, work, [t0ay(index), t0bx(index), t0cx(index)])
            if kind == J_Q2:

                def work():
                    add_chunks(keep2, (index, None, my, mx, pab), tmp, (None, pab), 1)
                    add_chunks(keep2, (index, z0, None, mx, pc), tmp, (None, pc), 1)

                copies = [
                    local(sem, i, r.at[index], tmp.at[:, p])
                    for i, (r, p) in enumerate(((r0ay, pa), (r0bx, pb), (r0cx, pc)))
                ]
                return pump([t0ay(index), t0bx(index), t0cx(index)], copies, work, [t0abz(index), t0cy(index)])
            if kind == J_Q3:

                def work():
                    add_to(keep2, (index, z0, my, mx, all0), tmp, (0, all0))

                copies = [local(sem, 0, r0abz.at[index], tmp.at[0, pab]), local(sem, 1, r0cy.at[index], tmp.at[0, pc])]
                return pump([t0abz(index), t0cy(index)], copies, work, [])
            if kind == J_FIN2:

                def work():
                    sum2[...] = r2[z1, z0].astype(F32) + tmp[0, all1].astype(F32)

                return pump([t2zz()], [local(sem, 0, r2zz, tmp.at[0, all1])], work, [])
            if kind == J_FIN1:

                def work():
                    sum1[...] = keep1[my, mx, z1, z0].astype(F32) + tmp[0, all1].astype(F32)

                return pump([t1zz()], [local(sem, 0, r1zz, tmp.at[0, all1])], work, [])
            if kind == J_FINO:

                def work():
                    here = pl.ds(pl.multiple_of(z1 * so, 16), so)
                    sumo[...] = keepo[z0, my, mx, here].astype(F32) + tmp[0, oa].astype(F32)

                return pump([tozz()], [local(sem, 0, rozz, tmp.at[0, oa])], work, [])
            if kind == J_FIN0:

                def work():
                    sum0[...] = keep2[z1, z0, my, mx, all0].astype(F32) + tmp[0, all0].astype(F32)

                return pump([t0zz()], [local(sem, 0, r0zz, tmp.at[0, all0])], work, [])
            if kind == J_SM1:

                def work():
                    sm_b[0] = sm[0] + sm_t[0]

                return pump([smx_send()], [local(L_S, 0, rsm.at[0, 0], sm_t.at[0])], work, [smy_send()])
            if kind == J_SM2:

                def work():
                    smc[0] = sm_b[0] + sm_t[0]

                return pump([smy_send()], [local(L_S, 0, rsm.at[1, 0], sm_t.at[0])], work, [smc_send(0)])
            if kind in (J_MD1, J_MD2):
                step, some = kind - J_MD1, pl.ds(1, clips)
                arrival, sends = (mdx_send, [mdy_send()]) if step == 0 else (mdy_send, [])
                source, result = (sm, sm_b) if step == 0 else (sm_b, small)

                def work():
                    result[some] = source[some] + sm_t[some]

                return pump([arrival()], [local(L_S, 1, rsm.at[step, some], sm_t.at[some])], work, sends)
            step = kind - J_SM3

            def work():
                if step < 2:
                    smc[step + 1] = smc[step] + sm_t[0]
                else:
                    small[0] = smc[step] + sm_t[0]

            sends = [smc_send(step + 1)] if step < 2 else []
            return pump([smc_send(step)], [local(L_S, 0, rsmc.at[step], sm_t.at[0])], work, sends)

        plain_sends = {
            S_1AX: t1ax,
            S_1BY: t1by,
            S_1AY: lambda _: t1ay(),
            S_1BX: lambda _: t1bx(),
            S_2Z: lambda _: t2z(),
            S_0ZZ: lambda _: t0zz(),
            S_SMX: lambda _: smx_send(),
            S_MDX: lambda _: mdx_send(),
            S_OUT: lambda k: row_send(R_OUT, k, out_h),
            S_IN: lambda k: row_send(R_IN, k, in_h),
        }

        def do(point):
            for what, kind, index in SCHEDULE.get(point, ()):
                if what == SEND:
                    plain_sends[kind](index).start()
                else:
                    job(kind, index, TMPS.get((kind, index), TMP_S))[what]()

        def do_in(points, index):
            for k, point in enumerate(points):
                if point in SCHEDULE:
                    pl.when(index == k)(lambda point=point: do(point))

        def weight(slot, src):
            return local(L_W, slot, src, ring.at[slot])

        def fc1_block(f):
            return weight(2 * (f % 2), fc1_h.at[:, pl.ds(pl.multiple_of(f * width, LANES), width)])

        def fc2_block(f):
            return weight(2 * (f % 2) + 1, fc2_h.at[pl.ds(pl.multiple_of(f * width, 16), width)])

        def fc2_block_at(f):
            return local(L_W, f, fc2_h.at[pl.ds(pl.multiple_of(f * width, 16), width)], ring.at[f])

        def qkv_block(i, slot):
            return weight(slot, wqkv_h.at[:, i * width : (i + 1) * width])

        def own_copies(src, dst, name):
            return local(name, 0, src, dst)

        def piece_of(ref, k, c, half):
            return ref[k, c, :, half * 8 : half * 8 + 8, :].astype(F32).reshape(plan.piece, width)

        def rows_at(c, half, k):
            return pl.ds(pl.multiple_of(c * plan.clip_rows + plan.row_of(0, half, k), 8), plan.piece)

        def arrive(name, k, src, dst):
            bit = (None, X, Y, XY)[k]
            return remote(name, k, src.at[:, :, pl.ds(partner[bit][1] * own, own)], dst.at[k], bit)

        barrier = pltpu.get_barrier_semaphore()
        for axis, where in partner:
            pl.semaphore_signal(barrier, inc=1, device_id={axis: where}, device_id_type=MESH)
        mine = pl.ds(frame * own, own)
        own_x = local(L_OWN, 2, x_h.at[:, :, mine], xin.at[0])
        own_x.start()
        for i in range(3):
            qkv_block(i, i).start()
        weight(3, wout_h).start()
        pl.semaphore_wait(barrier, len(partner))
        for k in (3, 1, 2):
            arrive(R_XIN, k, x_h, xin).start()
        sm[...] = jnp.zeros_like(sm)
        for i in range(6):
            values = raw_mod[:, i * width : (i + 1) * width].astype(F32)
            for c in range(clips):
                mod[c, i : i + 1, :] = values[c : c + 1, :]
        parts = [(qv_bias, 0), None, (qv_bias, 1), (out_bias, 0)] + [(fc1_bias, f) for f in range(n)] + [(fc2_bias, 0)]
        for i, part in enumerate(parts):
            if part is None:
                bias[i] = jnp.zeros((1, width), F32)
            else:
                bias[i] = part[0][pl.ds(part[1] * width, width)].astype(F32).reshape(1, width)

        def frame_of(axis):
            slot = lax.broadcasted_iota(jnp.int32, (block, block), axis) // 8
            k, local_frame = slot // fl, slot % fl
            low, high = k % 2, k // 2
            source = low + mx - 2 * low * mx + 2 * (high + my - 2 * high * my)
            return source * fl + local_frame

        lane_patch = lax.broadcasted_iota(jnp.int32, (block, block), 1) % 8
        row_patch = lax.broadcasted_iota(jnp.int32, (block, block), 0) % 8
        row_frame, lane_frame = frame_of(0), frame_of(1)
        for c in range(clips):
            count = counts_ref[c]
            valid[c] = jnp.where(row_frame < count, 1.0, 0.0)
            allowed[c] = jnp.where((lane_patch == row_patch) & (lane_frame < count), 0.0, NEGATIVE)

        def first_half(n1, proj, ctx, scores, lows, probs, n2):
            own_x.wait()

            @pl.loop(0, clips)
            def _(c):
                shift, scale = mod[c, 0:1, :], 1.0 + mod[c, 1:2, :]
                for half in range(plan.halves):
                    for k in range(n):
                        normed, _ = unit(piece_of(xin, k, c, half))
                        n1[rows_at(c, half, k), :] = (normed * scale + shift).astype(BF16)

            own_copies(n1, n1_h, L_N1).start()

            @pl.loop(0, 3)
            def _(i):
                local(L_W, i, fc2_h.at[pl.ds(0, width)], ring.at[i]).wait()
                proj[i] = (mm(n1[...], ring[i]) + bias[i]).astype(BF16)

            fc1_block(0).start()
            fc2_block(0).start()
            own_copies(proj, proj_h, L_PROJ).start()

            @pl.loop(0, blocks)
            def _(b):
                slot = b % 2
                here = pl.ds(pl.multiple_of(b * block, block), block)

                @pl.when(b >= 2)
                def _():
                    local(L_PROBS, slot, probs.at[slot], probs_h.at[b - 2]).wait()

                for h in range(HEADS):
                    _, start, size = head_window(h, plan.head_width)
                    cols = slice(start, start + size)
                    q = proj[0, here, cols] * head_mask(h, plan.head_width)
                    scores[h] = mm_cols(q, proj[1, here, cols]) * factor + allowed[b // plan.halves]
                for h in range(HEADS):
                    score = scores[h]
                    grown = jnp.exp(score - jnp.max(score, axis=-1, keepdims=True))
                    weights = grown * (1.0 / jnp.sum(grown, axis=-1, keepdims=True))
                    probs[slot, h] = weights
                    lows[h] = weights.astype(BF16)

                def head_context(h):
                    _, start, size = head_window(h, plan.head_width)
                    return [mm(lows[h], proj[2, here, start : start + size] * head_mask(h, plan.head_width))]

                def put_context(j, tiles):
                    ctx[here, j * LANES : (j + 1) * LANES] = tiles[0].astype(BF16)

                join_heads(plan.head_width, head_context, put_context)
                local(L_PROBS, slot, probs.at[slot], probs_h.at[b]).start()

            own_copies(ctx, ctx_h, L_CTX).start()
            weight(3, wout_h).wait()
            f1[...] = mm(ctx[...], ring[3]) + bias[3]
            own_copies(f1, att_h, L_ATT).start()

            @pl.loop(0, clips)
            def _(c):
                for half in range(plan.halves):
                    for k in range(n):
                        here = rows_at(c, half, k)
                        middle = piece_of(xin, k, c, half) + mod[c, 2:3, :] * f1[here, :]
                        f2[here, :] = middle
                        normed, _ = unit(middle)
                        n2[here, :] = (normed * (1.0 + mod[c, 4:5, :]) + mod[c, 3:4, :]).astype(BF16)

            own_copies(f2, mid_h, L_MID).start()
            own_copies(n1, n1_h, L_N1).wait()
            own_copies(proj, proj_h, L_PROJ).wait()
            own_copies(ctx, ctx_h, L_CTX).wait()
            for b in (blocks - 2, blocks - 1):
                local(L_PROBS, b % 2, probs.at[b % 2], probs_h.at[b]).wait()

        def mlp(n2, cin, own_cot, n2_turned, dbr, padded, act, act_turned, dh, res):
            padded[...] = jnp.zeros_like(padded)
            n2_turned[...] = n2[...].T
            acc[...] = jnp.zeros_like(acc)
            own_cot.wait()
            for k in (1, 2, 3):
                arrive(R_CIN, k, cot_h, cin).wait_recv()

            @pl.loop(0, clips)
            def _(c):
                for half in range(plan.halves):
                    for k in range(n):
                        here = rows_at(c, half, k)
                        piece = piece_of(cin, k, c, half) * valid[c, k * plan.piece : (k + 1) * plan.piece, 0:1]
                        dres[here, :] = piece.astype(BF16)
                        low = (piece * mod[c, 5:6, :]).astype(BF16)
                        dbr[here, :] = low
                        sm[0, 7:8, :] += jnp.sum(low.astype(F32), axis=0, keepdims=True)

            for f in range(n):
                padded[:, f * pad2 : f * pad2 + width // n] = dbr[:, f * (width // n) : (f + 1) * (width // n)]
            own_copies(f1, att_h, L_ATT).wait()
            own_copies(f2, mid_h, L_MID).wait()

            @pl.loop(0, n)
            def _(f):
                slot = 2 * (f % 2)

                @pl.when(f < n - 1)
                def _():
                    fc1_block(f + 1).start()
                    fc2_block(f + 1).start()

                @pl.when(f == n - 1)
                def _():
                    weight(0, wout_h).start()
                    qkv_block(0, 1).start()

                fc1_block(f).wait()
                f2[...] = mm(n2[...], ring[slot])
                first_bias = bias[4 + f]

                @pl.when(f >= 1)
                def _():
                    local(L_ACT, 0, act, act_h.at[f - 1]).wait()

                @pl.loop(0, rows // half_rows)
                def _(i):
                    here = pl.ds(pl.multiple_of(i * half_rows, half_rows), half_rows)
                    hidden = f2[here, :] + first_bias
                    square = hidden * hidden
                    bent = jnp.tanh(0.7978845608028654 * hidden * (1.0 + 0.044715 * square))
                    act[here, :] = (0.5 * hidden * (1.0 + bent)).astype(BF16)
                    slope = 0.7978845608028654 * (1.0 + 3.0 * 0.044715 * square)
                    f2[here, :] = 0.5 * (1.0 + bent) + 0.5 * hidden * (1.0 - bent * bent) * slope

                local(L_ACT, 0, act, act_h.at[f]).start()

                do_in(P_A, f)

                @pl.when(f >= 1)
                def _():
                    c1(f - 1).wait_send()
                    c2(f - 1).wait_send()

                act_turned[...] = act[...].T
                @pl.loop(0, 2)
                def _(i):
                    lanes = pl.ds(pl.multiple_of(i * 2 * pad2, LANES), 2 * pad2)
                    res[...] = mm(act_turned[...], padded[:, lanes])
                    for mine in (False, True):
                        part = core if mine else 1 - core
                        at = pl.ds(pl.multiple_of(part * span2, 8), span2)
                        for j in range(2):
                            pieces = [res[at, j * pad2 + t * LANES : j * pad2 + (t + 1) * LANES] for t in range(3)]
                            pieces[2] = fold_tile(pieces[2], 4, 32)
                            row = 0
                            for piece in pieces:
                                slab = slice(row, row + piece.shape[0])
                                if mine:
                                    keep2[f // 2, f % 2, i, j, slab, :] = piece.astype(BF16)
                                else:
                                    stage[0, i, j, slab, :] = piece.astype(BF16)
                                row += piece.shape[0]

                c2(f).start()
                do_in(P_B, f)

                fc2_block(f).wait()
                dh[...] = (mm_cols(dbr[...], ring[slot + 1]) * f2[...]).astype(BF16)
                sm[0, pl.ds(3 + f, 1), :] = jnp.sum(dh[...].astype(F32), axis=0, keepdims=True)

                do_in(P_C, f)

                for first, tiles in ((0, 5), (5, 4)):
                    lanes = slice(first * LANES, (first + tiles) * LANES)
                    res[:, : tiles * LANES] = mm(n2_turned[...], dh[:, lanes])
                    for mine in (False, True):
                        part = core if mine else 1 - core
                        for i in range(2):
                            for j in range(2):
                                at = pl.ds(pl.multiple_of((4 * i + 2 * j + part) * span1, 8), span1)
                                for t in range(tiles):
                                    slab = slice((first + t) * span1, (first + t + 1) * span1)
                                    values = res[at, t * LANES : (t + 1) * LANES].astype(BF16)
                                    if mine:
                                        keep1[f // 2, f % 2, i, j, slab, :] = values
                                    else:
                                        stage[1, i, j, slab, :] = values
                c1(f).start()

                do_in(P_D, f)
                acc[...] += mm_cols(dh[...], ring[slot])
                do_in(P_E, f)

            local(L_ACT, 0, act, act_h.at[n - 1]).wait()

        def two_halves(n2):
            own_cot = local(L_OWN, 3, cot_h.at[:, :, mine], cin.at[0])
            own_cot.start()
            for k in (1, 2, 3):
                arrive(R_XIN, k, x_h, xin).wait_recv()
            for k in (3, 1, 2):
                arrive(R_CIN, k, cot_h, cin).start()
            pl.run_scoped(
                functools.partial(first_half, n2=n2),
                pltpu.VMEM((rows, width), BF16),
                pltpu.VMEM((3, rows, width), BF16),
                pltpu.VMEM((rows, width), BF16),
                pltpu.VMEM((HEADS, block, block), F32),
                pltpu.VMEM((HEADS, block, block), BF16),
                pltpu.VMEM((2, HEADS, block, block), F32),
            )
            pl.run_scoped(
                functools.partial(mlp, n2, cin, own_cot),
                pltpu.VMEM((width, rows), BF16),
                pltpu.VMEM((rows, width), BF16),
                pltpu.VMEM((rows, n * pad2), BF16),
                pltpu.VMEM((rows, width), BF16),
                pltpu.VMEM((width, rows), BF16),
                pltpu.VMEM((rows, width), BF16),
                pltpu.VMEM((width, 2 * pad2), F32),
            )

        pl.run_scoped(two_halves, pltpu.VMEM((rows, width), BF16))

        def rest(datt, proj):
            own_copies(mid_h, f2, L_MID).start()
            own_copies(proj_h, proj, L_PROJ).start()
            qkv_block(1, 3).start()
            own_copies(ctx_h, ring.at[2, :rows], L_CTX).start()

            def attend(dctx, probs, scores, lows):
                def middle(att):
                    own_copies(att_h, att, L_ATT).start()
                    own_copies(mid_h, f2, L_MID).wait()
                    own_copies(att_h, att, L_ATT).wait()

                    @pl.loop(0, rows // half_rows)
                    def _(i):
                        here = pl.ds(pl.multiple_of(i * half_rows, half_rows), half_rows)
                        c = i // parts_per_clip
                        normed, inverse = unit_rows(f2, here)
                        grad = acc[here, :]
                        sm[1 + c, 3:4, :] += jnp.sum(grad, axis=0, keepdims=True)
                        sm[1 + c, 4:5, :] += jnp.sum(grad * normed, axis=0, keepdims=True)
                        d_middle = dres[here, :].astype(F32) + unit_back(normed, inverse, grad * (1.0 + mod[c, 4:5, :]))
                        acc[here, :] = d_middle
                        sm[1 + c, 2:3, :] += jnp.sum(d_middle * att[here, :], axis=0, keepdims=True)
                        low = (d_middle * mod[c, 2:3, :]).astype(BF16)
                        datt[here, :] = low
                        sm[0, 2:3, :] += jnp.sum(low.astype(F32), axis=0, keepdims=True)

                pl.run_scoped(middle, pltpu.VMEM((rows, width), F32))
                do(P_M1)
                local(L_PROBS, 0, probs_h.at[0], probs.at[0]).start()

                c1(3).wait_send()
                c2(3).wait_send()

                def out_grad(right_o, res):
                    wide = width // n
                    right_o[...] = jnp.zeros_like(right_o)
                    for f in range(n):
                        right_o[f, :, :wide] = datt[:, f * wide : (f + 1) * wide]
                    own_copies(ctx_h, ring.at[2, :rows], L_CTX).wait()
                    turned = ring[2, :rows, :].T
                    ring[2, :, rows : 2 * rows] = turned

                    @pl.loop(0, n)
                    def _(f):
                        res[...] = mm(ring[2, :, rows : 2 * rows], right_o[f])
                        for mine in (False, True):
                            part = core if mine else 1 - core
                            for i in range(2):
                                for j in range(2):
                                    at = pl.ds(pl.multiple_of((4 * i + 2 * j + part) * span1, 8), span1)
                                    pieces = [res[at, t * LANES : (t + 1) * LANES] for t in range(3)]
                                    pieces[2] = fold_tile(pieces[2], 3, 32)
                                    row = i * so
                                    for piece in pieces:
                                        slab = slice(row, row + piece.shape[0])
                                        if mine:
                                            keepo[j, f // 2, f % 2, slab, :] = piece.astype(BF16)
                                        else:
                                            stage[j, f // 2, f % 2, slab, :] = piece.astype(BF16)
                                        row += piece.shape[0]

                pl.run_scoped(
                    out_grad, pltpu.VMEM((n, rows, pad2), BF16), pltpu.VMEM((width, pad2), F32)
                )
                co().start()
                do(P_WO)
                weight(0, wout_h).wait()
                dctx[...] = mm_cols(datt[...], ring[0]).astype(BF16)
                qkv_block(2, 0).start()
                do(P_DC)
                own_copies(proj_h, proj, L_PROJ).wait()

                @pl.loop(0, blocks)
                def _(b):
                    slot = b % 2
                    here = pl.ds(pl.multiple_of(b * block, block), block)

                    @pl.when(b < blocks - 1)
                    def _():
                        local(L_PROBS, 1 - slot, probs_h.at[b + 1], probs.at[1 - slot]).start()

                    local(L_PROBS, slot, probs_h.at[b], probs.at[slot]).wait()
                    for h in range(HEADS):
                        _, start, size = head_window(h, plan.head_width)
                        cols = slice(start, start + size)
                        scores[h] = mm_cols(dctx[here, cols] * head_mask(h, plan.head_width), proj[2, here, cols])
                    for h in range(HEADS):
                        weights = probs[slot, h]
                        mixed = weights * scores[h]
                        d_score = mixed - weights * jnp.sum(mixed, axis=-1, keepdims=True)
                        lows[0, h] = d_score.astype(BF16)
                        lows[1, h] = weights.astype(BF16)

                    def head_grads(h):
                        _, start, size = head_window(h, plan.head_width)
                        keep = head_mask(h, plan.head_width)
                        cols = slice(start, start + size)
                        return [
                            mm(lows[0, h], proj[1, here, cols] * keep),
                            mm_rows(lows[0, h], proj[0, here, cols] * keep),
                            mm_rows(lows[1, h], dctx[here, cols] * keep),
                        ]

                    def put_grads(j, tiles):
                        lanes = slice(j * LANES, (j + 1) * LANES)
                        for part in range(3):
                            values = tiles[part] if part == 2 else tiles[part] * factor
                            low = values.astype(BF16)
                            proj[part, here, lanes] = low
                            if part != 1:
                                at = part // 2
                                sm[0, at : at + 1, lanes] += jnp.sum(low.astype(F32), axis=0, keepdims=True)

                    join_heads(plan.head_width, head_grads, put_grads)

                    do_in(P_AB, b)

            pl.run_scoped(
                attend,
                pltpu.VMEM((rows, width), BF16),
                pltpu.VMEM((2, HEADS, block, block), F32),
                pltpu.VMEM((HEADS, block, block), F32),
                pltpu.VMEM((2, HEADS, block, block), BF16),
            )

            def weight_grads(right_q, left, res):
                own_copies(n1_h, left, L_N1).start()
                right_q[...] = jnp.zeros_like(right_q)
                for f in range(n):
                    low, high = f * wq, (f + 1) * wq
                    for part in range(3):
                        a, b = max(low, part * width), min(high, (part + 1) * width)
                        if a < b:
                            right_q[f, :, a - low : b - low] = proj[part, :, a - part * width : b - part * width]
                own_copies(n1_h, left, L_N1).wait()
                ring[2, :, :rows] = left[...].T
                do(P_PK)
                for z in range(4):
                    t2ax(z).wait_send()
                    t2by(z).wait_send()
                    t2ay(z).wait_send()
                    t2bx(z).wait_send()
                co().wait_send()

                @pl.loop(0, 2 * n)
                def _(step):
                    j, f = step // n, step % n
                    lines = pl.ds(pl.multiple_of(j * 4 * span1, 16), 4 * span1)

                    @pl.when(j == 1)
                    def _():
                        c0(0, f).wait_send()

                    res[...] = mm(ring[2, lines, :rows], right_q[f])
                    for mine in (False, True):
                        part = core if mine else 1 - core
                        for i in range(2):
                            at = pl.ds(pl.multiple_of((2 * i + part) * span1, 8), span1)
                            for t in range(padq // LANES):
                                slab = slice(t * span1, (t + 1) * span1)
                                piece = res[at, t * LANES : (t + 1) * LANES].astype(BF16)
                                if mine:
                                    keep2[j, i, f // 2, f % 2, slab, :] = piece
                                else:
                                    stage[i, f // 2, f % 2, slab, :] = piece
                    c0(j, f).start()
                    do_in(P_WQ, step)

            pl.run_scoped(
                weight_grads,
                pltpu.VMEM((n, rows, padq), BF16),
                pltpu.VMEM((rows, width), BF16),
                pltpu.VMEM((4 * span1, padq), F32),
            )

            f1[...] = jnp.zeros_like(f1)

            @pl.loop(0, 3)
            def _(i):
                slot = (2 * i + 1) % 5
                local(L_W, slot, fc2_h.at[pl.ds(0, width)], ring.at[slot]).wait()
                f1[...] += mm_cols(proj[i], ring[slot])
                do_in(P_IN, i)

            for f in range(n):
                weight(f, fc2_h.at[pl.ds(f * width, width)]).start()

            @pl.loop(0, clips)
            def _(c):
                for half in range(plan.halves):
                    for k in range(n):
                        here = rows_at(c, half, k)
                        normed, inverse = unit(piece_of(xin, k, c, half))
                        grad = f1[here, :]
                        sm[1 + c, 0:1, :] += jnp.sum(grad, axis=0, keepdims=True)
                        sm[1 + c, 1:2, :] += jnp.sum(grad * normed, axis=0, keepdims=True)
                        total = acc[here, :] + unit_back(normed, inverse, grad * (1.0 + mod[c, 1:2, :]))
                        rows_out[k, c, :, half * 8 : half * 8 + 8, :] = total.reshape(fl, 8, width).astype(BF16)

            row_own(1, rows_out, in_h).start()
            do(P_INE)

            def branch(acts):
                for f in range(n):
                    local(L_ACTS, f, act_h.at[f], acts.at[f]).start()
                f1[...] = jnp.zeros_like(f1)

                @pl.loop(0, n)
                def _(f):
                    local(L_ACTS, f, act_h.at[f], acts.at[f]).wait()
                    fc2_block_at(f).wait()
                    f1[...] += mm(acts[f], ring[f])
                    do_in(P_G, f)

            pl.run_scoped(branch, pltpu.VMEM((n, rows, width), BF16))

            @pl.loop(0, clips)
            def _(c):
                for half in range(plan.halves):
                    for k in range(n):
                        here = rows_at(c, half, k)
                        value = f1[here, :] + bias[8]
                        sm[1 + c, 5:6, :] += jnp.sum(dres[here, :].astype(F32) * value, axis=0, keepdims=True)
                        total = valid[c, k * plan.piece : (k + 1) * plan.piece, 0:1] * (
                            f2[here, :] + mod[c, 5:6, :] * value
                        )
                        cin[k, c, :, half * 8 : half * 8 + 8, :] = total.reshape(fl, 8, width).astype(BF16)

            row_own(0, cin, out_h).start()
            do(P_O)

            for k in (1, 2, 3):
                arrive(R_XIN, k, x_h, xin).wait_send()
                arrive(R_CIN, k, cot_h, cin).wait_send()
            row_own(1, rows_out, in_h).wait()
            row_own(0, cin, out_h).wait()
            for k in (1, 2, 3):
                row_send(R_OUT, k, out_h, True).wait_recv()
                row_send(R_IN, k, in_h, True).wait_recv()
                row_send(R_IN, k, in_h).wait_send()
                row_send(R_OUT, k, out_h).wait_send()
            for transfer in (smx_send, smy_send, mdx_send, mdy_send):
                transfer().wait_send()
            for i in range(3):
                smc_send(i).wait_send()
            for f in range(n):
                t1z(f).wait_send()
                c0(1, f).wait_send()
            for j in range(2):
                for transfer in (t1ax, t1by, t0ax, t0by, t0cz, t0ay, t0bx, t0cx, t0abz, t0cy):
                    transfer(j).wait_send()
            for transfer in (t2z, t2zz, t1ay, t1bx, t1zz, toax, toby, toay, tobx, toz, tozz, t0zz):
                transfer().wait_send()

        pl.run_scoped(rest, pltpu.VMEM((rows, width), BF16), pltpu.VMEM((3, rows, width), BF16))

    lanes = LANES
    image = shape((clips, fl, plan.patches, width), BF16)
    arriving = [
        (4, 2, 2, s1), (4, 2, 2, s1), (2, 2, 2, 2, s0), (2, 2, 2, 2 * so),
        (4, 2, a1), (4, 2, s1 - a1), (4, a1), (4, s1 - a1), (2, s1), (s1,),
        (4, 2, s1), (2, 2, a1), (2, 2, s1 - a1), (2, a1), (2, s1 - a1), (s1,),
        (2, 2, so), (2, 2, so), (2, so), (2, so), (2 * so,), (so,),
        (2, 2, 2, a0), (2, 2, 2, a0), (2, 2, 2, a0), (2, 2, a0), (2, 2, a0), (2, 2, a0), (2, 2 * a0), (2, a0), (s0,),
    ]
    vmem = pl.BlockSpec(memory_space=pltpu.VMEM)
    smalls = (1 + clips, 8, width)
    out_shape = (
        [image, image, shape((s1, lanes), F32), shape((s1, lanes), F32), shape((s0, lanes), F32), shape((so, lanes), F32), shape(smalls, F32)]
        + [shape(dims + (lanes,), BF16) for dims in arriving]
        + [shape((2,) + smalls, F32), shape((3, 8, width), F32)]
        + [shape((rows, width), BF16)] * 2
        + [shape((3, rows, width), BF16), shape((blocks, HEADS, block, block), F32)]
        + [shape((rows, width), F32)] * 2
        + [shape((n, rows, width), BF16)]
    )
    out_specs = [ANY, ANY] + [vmem] * 5 + [ANY] * (len(arriving) + 9)
    scratch = [
        pltpu.VMEM((2, 2, 2, 2, s1, lanes), BF16),
        pltpu.VMEM((2, 2, 2, 2, s1, lanes), BF16),
        pltpu.VMEM((2, 2, 2, 2 * so, lanes), BF16),
        pltpu.VMEM((2, 2, s1, lanes), BF16),
        pltpu.VMEM((2, 2, 2, s1, lanes), BF16),
        pltpu.VMEM((2, 2, s1, lanes), BF16),
        pltpu.VMEM((2, 2, s1, lanes), BF16),
        pltpu.VMEM((2, 4 * so, lanes), BF16),
        pltpu.VMEM((2, 4 * so, lanes), BF16),
        pltpu.VMEM((rows, width), BF16),
        pltpu.VMEM((rows, width), F32),
        pltpu.VMEM((rows, width), F32),
        pltpu.VMEM((rows, width), F32),
        pltpu.VMEM((4, width, width), BF16),
        pltpu.VMEM((n, clips, fl, own, width), BF16),
        pltpu.VMEM(smalls, F32),
        pltpu.VMEM(smalls, F32),
        pltpu.VMEM(smalls, F32),
        pltpu.VMEM((3, 8, width), F32),
        pltpu.VMEM((n, clips, fl, own, width), BF16),
        pltpu.VMEM((n, clips, fl, own, width), BF16),
        pltpu.VMEM((clips, 8, width), F32),
        pltpu.VMEM((9, 1, width), F32),
        pltpu.VMEM((clips, block, block), F32),
        pltpu.VMEM((clips, block, block), F32),
        pltpu.SemaphoreType.DMA((sum(REMOTE_SIZES),)),
        pltpu.SemaphoreType.DMA((sum(REMOTE_SIZES),)),
        pltpu.SemaphoreType.DMA((sum(LOCAL_SIZES),)),
    ]
    result = pl.pallas_call(
        body,
        in_specs=[ANY] * 6 + [vmem, pl.BlockSpec(memory_space=pltpu.SMEM)] + [vmem] * 4,
        out_specs=out_specs,
        out_shape=out_shape,
        scratch_shapes=scratch,
        compiler_params=pltpu.CompilerParams(
            vmem_limit_bytes=VMEM_LIMIT, collective_id=0, has_side_effects=True
        ),
        cost_estimate=cost(45e9, 200e6),
        name="layer",
    )(x, cotangent, qkv_weight, out_weight, fc1_weight, fc2_weight, modulation, counts, *biases)
    return result[:7]


def close(plan, images, small, sums, layouts):
    n, width, clips = plan.frame_axis, plan.width, plan.clips
    m = len(images)

    def body(*refs):
        refs = list(refs)

        def take(count):
            got = refs[:count]
            del refs[:count]
            return got

        image_in, (vectors,), sums_in = take(m), take(1), take(len(sums))
        image_out, outs_h = take(m), take(len(layouts))
        d_mod, d_qv, d_out, d_fc1, d_fc2 = take(5)
        ins, outs, (turn, held, sems) = take(len(sums)), take(len(layouts)), take(3)
        arrive = [pltpu.make_async_copy(sums_in[i], ins[i], sems.at[i]) for i in range(len(sums))]
        arrive += [pltpu.make_async_copy(image_in[i], held.at[i], sems.at[len(sums) + i]) for i in range(m)]
        there = len(arrive)
        leave = [pltpu.make_async_copy(outs[i], outs_h[i], sems.at[there + i]) for i in range(len(layouts))]
        leave += [pltpu.make_async_copy(held.at[i], image_out[i], sems.at[there + len(layouts) + i]) for i in range(m)]
        for copy in arrive:
            copy.start()
        frame = lax.axis_index("frame")

        def cut(first, k, size):
            low, high, pieces = k * size, (k + 1) * size, []
            while low < high:
                row, at = low // width, low % width
                end = min(width, at + high - low)
                pieces.append(vectors[first[0], first[1] + row : first[1] + row + 1, at:end])
                low += end - at
            return pieces[0] if len(pieces) == 1 else jnp.concatenate(pieces, axis=1)

        for k in range(n):

            @pl.when(frame == k)
            def _(k=k):
                for c in range(clips):
                    d_mod[c : c + 1, :] = cut((1 + c, 0), k, 6 * width // n)
                d_qv[...] = cut((0, 0), k, 2 * width // n).reshape(2 * width // n)
                d_out[...] = cut((0, 2), k, width // n).reshape(width // n)
                d_fc1[...] = cut((0, 3), k, width).reshape(width)
                d_fc2[...] = cut((0, 7), k, width // n).reshape(width // n)

        for at, (which, first, span, tiles, used, folds, turned) in enumerate(layouts):
            ref, out = ins[which], outs[at]
            arrive[which].wait()
            to = turn if turned else out
            for j in range(tiles):
                to[:, j * LANES : (j + 1) * LANES] = ref[first + j * span : first + (j + 1) * span, :]
            if used:
                tile = ref[first + tiles * span : first + tiles * span + span // folds, :]
                for g in range(folds):
                    moved = tile if g == 0 else pltpu.roll(tile, LANES - g * used, 1)
                    here = slice(g * (span // folds), (g + 1) * (span // folds))
                    to[here, tiles * LANES : tiles * LANES + used] = moved[:, :used]
            if turned:
                out[...] = turn[...].T
            leave[at].start()
        for i in range(m):
            arrive[len(sums) + i].wait()
            leave[len(layouts) + i].start()
        for copy in leave:
            copy.wait()

    dims = [(span, tiles * LANES + used) for _, _, span, tiles, used, _, _ in layouts]
    grads = [shape(d[::-1] if layout[-1] else d, F32) for d, layout in zip(dims, layouts)]
    sizes = (2 * width // n, width // n, width, width // n)
    vectors = [shape((clips, 6 * width // n), F32)] + [shape((size,), F32) for size in sizes]
    made = grads + vectors
    return pl.pallas_call(
        body,
        grid=(1,),
        in_specs=[ANY] * m + [whole(small.shape)] + [ANY] * len(sums),
        out_specs=[ANY] * (m + len(grads)) + [whole(s.shape) for s in vectors],
        out_shape=[shape(image.shape, image.dtype) for image in images] + made,
        scratch_shapes=[pltpu.VMEM(s.shape, s.dtype) for s in list(sums) + grads]
        + [
            pltpu.VMEM(dims[0], F32),
            pltpu.VMEM((m,) + images[0].shape, images[0].dtype),
            pltpu.SemaphoreType.DMA((2 * m + len(sums) + len(layouts),)),
        ],
        compiler_params=params(),
        cost_estimate=cost(0, 14e6),
        name="close",
    )(*images, small, *sums)


def fast_layer(
    mesh,
    block_input,
    modulation,
    frame_counts,
    qkv_weight,
    qv_bias,
    out_weight,
    out_bias,
    fc1_weight,
    fc1_bias,
    fc2_weight,
    fc2_bias,
    out_cotangent,
):
    plan = Plan(mesh, block_input.shape, qkv_weight.shape, fc1_weight.shape)
    n, width = plan.frame_axis, plan.width
    biases = (qv_bias, out_bias, fc1_bias, fc2_bias)
    block_output, input_grad, sum2, sum1, sum0, sumo, small = whole_layer(
        plan, block_input, out_cotangent, modulation, frame_counts, biases, qkv_weight, out_weight, fc1_weight, fc2_weight
    )
    span2, span1 = plan.ff // plan.clip_axis, width // plan.clip_axis
    (block_output, input_grad, fc2_turned, fc1_out, qkv_out, out_out, d_modulation, d_qv, d_out, d_fc1, d_fc2) = close(
        plan,
        (block_output, input_grad),
        small,
        (sum2, sum1, sum0, sumo),
        (
            (0, 0, span2, 2, 32, 4, True),
            (1, 0, span1, 9, 0, 1, False),
            (2, 0, span1, 6, 96, 1, False),
            (3, 0, span1, 2, 32, 3, False),
        ),
    )
    return (
        block_output,
        input_grad,
        d_modulation,
        qkv_out,
        d_qv,
        out_out,
        d_out,
        fc1_out,
        d_fc1,
        fc2_turned.T,
        d_fc2,
    )


def solution(mesh):
    placed = (
        P("clip", "frame", None, None),
        P("clip", None),
        P("clip"),
        P(),
        P(),
        P(),
        P(),
        P(),
        P(),
        P(),
        P(),
        P("clip", "frame", None, None),
    )
    def layer(*arrays):
        if fits(mesh, arrays[0].shape, arrays[3].shape, arrays[7].shape):
            return fast_layer(mesh, *arrays)
        return on_device(*arrays)

    return jax.shard_map(
        layer,
        mesh=mesh,
        in_specs=placed,
        out_specs=(
            P("clip", "frame", None, None),
            P("clip", "frame", None, None),
            P("clip", "frame"),
            P("clip", "frame"),
            P("frame"),
            P("clip", "frame"),
            P("frame"),
            P("clip", "frame"),
            P("frame"),
            P("clip", "frame"),
            P("frame"),
        ),
        check_vma=False,
    )
```

```python
import functools

import jax
import jax.numpy as jnp
from jax import lax
from jax.experimental import pallas as pl
from jax.experimental.pallas import tpu as pltpu
from jax.sharding import PartitionSpec as P

HEADS = 16


EPSILON = 1e-06
NEGATIVE = -1e30


def normalize(values):
    centred = values - jnp.mean(values, axis=-1, keepdims=True)
    variance = jnp.mean(centred * centred, axis=-1, keepdims=True)
    return centred * lax.rsqrt(variance + EPSILON)


def modulate(values, shift_term, scale_term):
    return normalize(values) * (1.0 + scale_term) + shift_term


def gelu_tanh(inputs):
    return jax.nn.gelu(inputs, approximate=True)


def contract_rows(left, right):
    return lax.dot_general(
        left, right, (((0,), (0,)), ((), ())), preferred_element_type=jnp.float32
    )


def contract_cols(left, right):
    return lax.dot_general(
        left, right, (((1,), (1,)), ((), ())), preferred_element_type=jnp.float32
    )


def on_device(
    block_input,
    modulation,
    frame_counts,
    qkv_weight,
    qv_bias,
    out_weight,
    out_bias,
    fc1_weight,
    fc1_bias,
    fc2_weight,
    fc2_bias,
    out_cotangent,
):
    swapped = lax.all_to_all(block_input, "frame", split_axis=2, concat_axis=1, tiled=True)
    clip_count, frames, patches, model_width = swapped.shape
    head_width = model_width // HEADS
    row_count = clip_count * frames * patches
    factor = head_width ** (-0.5)
    frame_valid = (jnp.arange(frames)[None, :] < frame_counts[:, None]).astype(jnp.float32)
    valid_rows = frame_valid[:, :, None, None]
    key_valid = frame_valid[:, None, None, None, :] > 0.5
    modulators = modulation.astype(jnp.float32).reshape(clip_count, 6, model_width)[
        :, :, None, None, :
    ]
    shift_one = modulators[:, 0]
    scale_one = modulators[:, 1]
    gate_one = modulators[:, 2]
    shift_two = modulators[:, 3]
    scale_two = modulators[:, 4]
    gate_two = modulators[:, 5]
    residual = swapped.astype(jnp.float32)
    normed_full, modulate_back_one = jax.vjp(modulate, residual, shift_one, scale_one)
    normed_one = normed_full.astype(jnp.bfloat16).reshape(row_count, model_width)
    bias_full = jnp.concatenate(
        [qv_bias[:model_width], jnp.zeros((model_width,), jnp.bfloat16), qv_bias[model_width:]]
    ).astype(jnp.float32)
    projected = (
        jnp.dot(normed_one, qkv_weight, preferred_element_type=jnp.float32) + bias_full
    ).astype(jnp.bfloat16)
    shaped = projected.reshape(clip_count, frames, patches, 3, HEADS, head_width)
    queries = shaped[:, :, :, 0]
    keys_all = shaped[:, :, :, 1]
    values_all = shaped[:, :, :, 2]
    scores = (
        jnp.einsum("cfphd,cgphd->cphfg", queries, keys_all, preferred_element_type=jnp.float32)
        * factor
    )
    scores = jnp.where(key_valid, scores, NEGATIVE)
    row_peak = jnp.max(scores, axis=-1, keepdims=True)
    exponent = jnp.exp(scores - row_peak)
    attention_weights = exponent / jnp.sum(exponent, axis=-1, keepdims=True)
    weights_low = attention_weights.astype(jnp.bfloat16)
    context = jnp.einsum(
        "cphfg,cgphd->cfphd", weights_low, values_all, preferred_element_type=jnp.float32
    )
    context_low = context.astype(jnp.bfloat16).reshape(row_count, model_width)
    attended = jnp.dot(
        context_low, out_weight, preferred_element_type=jnp.float32
    ) + out_bias.astype(jnp.float32)
    attended = attended.reshape(clip_count, frames, patches, model_width)
    middle = residual + gate_one * attended
    normed_mid, modulate_back_two = jax.vjp(modulate, middle, shift_two, scale_two)
    normed_two = normed_mid.astype(jnp.bfloat16).reshape(row_count, model_width)
    hidden = jnp.dot(normed_two, fc1_weight, preferred_element_type=jnp.float32) + fc1_bias.astype(
        jnp.float32
    )
    activated_full, gelu_back = jax.vjp(gelu_tanh, hidden)
    activated = activated_full.astype(jnp.bfloat16)
    branch_two = jnp.dot(
        activated, fc2_weight, preferred_element_type=jnp.float32
    ) + fc2_bias.astype(jnp.float32)
    branch_two = branch_two.reshape(clip_count, frames, patches, model_width)
    result = valid_rows * (middle + gate_two * branch_two)
    block_output = lax.all_to_all(
        result.astype(jnp.bfloat16), "frame", split_axis=1, concat_axis=2, tiled=True
    )
    cotangent = lax.all_to_all(
        out_cotangent, "frame", split_axis=2, concat_axis=1, tiled=True
    ).astype(jnp.float32)
    d_result = valid_rows * cotangent
    d_gate_two = jnp.sum(d_result * branch_two, axis=(1, 2))
    d_branch = (d_result * gate_two).astype(jnp.bfloat16).reshape(row_count, model_width)
    d_fc2_bias = jnp.sum(d_branch.astype(jnp.float32), axis=0)
    d_fc2_weight = contract_rows(activated, d_branch)
    d_activated = contract_cols(d_branch, fc2_weight)
    d_hidden = gelu_back(d_activated)[0].astype(jnp.bfloat16)
    d_fc1_bias = jnp.sum(d_hidden.astype(jnp.float32), axis=0)
    d_fc1_weight = contract_rows(normed_two, d_hidden)
    d_normed_two = contract_cols(d_hidden, fc1_weight).reshape(
        clip_count, frames, patches, model_width
    )
    d_middle_norm, d_shift_two, d_scale_two = modulate_back_two(d_normed_two)
    d_middle = d_result + d_middle_norm
    d_gate_one = jnp.sum(d_middle * attended, axis=(1, 2))
    d_attended = (d_middle * gate_one).astype(jnp.bfloat16).reshape(row_count, model_width)
    d_out_bias = jnp.sum(d_attended.astype(jnp.float32), axis=0)
    d_out_weight = contract_rows(context_low, d_attended)
    d_context = contract_cols(d_attended, out_weight).astype(jnp.bfloat16)
    d_context = d_context.reshape(clip_count, frames, patches, HEADS, head_width)
    d_weights = jnp.einsum(
        "cfphd,cgphd->cphfg", d_context, values_all, preferred_element_type=jnp.float32
    )
    d_values = jnp.einsum(
        "cphfg,cfphd->cgphd", weights_low, d_context, preferred_element_type=jnp.float32
    )
    d_scores = attention_weights * (
        d_weights - jnp.sum(attention_weights * d_weights, axis=-1, keepdims=True)
    )
    d_scores = d_scores.astype(jnp.bfloat16)
    d_queries = (
        jnp.einsum("cphfg,cgphd->cfphd", d_scores, keys_all, preferred_element_type=jnp.float32)
        * factor
    )
    d_keys = (
        jnp.einsum("cphfg,cfphd->cgphd", d_scores, queries, preferred_element_type=jnp.float32)
        * factor
    )
    d_projected = (
        jnp.stack([d_queries, d_keys, d_values], axis=3)
        .astype(jnp.bfloat16)
        .reshape(row_count, 3 * model_width)
    )
    column_sums = jnp.sum(d_projected.astype(jnp.float32), axis=0)
    d_qv_bias = jnp.concatenate([column_sums[:model_width], column_sums[2 * model_width :]])
    d_qkv_weight = contract_rows(normed_one, d_projected)
    d_normed_one = contract_cols(d_projected, qkv_weight).reshape(
        clip_count, frames, patches, model_width
    )
    d_residual, d_shift_one, d_scale_one = modulate_back_one(d_normed_one)
    d_input = d_middle + d_residual
    input_grad = lax.all_to_all(
        d_input.astype(jnp.bfloat16), "frame", split_axis=1, concat_axis=2, tiled=True
    )
    d_modulation = jnp.stack(
        [
            d_shift_one.reshape(clip_count, model_width),
            d_scale_one.reshape(clip_count, model_width),
            d_gate_one,
            d_shift_two.reshape(clip_count, model_width),
            d_scale_two.reshape(clip_count, model_width),
            d_gate_two,
        ],
        axis=1,
    ).reshape(clip_count, 6 * model_width)
    every_part = (
        lax.psum_scatter(d_qkv_weight, "frame", scatter_dimension=1, tiled=True),
        lax.psum_scatter(d_out_weight, "frame", scatter_dimension=1, tiled=True),
        lax.psum_scatter(d_fc1_weight, "frame", scatter_dimension=1, tiled=True),
        lax.psum_scatter(d_fc2_weight, "frame", scatter_dimension=1, tiled=True),
        lax.psum_scatter(d_modulation, "frame", scatter_dimension=1, tiled=True),
        lax.psum_scatter(d_qv_bias, "frame", scatter_dimension=0, tiled=True),
        lax.psum_scatter(d_out_bias, "frame", scatter_dimension=0, tiled=True),
        lax.psum_scatter(d_fc1_bias, "frame", scatter_dimension=0, tiled=True),
        lax.psum_scatter(d_fc2_bias, "frame", scatter_dimension=0, tiled=True),
    )
    every_mat = (
        lax.psum_scatter(every_part[0], "clip", scatter_dimension=0, tiled=True),
        lax.psum_scatter(every_part[1], "clip", scatter_dimension=0, tiled=True),
        lax.psum_scatter(every_part[2], "clip", scatter_dimension=0, tiled=True),
        lax.psum_scatter(every_part[3], "clip", scatter_dimension=0, tiled=True),
    )
    qkv_grad = every_mat[0]
    out_grad = every_mat[1]
    fc1_grad = every_mat[2]
    fc2_grad = every_mat[3]
    modulation_grad = every_part[4]
    bias_parts = (every_part[5], every_part[6], every_part[7], every_part[8])
    bias_totals = lax.psum((bias_parts[0], bias_parts[1], bias_parts[2], bias_parts[3]), "clip")
    return (
        block_output,
        input_grad,
        modulation_grad,
        qkv_grad,
        bias_totals[0],
        out_grad,
        bias_totals[1],
        fc1_grad,
        bias_totals[2],
        fc2_grad,
        bias_totals[3],
    )


LANES = 128
VMEM_LIMIT = 61 * 1024 * 1024
ROWS_DN = (((0,), (0,)), ((), ()))
COLS_DN = (((1,), (1,)), ((), ()))
F32 = jnp.float32
BF16 = jnp.bfloat16


def mm(left, right):
    return jnp.dot(left, right, preferred_element_type=F32)


def mm_cols(left, right):
    return lax.dot_general(left, right, COLS_DN, preferred_element_type=F32)


def mm_rows(left, right):
    return lax.dot_general(left, right, ROWS_DN, preferred_element_type=F32)


def unit(values):
    centred = values - jnp.mean(values, axis=-1, keepdims=True)
    variance = jnp.mean(centred * centred, axis=-1, keepdims=True)
    inverse = lax.rsqrt(variance + EPSILON)
    return centred * inverse, inverse


def unit_back(unit_values, inverse, grad):
    mean_grad = jnp.mean(grad, axis=-1, keepdims=True)
    mean_dot = jnp.mean(grad * unit_values, axis=-1, keepdims=True)
    return (grad - mean_grad - unit_values * mean_dot) * inverse


def params(**more):
    return pltpu.CompilerParams(vmem_limit_bytes=VMEM_LIMIT, **more)


def cost(flops, moved, transcendentals=0):
    return pl.CostEstimate(flops=int(flops), bytes_accessed=int(moved), transcendentals=int(transcendentals))


def shape(dims, kind):
    return jax.ShapeDtypeStruct(tuple(dims), kind)


def whole(dims, buffers=1):
    zeros = (0,) * len(dims)
    return pl.BlockSpec(tuple(dims), lambda *_: zeros, pipeline_mode=pl.Buffered(buffers))


ANY = pl.BlockSpec(memory_space=pl.ANY)


def head_window(head, width):
    low = head * width
    start = low // LANES * LANES
    size = LANES if low - start + width <= LANES else 2 * LANES
    return low, start, size


def head_mask(head, width):
    low, start, size = head_window(head, width)
    lane = lax.broadcasted_iota(jnp.int32, (1, size), 1) + start
    return jnp.where((lane >= low) & (lane < low + width), 1.0, 0.0).astype(BF16)


class Plan:
    def __init__(self, mesh, x, qkv_weight, fc1_weight):
        self.clip_axis = mesh.shape["clip"]
        self.frame_axis = mesh.shape["frame"]
        self.clips, self.local_frames, self.patches, self.width = x
        self.own_patches = self.patches // self.frame_axis
        self.halves = self.own_patches // 8
        self.frames = self.local_frames * self.frame_axis
        self.ff = fc1_weight[1]
        self.rows = self.clips * self.frames * self.own_patches
        self.clip_rows = self.rows // self.clips
        self.block = self.frames * 8
        self.blocks = self.rows // self.block
        self.piece = self.local_frames * 8
        self.head_width = self.width // HEADS
        self.chunk_dims = (self.clips, self.halves, self.local_frames, 8, self.width)
        self.zs = self.clip_axis // 2

    def row_of(self, clip, half, k):
        return ((clip * self.halves + half) * self.frame_axis + k) * self.piece


def fits(mesh, x, qkv_weight, fc1_weight):
    clip_axis, frame_axis = mesh.shape["clip"], mesh.shape["frame"]
    width, ff = x[3], fc1_weight[1]
    return (
        clip_axis == 8
        and frame_axis == 4
        and x[2] // frame_axis % 8 == 0
        and x[1] * frame_axis * 8 == LANES
        and width == 1152
        and ff == 4 * width
        and qkv_weight[1] == 3 * width
    )


def fold_tile(tile, folds, used):
    rows = tile.shape[0] // folds
    total = tile[:rows]
    for g in range(1, folds):
        total = total + pltpu.roll(tile[g * rows : (g + 1) * rows], g * used, 1)
    return total


MESH = pl.DeviceIdType.MESH


def unit_rows(ref, here):
    return unit(ref[here, :])


class Later:
    def __init__(self, make):
        self.make = make

    def start(self):
        self.make().start()

    def wait(self):
        self.make().wait()

    def wait_recv(self):
        self.make().wait_recv()

    def wait_send(self):
        self.make().wait_send()


REMOTE_SIZES = (4, 4, 8, 1, 4, 4, 4, 4, 1, 1, 4, 2, 2, 1, 1, 1, 1, 1, 1, 1, 1, 1, 2, 2, 2, 2, 2, 2, 2, 2, 1, 4, 4, 2, 2, 3, 4, 4)
(
    R_C2, R_C1, R_C0, R_CO, R_2AX, R_2BY, R_2AY, R_2BX, R_2Z, R_2ZZ, R_1Z, R_1AX, R_1BY, R_1AY, R_1BX, R_1ZZ, R_OAX, R_OBY, R_OAY, R_OBX, R_OZ, R_OZZ, R_0AX, R_0BY, R_0CZ, R_0AY, R_0BX, R_0CX, R_0ABZ, R_0CY, R_0ZZ, R_OUT, R_IN, R_SMX, R_SMY, R_SMC, R_XIN, R_CIN,
) = REMOTE_AT = tuple(sum(REMOTE_SIZES[:i]) for i in range(len(REMOTE_SIZES)))
LOCAL_SIZES = (4, 6, 6, 6, 6, 2, 1, 1, 1, 2, 1, 1, 4, 1, 4)
(
    L_W, L_A, L_B, L_C, L_D, L_S, L_MID, L_ATT, L_PROJ, L_PROBS, L_N1, L_CTX, L_OWN, L_ACT, L_ACTS,
) = LOCAL_AT = tuple(sum(LOCAL_SIZES[:i]) for i in range(len(LOCAL_SIZES)))
CORE, Z0, Z1, X, Y, XY = range(6)


LOAD, RUN, SEND = range(3)
TMP_A, TMP_B, TMP_C, TMP_D, TMP_S = range(5)
(J_C1, J_C2, J_Z0, J_XY1, J_XY2, J_1A, J_1B, J_1XY2, J_2Z, J_CO, J_O1, J_O2, J_OZ, J_C0, J_Q1, J_Q2, J_Q3, J_FIN2, J_FIN1, J_FINO, J_FIN0, J_SM1, J_SM2, J_SM3, J_SM4, J_SM5, J_MD1, J_MD2) = range(28)
(S_1AX, S_1BY, S_1AY, S_1BX, S_2Z, S_0ZZ, S_SMX, S_MDX, S_OUT, S_IN) = range(10)
P_A = tuple((0, k) for k in range(4))
P_B = tuple((1, k) for k in range(4))
P_C = tuple((2, k) for k in range(4))
P_D = tuple((3, k) for k in range(4))
P_E = tuple((4, k) for k in range(4))
P_G = tuple((5, k) for k in range(4))
P_AB = tuple((6, k) for k in range(4))
P_WQ = tuple((7, k) for k in range(8))
P_IN = tuple((9, k) for k in range(3))
P_M1, P_O, P_WO, P_DC, P_PK, P_INE = ((8, k) for k in range(6))
SCHEDULE = {
    P_E[0]: (
        (LOAD, J_C2, 0),
    ),
    P_A[1]: (
        (RUN, J_C2, 0),
        (LOAD, J_C1, 0),
    ),
    P_B[1]: (
        (RUN, J_C1, 0),
    ),
    P_D[1]: (
        (LOAD, J_C2, 1),
    ),
    P_E[1]: (
        (RUN, J_C2, 1),
    ),
    P_A[2]: (
        (LOAD, J_C1, 1),
        (LOAD, J_XY1, 0),
    ),
    P_B[2]: (
        (RUN, J_C1, 1),
    ),
    P_D[2]: (
        (RUN, J_XY1, 0),
    ),
    P_E[2]: (
        (LOAD, J_XY1, 1),
    ),
    P_A[3]: (
        (LOAD, J_C2, 2),
        (RUN, J_XY1, 1),
        (LOAD, J_C1, 2),
    ),
    P_B[3]: (
        (LOAD, J_Z0, 0),
        (RUN, J_C2, 2),
        (LOAD, J_XY2, 0),
    ),
    P_C[3]: (
        (RUN, J_C1, 2),
    ),
    P_D[3]: (
        (RUN, J_Z0, 0),
        (LOAD, J_C2, 3),
    ),
    P_E[3]: (
        (RUN, J_C2, 3),
        (RUN, J_XY2, 0),
    ),
    P_M1: (
        (LOAD, J_C1, 3),
        (LOAD, J_XY1, 2),
    ),
    P_WO: (
        (RUN, J_C1, 3),
        (LOAD, J_XY2, 1),
        (RUN, J_XY1, 2),
    ),
    P_DC: (
        (RUN, J_XY2, 1),
        (LOAD, J_XY1, 3),
    ),
    P_AB[0]: (
        (RUN, J_XY1, 3),
    ),
    P_AB[1]: (
        (LOAD, J_CO, 0),
    ),
    P_AB[2]: (
        (RUN, J_CO, 0),
        (LOAD, J_XY2, 2),
        (RUN, J_XY2, 2),
        (LOAD, J_XY2, 3),
    ),
    P_AB[3]: (
        (RUN, J_XY2, 3),
        (LOAD, J_Z0, 1),
    ),
    P_PK: (
        (RUN, J_Z0, 1),
        (SEND, S_1AX, 0),
    ),
    P_WQ[0]: (
        (LOAD, J_Z0, 2),
    ),
    P_WQ[1]: (
        (RUN, J_Z0, 2),
    ),
    P_WQ[2]: (
        (SEND, S_1BY, 0),
        (SEND, S_2Z, 0),
    ),
    P_WQ[4]: (
        (LOAD, J_Z0, 3),
    ),
    P_WQ[5]: (
        (RUN, J_Z0, 3),
        (SEND, S_1AX, 1),
        (SEND, S_1BY, 1),
    ),
    P_WQ[6]: (
        (LOAD, J_C0, 0),
    ),
    P_WQ[7]: (
        (LOAD, J_O1, 0),
        (RUN, J_O1, 0),
    ),
    P_IN[0]: (
        (LOAD, J_1A, 0),
        (RUN, J_1A, 0),
        (RUN, J_C0, 0),
    ),
    P_IN[1]: (
        (LOAD, J_1B, 0),
    ),
    P_IN[2]: (
        (RUN, J_1B, 0),
        (LOAD, J_C0, 1),
    ),
    P_INE: (
        (RUN, J_C0, 1),
        (SEND, S_SMX, 0),
    ),
    P_G[0]: (
        (LOAD, J_2Z, 0),
        (RUN, J_2Z, 0),
        (LOAD, J_1B, 1),
        (RUN, J_1B, 1),
    ),
    P_G[1]: (
        (SEND, S_1BX, 0),
        (LOAD, J_1A, 1),
    ),
    P_G[2]: (
        (RUN, J_1A, 1),
        (LOAD, J_O2, 0),
        (LOAD, J_SM1, 0),
        (LOAD, J_Q1, 0),
        (RUN, J_Q1, 0),
        (RUN, J_O2, 0),
        (RUN, J_SM1, 0),
        (SEND, S_1AY, 0),
        (LOAD, J_Q1, 1),
        (LOAD, J_SM2, 0),
        (RUN, J_SM2, 0),
        (LOAD, J_SM3, 0),
        (RUN, J_SM3, 0),
        (RUN, J_Q1, 1),
        (LOAD, J_OZ, 0),
    ),
    P_G[3]: (
        (LOAD, J_SM4, 0),
        (RUN, J_OZ, 0),
        (LOAD, J_Q2, 0),
        (RUN, J_SM4, 0),
        (RUN, J_Q2, 0),
        (LOAD, J_1XY2, 0),
    ),
    P_O: (
        (SEND, S_OUT, 3),
        (SEND, S_OUT, 1),
        (SEND, S_OUT, 2),
        (RUN, J_1XY2, 0),
        (LOAD, J_SM5, 0),
        (LOAD, J_Q2, 1),
        (RUN, J_Q2, 1),
        (LOAD, J_FINO, 0),
        (SEND, S_MDX, 0),
        (RUN, J_FINO, 0),
        (LOAD, J_FIN2, 0),
        (LOAD, J_Q3, 0),
        (RUN, J_Q3, 0),
        (LOAD, J_MD1, 0),
        (RUN, J_MD1, 0),
        (RUN, J_SM5, 0),
        (LOAD, J_Q3, 1),
        (RUN, J_FIN2, 0),
        (SEND, S_IN, 3),
        (SEND, S_IN, 1),
        (SEND, S_IN, 2),
        (RUN, J_Q3, 1),
        (SEND, S_0ZZ, 0),
        (LOAD, J_FIN1, 0),
        (RUN, J_FIN1, 0),
        (LOAD, J_MD2, 0),
        (LOAD, J_FIN0, 0),
        (RUN, J_MD2, 0),
        (RUN, J_FIN0, 0),
    ),
}
TMPS = {
    (J_1A, 0): TMP_C,
    (J_1A, 1): TMP_C,
    (J_1B, 0): TMP_C,
    (J_1B, 1): TMP_D,
    (J_1XY2, 0): TMP_D,
    (J_2Z, 0): TMP_C,
    (J_C1, 0): TMP_A,
    (J_C1, 1): TMP_A,
    (J_C1, 2): TMP_A,
    (J_C1, 3): TMP_A,
    (J_C2, 0): TMP_B,
    (J_C2, 1): TMP_B,
    (J_C2, 2): TMP_B,
    (J_C2, 3): TMP_B,
    (J_FIN0, 0): TMP_D,
    (J_FIN1, 0): TMP_D,
    (J_FIN2, 0): TMP_C,
    (J_FINO, 0): TMP_C,
    (J_O1, 0): TMP_C,
    (J_O2, 0): TMP_C,
    (J_OZ, 0): TMP_C,
    (J_Q1, 0): TMP_A,
    (J_Q1, 1): TMP_B,
    (J_Q2, 0): TMP_C,
    (J_Q2, 1): TMP_D,
    (J_Q3, 0): TMP_D,
    (J_Q3, 1): TMP_D,
    (J_XY1, 0): TMP_D,
    (J_XY1, 1): TMP_C,
    (J_XY1, 2): TMP_D,
    (J_XY1, 3): TMP_D,
    (J_XY2, 0): TMP_D,
    (J_XY2, 1): TMP_C,
    (J_XY2, 2): TMP_C,
    (J_XY2, 3): TMP_D,
    (J_Z0, 0): TMP_C,
    (J_Z0, 1): TMP_D,
    (J_Z0, 2): TMP_C,
    (J_Z0, 3): TMP_D,
}


def join_heads(width, head_parts, put):
    waiting = {}
    for h in range(HEADS):
        _, start, size = head_window(h, width)
        values = head_parts(h)
        for t in range(size // LANES):
            tiles = [value[:, t * LANES : (t + 1) * LANES] for value in values]
            j = start // LANES + t
            waiting[j] = [a + b for a, b in zip(waiting[j], tiles)] if j in waiting else tiles
        ahead = head_window(h + 1, width)[1] // LANES if h + 1 < HEADS else HEADS * width
        for j in sorted(waiting):
            if j < ahead:
                put(j, waiting.pop(j))


def whole_layer(plan, x, cotangent, modulation, counts, biases, qkv_weight, out_weight, fc1_weight, fc2_weight):
    n, rows, width, ff = plan.frame_axis, plan.rows, plan.width, plan.ff
    own, fl, clips = plan.own_patches, plan.local_frames, plan.clips
    span2, span1 = ff // plan.clip_axis, width // plan.clip_axis
    s1, s0, so = 9 * span1, 7 * span1, 2 * span1 + span1 // 3
    a1, a0 = 640, s0 // 3
    pad2, padq, wq = 384, 896, 3 * width // n
    blocks, block = plan.blocks, plan.block
    factor = plan.head_width ** (-0.5)
    half_rows = 128
    parts_per_clip = plan.clip_rows // half_rows

    def body(*refs):
        refs = list(refs)

        def take(count):
            got = refs[:count]
            del refs[:count]
            return got

        (x_h, cot_h, wqkv_h, wout_h, fc1_h, fc2_h, raw_mod, counts_ref, qv_bias, out_bias, fc1_bias, fc2_bias) = take(12)
        (out_h, in_h) = take(2)
        sum2, sum1, sum0, sumo, small = take(5)
        (rc2, rc1, rc0, rco, r2ax, r2by, r2ay, r2bx, r2z, r2zz) = take(10)
        (r1z, r1ax, r1by, r1ay, r1bx, r1zz) = take(6)
        (roax, roby, roay, robx, roz, rozz) = take(6)
        (r0ax, r0by, r0cz, r0ay, r0bx, r0cx, r0abz, r0cy, r0zz, rsm, rsmc) = take(11)
        (n1_h, ctx_h, proj_h, probs_h, att_h, mid_h, act_h) = take(7)
        (keep2, keep1, keepo, r2, stage, tmp_a, tmp_b, tmp_c, tmp_d, dres, acc, f1, f2, ring, rows_out, sm, sm_b, sm_t, smc) = take(19)
        (xin, cin, mod, bias, allowed, valid) = take(6)
        send_sem, recv_sem, local_sem = take(3)

        frame, clip = lax.axis_index("frame"), lax.axis_index("clip")
        mx, my = frame % 2, frame // 2
        core, z0, z1 = clip % 2, clip // 2 % 2, clip // 4
        partner = (
            ("clip", clip + 1 - 2 * core),
            ("clip", clip + 2 - 4 * z0),
            ("clip", clip + 4 - 8 * z1),
            ("frame", frame + 1 - 2 * mx),
            ("frame", frame + 2 - 4 * my),
            ("frame", n - 1 - frame),
        )

        def remote(name, index, src, dst, bit):
            axis, where = partner[bit]
            at = name + index
            return Later(
                lambda: pltpu.make_async_remote_copy(
                    src_ref=src,
                    dst_ref=dst,
                    send_sem=send_sem.at[at],
                    recv_sem=recv_sem.at[at],
                    device_id={axis: where},
                    device_id_type=MESH,
                )
            )

        def local(name, index, src, dst):
            return Later(lambda: pltpu.make_async_copy(src, dst, local_sem.at[name + index]))

        lo1, hi1 = pl.ds(0, a1), pl.ds(a1, s1 - a1)
        pa, pb, pc, pab, all0 = pl.ds(0, a0), pl.ds(a0, a0), pl.ds(2 * a0, a0), pl.ds(0, 2 * a0), pl.ds(0, s0)
        oa, ob, oab = pl.ds(0, so), pl.ds(so, so), pl.ds(0, 2 * so)
        all1 = pl.ds(0, s1)

        def c2(z):
            return remote(R_C2, z, stage.at[0, :, :, all1], rc2.at[z], CORE)

        def c1(f):
            return remote(R_C1, f, stage.at[1, :, :, all1], rc1.at[f], CORE)

        def c0(j, f):
            return remote(R_C0, 4 * j + f, stage.at[:, f // 2, f % 2, all0], rc0.at[j, :, f // 2, f % 2], CORE)

        def co():
            return remote(R_CO, 0, stage.at[:, :, :, oab], rco, CORE)

        def t2ax(z):
            return remote(R_2AX, z, keep2.at[z // 2, z % 2, :, 1 - mx, lo1], r2ax.at[z], X)

        def t2by(z):
            return remote(R_2BY, z, keep2.at[z // 2, z % 2, 1 - my, :, hi1], r2by.at[z], Y)

        def t2ay(z):
            return remote(R_2AY, z, keep2.at[z // 2, z % 2, 1 - my, mx, lo1], r2ay.at[z], Y)

        def t2bx(z):
            return remote(R_2BX, z, keep2.at[z // 2, z % 2, my, 1 - mx, hi1], r2bx.at[z], X)

        def t2z():
            return remote(R_2Z, 0, r2.at[:, 1 - z0], r2z, Z0)

        def t2zz():
            return remote(R_2ZZ, 0, r2.at[1 - z1, z0], r2zz, Z1)

        def t1z(f):
            return remote(R_1Z, f, keep1.at[f // 2, f % 2, :, 1 - z0], r1z.at[f], Z0)

        def t1ax(y):
            return remote(R_1AX, y, keep1.at[y, 1 - mx, :, z0, lo1], r1ax.at[y], X)

        def t1by(x):
            return remote(R_1BY, x, keep1.at[1 - my, x, :, z0, hi1], r1by.at[x], Y)

        def t1ay():
            return remote(R_1AY, 0, keep1.at[1 - my, mx, :, z0, lo1], r1ay, Y)

        def t1bx():
            return remote(R_1BX, 0, keep1.at[my, 1 - mx, :, z0, hi1], r1bx, X)

        def t1zz():
            return remote(R_1ZZ, 0, keep1.at[my, mx, 1 - z1, z0], r1zz, Z1)

        def toax():
            return remote(R_OAX, 0, keepo.at[:, :, 1 - mx, oa], roax, X)

        def toby():
            return remote(R_OBY, 0, keepo.at[:, 1 - my, :, ob], roby, Y)

        def toay():
            return remote(R_OAY, 0, keepo.at[:, 1 - my, mx, oa], roay, Y)

        def tobx():
            return remote(R_OBX, 0, keepo.at[:, my, 1 - mx, ob], robx, X)

        def toz():
            return remote(R_OZ, 0, keepo.at[1 - z0, my, mx], roz, Z0)

        def tozz():
            there = pl.ds(pl.multiple_of((1 - z1) * so, 16), so)
            return remote(R_OZZ, 0, keepo.at[z0, my, mx, there], rozz, Z1)

        def t0ax(j):
            return remote(R_0AX, j, keep2.at[j, :, :, 1 - mx, pa], r0ax.at[j], X)

        def t0by(j):
            return remote(R_0BY, j, keep2.at[j, :, 1 - my, :, pb], r0by.at[j], Y)

        def t0cz(j):
            return remote(R_0CZ, j, keep2.at[j, 1 - z0, :, :, pc], r0cz.at[j], Z0)

        def t0ay(j):
            return remote(R_0AY, j, keep2.at[j, :, 1 - my, mx, pa], r0ay.at[j], Y)

        def t0bx(j):
            return remote(R_0BX, j, keep2.at[j, :, my, 1 - mx, pb], r0bx.at[j], X)

        def t0cx(j):
            return remote(R_0CX, j, keep2.at[j, z0, :, 1 - mx, pc], r0cx.at[j], X)

        def t0abz(j):
            return remote(R_0ABZ, j, keep2.at[j, 1 - z0, my, mx, pab], r0abz.at[j], Z0)

        def t0cy(j):
            return remote(R_0CY, j, keep2.at[j, z0, 1 - my, mx, pc], r0cy.at[j], Y)

        def t0zz():
            return remote(R_0ZZ, 0, keep2.at[1 - z1, z0, my, mx, all0], r0zz, Z1)

        def row_send(name, k, dst, arriving=False):
            bit = (None, X, Y, XY)[k]
            place = partner[bit][1] if arriving else frame
            src = rows_out if name == R_IN else cin
            return remote(name, k, src.at[k], dst.at[:, :, pl.ds(place * own, own)], bit)

        def row_own(index, src, dst):
            return local(L_OWN, index, src.at[0], dst.at[:, :, pl.ds(frame * own, own)])

        def smx_send():
            return remote(R_SMX, 0, sm.at[0], rsm.at[0, 0], X)

        def smy_send():
            return remote(R_SMY, 0, sm_b.at[0], rsm.at[1, 0], Y)

        def mdx_send():
            return remote(R_SMX, 1, sm.at[pl.ds(1, clips)], rsm.at[0, pl.ds(1, clips)], X)

        def mdy_send():
            return remote(R_SMY, 1, sm_b.at[pl.ds(1, clips)], rsm.at[1, pl.ds(1, clips)], Y)

        def smc_send(i):
            return remote(R_SMC, i, smc.at[i], rsmc.at[i], (CORE, Z0, Z1)[i])

        def add_to(ref, at, other, other_at):
            ref[at] = ref[at] + other[other_at]

        def add_chunks(ref, at, other, other_at, count):
            for i in range(2):
                for k in range(2 if count == 2 else 1):
                    fill = iter((i, k))
                    here = tuple(next(fill) if p is None else p for p in at)
                    fill = iter((i, k))
                    there = tuple(next(fill) if p is None else p for p in other_at)
                    add_to(ref, here, other, there)

        def pump(arrivals, copies, work, sends):
            def load():
                for transfer in arrivals:
                    transfer.wait_recv()
                for copy in copies:
                    copy.start()

            def run():
                for copy in copies:
                    copy.wait()
                work()
                for transfer in sends:
                    transfer.start()

            return load, run

        def job(kind, index, tmps):
            tmp = (tmp_a, tmp_b, tmp_c, tmp_d, None)[tmps]
            sem = (L_A, L_B, L_C, L_D, L_S)[tmps]
            pair = (index // 2, index % 2)
            if kind == J_C1:

                def work():
                    add_chunks(keep1, pair + (None, None), tmp, (None, None, all1), 2)

                return pump([c1(index)], [local(sem, 0, rc1.at[index], tmp.at[:, :, all1])], work, [t1z(index)])
            if kind == J_C2:

                def work():
                    add_chunks(keep2, pair + (None, None, all1), tmp, (None, None, all1), 2)

                sends = [t2ax(index), t2by(index)]
                return pump([c2(index)], [local(sem, 0, rc2.at[index], tmp.at[:, :, all1])], work, sends)
            if kind == J_Z0:

                def work():
                    add_chunks(keep1, pair + (None, z0), tmp, (None, all1), 1)

                return pump([t1z(index)], [local(sem, 0, r1z.at[index], tmp.at[:, all1])], work, [])
            if kind == J_XY1:

                def work():
                    add_chunks(keep2, pair + (None, mx, lo1), tmp, (None, lo1), 1)
                    add_chunks(keep2, pair + (my, None, hi1), tmp, (None, hi1), 1)

                copies = [
                    local(sem, 0, r2ax.at[index], tmp.at[:, lo1]),
                    local(sem, 1, r2by.at[index], tmp.at[:, hi1]),
                ]
                return pump([t2ax(index), t2by(index)], copies, work, [t2ay(index), t2bx(index)])
            if kind == J_XY2:

                def work():
                    r2[pair] = keep2[pair + (my, mx, all1)] + tmp[0, all1]

                copies = [
                    local(sem, 0, r2ay.at[index], tmp.at[0, lo1]),
                    local(sem, 1, r2bx.at[index], tmp.at[0, hi1]),
                ]
                return pump([t2ay(index), t2bx(index)], copies, work, [])
            if kind == J_1A:

                def work():
                    add_chunks(keep1, (index, mx, None, z0, lo1), tmp, (None, lo1), 1)

                return pump([t1ax(index)], [local(sem, 0, r1ax.at[index], tmp.at[:, lo1])], work, [])
            if kind == J_1B:

                def work():
                    add_chunks(keep1, (my, index, None, z0, hi1), tmp, (None, hi1), 1)

                return pump([t1by(index)], [local(sem, 0, r1by.at[index], tmp.at[:, hi1])], work, [])
            if kind == J_1XY2:

                def work():
                    add_chunks(keep1, (my, mx, None, z0, all1), tmp, (None, all1), 1)

                copies = [local(sem, 0, r1ay, tmp.at[:, lo1]), local(sem, 1, r1bx, tmp.at[:, hi1])]
                return pump([t1ay(), t1bx()], copies, work, [t1zz()])
            if kind == J_2Z:

                def work():
                    add_chunks(r2, (None, z0), tmp, (None, all1), 1)

                return pump([t2z()], [local(sem, 0, r2z, tmp.at[:, all1])], work, [t2zz()])
            if kind == J_CO:

                def work():
                    add_chunks(keepo, (0, None, None), tmp_a, (None, None, oab), 2)
                    add_chunks(keepo, (1, None, None), tmp_b, (None, None, oab), 2)

                copies = [
                    local(L_A, 0, rco.at[0], tmp_a.at[:, :, oab]),
                    local(L_B, 0, rco.at[1], tmp_b.at[:, :, oab]),
                ]
                return pump([co()], copies, work, [toax(), toby()])
            if kind == J_O1:

                def work():
                    for i in range(2):
                        add_chunks(keepo, (i, None, mx, oa), tmp, (None, pl.ds(i * so, so)), 1)
                        add_chunks(keepo, (i, my, None, ob), tmp, (None, pl.ds((2 + i) * so, so)), 1)

                copies = [local(sem, i, roax.at[i], tmp.at[:, pl.ds(i * so, so)]) for i in range(2)]
                copies += [local(sem, 2 + i, roby.at[i], tmp.at[:, pl.ds((2 + i) * so, so)]) for i in range(2)]
                return pump([toax(), toby()], copies, work, [toay(), tobx()])
            if kind == J_O2:

                def work():
                    add_chunks(keepo, (None, my, mx, oab), tmp, (None, oab), 1)

                copies = [local(sem, 0, roay, tmp.at[:, oa]), local(sem, 1, robx, tmp.at[:, ob])]
                return pump([toay(), tobx()], copies, work, [toz()])
            if kind == J_OZ:

                def work():
                    add_to(keepo, (z0, my, mx), tmp, (0, oab))

                return pump([toz()], [local(sem, 0, roz, tmp.at[0, oab])], work, [tozz()])
            if kind == J_C0:

                def work():
                    add_chunks(keep2, (index, 0, None, None, all0), tmp_a, (None, None, all0), 2)
                    add_chunks(keep2, (index, 1, None, None, all0), tmp_b, (None, None, all0), 2)

                copies = [
                    local(L_A, 0, rc0.at[index, 0], tmp_a.at[:, :, all0]),
                    local(L_B, 0, rc0.at[index, 1], tmp_b.at[:, :, all0]),
                ]
                sends = [t0ax(index), t0by(index), t0cz(index)]
                return pump([c0(index, f) for f in range(n)], copies, work, sends)
            if kind == J_Q1:

                def work():
                    add_chunks(keep2, (index, None, None, mx, pa), tmp, (None, None, pa), 2)
                    add_chunks(keep2, (index, None, my, None, pb), tmp, (None, None, pb), 2)
                    add_chunks(keep2, (index, z0, None, None, pc), tmp, (None, None, pc), 2)

                copies = [
                    local(sem, i, r.at[index], tmp.at[:, :, p])
                    for i, (r, p) in enumerate(((r0ax, pa), (r0by, pb), (r0cz, pc)))
                ]
                arrivals = [t0ax(index), t0by(index), t0cz(index)]
                return pump(arrivals, copies, work, [t0ay(index), t0bx(index), t0cx(index)])
            if kind == J_Q2:

                def work():
                    add_chunks(keep2, (index, None, my, mx, pab), tmp, (None, pab), 1)
                    add_chunks(keep2, (index, z0, None, mx, pc), tmp, (None, pc), 1)

                copies = [
                    local(sem, i, r.at[index], tmp.at[:, p])
                    for i, (r, p) in enumerate(((r0ay, pa), (r0bx, pb), (r0cx, pc)))
                ]
                return pump([t0ay(index), t0bx(index), t0cx(index)], copies, work, [t0abz(index), t0cy(index)])
            if kind == J_Q3:

                def work():
                    add_to(keep2, (index, z0, my, mx, all0), tmp, (0, all0))

                copies = [local(sem, 0, r0abz.at[index], tmp.at[0, pab]), local(sem, 1, r0cy.at[index], tmp.at[0, pc])]
                return pump([t0abz(index), t0cy(index)], copies, work, [])
            if kind == J_FIN2:

                def work():
                    sum2[...] = r2[z1, z0].astype(F32) + tmp[0, all1].astype(F32)

                return pump([t2zz()], [local(sem, 0, r2zz, tmp.at[0, all1])], work, [])
            if kind == J_FIN1:

                def work():
                    sum1[...] = keep1[my, mx, z1, z0].astype(F32) + tmp[0, all1].astype(F32)

                return pump([t1zz()], [local(sem, 0, r1zz, tmp.at[0, all1])], work, [])
            if kind == J_FINO:

                def work():
                    here = pl.ds(pl.multiple_of(z1 * so, 16), so)
                    sumo[...] = keepo[z0, my, mx, here].astype(F32) + tmp[0, oa].astype(F32)

                return pump([tozz()], [local(sem, 0, rozz, tmp.at[0, oa])], work, [])
            if kind == J_FIN0:

                def work():
                    sum0[...] = keep2[z1, z0, my, mx, all0].astype(F32) + tmp[0, all0].astype(F32)

                return pump([t0zz()], [local(sem, 0, r0zz, tmp.at[0, all0])], work, [])
            if kind == J_SM1:

                def work():
                    sm_b[0] = sm[0] + sm_t[0]

                return pump([smx_send()], [local(L_S, 0, rsm.at[0, 0], sm_t.at[0])], work, [smy_send()])
            if kind == J_SM2:

                def work():
                    smc[0] = sm_b[0] + sm_t[0]

                return pump([smy_send()], [local(L_S, 0, rsm.at[1, 0], sm_t.at[0])], work, [smc_send(0)])
            if kind in (J_MD1, J_MD2):
                step, some = kind - J_MD1, pl.ds(1, clips)
                arrival, sends = (mdx_send, [mdy_send()]) if step == 0 else (mdy_send, [])
                source, result = (sm, sm_b) if step == 0 else (sm_b, small)

                def work():
                    result[some] = source[some] + sm_t[some]

                return pump([arrival()], [local(L_S, 1, rsm.at[step, some], sm_t.at[some])], work, sends)
            step = kind - J_SM3

            def work():
                if step < 2:
                    smc[step + 1] = smc[step] + sm_t[0]
                else:
                    small[0] = smc[step] + sm_t[0]

            sends = [smc_send(step + 1)] if step < 2 else []
            return pump([smc_send(step)], [local(L_S, 0, rsmc.at[step], sm_t.at[0])], work, sends)

        plain_sends = {
            S_1AX: t1ax,
            S_1BY: t1by,
            S_1AY: lambda _: t1ay(),
            S_1BX: lambda _: t1bx(),
            S_2Z: lambda _: t2z(),
            S_0ZZ: lambda _: t0zz(),
            S_SMX: lambda _: smx_send(),
            S_MDX: lambda _: mdx_send(),
            S_OUT: lambda k: row_send(R_OUT, k, out_h),
            S_IN: lambda k: row_send(R_IN, k, in_h),
        }

        def do(point):
            for what, kind, index in SCHEDULE.get(point, ()):
                if what == SEND:
                    plain_sends[kind](index).start()
                else:
                    job(kind, index, TMPS.get((kind, index), TMP_S))[what]()

        def do_in(points, index):
            for k, point in enumerate(points):
                if point in SCHEDULE:
                    pl.when(index == k)(lambda point=point: do(point))

        def weight(slot, src):
            return local(L_W, slot, src, ring.at[slot])

        def fc1_block(f):
            return weight(2 * (f % 2), fc1_h.at[:, pl.ds(pl.multiple_of(f * width, LANES), width)])

        def fc2_block(f):
            return weight(2 * (f % 2) + 1, fc2_h.at[pl.ds(pl.multiple_of(f * width, 16), width)])

        def fc2_block_at(f):
            return local(L_W, f, fc2_h.at[pl.ds(pl.multiple_of(f * width, 16), width)], ring.at[f])

        def qkv_block(i, slot):
            return weight(slot, wqkv_h.at[:, i * width : (i + 1) * width])

        def own_copies(src, dst, name):
            return local(name, 0, src, dst)

        def piece_of(ref, k, c, half):
            return ref[k, c, :, half * 8 : half * 8 + 8, :].astype(F32).reshape(plan.piece, width)

        def rows_at(c, half, k):
            return pl.ds(pl.multiple_of(c * plan.clip_rows + plan.row_of(0, half, k), 8), plan.piece)

        def arrive(name, k, src, dst):
            bit = (None, X, Y, XY)[k]
            return remote(name, k, src.at[:, :, pl.ds(partner[bit][1] * own, own)], dst.at[k], bit)

        barrier = pltpu.get_barrier_semaphore()
        for axis, where in partner:
            pl.semaphore_signal(barrier, inc=1, device_id={axis: where}, device_id_type=MESH)
        mine = pl.ds(frame * own, own)
        own_x = local(L_OWN, 2, x_h.at[:, :, mine], xin.at[0])
        own_x.start()
        for i in range(3):
            qkv_block(i, i).start()
        weight(3, wout_h).start()
        pl.semaphore_wait(barrier, len(partner))
        for k in (3, 1, 2):
            arrive(R_XIN, k, x_h, xin).start()
        sm[...] = jnp.zeros_like(sm)
        for i in range(6):
            values = raw_mod[:, i * width : (i + 1) * width].astype(F32)
            for c in range(clips):
                mod[c, i : i + 1, :] = values[c : c + 1, :]
        parts = [(qv_bias, 0), None, (qv_bias, 1), (out_bias, 0)] + [(fc1_bias, f) for f in range(n)] + [(fc2_bias, 0)]
        for i, part in enumerate(parts):
            if part is None:
                bias[i] = jnp.zeros((1, width), F32)
            else:
                bias[i] = part[0][pl.ds(part[1] * width, width)].astype(F32).reshape(1, width)

        def frame_of(axis):
            slot = lax.broadcasted_iota(jnp.int32, (block, block), axis) // 8
            k, local_frame = slot // fl, slot % fl
            low, high = k % 2, k // 2
            source = low + mx - 2 * low * mx + 2 * (high + my - 2 * high * my)
            return source * fl + local_frame

        lane_patch = lax.broadcasted_iota(jnp.int32, (block, block), 1) % 8
        row_patch = lax.broadcasted_iota(jnp.int32, (block, block), 0) % 8
        row_frame, lane_frame = frame_of(0), frame_of(1)
        for c in range(clips):
            count = counts_ref[c]
            valid[c] = jnp.where(row_frame < count, 1.0, 0.0)
            allowed[c] = jnp.where((lane_patch == row_patch) & (lane_frame < count), 0.0, NEGATIVE)

        def first_half(n1, proj, ctx, scores, lows, probs, n2):
            own_x.wait()

            @pl.loop(0, clips)
            def _(c):
                shift, scale = mod[c, 0:1, :], 1.0 + mod[c, 1:2, :]
                for half in range(plan.halves):
                    for k in range(n):
                        normed, _ = unit(piece_of(xin, k, c, half))
                        n1[rows_at(c, half, k), :] = (normed * scale + shift).astype(BF16)

            own_copies(n1, n1_h, L_N1).start()

            @pl.loop(0, 3)
            def _(i):
                local(L_W, i, fc2_h.at[pl.ds(0, width)], ring.at[i]).wait()
                proj[i] = (mm(n1[...], ring[i]) + bias[i]).astype(BF16)

            fc1_block(0).start()
            fc2_block(0).start()
            own_copies(proj, proj_h, L_PROJ).start()

            @pl.loop(0, blocks)
            def _(b):
                slot = b % 2
                here = pl.ds(pl.multiple_of(b * block, block), block)

                @pl.when(b >= 2)
                def _():
                    local(L_PROBS, slot, probs.at[slot], probs_h.at[b - 2]).wait()

                for h in range(HEADS):
                    _, start, size = head_window(h, plan.head_width)
                    cols = slice(start, start + size)
                    q = proj[0, here, cols] * head_mask(h, plan.head_width)
                    scores[h] = mm_cols(q, proj[1, here, cols]) * factor + allowed[b // plan.halves]
                for h in range(HEADS):
                    score = scores[h]
                    grown = jnp.exp(score - jnp.max(score, axis=-1, keepdims=True))
                    weights = grown * (1.0 / jnp.sum(grown, axis=-1, keepdims=True))
                    probs[slot, h] = weights
                    lows[h] = weights.astype(BF16)

                def head_context(h):
                    _, start, size = head_window(h, plan.head_width)
                    return [mm(lows[h], proj[2, here, start : start + size] * head_mask(h, plan.head_width))]

                def put_context(j, tiles):
                    ctx[here, j * LANES : (j + 1) * LANES] = tiles[0].astype(BF16)

                join_heads(plan.head_width, head_context, put_context)
                local(L_PROBS, slot, probs.at[slot], probs_h.at[b]).start()

            own_copies(ctx, ctx_h, L_CTX).start()
            weight(3, wout_h).wait()
            f1[...] = mm(ctx[...], ring[3]) + bias[3]
            own_copies(f1, att_h, L_ATT).start()

            @pl.loop(0, clips)
            def _(c):
                for half in range(plan.halves):
                    for k in range(n):
                        here = rows_at(c, half, k)
                        middle = piece_of(xin, k, c, half) + mod[c, 2:3, :] * f1[here, :]
                        f2[here, :] = middle
                        normed, _ = unit(middle)
                        n2[here, :] = (normed * (1.0 + mod[c, 4:5, :]) + mod[c, 3:4, :]).astype(BF16)

            own_copies(f2, mid_h, L_MID).start()
            own_copies(n1, n1_h, L_N1).wait()
            own_copies(proj, proj_h, L_PROJ).wait()
            own_copies(ctx, ctx_h, L_CTX).wait()
            for b in (blocks - 2, blocks - 1):
                local(L_PROBS, b % 2, probs.at[b % 2], probs_h.at[b]).wait()

        def mlp(n2, cin, own_cot, n2_turned, dbr, padded, act, act_turned, dh, res):
            padded[...] = jnp.zeros_like(padded)
            n2_turned[...] = n2[...].T
            acc[...] = jnp.zeros_like(acc)
            own_cot.wait()
            for k in (1, 2, 3):
                arrive(R_CIN, k, cot_h, cin).wait_recv()

            @pl.loop(0, clips)
            def _(c):
                for half in range(plan.halves):
                    for k in range(n):
                        here = rows_at(c, half, k)
                        piece = piece_of(cin, k, c, half) * valid[c, k * plan.piece : (k + 1) * plan.piece, 0:1]
                        dres[here, :] = piece.astype(BF16)
                        low = (piece * mod[c, 5:6, :]).astype(BF16)
                        dbr[here, :] = low
                        sm[0, 7:8, :] += jnp.sum(low.astype(F32), axis=0, keepdims=True)

            for f in range(n):
                padded[:, f * pad2 : f * pad2 + width // n] = dbr[:, f * (width // n) : (f + 1) * (width // n)]
            own_copies(f1, att_h, L_ATT).wait()
            own_copies(f2, mid_h, L_MID).wait()

            @pl.loop(0, n)
            def _(f):
                slot = 2 * (f % 2)

                @pl.when(f < n - 1)
                def _():
                    fc1_block(f + 1).start()
                    fc2_block(f + 1).start()

                @pl.when(f == n - 1)
                def _():
                    weight(0, wout_h).start()
                    qkv_block(0, 1).start()

                fc1_block(f).wait()
                f2[...] = mm(n2[...], ring[slot])
                first_bias = bias[4 + f]

                @pl.when(f >= 1)
                def _():
                    local(L_ACT, 0, act, act_h.at[f - 1]).wait()

                @pl.loop(0, rows // half_rows)
                def _(i):
                    here = pl.ds(pl.multiple_of(i * half_rows, half_rows), half_rows)
                    hidden = f2[here, :] + first_bias
                    square = hidden * hidden
                    bent = jnp.tanh(0.7978845608028654 * hidden * (1.0 + 0.044715 * square))
                    act[here, :] = (0.5 * hidden * (1.0 + bent)).astype(BF16)
                    slope = 0.7978845608028654 * (1.0 + 3.0 * 0.044715 * square)
                    f2[here, :] = 0.5 * (1.0 + bent) + 0.5 * hidden * (1.0 - bent * bent) * slope

                local(L_ACT, 0, act, act_h.at[f]).start()

                do_in(P_A, f)

                @pl.when(f >= 1)
                def _():
                    c1(f - 1).wait_send()
                    c2(f - 1).wait_send()

                act_turned[...] = act[...].T
                @pl.loop(0, 2)
                def _(i):
                    lanes = pl.ds(pl.multiple_of(i * 2 * pad2, LANES), 2 * pad2)
                    res[...] = mm(act_turned[...], padded[:, lanes])
                    for mine in (False, True):
                        part = core if mine else 1 - core
                        at = pl.ds(pl.multiple_of(part * span2, 8), span2)
                        for j in range(2):
                            pieces = [res[at, j * pad2 + t * LANES : j * pad2 + (t + 1) * LANES] for t in range(3)]
                            pieces[2] = fold_tile(pieces[2], 4, 32)
                            row = 0
                            for piece in pieces:
                                slab = slice(row, row + piece.shape[0])
                                if mine:
                                    keep2[f // 2, f % 2, i, j, slab, :] = piece.astype(BF16)
                                else:
                                    stage[0, i, j, slab, :] = piece.astype(BF16)
                                row += piece.shape[0]

                c2(f).start()
                do_in(P_B, f)

                fc2_block(f).wait()
                dh[...] = (mm_cols(dbr[...], ring[slot + 1]) * f2[...]).astype(BF16)
                sm[0, pl.ds(3 + f, 1), :] = jnp.sum(dh[...].astype(F32), axis=0, keepdims=True)

                do_in(P_C, f)

                for first, tiles in ((0, 5), (5, 4)):
                    lanes = slice(first * LANES, (first + tiles) * LANES)
                    res[:, : tiles * LANES] = mm(n2_turned[...], dh[:, lanes])
                    for mine in (False, True):
                        part = core if mine else 1 - core
                        for i in range(2):
                            for j in range(2):
                                at = pl.ds(pl.multiple_of((4 * i + 2 * j + part) * span1, 8), span1)
                                for t in range(tiles):
                                    slab = slice((first + t) * span1, (first + t + 1) * span1)
                                    values = res[at, t * LANES : (t + 1) * LANES].astype(BF16)
                                    if mine:
                                        keep1[f // 2, f % 2, i, j, slab, :] = values
                                    else:
                                        stage[1, i, j, slab, :] = values
                c1(f).start()

                do_in(P_D, f)
                acc[...] += mm_cols(dh[...], ring[slot])
                do_in(P_E, f)

            local(L_ACT, 0, act, act_h.at[n - 1]).wait()

        def two_halves(n2):
            own_cot = local(L_OWN, 3, cot_h.at[:, :, mine], cin.at[0])
            own_cot.start()
            for k in (1, 2, 3):
                arrive(R_XIN, k, x_h, xin).wait_recv()
            for k in (3, 1, 2):
                arrive(R_CIN, k, cot_h, cin).start()
            pl.run_scoped(
                functools.partial(first_half, n2=n2),
                pltpu.VMEM((rows, width), BF16),
                pltpu.VMEM((3, rows, width), BF16),
                pltpu.VMEM((rows, width), BF16),
                pltpu.VMEM((HEADS, block, block), F32),
                pltpu.VMEM((HEADS, block, block), BF16),
                pltpu.VMEM((2, HEADS, block, block), F32),
            )
            pl.run_scoped(
                functools.partial(mlp, n2, cin, own_cot),
                pltpu.VMEM((width, rows), BF16),
                pltpu.VMEM((rows, width), BF16),
                pltpu.VMEM((rows, n * pad2), BF16),
                pltpu.VMEM((rows, width), BF16),
                pltpu.VMEM((width, rows), BF16),
                pltpu.VMEM((rows, width), BF16),
                pltpu.VMEM((width, 2 * pad2), F32),
            )

        pl.run_scoped(two_halves, pltpu.VMEM((rows, width), BF16))

        def rest(datt, proj):
            own_copies(mid_h, f2, L_MID).start()
            own_copies(proj_h, proj, L_PROJ).start()
            qkv_block(1, 3).start()
            own_copies(ctx_h, ring.at[2, :rows], L_CTX).start()

            def attend(dctx, probs, scores, lows):
                def middle(att):
                    own_copies(att_h, att, L_ATT).start()
                    own_copies(mid_h, f2, L_MID).wait()
                    own_copies(att_h, att, L_ATT).wait()

                    @pl.loop(0, rows // half_rows)
                    def _(i):
                        here = pl.ds(pl.multiple_of(i * half_rows, half_rows), half_rows)
                        c = i // parts_per_clip
                        normed, inverse = unit_rows(f2, here)
                        grad = acc[here, :]
                        sm[1 + c, 3:4, :] += jnp.sum(grad, axis=0, keepdims=True)
                        sm[1 + c, 4:5, :] += jnp.sum(grad * normed, axis=0, keepdims=True)
                        d_middle = dres[here, :].astype(F32) + unit_back(normed, inverse, grad * (1.0 + mod[c, 4:5, :]))
                        acc[here, :] = d_middle
                        sm[1 + c, 2:3, :] += jnp.sum(d_middle * att[here, :], axis=0, keepdims=True)
                        low = (d_middle * mod[c, 2:3, :]).astype(BF16)
                        datt[here, :] = low
                        sm[0, 2:3, :] += jnp.sum(low.astype(F32), axis=0, keepdims=True)

                pl.run_scoped(middle, pltpu.VMEM((rows, width), F32))
                do(P_M1)
                local(L_PROBS, 0, probs_h.at[0], probs.at[0]).start()

                c1(3).wait_send()
                c2(3).wait_send()

                def out_grad(right_o, res):
                    wide = width // n
                    right_o[...] = jnp.zeros_like(right_o)
                    for f in range(n):
                        right_o[f, :, :wide] = datt[:, f * wide : (f + 1) * wide]
                    own_copies(ctx_h, ring.at[2, :rows], L_CTX).wait()
                    turned = ring[2, :rows, :].T
                    ring[2, :, rows : 2 * rows] = turned

                    @pl.loop(0, n)
                    def _(f):
                        res[...] = mm(ring[2, :, rows : 2 * rows], right_o[f])
                        for mine in (False, True):
                            part = core if mine else 1 - core
                            for i in range(2):
                                for j in range(2):
                                    at = pl.ds(pl.multiple_of((4 * i + 2 * j + part) * span1, 8), span1)
                                    pieces = [res[at, t * LANES : (t + 1) * LANES] for t in range(3)]
                                    pieces[2] = fold_tile(pieces[2], 3, 32)
                                    row = i * so
                                    for piece in pieces:
                                        slab = slice(row, row + piece.shape[0])
                                        if mine:
                                            keepo[j, f // 2, f % 2, slab, :] = piece.astype(BF16)
                                        else:
                                            stage[j, f // 2, f % 2, slab, :] = piece.astype(BF16)
                                        row += piece.shape[0]

                pl.run_scoped(
                    out_grad, pltpu.VMEM((n, rows, pad2), BF16), pltpu.VMEM((width, pad2), F32)
                )
                co().start()
                do(P_WO)
                weight(0, wout_h).wait()
                dctx[...] = mm_cols(datt[...], ring[0]).astype(BF16)
                qkv_block(2, 0).start()
                do(P_DC)
                own_copies(proj_h, proj, L_PROJ).wait()

                @pl.loop(0, blocks)
                def _(b):
                    slot = b % 2
                    here = pl.ds(pl.multiple_of(b * block, block), block)

                    @pl.when(b < blocks - 1)
                    def _():
                        local(L_PROBS, 1 - slot, probs_h.at[b + 1], probs.at[1 - slot]).start()

                    local(L_PROBS, slot, probs_h.at[b], probs.at[slot]).wait()
                    for h in range(HEADS):
                        _, start, size = head_window(h, plan.head_width)
                        cols = slice(start, start + size)
                        scores[h] = mm_cols(dctx[here, cols] * head_mask(h, plan.head_width), proj[2, here, cols])
                    for h in range(HEADS):
                        weights = probs[slot, h]
                        mixed = weights * scores[h]
                        d_score = mixed - weights * jnp.sum(mixed, axis=-1, keepdims=True)
                        lows[0, h] = d_score.astype(BF16)
                        lows[1, h] = weights.astype(BF16)

                    def head_grads(h):
                        _, start, size = head_window(h, plan.head_width)
                        keep = head_mask(h, plan.head_width)
                        cols = slice(start, start + size)
                        return [
                            mm(lows[0, h], proj[1, here, cols] * keep),
                            mm_rows(lows[0, h], proj[0, here, cols] * keep),
                            mm_rows(lows[1, h], dctx[here, cols] * keep),
                        ]

                    def put_grads(j, tiles):
                        lanes = slice(j * LANES, (j + 1) * LANES)
                        for part in range(3):
                            values = tiles[part] if part == 2 else tiles[part] * factor
                            low = values.astype(BF16)
                            proj[part, here, lanes] = low
                            if part != 1:
                                at = part // 2
                                sm[0, at : at + 1, lanes] += jnp.sum(low.astype(F32), axis=0, keepdims=True)

                    join_heads(plan.head_width, head_grads, put_grads)

                    do_in(P_AB, b)

            pl.run_scoped(
                attend,
                pltpu.VMEM((rows, width), BF16),
                pltpu.VMEM((2, HEADS, block, block), F32),
                pltpu.VMEM((HEADS, block, block), F32),
                pltpu.VMEM((2, HEADS, block, block), BF16),
            )

            def weight_grads(right_q, left, res):
                own_copies(n1_h, left, L_N1).start()
                right_q[...] = jnp.zeros_like(right_q)
                for f in range(n):
                    low, high = f * wq, (f + 1) * wq
                    for part in range(3):
                        a, b = max(low, part * width), min(high, (part + 1) * width)
                        if a < b:
                            right_q[f, :, a - low : b - low] = proj[part, :, a - part * width : b - part * width]
                own_copies(n1_h, left, L_N1).wait()
                ring[2, :, :rows] = left[...].T
                do(P_PK)
                for z in range(4):
                    t2ax(z).wait_send()
                    t2by(z).wait_send()
                    t2ay(z).wait_send()
                    t2bx(z).wait_send()
                co().wait_send()

                @pl.loop(0, 2 * n)
                def _(step):
                    j, f = step // n, step % n
                    lines = pl.ds(pl.multiple_of(j * 4 * span1, 16), 4 * span1)

                    @pl.when(j == 1)
                    def _():
                        c0(0, f).wait_send()

                    res[...] = mm(ring[2, lines, :rows], right_q[f])
                    for mine in (False, True):
                        part = core if mine else 1 - core
                        for i in range(2):
                            at = pl.ds(pl.multiple_of((2 * i + part) * span1, 8), span1)
                            for t in range(padq // LANES):
                                slab = slice(t * span1, (t + 1) * span1)
                                piece = res[at, t * LANES : (t + 1) * LANES].astype(BF16)
                                if mine:
                                    keep2[j, i, f // 2, f % 2, slab, :] = piece
                                else:
                                    stage[i, f // 2, f % 2, slab, :] = piece
                    c0(j, f).start()
                    do_in(P_WQ, step)

            pl.run_scoped(
                weight_grads,
                pltpu.VMEM((n, rows, padq), BF16),
                pltpu.VMEM((rows, width), BF16),
                pltpu.VMEM((4 * span1, padq), F32),
            )

            f1[...] = jnp.zeros_like(f1)

            @pl.loop(0, 3)
            def _(i):
                slot = (2 * i + 1) % 5
                local(L_W, slot, fc2_h.at[pl.ds(0, width)], ring.at[slot]).wait()
                f1[...] += mm_cols(proj[i], ring[slot])
                do_in(P_IN, i)

            for f in range(n):
                weight(f, fc2_h.at[pl.ds(f * width, width)]).start()

            @pl.loop(0, clips)
            def _(c):
                for half in range(plan.halves):
                    for k in range(n):
                        here = rows_at(c, half, k)
                        normed, inverse = unit(piece_of(xin, k, c, half))
                        grad = f1[here, :]
                        sm[1 + c, 0:1, :] += jnp.sum(grad, axis=0, keepdims=True)
                        sm[1 + c, 1:2, :] += jnp.sum(grad * normed, axis=0, keepdims=True)
                        total = acc[here, :] + unit_back(normed, inverse, grad * (1.0 + mod[c, 1:2, :]))
                        rows_out[k, c, :, half * 8 : half * 8 + 8, :] = total.reshape(fl, 8, width).astype(BF16)

            row_own(1, rows_out, in_h).start()
            do(P_INE)

            def branch(acts):
                for f in range(n):
                    local(L_ACTS, f, act_h.at[f], acts.at[f]).start()
                f1[...] = jnp.zeros_like(f1)

                @pl.loop(0, n)
                def _(f):
                    local(L_ACTS, f, act_h.at[f], acts.at[f]).wait()
                    fc2_block_at(f).wait()
                    f1[...] += mm(acts[f], ring[f])
                    do_in(P_G, f)

            pl.run_scoped(branch, pltpu.VMEM((n, rows, width), BF16))

            @pl.loop(0, clips)
            def _(c):
                for half in range(plan.halves):
                    for k in range(n):
                        here = rows_at(c, half, k)
                        value = f1[here, :] + bias[8]
                        sm[1 + c, 5:6, :] += jnp.sum(dres[here, :].astype(F32) * value, axis=0, keepdims=True)
                        total = valid[c, k * plan.piece : (k + 1) * plan.piece, 0:1] * (
                            f2[here, :] + mod[c, 5:6, :] * value
                        )
                        cin[k, c, :, half * 8 : half * 8 + 8, :] = total.reshape(fl, 8, width).astype(BF16)

            row_own(0, cin, out_h).start()
            do(P_O)

            for k in (1, 2, 3):
                arrive(R_XIN, k, x_h, xin).wait_send()
                arrive(R_CIN, k, cot_h, cin).wait_send()
            row_own(1, rows_out, in_h).wait()
            row_own(0, cin, out_h).wait()
            for k in (1, 2, 3):
                row_send(R_OUT, k, out_h, True).wait_recv()
                row_send(R_IN, k, in_h, True).wait_recv()
                row_send(R_IN, k, in_h).wait_send()
                row_send(R_OUT, k, out_h).wait_send()
            for transfer in (smx_send, smy_send, mdx_send, mdy_send):
                transfer().wait_send()
            for i in range(3):
                smc_send(i).wait_send()
            for f in range(n):
                t1z(f).wait_send()
                c0(1, f).wait_send()
            for j in range(2):
                for transfer in (t1ax, t1by, t0ax, t0by, t0cz, t0ay, t0bx, t0cx, t0abz, t0cy):
                    transfer(j).wait_send()
            for transfer in (t2z, t2zz, t1ay, t1bx, t1zz, toax, toby, toay, tobx, toz, tozz, t0zz):
                transfer().wait_send()

        pl.run_scoped(rest, pltpu.VMEM((rows, width), BF16), pltpu.VMEM((3, rows, width), BF16))

    lanes = LANES
    image = shape((clips, fl, plan.patches, width), BF16)
    arriving = [
        (4, 2, 2, s1), (4, 2, 2, s1), (2, 2, 2, 2, s0), (2, 2, 2, 2 * so),
        (4, 2, a1), (4, 2, s1 - a1), (4, a1), (4, s1 - a1), (2, s1), (s1,),
        (4, 2, s1), (2, 2, a1), (2, 2, s1 - a1), (2, a1), (2, s1 - a1), (s1,),
        (2, 2, so), (2, 2, so), (2, so), (2, so), (2 * so,), (so,),
        (2, 2, 2, a0), (2, 2, 2, a0), (2, 2, 2, a0), (2, 2, a0), (2, 2, a0), (2, 2, a0), (2, 2 * a0), (2, a0), (s0,),
    ]
    vmem = pl.BlockSpec(memory_space=pltpu.VMEM)
    smalls = (1 + clips, 8, width)
    out_shape = (
        [image, image, shape((s1, lanes), F32), shape((s1, lanes), F32), shape((s0, lanes), F32), shape((so, lanes), F32), shape(smalls, F32)]
        + [shape(dims + (lanes,), BF16) for dims in arriving]
        + [shape((2,) + smalls, F32), shape((3, 8, width), F32)]
        + [shape((rows, width), BF16)] * 2
        + [shape((3, rows, width), BF16), shape((blocks, HEADS, block, block), F32)]
        + [shape((rows, width), F32)] * 2
        + [shape((n, rows, width), BF16)]
    )
    out_specs = [ANY, ANY] + [vmem] * 5 + [ANY] * (len(arriving) + 9)
    scratch = [
        pltpu.VMEM((2, 2, 2, 2, s1, lanes), BF16),
        pltpu.VMEM((2, 2, 2, 2, s1, lanes), BF16),
        pltpu.VMEM((2, 2, 2, 2 * so, lanes), BF16),
        pltpu.VMEM((2, 2, s1, lanes), BF16),
        pltpu.VMEM((2, 2, 2, s1, lanes), BF16),
        pltpu.VMEM((2, 2, s1, lanes), BF16),
        pltpu.VMEM((2, 2, s1, lanes), BF16),
        pltpu.VMEM((2, 4 * so, lanes), BF16),
        pltpu.VMEM((2, 4 * so, lanes), BF16),
        pltpu.VMEM((rows, width), BF16),
        pltpu.VMEM((rows, width), F32),
        pltpu.VMEM((rows, width), F32),
        pltpu.VMEM((rows, width), F32),
        pltpu.VMEM((4, width, width), BF16),
        pltpu.VMEM((n, clips, fl, own, width), BF16),
        pltpu.VMEM(smalls, F32),
        pltpu.VMEM(smalls, F32),
        pltpu.VMEM(smalls, F32),
        pltpu.VMEM((3, 8, width), F32),
        pltpu.VMEM((n, clips, fl, own, width), BF16),
        pltpu.VMEM((n, clips, fl, own, width), BF16),
        pltpu.VMEM((clips, 8, width), F32),
        pltpu.VMEM((9, 1, width), F32),
        pltpu.VMEM((clips, block, block), F32),
        pltpu.VMEM((clips, block, block), F32),
        pltpu.SemaphoreType.DMA((sum(REMOTE_SIZES),)),
        pltpu.SemaphoreType.DMA((sum(REMOTE_SIZES),)),
        pltpu.SemaphoreType.DMA((sum(LOCAL_SIZES),)),
    ]
    result = pl.pallas_call(
        body,
        in_specs=[ANY] * 6 + [vmem, pl.BlockSpec(memory_space=pltpu.SMEM)] + [vmem] * 4,
        out_specs=out_specs,
        out_shape=out_shape,
        scratch_shapes=scratch,
        compiler_params=pltpu.CompilerParams(
            vmem_limit_bytes=VMEM_LIMIT, collective_id=0, has_side_effects=True
        ),
        cost_estimate=cost(45e9, 200e6),
        name="layer",
    )(x, cotangent, qkv_weight, out_weight, fc1_weight, fc2_weight, modulation, counts, *biases)
    return result[:7]


def close(plan, images, small, sums, layouts):
    n, width, clips = plan.frame_axis, plan.width, plan.clips
    m = len(images)

    def body(*refs):
        refs = list(refs)

        def take(count):
            got = refs[:count]
            del refs[:count]
            return got

        image_in, (vectors,), sums_in = take(m), take(1), take(len(sums))
        image_out, outs_h = take(m), take(len(layouts))
        d_mod, d_qv, d_out, d_fc1, d_fc2 = take(5)
        ins, outs, (turn, held, sems) = take(len(sums)), take(len(layouts)), take(3)
        arrive = [pltpu.make_async_copy(sums_in[i], ins[i], sems.at[i]) for i in range(len(sums))]
        arrive += [pltpu.make_async_copy(image_in[i], held.at[i], sems.at[len(sums) + i]) for i in range(m)]
        there = len(arrive)
        leave = [pltpu.make_async_copy(outs[i], outs_h[i], sems.at[there + i]) for i in range(len(layouts))]
        leave += [pltpu.make_async_copy(held.at[i], image_out[i], sems.at[there + len(layouts) + i]) for i in range(m)]
        for copy in arrive:
            copy.start()
        frame = lax.axis_index("frame")

        def cut(first, k, size):
            low, high, pieces = k * size, (k + 1) * size, []
            while low < high:
                row, at = low // width, low % width
                end = min(width, at + high - low)
                pieces.append(vectors[first[0], first[1] + row : first[1] + row + 1, at:end])
                low += end - at
            return pieces[0] if len(pieces) == 1 else jnp.concatenate(pieces, axis=1)

        for k in range(n):

            @pl.when(frame == k)
            def _(k=k):
                for c in range(clips):
                    d_mod[c : c + 1, :] = cut((1 + c, 0), k, 6 * width // n)
                d_qv[...] = cut((0, 0), k, 2 * width // n).reshape(2 * width // n)
                d_out[...] = cut((0, 2), k, width // n).reshape(width // n)
                d_fc1[...] = cut((0, 3), k, width).reshape(width)
                d_fc2[...] = cut((0, 7), k, width // n).reshape(width // n)

        for at, (which, first, span, tiles, used, folds, turned) in enumerate(layouts):
            ref, out = ins[which], outs[at]
            arrive[which].wait()
            to = turn if turned else out
            for j in range(tiles):
                to[:, j * LANES : (j + 1) * LANES] = ref[first + j * span : first + (j + 1) * span, :]
            if used:
                tile = ref[first + tiles * span : first + tiles * span + span // folds, :]
                for g in range(folds):
                    moved = tile if g == 0 else pltpu.roll(tile, LANES - g * used, 1)
                    here = slice(g * (span // folds), (g + 1) * (span // folds))
                    to[here, tiles * LANES : tiles * LANES + used] = moved[:, :used]
            if turned:
                out[...] = turn[...].T
            leave[at].start()
        for i in range(m):
            arrive[len(sums) + i].wait()
            leave[len(layouts) + i].start()
        for copy in leave:
            copy.wait()

    dims = [(span, tiles * LANES + used) for _, _, span, tiles, used, _, _ in layouts]
    grads = [shape(d[::-1] if layout[-1] else d, F32) for d, layout in zip(dims, layouts)]
    sizes = (2 * width // n, width // n, width, width // n)
    vectors = [shape((clips, 6 * width // n), F32)] + [shape((size,), F32) for size in sizes]
    made = grads + vectors
    return pl.pallas_call(
        body,
        grid=(1,),
        in_specs=[ANY] * m + [whole(small.shape)] + [ANY] * len(sums),
        out_specs=[ANY] * (m + len(grads)) + [whole(s.shape) for s in vectors],
        out_shape=[shape(image.shape, image.dtype) for image in images] + made,
        scratch_shapes=[pltpu.VMEM(s.shape, s.dtype) for s in list(sums) + grads]
        + [
            pltpu.VMEM(dims[0], F32),
            pltpu.VMEM((m,) + images[0].shape, images[0].dtype),
            pltpu.SemaphoreType.DMA((2 * m + len(sums) + len(layouts),)),
        ],
        compiler_params=params(),
        cost_estimate=cost(0, 14e6),
        name="close",
    )(*images, small, *sums)


def fast_layer(
    mesh,
    block_input,
    modulation,
    frame_counts,
    qkv_weight,
    qv_bias,
    out_weight,
    out_bias,
    fc1_weight,
    fc1_bias,
    fc2_weight,
    fc2_bias,
    out_cotangent,
):
    plan = Plan(mesh, block_input.shape, qkv_weight.shape, fc1_weight.shape)
    n, width = plan.frame_axis, plan.width
    biases = (qv_bias, out_bias, fc1_bias, fc2_bias)
    block_output, input_grad, sum2, sum1, sum0, sumo, small = whole_layer(
        plan, block_input, out_cotangent, modulation, frame_counts, biases, qkv_weight, out_weight, fc1_weight, fc2_weight
    )
    span2, span1 = plan.ff // plan.clip_axis, width // plan.clip_axis
    (block_output, input_grad, fc2_turned, fc1_out, qkv_out, out_out, d_modulation, d_qv, d_out, d_fc1, d_fc2) = close(
        plan,
        (block_output, input_grad),
        small,
        (sum2, sum1, sum0, sumo),
        (
            (0, 0, span2, 2, 32, 4, True),
            (1, 0, span1, 9, 0, 1, False),
            (2, 0, span1, 6, 96, 1, False),
            (3, 0, span1, 2, 32, 3, False),
        ),
    )
    return (
        block_output,
        input_grad,
        d_modulation,
        qkv_out,
        d_qv,
        out_out,
        d_out,
        fc1_out,
        d_fc1,
        fc2_turned.T,
        d_fc2,
    )


def solution(mesh):
    placed = (
        P("clip", "frame", None, None),
        P("clip", None),
        P("clip"),
        P(),
        P(),
        P(),
        P(),
        P(),
        P(),
        P(),
        P(),
        P("clip", "frame", None, None),
    )
    def layer(*arrays):
        if fits(mesh, arrays[0].shape, arrays[3].shape, arrays[7].shape):
            return fast_layer(mesh, *arrays)
        return on_device(*arrays)

    return jax.shard_map(
        layer,
        mesh=mesh,
        in_specs=placed,
        out_specs=(
            P("clip", "frame", None, None),
            P("clip", "frame", None, None),
            P("clip", "frame"),
            P("clip", "frame"),
            P("frame"),
            P("clip", "frame"),
            P("frame"),
            P("clip", "frame"),
            P("frame"),
            P("clip", "frame"),
            P("frame"),
        ),
        check_vma=False,
    )
```
